256 devices in a mesh: rows: 32 (over z, x_lo, core), cols: 8 (over x_hi, y).
Axes of the slice: x: 4 (x_hi: 2, x_lo: 2; x = x_hi * 2 + x_lo), y: 4, z: 8, core: 2. Of those that a mesh axis runs over, the one named last changes fastest.
Arguments:
- frames_in: bfloat16 [3, 192, 64, 256], P(None, 'rows', 'cols'), may hold values from -6 to 6
- cotangent: bfloat16 [3, 192, 64, 256], P(None, 'rows', 'cols'), may hold values from -6 to 6
- core: float32 [110592], P(('rows', 'cols')), may hold values from -0.3 to 0.3
- moment_one: float32 [110592], P(('rows', 'cols')), may hold values from -0.6 to 0.6
- moment_two: float32 [110592], P(('rows', 'cols')), may hold values from 0.01 to 0.16
- u_in: bfloat16 [256, 64], replicated, may hold values from -0.375 to 0.375
- u_out: bfloat16 [256, 64], replicated, may hold values from -0.375 to 0.375
Outputs:
- frames_grad: bfloat16 [3, 192, 64, 256], P(None, 'rows', 'cols')
- core_next: float32 [110592], P(('rows', 'cols'))
- moment_one_next: float32 [110592], P(('rows', 'cols'))
- moment_two_next: float32 [110592], P(('rows', 'cols'))
- kernel_next: bfloat16 [27, 256, 256], replicated
The draws below stay inside these ranges and needn't reach their ends.
All inputs are finite; a program needn't handle non-finite values.
Results may differ from the reference program's by a relative error of at most 0.014.
Values may be sent and summed in bfloat16 or wider, within the bound.
No kernel may reach another device: no remote copies, remote signals or barrier semaphores. Data moves between devices by JAX's collectives and lax.ppermute only.
A program may use at most 64 MiB of HBM per device.

```python
import math
import jax
import jax.numpy as jnp
from jax import lax

C = 256
RANK = 64
TAPS = 27
FRAMES = 3
H = 192
W = 64
CORE = 110592
NCELLS = 36864


def shard_levels(stream_key, dims, pieces, least, top_value):
    level, own = 1.0, jax.random.fold_in(stream_key, 6)
    for dim, shards_of in pieces:
        draws = jnp.exp(jax.random.uniform(jax.random.fold_in(own, dim), (shards_of,), jnp.float32, least / len(pieces), top_value / len(pieces)))
        level = level * jnp.repeat(draws, dims[dim] // shards_of).reshape([-1 if axis == dim else 1 for axis in range(len(dims))])
    return level


def noise(stream_key, dims, width, most, pieces=(), dtype=jnp.bfloat16):
    loudness = shard_levels(stream_key, dims, pieces, -0.22, 0.18) if pieces else 1.0
    drawn = jax.random.normal(stream_key, dims, jnp.float32) * width * loudness
    return jnp.minimum(jnp.maximum(drawn, -most), most).astype(dtype)


def setup_inputs(seed: int = 0) -> dict:
    key_list = jax.random.split(jax.random.key(seed), 8)
    frames_in = noise(key_list[0], (FRAMES, H, W, C), 1.0, 6.0, ((1, 32), (2, 8)))
    cotangent = noise(key_list[1], (FRAMES, H, W, C), 1.0, 6.0, ((1, 32), (2, 8)))
    core = noise(key_list[2], (CORE,), 0.05, 0.3, ((0, 256),), jnp.float32)
    moment_one = noise(key_list[3], (CORE,), 0.1, 0.6, ((0, 256),), jnp.float32)
    moment_two = jnp.clip(jnp.exp(math.log(0.16) - 2.7725887 * jax.random.uniform(key_list[4], (CORE,), jnp.float32) ** shard_levels(key_list[4], (CORE,), ((0, 256),), -0.2, 0.2)), 0.01, 0.16)
    u_in = noise(key_list[5], (C, RANK), C ** -0.5, 0.375)
    u_out = noise(key_list[6], (C, RANK), C ** -0.5, 0.375)
    return {"frames_in": frames_in, "cotangent": cotangent, "core": core, "moment_one": moment_one, "moment_two": moment_two, "u_in": u_in, "u_out": u_out}


beta_one = 0.9
beta_two = 0.999
learn_rate = 0.06
epsilon = 1e-08
fix_one = 1.0 - 0.9 ** 10
fix_two = 1.0 - 0.999 ** 10

def build(flat_core, u_in, u_out):
    cube = flat_core.reshape(TAPS, RANK, RANK).astype(jnp.bfloat16)
    halfway = jnp.einsum('tpq,oq->tpo', cube.astype(jnp.float32), u_out.astype(jnp.float32), precision=lax.Precision.HIGHEST).astype(jnp.bfloat16)
    kernel = jnp.einsum('ip,tpo->tio', u_in.astype(jnp.float32), halfway.astype(jnp.float32), precision=lax.Precision.HIGHEST)
    return kernel.astype(jnp.bfloat16)

def offsets():
    return [(a, b, c) for a in range(3) for b in range(3) for c in range(3)]

def forward_sum(padded, kernel, frames, rows, cols):
    chans = padded.shape[3]
    total = jnp.zeros((frames * rows * cols, kernel.shape[2]), jnp.float32)
    for tap, (a, b, c) in enumerate(offsets()):
        piece = padded[a:a + frames, b:b + rows, c:c + cols, :].reshape(-1, chans)
        total = total + jnp.dot(piece, kernel[tap], preferred_element_type=jnp.float32)
    return total.reshape(frames, rows, cols, -1)

def backward_sum(padded, kernel, frames, rows, cols):
    chans = padded.shape[3]
    total = jnp.zeros((frames * rows * cols, kernel.shape[1]), jnp.float32)
    for tap, (a, b, c) in enumerate(offsets()):
        piece = padded[2 - a:2 - a + frames, 2 - b:2 - b + rows, 2 - c:2 - c + cols, :].reshape(-1, chans)
        total = total + lax.dot_general(piece, kernel[tap], (((1,), (1,)), ((), ())), preferred_element_type=jnp.float32)
    return total.reshape(frames, rows, cols, -1)

def core_terms(padded, slope, u_in, u_out, frames, rows, cols):
    chans = padded.shape[3]
    shape_pad = padded.shape
    in_proj = jnp.dot(padded.reshape(-1, chans), u_in, preferred_element_type=jnp.float32).astype(jnp.bfloat16)
    in_proj = in_proj.reshape(shape_pad[0], shape_pad[1], shape_pad[2], -1)
    out_proj = jnp.dot(slope.reshape(-1, chans), u_out, preferred_element_type=jnp.float32).astype(jnp.bfloat16)
    grads = []
    for tap, (a, b, c) in enumerate(offsets()):
        piece = in_proj[a:a + frames, b:b + rows, c:c + cols, :].reshape(-1, in_proj.shape[3])
        grads.append(lax.dot_general(piece, out_proj, (((0,), (0,)), ((), ())), preferred_element_type=jnp.float32))
    return jnp.stack(grads).reshape(-1)

def reference(frames_in, cotangent, core, moment_one, moment_two, u_in, u_out):
    frames, rows, cols = (frames_in.shape[0], frames_in.shape[1], frames_in.shape[2])
    kernel = build(core, u_in, u_out)
    width_pad = ((1, 1), (1, 1), (1, 1), (0, 0))
    padded = jnp.pad(frames_in, width_pad)
    pre = forward_sum(padded, kernel, frames, rows, cols)
    sig = jax.nn.sigmoid(pre)
    slope = (cotangent.astype(jnp.float32) * sig * (1.0 + pre * (1.0 - sig))).astype(jnp.bfloat16)
    slope_pad = jnp.pad(slope, width_pad)
    frames_grad = backward_sum(slope_pad, kernel, frames, rows, cols).astype(jnp.bfloat16)
    core_grad = core_terms(padded, slope, u_in, u_out, frames, rows, cols) / math.sqrt(NCELLS)
    moment_one_next = beta_one * moment_one + (1.0 - beta_one) * core_grad
    moment_two_next = beta_two * moment_two + (1.0 - beta_two) * core_grad * core_grad
    core_next = core - learn_rate * (moment_one_next / fix_one) / (jnp.sqrt(moment_two_next / fix_two) + epsilon)
    kernel_next = build(core_next, u_in, u_out)
    return (frames_grad, core_next, moment_one_next, moment_two_next, kernel_next)
```

```python
import jax
import jax.numpy as jnp
import numpy as np
from jax import lax
from jax.experimental import pallas as pl
from jax.experimental.pallas import tpu as pltpu
from jax.sharding import PartitionSpec as P

beta_one = 0.9
beta_two = 0.999
learn_rate = 0.06
epsilon = 1e-08
fix_one = 1.0 - 0.9**10
fix_two = 1.0 - 0.999**10

BF = jnp.bfloat16
F32 = jnp.float32
AXES = ("rows", "cols")

OWN = 432
FRAMES, ROWS, COLS = 3, 6, 8
CELLS = FRAMES * ROWS * COLS
SIDE = FRAMES * 8
TABLE = 864


def ring_tables():
    take = np.zeros((216, 512), np.float32)
    wrap = np.zeros((256, 128), np.float32)
    for r in range(8):
        for c in range(8):
            first = 27 * c // 8
            col = 32 * r + 4 * c
            for j in range(4):
                take[27 * r + first + j, col + j] = 1
            over = 48 * c % 128 + OWN - 512
            if over > 0:
                take[27 * r + first + 4, 256 + col] = 1
                wrap[col, :over] = 1
    return take, wrap


def dot(a, b):
    return jnp.dot(a, b, preferred_element_type=F32)


def dot_nt(a, b):
    return lax.dot_general(a, b, (((1,), (1,)), ((), ())), preferred_element_type=F32)


def dot_tn(a, b):
    return lax.dot_general(a, b, (((0,), (0,)), ((), ())), preferred_element_type=F32)


def lane(shape):
    return lax.broadcasted_iota(jnp.int32, shape, 1)


def sublane(shape):
    return lax.broadcasted_iota(jnp.int32, shape, 0)


def ring_shift():
    return lax.rem(lax.axis_index("cols") * 48, 128)


def to_ring(v, shift):
    turned = pltpu.roll(v, shift, axis=1)
    above = jnp.concatenate([turned[3:4], turned[0:3]], axis=0)
    return jnp.where(lane(v.shape) >= shift, turned, above)


def from_ring(v, shift):
    turned = pltpu.roll(v, lax.rem(128 - shift, 128), axis=1)
    below = jnp.concatenate([turned[1:4], turned[0:1]], axis=0)
    return jnp.where(lane(v.shape) < 128 - shift, turned, below)


def in_ring(shift):
    place = sublane((4, 128)) * 128 + lane((4, 128)) - shift
    place = jnp.where(place < 0, place + 512, place)
    return place < OWN


def load_flat(ref, scratch):
    scratch[...] = jnp.zeros_like(scratch)
    for k in range(3):
        scratch[k, :] = ref[pl.ds(128 * k, 128)]
    scratch[3, 0 : OWN - 384] = ref[pl.ds(384, OWN - 384)]
    return scratch[0:4, :]


def store_flat(ref, v):
    for k in range(3):
        ref[pl.ds(128 * k, 128)] = v[k]
    ref[pl.ds(384, OWN - 384)] = v[3, 0 : OWN - 384]


def spread(ref, v):
    block = jnp.concatenate([v, v, v, v], axis=0).astype(BF)
    for k in range(64):
        ref[16 * k : 16 * k + 16, :] = block


def start_kernel(core_ref, x_ref, send_ref, first_ref, last_ref, flat):
    spread(send_ref, to_ring(load_flat(core_ref, flat), ring_shift()))
    for f in range(FRAMES):
        first_ref[f] = x_ref[f, 0]
        last_ref[f] = x_ref[f, ROWS - 1]


def sides_kernel(own_ref, above_ref, below_ref, low_ref, high_ref, low, high):
    for f in range(FRAMES):
        for y in range(8):
            if y == 0:
                tile = above_ref[f]
            elif y == 7:
                tile = below_ref[f]
            else:
                tile = own_ref[f, y - 1]
            tile = tile.astype(F32)
            low[8 * f + y : 8 * f + y + 1, :] = tile[0:1, :]
            high[8 * f + y : 8 * f + y + 1, :] = tile[7:8, :]
    low_ref[...] = low[...].astype(BF)
    high_ref[...] = high[...].astype(BF)


def shifted(tile, left, right, bounds, period):
    at = lane(tile.shape) % period
    row = sublane(tile.shape)
    back = jnp.where(row == 0, left, pltpu.roll(tile, 1, axis=0))
    ahead = jnp.where(row == 7, right, pltpu.roll(tile, 7, axis=0))
    return jnp.where(at < bounds[0], back, jnp.where(at < bounds[1], tile, ahead))


def rank_kernel(
    x_ref, above_ref, below_ref, left_ref, right_ref, ut_ref, core_ref, one_ref, two_ref,
    q_ref, ring_ref, proj, edge, flat,
):
    pick_row = sublane((256, 64))
    pick_at = pick_row % 128
    pick = (lane((256, 64)) == (pick_at % 32) * 2 + pick_row // 128) & (pick_at < 96)
    wide = dot(pick.astype(BF), ut_ref[...]).astype(BF)

    def project(v):
        return dot_nt(v, wide).astype(BF).astype(F32)

    own = project(x_ref[...])
    above = project(above_ref[...])
    below = project(below_ref[...])
    for f in range(FRAMES):
        proj[f, 0] = above[8 * f : 8 * f + 8]
        proj[f, 7] = below[8 * f : 8 * f + 8]
        for y in range(ROWS):
            at = 48 * f + 8 * y
            proj[f, y + 1] = own[at : at + 8]
    edge[0] = project(left_ref[...])
    edge[1] = project(right_ref[...])
    for f in range(FRAMES):
        for y in range(8):
            k = 8 * f + y
            left = jnp.broadcast_to(edge[0, k : k + 1, :], (8, 256))
            right = jnp.broadcast_to(edge[1, k : k + 1, :], (8, 256))
            proj[f, y] = shifted(proj[f, y], left, right, (32, 64), 128)
    for b in range(3):
        q_ref[b, 0:48, :] = jnp.zeros((48, 256), BF)
        q_ref[b, 192:240, :] = jnp.zeros((48, 256), BF)
        for f in range(FRAMES):
            rows = proj[f, b : b + ROWS].reshape(48, 256)
            q_ref[b, 48 * f + 48 : 48 * f + 96, :] = rows.astype(BF)
    shift = ring_shift()
    for k, ref in enumerate((core_ref, one_ref, two_ref)):
        ring_ref[k] = to_ring(load_flat(ref, flat), shift)


def gather_table(got_ref, take_ref, wrap_ref, table_ref):
    over = wrap_ref[...] > 0
    take = take_ref[...]
    for g in range(4):
        block = got_ref[256 * g : 256 * g + 256, :]
        none = jnp.zeros_like(block)
        both = jnp.concatenate(
            [jnp.where(over, none, block), jnp.where(over, block, none)], axis=0
        )
        table_ref[216 * g : 216 * g + 216, :] = dot(take, both)


def forward_kernel(
    got_ref, q_ref, cot_ref, ot_ref, take_ref, give_ref, wrap_ref,
    send_ref, table_out, outp_ref, first_ref, last_ref, table, grads,
):
    gather_table(got_ref, take_ref, wrap_ref, table)
    table_out[...] = table[...].astype(BF)
    even = jnp.zeros((CELLS, 128), F32)
    odd = jnp.zeros((CELLS, 128), F32)
    for a in range(3):
        for b in range(3):
            k = 3 * a + b
            weights = table_out[96 * k : 96 * k + 96, :]
            rows = q_ref[b, 48 * a : 48 * a + CELLS, :]
            even = even + dot(rows[:, 0:96], weights)
            odd = odd + dot(rows[:, 128:224], weights)
    mid = (even[:, 0:64] + odd[:, 64:128]).astype(BF)
    pre = dot(mid, ot_ref[...])
    sig = jax.nn.sigmoid(pre)
    slope = (cot_ref[...].astype(F32) * sig * (1.0 + pre * (1.0 - sig))).astype(BF)
    ot = ot_ref[...]
    out_t = dot_nt(ot, slope).astype(BF)
    wide = jnp.concatenate([ot, ot, ot, ot], axis=0)
    outp = dot_nt(slope, wide)
    outp_ref[...] = outp.astype(BF)
    for f in range(FRAMES):
        first_ref[8 * f : 8 * f + 8, :] = outp[48 * f : 48 * f + 8].astype(BF)
        last_ref[8 * f : 8 * f + 8, :] = outp[48 * f + 40 : 48 * f + 48].astype(BF)
    for a in range(3):
        for b in range(3):
            k = 3 * a + b
            part = dot(out_t, q_ref[b, 48 * a : 48 * a + CELLS, :])
            stack = jnp.concatenate([part[:, 0:128], part[:, 128:256]], axis=0)
            grads[96 * k : 96 * k + 96, :] = stack.T[0:96, :]
    over = wrap_ref[...] > 0
    give = give_ref[...]
    for g in range(4):
        part = dot(give, grads[216 * g : 216 * g + 216, :].astype(BF))
        send_ref[256 * g : 256 * g + 256, :] = jnp.where(over, part[256:512], part[0:256]).astype(BF)


def backward_kernel(
    outp_ref, above_ref, below_ref, left_ref, right_ref, table_ref, ut_ref, grad_ref, tiles, edge, qs
):
    own = outp_ref[...].astype(F32)
    above = above_ref[...].astype(F32)
    below = below_ref[...].astype(F32)
    for f in range(FRAMES):
        tiles[f, 0] = above[8 * f : 8 * f + 8]
        tiles[f, 7] = below[8 * f : 8 * f + 8]
        for y in range(ROWS):
            at = 48 * f + 8 * y
            tiles[f, y + 1] = own[at : at + 8]
    edge[0] = left_ref[...].astype(F32)
    edge[1] = right_ref[...].astype(F32)
    for f in range(FRAMES):
        for y in range(8):
            k = 8 * f + y
            left = jnp.broadcast_to(edge[0, k : k + 1, :], (8, 256))
            right = jnp.broadcast_to(edge[1, k : k + 1, :], (8, 256))
            tiles[f, y] = shifted(tiles[f, y], left, right, (64, 128), 256)
    for b in range(3):
        qs[b, 0:48, :] = jnp.zeros((48, 256), BF)
        qs[b, 192:240, :] = jnp.zeros((48, 256), BF)
        for f in range(FRAMES):
            rows = tiles[f, b : b + ROWS].reshape(48, 256)
            qs[b, 48 * f + 48 : 48 * f + 96, :] = rows.astype(BF)
    total = jnp.zeros((CELLS, 64), F32)
    for a in range(3):
        for b in range(3):
            rows = qs[2 - b, 48 * (2 - a) : 48 * (2 - a) + CELLS, :]
            for c in range(3):
                t = 9 * a + 3 * b + c
                part = table_ref[32 * t : 32 * t + 32, :]
                cube = jnp.concatenate([part[:, 0:64], part[:, 64:128]], axis=0)
                piece = rows[:, 64 * (2 - c) : 64 * (2 - c) + 64]
                total = total + dot_nt(piece, cube)
    pick_row = sublane((64, 64))
    pick = lane((64, 64)) == (pick_row % 32) * 2 + pick_row // 32
    ut = dot(pick.astype(BF), ut_ref[...]).astype(BF)
    grad_ref[...] = dot(total.astype(BF), ut).astype(BF)


def adam_kernel(got_ref, ring_ref, send_ref, next_ref):
    total = jnp.zeros((8, 128), F32)
    for g in range(8):
        part = got_ref[128 * g : 128 * g + 128, :].astype(F32)
        total = total + part.reshape(16, 8, 128).sum(axis=0)
    grad = (total[0:4] + total[4:8]) * (1.0 / 192.0)
    core, one, two = ring_ref[0], ring_ref[1], ring_ref[2]
    one = beta_one * one + (1.0 - beta_one) * grad
    two = beta_two * two + (1.0 - beta_two) * grad * grad
    core = core - learn_rate * (one / fix_one) / (jnp.sqrt(two / fix_two) + epsilon)
    next_ref[0] = core
    next_ref[1] = one
    next_ref[2] = two
    spread(send_ref, jnp.where(in_ring(ring_shift()), core, 0.0))


def flat_kernel(next_ref, core_ref, one_ref, two_ref):
    shift = ring_shift()
    for k, ref in enumerate((core_ref, one_ref, two_ref)):
        store_flat(ref, from_ring(next_ref[k], shift))


def build_kernel(got_ref, ut_ref, ot_ref, take_ref, wrap_ref, out_ref, table, half, result, sems):
    gather_table(got_ref, take_ref, wrap_ref, table)
    cube = table[...].astype(BF)
    even = dot(cube[:, 0:64], ot_ref[...]).astype(BF)
    odd = dot(cube[:, 64:128], ot_ref[...]).astype(BF)
    for t in range(27):
        half[t, 0:32, :] = even[32 * t : 32 * t + 32]
        half[t, 32:64, :] = odd[32 * t : 32 * t + 32]
    pick_row = sublane((64, 64))
    pick = lane((64, 64)) == (pick_row % 32) * 2 + pick_row // 32
    ut = dot(pick.astype(BF), ut_ref[...]).astype(BF)
    u = ut.astype(F32).T.astype(BF)
    for a in range(9):
        for t in range(3 * a, 3 * a + 3):
            result[t] = dot(u, half[t]).astype(BF)
        pltpu.make_async_copy(
            result.at[pl.ds(3 * a, 3)], out_ref.at[pl.ds(3 * a, 3)], sems.at[a]
        ).start()
    for a in range(9):
        pltpu.make_async_copy(
            result.at[pl.ds(3 * a, 3)], out_ref.at[pl.ds(3 * a, 3)], sems.at[a]
        ).wait()


def call(kernel, outs, scratch, args, out_specs=None, flops=10**7, nbytes=10**6):
    whole = pl.BlockSpec(memory_space=pltpu.VMEM)
    return pl.pallas_call(
        kernel,
        out_shape=[jax.ShapeDtypeStruct(shape, dtype) for shape, dtype in outs],
        in_specs=[whole] * len(args),
        out_specs=out_specs or [whole] * len(outs),
        scratch_shapes=scratch,
        compiler_params=pltpu.CompilerParams(vmem_limit_bytes=32 << 20),
        cost_estimate=pl.CostEstimate(flops=flops, bytes_accessed=nbytes, transcendentals=0),
    )(*args)


def both_ways(high, low, axis):
    count = lax.axis_size(axis)
    forward = [(i, i + 1) for i in range(count - 1)]
    backward = [(i + 1, i) for i in range(count - 1)]
    return lax.ppermute(high, axis, forward), lax.ppermute(low, axis, backward)


def exchange(x):
    return lax.all_to_all(x, AXES, 0, 0, tiled=True)


def body(frames_in, cotangent, core, moment_one, moment_two, u_in, u_out):
    take_np, wrap_np = ring_tables()
    take = jnp.asarray(take_np, BF)
    give = jnp.asarray(take_np.T.copy(), BF)
    wrap = jnp.asarray(wrap_np, F32)
    ut, ot = u_in.T, u_out.T
    vm = pltpu.VMEM

    send, first, last = call(
        start_kernel,
        [((1024, 128), BF), ((FRAMES, 8, 256), BF), ((FRAMES, 8, 256), BF)],
        [vm((8, 128), F32)],
        [core, frames_in],
    )
    got = exchange(send)
    above, below = both_ways(last, first, "rows")
    low, high = call(
        sides_kernel, [((SIDE, 256), BF)] * 2, [vm((SIDE, 256), F32)] * 2, [frames_in, above, below]
    )
    left, right = both_ways(high, low, "cols")
    q, ring = call(
        rank_kernel,
        [((3, 240, 256), BF), ((3, 4, 128), F32)],
        [vm((FRAMES, 8, 8, 256), F32), vm((2, SIDE, 256), F32), vm((8, 128), F32)],
        [
            frames_in.reshape(CELLS, 256), above.reshape(SIDE, 256), below.reshape(SIDE, 256),
            left, right, ut, core, moment_one, moment_two,
        ],
    )
    send, table, outp, first, last = call(
        forward_kernel,
        [
            ((1024, 128), BF), ((TABLE, 128), BF), ((CELLS, 256), BF), ((SIDE, 256), BF), ((SIDE, 256), BF),
        ],
        [vm((TABLE, 128), F32), vm((TABLE, 128), F32)],
        [got, q, cotangent.reshape(CELLS, 256), ot, take, give, wrap],
    )
    got = exchange(send)
    above, below = both_ways(last, first, "rows")
    low, high = call(
        sides_kernel,
        [((SIDE, 256), BF)] * 2,
        [vm((SIDE, 256), F32)] * 2,
        [
            outp.reshape(FRAMES, ROWS, COLS, 256), above.reshape(FRAMES, 8, 256), below.reshape(FRAMES, 8, 256),
        ],
    )
    left, right = both_ways(high, low, "cols")
    (frames_grad,) = call(
        backward_kernel,
        [((CELLS, 256), BF)],
        [vm((FRAMES, 8, 8, 256), F32), vm((2, SIDE, 256), F32), vm((3, 240, 256), BF)],
        [outp, above, below, left, right, table, ut],
    )
    send, latest = call(adam_kernel, [((1024, 128), BF), ((3, 4, 128), F32)], [], [got, ring])
    got = exchange(send)
    core_next, one_next, two_next = call(flat_kernel, [((OWN,), F32)] * 3, [], [latest])
    (kernel_next,) = call(
        build_kernel,
        [((27, 256, 256), BF)],
        [
            vm((TABLE, 128), F32), vm((27, 64, 256), BF), vm((27, 256, 256), BF),
            pltpu.SemaphoreType.DMA((9,)),
        ],
        [got, ut, ot, take, wrap],
        out_specs=[pl.BlockSpec(memory_space=pl.ANY)],
    )
    frames_grad = frames_grad.reshape(FRAMES, ROWS, COLS, 256)
    return frames_grad, core_next, one_next, two_next, kernel_next


def solution(mesh):
    in_specs = (
        P(None, "rows", "cols", None),
        P(None, "rows", "cols", None),
        P(AXES),
        P(AXES),
        P(AXES),
        P(),
        P(),
    )
    out_specs = (
        P(None, "rows", "cols", None),
        P(AXES),
        P(AXES),
        P(AXES),
        P(),
    )
    return jax.shard_map(body, mesh=mesh, in_specs=in_specs, out_specs=out_specs, check_vma=False)
```

```python
import jax
import jax.numpy as jnp
import numpy as np
from jax import lax
from jax.experimental import pallas as pl
from jax.experimental.pallas import tpu as pltpu
from jax.sharding import PartitionSpec as P

beta_one = 0.9
beta_two = 0.999
learn_rate = 0.06
epsilon = 1e-08
fix_one = 1.0 - 0.9**10
fix_two = 1.0 - 0.999**10

BF = jnp.bfloat16
F32 = jnp.float32
AXES = ("rows", "cols")

OWN = 432
FRAMES, ROWS, COLS = 3, 6, 8
CELLS = FRAMES * ROWS * COLS
SIDE = FRAMES * 8
TABLE = 864


RELAYS = ((7, 0, 0), (4, 0, 0), (3, 3, 64))
SLOTS = ((0, 24, -8), (24, 24, 8), (48, 18, -1), (66, 18, 1), (84, 3, -9), (87, 3, -7), (90, 3, 7), (93, 3, 9))


def ring_tables():
    take = np.zeros((216, 512), np.float32)
    give = np.zeros((512, 240), np.float32)
    over = np.zeros((256, 128), np.float32)
    for r in range(8):
        for c in range(8):
            first = 27 * r + 27 * c // 8
            col = 32 * r + 4 * c
            for j in range(4):
                take[first + j, col + j] = 1
                give[col + j, first + j] = 1
            wrapped = 48 * c % 128 + OWN - 512
            if wrapped > 0:
                take[first + 4, 256 + col] = 1
                give[256 + col, first + 4] = 1
                over[col, :wrapped] = 1
        for k, (c, j, at) in enumerate(RELAYS):
            col = 32 * r + 4 * c + j
            give[256 + col, 216 + 8 * k + r] = 1
            over[col, at : at + 64] = 1
    return take, give, over


def dot(a, b):
    return jnp.dot(a, b, preferred_element_type=F32)


def dot_nt(a, b):
    return lax.dot_general(a, b, (((1,), (1,)), ((), ())), preferred_element_type=F32)


def dot_tn(a, b):
    return lax.dot_general(a, b, (((0,), (0,)), ((), ())), preferred_element_type=F32)


def lane(shape):
    return lax.broadcasted_iota(jnp.int32, shape, 1)


def sublane(shape):
    return lax.broadcasted_iota(jnp.int32, shape, 0)


def ring_shift():
    return lax.rem(lax.axis_index("cols") * 48, 128)


def to_ring(v, shift):
    turned = pltpu.roll(v, shift, axis=1)
    above = jnp.concatenate([turned[3:4], turned[0:3]], axis=0)
    return jnp.where(lane(v.shape) >= shift, turned, above)


def from_ring(v, shift):
    turned = pltpu.roll(v, lax.rem(128 - shift, 128), axis=1)
    below = jnp.concatenate([turned[1:4], turned[0:1]], axis=0)
    return jnp.where(lane(v.shape) < 128 - shift, turned, below)


def in_ring(shift):
    place = sublane((4, 128)) * 128 + lane((4, 128)) - shift
    place = jnp.where(place < 0, place + 512, place)
    return place < OWN


def load_flat(ref, scratch):
    scratch[...] = jnp.zeros_like(scratch)
    for k in range(3):
        scratch[k, :] = ref[pl.ds(128 * k, 128)]
    scratch[3, 0 : OWN - 384] = ref[pl.ds(384, OWN - 384)]
    return scratch[0:4, :]


def store_flat(ref, v):
    for k in range(3):
        ref[pl.ds(128 * k, 128)] = v[k]
    ref[pl.ds(384, OWN - 384)] = v[3, 0 : OWN - 384]


def fetch(pairs, sems):
    copies = [pltpu.make_async_copy(src, dst, sems.at[k]) for k, (src, dst) in enumerate(pairs)]
    for copy in copies:
        copy.start()
    return copies


def start_kernel(core_ref, x_ref, send_ref, first_ref, last_ref, own, flat, sems):
    copies = fetch(
        ((core_ref, own), (x_ref.at[:, 0], first_ref), (x_ref.at[:, ROWS - 1], last_ref)), sems
    )
    copies[0].wait()
    v = to_ring(load_flat(own, flat), ring_shift())
    block = jnp.concatenate([v, v, v, v], axis=0).astype(BF)
    for k in range(64):
        send_ref[16 * k : 16 * k + 16, :] = block
    copies[1].wait()
    copies[2].wait()


def sides_kernel(own_ref, above_ref, below_ref, low_ref, high_ref, low, high):
    for f in range(FRAMES):
        for y in range(8):
            if y == 0:
                tile = above_ref[f]
            elif y == 7:
                tile = below_ref[f]
            else:
                tile = own_ref[f, y - 1]
            tile = tile.astype(F32)
            low[8 * f + y : 8 * f + y + 1, :] = tile[0:1, :]
            high[8 * f + y : 8 * f + y + 1, :] = tile[7:8, :]
    low_ref[...] = low[...].astype(BF)
    high_ref[...] = high[...].astype(BF)


def shifted(tile, left, right, bounds, period):
    at = lane(tile.shape) % period
    row = sublane(tile.shape)
    back = jnp.where(row == 0, left, pltpu.roll(tile, 1, axis=0))
    ahead = jnp.where(row == 7, right, pltpu.roll(tile, 7, axis=0))
    return jnp.where(at < bounds[0], back, jnp.where(at < bounds[1], tile, ahead))


def fetch_kernel(
    x_ref, ut_ref, ot_ref, cot_ref, core_ref, one_ref, two_ref, take_ref, give_ref, over_ref,
    own_ref, wide_ref, utp_ref, u_ref, ring_ref, ot_out, cot_out, take_out, give_out, over_out,
    x, ut, owns, flat, sems,
):
    copies = fetch(
        (
            (ut_ref, ut), (x_ref, x), (core_ref, owns[0]), (one_ref, owns[1]), (two_ref, owns[2]),
            (take_ref, take_out), (give_ref, give_out), (over_ref, over_out), (ot_ref, ot_out), (cot_ref, cot_out),
        ),
        sems,
    )
    row = sublane((256, 64))
    at = row % 128
    pick = (lane((256, 64)) == (at % 32) * 2 + row // 128) & (at < 96)
    half_row = sublane((64, 64))
    half_pick = lane((64, 64)) == (half_row % 32) * 2 + half_row // 32
    copies[0].wait()
    wide = dot(pick.astype(BF), ut[...]).astype(BF)
    wide_ref[...] = wide
    utp = dot(half_pick.astype(BF), ut[...])
    utp_ref[...] = utp.astype(BF)
    u_ref[...] = utp.T.astype(BF)
    copies[1].wait()
    own_ref[...] = dot_nt(x[...], wide).astype(BF).astype(F32)
    shift = ring_shift()
    for k in range(3):
        copies[2 + k].wait()
        ring_ref[k] = to_ring(load_flat(owns[k], flat), shift)
    for k in range(5, 10):
        copies[k].wait()


def stack_rows(tiles, out_ref):
    for b in range(3):
        out_ref[b, 0:48, :] = jnp.zeros((48, 256), BF)
        out_ref[b, 192:240, :] = jnp.zeros((48, 256), BF)
        for f in range(FRAMES):
            rows = tiles[f, b : b + ROWS].reshape(48, 256)
            out_ref[b, 48 * f + 48 : 48 * f + 96, :] = rows.astype(BF)


def rank_kernel(own_ref, wide_ref, above_ref, below_ref, left_ref, right_ref, q_ref, tiles, edge):
    wide = wide_ref[...]

    def project(v):
        return dot_nt(v, wide).astype(BF).astype(F32)

    above = project(above_ref[...])
    below = project(below_ref[...])
    for f in range(FRAMES):
        tiles[f, 0] = above[8 * f : 8 * f + 8]
        tiles[f, 7] = below[8 * f : 8 * f + 8]
        for y in range(ROWS):
            at = 48 * f + 8 * y
            tiles[f, y + 1] = own_ref[at : at + 8, :]
    edge[0] = project(left_ref[...])
    edge[1] = project(right_ref[...])
    for f in range(FRAMES):
        for y in range(8):
            k = 8 * f + y
            left = jnp.broadcast_to(edge[0, k : k + 1, :], (8, 256))
            right = jnp.broadcast_to(edge[1, k : k + 1, :], (8, 256))
            tiles[f, y] = shifted(tiles[f, y], left, right, (32, 64), 128)
    stack_rows(tiles, q_ref)


def gather_table(got_ref, take_ref, over_ref, table_ref):
    over = over_ref[...] > 0
    take = take_ref[...]
    for g in range(4):
        block = got_ref[256 * g : 256 * g + 256, :]
        none = jnp.zeros_like(block)
        both = jnp.concatenate(
            [jnp.where(over, none, block), jnp.where(over, block, none)], axis=0
        )
        table_ref[216 * g : 216 * g + 216, :] = dot(take, both)


def forward_kernel(
    got_ref, q_ref, cot_ref, ot_ref, take_ref, give_ref, over_ref,
    send_ref, table_out, outp_ref, table, grads, border, pixels,
):
    gather_table(got_ref, take_ref, over_ref, table)
    table_out[...] = table[...].astype(BF)
    even = jnp.zeros((CELLS, 128), F32)
    odd = jnp.zeros((CELLS, 128), F32)
    for a in range(3):
        for b in range(3):
            k = 3 * a + b
            weights = table_out[96 * k : 96 * k + 96, :]
            rows = q_ref[b, 48 * a : 48 * a + CELLS, :]
            even = even + dot(rows[:, 0:96], weights)
            odd = odd + dot(rows[:, 128:224], weights)
    mid = (even[:, 0:64] + odd[:, 64:128]).astype(BF)
    pre = dot(mid, ot_ref[...])
    sig = jax.nn.sigmoid(pre)
    slope = (cot_ref[...].astype(F32) * sig * (1.0 + pre * (1.0 - sig))).astype(BF)
    ot = ot_ref[...]
    out_t = dot_nt(ot, slope).astype(BF)
    wide = jnp.concatenate([ot, ot, ot, ot], axis=0)
    outp = dot_nt(slope, wide).astype(BF).astype(F32)
    outp_ref[...] = outp
    border[...] = outp[:, 0:128]
    for f in range(FRAMES):
        pixels[8 * f : 8 * f + 8, :] = border[48 * f : 48 * f + 8, :]
        pixels[24 + 8 * f : 32 + 8 * f, :] = border[48 * f + 40 : 48 * f + 48, :]
    pixels[48:66, :] = border[pl.ds(0, 18, stride=8), :]
    pixels[66:84, :] = border[pl.ds(7, 18, stride=8), :]
    for k, cell in enumerate((0, 7, 40, 47)):
        pixels[84 + 3 * k : 87 + 3 * k, :] = border[pl.ds(cell, 3, stride=48), :]
    for a in range(3):
        for b in range(3):
            k = 3 * a + b
            part = dot(out_t, q_ref[b, 48 * a : 48 * a + CELLS, :])
            stack = jnp.concatenate([part[:, 0:128], part[:, 128:256]], axis=0)
            grads[96 * k : 96 * k + 96, :] = stack.T[0:96, :]
    over = over_ref[...] > 0
    give = give_ref[...]
    for g in range(4):
        source = [grads[216 * g : 216 * g + 216, :]]
        for k in range(3):
            source.append(pixels[32 * k + 8 * g : 32 * k + 8 * g + 8, :])
        part = dot(give, jnp.concatenate(source, axis=0).astype(BF))
        send_ref[256 * g : 256 * g + 256, :] = jnp.where(over, part[256:512], part[0:256]).astype(BF)


def adam_kernel(got_ref, ring_ref, send_ref, next_ref, passed):
    total = jnp.zeros((8, 128), F32)
    passed[0:40, :] = jnp.zeros((40, 128), F32)
    passed[1064:1104, :] = jnp.zeros((40, 128), F32)
    for g in range(8):
        part = got_ref[128 * g : 128 * g + 128, :].astype(F32)
        passed[128 * g + 40 : 128 * g + 168, :] = part
        total = total + part.reshape(16, 8, 128).sum(axis=0)
    grad = (total[0:4] + total[4:8]) * (1.0 / 192.0)
    core, one, two = ring_ref[0], ring_ref[1], ring_ref[2]
    one = beta_one * one + (1.0 - beta_one) * grad
    two = beta_two * two + (1.0 - beta_two) * grad * grad
    core = core - learn_rate * (one / fix_one) / (jnp.sqrt(two / fix_two) + epsilon)
    next_ref[0] = core
    next_ref[1] = one
    next_ref[2] = two
    own = jnp.where(in_ring(ring_shift()), core, 0.0)
    own = jnp.concatenate([own, own], axis=0)
    row, col = lax.axis_index("rows"), lax.axis_index("cols")
    slot, mask = row, jnp.zeros((8, 128), jnp.bool_)
    for k, (c, j, at) in enumerate(RELAYS):
        slot = slot + jnp.where(col == c, 32 * k, 0)
        spot = (sublane((8, 128)) % 4 == j) & (lane((8, 128)) // 64 == at // 64)
        mask = mask | (spot & (jnp.full((8, 128), col, jnp.int32) == c))
    move = 0
    for first, count, offset in SLOTS:
        move = move + jnp.where((slot >= first) & (slot < first + count), 4 * offset, 0)
    for k in range(64):
        upper = passed[pl.ds(40 + 16 * k - move, 8), :]
        lower = passed[pl.ds(48 + 16 * k - move, 8), :]
        block = jnp.concatenate([jnp.where(mask, upper, own), jnp.where(mask, lower, own)], axis=0)
        send_ref[16 * k : 16 * k + 16, :] = block.astype(BF)


def flat_kernel(next_ref, core_ref, one_ref, two_ref):
    shift = ring_shift()
    for k, ref in enumerate((core_ref, one_ref, two_ref)):
        store_flat(ref, from_ring(next_ref[k], shift))


def finish_kernel(
    got_ref, outp_ref, old_ref, utp_ref, u_ref, ot_ref, take_ref, over_ref,
    out_ref, grad_ref, table, half, result, got, pixels, tiles, qs, sems,
):
    gather_table(got_ref, take_ref, over_ref, table)
    cube = table[...].astype(BF)
    even = dot(cube[:, 0:64], ot_ref[...]).astype(BF)
    odd = dot(cube[:, 64:128], ot_ref[...]).astype(BF)
    for t in range(27):
        half[t, 0:32, :] = even[32 * t : 32 * t + 32]
        half[t, 32:64, :] = odd[32 * t : 32 * t + 32]
    u = u_ref[...]

    def store(a):
        part = pl.ds(3 * a, 3)
        return pltpu.make_async_copy(result.at[part], out_ref.at[part], sems.at[a])

    for a in range(9):
        for t in range(3 * a, 3 * a + 3):
            result[t] = dot(u, half[t]).astype(BF)
        store(a).start()

    for g in range(4):
        got[256 * g : 256 * g + 256, :] = got_ref[256 * g : 256 * g + 256, :].astype(F32)
    for k, (c, j, at) in enumerate(RELAYS):
        rows = got[pl.ds(4 * c + j, 32, stride=32), :]
        pixels[32 * k : 32 * k + 32, 0:128] = jnp.where(lane((32, 128)) // 64 == at // 64, rows, 0.0)
    spread = (sublane((128, 256)) % 64 == lane((128, 256)) % 64).astype(BF)
    pixels[...] = dot(pixels[:, 0:128].astype(BF), spread)
    row, col = lax.axis_index("rows"), lax.axis_index("cols")
    zero = jnp.zeros((8, 256), F32)

    def inside(flag, v):
        return jnp.where(jnp.full((8, 256), flag.astype(jnp.int32), jnp.int32) > 0, v, zero)

    def spot(k):
        return jnp.broadcast_to(pixels[k : k + 1, :], (8, 256))

    for f in range(FRAMES):
        for y in range(8):
            if y == 0:
                tile, left, right = pixels[24 + 8 * f : 32 + 8 * f, :], spot(93 + f), spot(90 + f)
            elif y == 7:
                tile, left, right = pixels[8 * f : 8 * f + 8, :], spot(87 + f), spot(84 + f)
            else:
                at = 48 * f + 8 * (y - 1)
                tile = outp_ref[at : at + 8, :]
                left, right = spot(66 + 6 * f + y - 1), spot(48 + 6 * f + y - 1)
            tile = shifted(tile, inside(col > 0, left), inside(col < 7, right), (64, 128), 256)
            if y == 0:
                tile = inside(row > 0, tile)
            elif y == 7:
                tile = inside(row < 31, tile)
            tiles[f, y] = tile
    stack_rows(tiles, qs)
    total = jnp.zeros((CELLS, 64), F32)
    for a in range(3):
        for b in range(3):
            rows = qs[2 - b, 48 * (2 - a) : 48 * (2 - a) + CELLS, :]
            for c in range(3):
                t = 9 * a + 3 * b + c
                part = old_ref[32 * t : 32 * t + 32, :]
                cube = jnp.concatenate([part[:, 0:64], part[:, 64:128]], axis=0)
                piece = rows[:, 64 * (2 - c) : 64 * (2 - c) + 64]
                total = total + dot_nt(piece, cube)
    grad_ref[...] = dot(total.astype(BF), utp_ref[...]).astype(BF)
    for a in range(9):
        store(a).wait()


def call(kernel, args, outs, scratch, flops=10**7):
    def spec(far):
        return pl.BlockSpec(memory_space=pl.ANY if far else pltpu.VMEM)

    return pl.pallas_call(
        kernel,
        out_shape=[jax.ShapeDtypeStruct(shape, dtype) for shape, dtype, _ in outs],
        in_specs=[spec(far) for _, far in args],
        out_specs=[spec(far) for _, _, far in outs],
        scratch_shapes=scratch,
        compiler_params=pltpu.CompilerParams(vmem_limit_bytes=32 << 20),
        cost_estimate=pl.CostEstimate(flops=flops, bytes_accessed=10**5, transcendentals=0),
    )(*[arg for arg, _ in args])


def near(*args):
    return [(arg, False) for arg in args]


def far(*args):
    return [(arg, True) for arg in args]


def both_ways(high, low, axis):
    count = lax.axis_size(axis)
    forward = [(i, i + 1) for i in range(count - 1)]
    backward = [(i + 1, i) for i in range(count - 1)]
    return lax.ppermute(high, axis, forward), lax.ppermute(low, axis, backward)


def exchange(x):
    return lax.all_to_all(x, AXES, 0, 0, tiled=True)


def body(frames_in, cotangent, core, moment_one, moment_two, u_in, u_out):
    take, give, over = ring_tables()
    take, give, over = jnp.asarray(take, BF), jnp.asarray(give, BF), jnp.asarray(over, F32)
    vm, dma = pltpu.VMEM, pltpu.SemaphoreType.DMA
    edge = (FRAMES, 8, 256)

    send, first, last = call(
        start_kernel,
        far(core, frames_in),
        [((1024, 128), BF, False), (edge, BF, False), (edge, BF, False)],
        [vm((OWN,), F32), vm((8, 128), F32), dma((3,))],
    )
    above, below = both_ways(last, first, "rows")
    got = exchange(send)
    own, wide, utp, u, ring, ot, cot, take, give, over = call(
        fetch_kernel,
        far(
            frames_in.reshape(CELLS, 256), u_in.T, u_out.T, cotangent.reshape(CELLS, 256),
            core, moment_one, moment_two, take, give, over,
        ),
        [
            ((CELLS, 256), F32, False), ((256, 256), BF, False), ((64, 256), BF, False), ((256, 64), BF, False),
            ((3, 4, 128), F32, False), ((64, 256), BF, False), ((CELLS, 256), BF, False),
            ((216, 512), BF, False), ((512, 240), BF, False), ((256, 128), F32, False),
        ],
        [
            vm((CELLS, 256), BF), vm((64, 256), BF), [vm((OWN,), F32) for _ in range(3)], vm((8, 128), F32),
            dma((10,)),
        ],
    )
    low, high = call(
        sides_kernel,
        near(frames_in, above, below),
        [((SIDE, 256), BF, False)] * 2,
        [vm((SIDE, 256), F32)] * 2,
    )
    left, right = both_ways(high, low, "cols")
    (q,) = call(
        rank_kernel,
        near(own, wide, above.reshape(SIDE, 256), below.reshape(SIDE, 256), left, right),
        [((3, 240, 256), BF, False)],
        [vm((FRAMES, 8, 8, 256), F32), vm((2, SIDE, 256), F32)],
    )
    send, table, outp = call(
        forward_kernel,
        near(got, q, cot, ot, take, give, over),
        [((1024, 128), BF, False), ((TABLE, 128), BF, False), ((CELLS, 256), F32, False)],
        [vm((TABLE, 128), F32), vm((TABLE, 128), F32), vm((CELLS, 128), F32), vm((96, 128), F32)],
    )
    got = exchange(send)
    send, latest = call(
        adam_kernel,
        near(got, ring),
        [((1024, 128), BF, False), ((3, 4, 128), F32, False)],
        [vm((1104, 128), F32)],
    )
    got = exchange(send)
    core_next, one_next, two_next = call(flat_kernel, near(latest), [((OWN,), F32, False)] * 3, [])
    got, core_next, one_next, two_next = lax.optimization_barrier((got, core_next, one_next, two_next))
    kernel_next, frames_grad = call(
        finish_kernel,
        near(got, outp, table, utp, u, ot, take, over),
        [((27, 256, 256), BF, True), ((CELLS, 256), BF, False)],
        [
            vm((TABLE, 128), F32), vm((27, 64, 256), BF), vm((27, 256, 256), BF), vm((1024, 128), F32),
            vm((96, 256), F32), vm((FRAMES, 8, 8, 256), F32), vm((3, 240, 256), BF), dma((9,)),
        ],
    )
    frames_grad = frames_grad.reshape(FRAMES, ROWS, COLS, 256)
    return frames_grad, core_next, one_next, two_next, kernel_next


def solution(mesh):
    in_specs = (
        P(None, "rows", "cols", None),
        P(None, "rows", "cols", None),
        P(AXES),
        P(AXES),
        P(AXES),
        P(),
        P(),
    )
    out_specs = (
        P(None, "rows", "cols", None),
        P(AXES),
        P(AXES),
        P(AXES),
        P(),
    )
    return jax.shard_map(body, mesh=mesh, in_specs=in_specs, out_specs=out_specs, check_vma=False)
```

```python
import jax
import jax.numpy as jnp
import numpy as np
from jax import lax
from jax.experimental import pallas as pl
from jax.experimental.pallas import tpu as pltpu
from jax.sharding import PartitionSpec as P

beta_one = 0.9
beta_two = 0.999
learn_rate = 0.06
epsilon = 1e-08
fix_one = 1.0 - 0.9**10
fix_two = 1.0 - 0.999**10

BF = jnp.bfloat16
F32 = jnp.float32
AXES = ("rows", "cols")

OWN = 432
FRAMES, ROWS, COLS = 3, 6, 8
CELLS = FRAMES * ROWS * COLS
SIDE = FRAMES * 8
TABLE = 864


RELAYS = ((7, 0, 0), (4, 0, 0), (3, 3, 64))
SLOTS = ((0, 24, -8), (24, 24, 8), (48, 18, -1), (66, 18, 1), (84, 3, -9), (87, 3, -7), (90, 3, 7), (93, 3, 9))


def ring_tables():
    take = np.zeros((216, 512), np.float32)
    give = np.zeros((512, 240), np.float32)
    over = np.zeros((256, 128), np.float32)
    for r in range(8):
        for c in range(8):
            first = 27 * r + 27 * c // 8
            col = 32 * r + 4 * c
            for j in range(4):
                take[first + j, col + j] = 1
                give[col + j, first + j] = 1
            wrapped = 48 * c % 128 + OWN - 512
            if wrapped > 0:
                take[first + 4, 256 + col] = 1
                give[256 + col, first + 4] = 1
                over[col, :wrapped] = 1
        for k, (c, j, at) in enumerate(RELAYS):
            col = 32 * r + 4 * c + j
            give[256 + col, 216 + 8 * k + r] = 1
            over[col, at : at + 64] = 1
    return take, give, over


def dot(a, b):
    return jnp.dot(a, b, preferred_element_type=F32)


def dot_nt(a, b):
    return lax.dot_general(a, b, (((1,), (1,)), ((), ())), preferred_element_type=F32)


def dot_tn(a, b):
    return lax.dot_general(a, b, (((0,), (0,)), ((), ())), preferred_element_type=F32)


def lane(shape):
    return lax.broadcasted_iota(jnp.int32, shape, 1)


def sublane(shape):
    return lax.broadcasted_iota(jnp.int32, shape, 0)


def ring_shift():
    return lax.rem(lax.axis_index("cols") * 48, 128)


def to_ring(v, shift):
    turned = pltpu.roll(v, shift, axis=1)
    above = jnp.concatenate([turned[3:4], turned[0:3]], axis=0)
    return jnp.where(lane(v.shape) >= shift, turned, above)


def from_ring(v, shift):
    turned = pltpu.roll(v, lax.rem(128 - shift, 128), axis=1)
    below = jnp.concatenate([turned[1:4], turned[0:1]], axis=0)
    return jnp.where(lane(v.shape) < 128 - shift, turned, below)


def in_ring(shift):
    place = sublane((4, 128)) * 128 + lane((4, 128)) - shift
    place = jnp.where(place < 0, place + 512, place)
    return place < OWN


def load_flat(ref, scratch):
    scratch[...] = jnp.zeros_like(scratch)
    for k in range(3):
        scratch[k, :] = ref[pl.ds(128 * k, 128)]
    scratch[3, 0 : OWN - 384] = ref[pl.ds(384, OWN - 384)]
    return scratch[0:4, :]


def store_flat(ref, v):
    for k in range(3):
        ref[pl.ds(128 * k, 128)] = v[k]
    ref[pl.ds(384, OWN - 384)] = v[3, 0 : OWN - 384]


def fetch(pairs, sems):
    copies = [pltpu.make_async_copy(src, dst, sems.at[k]) for k, (src, dst) in enumerate(pairs)]
    for copy in copies:
        copy.start()
    return copies


def start_kernel(core_ref, x_ref, send_ref, first_ref, last_ref, inner_ref, own, flat, sems):
    copies = fetch(
        (
            (core_ref, own), (x_ref.at[:, 0], first_ref), (x_ref.at[:, ROWS - 1], last_ref), (x_ref, inner_ref),
        ),
        sems,
    )
    copies[0].wait()
    v = to_ring(load_flat(own, flat), ring_shift())
    block = jnp.concatenate([v, v, v, v], axis=0).astype(BF)
    for k in range(64):
        send_ref[16 * k : 16 * k + 16, :] = block
    for k in range(1, 4):
        copies[k].wait()


def sides_kernel(own_ref, above_ref, below_ref, low_ref, high_ref, low, high):
    for f in range(FRAMES):
        for y in range(8):
            if y == 0:
                tile = above_ref[f]
            elif y == 7:
                tile = below_ref[f]
            else:
                tile = own_ref[f, y - 1]
            tile = tile.astype(F32)
            low[8 * f + y : 8 * f + y + 1, :] = tile[0:1, :]
            high[8 * f + y : 8 * f + y + 1, :] = tile[7:8, :]
    low_ref[...] = low[...].astype(BF)
    high_ref[...] = high[...].astype(BF)


def shifted(tile, left, right, bounds, period):
    at = lane(tile.shape) % period
    row = sublane(tile.shape)
    back = jnp.where(row == 0, left, pltpu.roll(tile, 1, axis=0))
    ahead = jnp.where(row == 7, right, pltpu.roll(tile, 7, axis=0))
    return jnp.where(at < bounds[0], back, jnp.where(at < bounds[1], tile, ahead))


def fetch_kernel(
    x_ref, ut_ref, ot_ref, cot_ref, core_ref, one_ref, two_ref, take_ref, give_ref, over_ref,
    own_ref, wide_ref, utp_ref, u_ref, ring_ref, ot_out, cot_out, take_out, give_out, over_out,
    ut, owns, flat, sems,
):
    copies = fetch(
        (
            (ut_ref, ut), (core_ref, owns[0]), (one_ref, owns[1]), (two_ref, owns[2]),
            (take_ref, take_out), (give_ref, give_out), (over_ref, over_out), (ot_ref, ot_out), (cot_ref, cot_out),
        ),
        sems,
    )
    row = sublane((256, 64))
    at = row % 128
    pick = (lane((256, 64)) == (at % 32) * 2 + row // 128) & (at < 96)
    half_row = sublane((64, 64))
    half_pick = lane((64, 64)) == (half_row % 32) * 2 + half_row // 32
    copies[0].wait()
    wide = dot(pick.astype(BF), ut[...]).astype(BF)
    wide_ref[...] = wide
    utp = dot(half_pick.astype(BF), ut[...])
    utp_ref[...] = utp.astype(BF)
    u_ref[...] = utp.T.astype(BF)
    own_ref[...] = dot_nt(x_ref[...], wide).astype(BF).astype(F32)
    shift = ring_shift()
    for k in range(3):
        copies[1 + k].wait()
        ring_ref[k] = to_ring(load_flat(owns[k], flat), shift)
    for k in range(4, 9):
        copies[k].wait()


def stack_rows(tiles, out_ref):
    for b in range(3):
        out_ref[b, 0:48, :] = jnp.zeros((48, 256), BF)
        out_ref[b, 192:240, :] = jnp.zeros((48, 256), BF)
        for f in range(FRAMES):
            rows = tiles[f, b : b + ROWS].reshape(48, 256)
            out_ref[b, 48 * f + 48 : 48 * f + 96, :] = rows.astype(BF)


def rank_kernel(own_ref, wide_ref, above_ref, below_ref, left_ref, right_ref, q_ref, tiles, edge):
    wide = wide_ref[...]

    def project(v):
        return dot_nt(v, wide).astype(BF).astype(F32)

    above = project(above_ref[...])
    below = project(below_ref[...])
    for f in range(FRAMES):
        tiles[f, 0] = above[8 * f : 8 * f + 8]
        tiles[f, 7] = below[8 * f : 8 * f + 8]
        for y in range(ROWS):
            at = 48 * f + 8 * y
            tiles[f, y + 1] = own_ref[at : at + 8, :]
    edge[0] = project(left_ref[...])
    edge[1] = project(right_ref[...])
    for f in range(FRAMES):
        for y in range(8):
            k = 8 * f + y
            left = jnp.broadcast_to(edge[0, k : k + 1, :], (8, 256))
            right = jnp.broadcast_to(edge[1, k : k + 1, :], (8, 256))
            tiles[f, y] = shifted(tiles[f, y], left, right, (32, 64), 128)
    stack_rows(tiles, q_ref)


def gather_table(got_ref, take_ref, over_ref, table_ref):
    over = over_ref[...] > 0
    take = take_ref[...]
    for g in range(4):
        block = got_ref[256 * g : 256 * g + 256, :]
        none = jnp.zeros_like(block)
        both = jnp.concatenate(
            [jnp.where(over, none, block), jnp.where(over, block, none)], axis=0
        )
        table_ref[216 * g : 216 * g + 216, :] = dot(take, both)


def forward_kernel(
    got_ref, q_ref, cot_ref, ot_ref, take_ref, give_ref, over_ref,
    send_ref, table_out, outp_ref, table, grads, border, pixels,
):
    gather_table(got_ref, take_ref, over_ref, table)
    table_out[...] = table[...].astype(BF)
    even = jnp.zeros((CELLS, 128), F32)
    odd = jnp.zeros((CELLS, 128), F32)
    for a in range(3):
        for b in range(3):
            k = 3 * a + b
            weights = table_out[96 * k : 96 * k + 96, :]
            rows = q_ref[b, 48 * a : 48 * a + CELLS, :]
            even = even + dot(rows[:, 0:96], weights)
            odd = odd + dot(rows[:, 128:224], weights)
    mid = (even[:, 0:64] + odd[:, 64:128]).astype(BF)
    pre = dot(mid, ot_ref[...])
    sig = jax.nn.sigmoid(pre)
    slope = (cot_ref[...].astype(F32) * sig * (1.0 + pre * (1.0 - sig))).astype(BF)
    ot = ot_ref[...]
    out_t = dot_nt(ot, slope).astype(BF)
    wide = jnp.concatenate([ot, ot, ot, ot], axis=0)
    outp = dot_nt(slope, wide).astype(BF).astype(F32)
    outp_ref[...] = outp
    border[...] = outp[:, 0:128]
    for f in range(FRAMES):
        pixels[8 * f : 8 * f + 8, :] = border[48 * f : 48 * f + 8, :]
        pixels[24 + 8 * f : 32 + 8 * f, :] = border[48 * f + 40 : 48 * f + 48, :]
    pixels[48:66, :] = border[pl.ds(0, 18, stride=8), :]
    pixels[66:84, :] = border[pl.ds(7, 18, stride=8), :]
    for k, cell in enumerate((0, 7, 40, 47)):
        pixels[84 + 3 * k : 87 + 3 * k, :] = border[pl.ds(cell, 3, stride=48), :]
    for a in range(3):
        for b in range(3):
            k = 3 * a + b
            part = dot(out_t, q_ref[b, 48 * a : 48 * a + CELLS, :])
            stack = jnp.concatenate([part[:, 0:128], part[:, 128:256]], axis=0)
            grads[96 * k : 96 * k + 96, :] = stack.T[0:96, :]
    over = over_ref[...] > 0
    give = give_ref[...]
    for g in range(4):
        source = [grads[216 * g : 216 * g + 216, :]]
        for k in range(3):
            source.append(pixels[32 * k + 8 * g : 32 * k + 8 * g + 8, :])
        part = dot(give, jnp.concatenate(source, axis=0).astype(BF))
        send_ref[256 * g : 256 * g + 256, :] = jnp.where(over, part[256:512], part[0:256]).astype(BF)


def adam_kernel(got_ref, ring_ref, send_ref, next_ref, passed):
    total = jnp.zeros((8, 128), F32)
    passed[0:40, :] = jnp.zeros((40, 128), F32)
    passed[1064:1104, :] = jnp.zeros((40, 128), F32)
    for g in range(8):
        part = got_ref[128 * g : 128 * g + 128, :].astype(F32)
        passed[128 * g + 40 : 128 * g + 168, :] = part
        total = total + part.reshape(16, 8, 128).sum(axis=0)
    grad = (total[0:4] + total[4:8]) * (1.0 / 192.0)
    core, one, two = ring_ref[0], ring_ref[1], ring_ref[2]
    one = beta_one * one + (1.0 - beta_one) * grad
    two = beta_two * two + (1.0 - beta_two) * grad * grad
    core = core - learn_rate * (one / fix_one) / (jnp.sqrt(two / fix_two) + epsilon)
    next_ref[0] = core
    next_ref[1] = one
    next_ref[2] = two
    own = jnp.where(in_ring(ring_shift()), core, 0.0)
    own = jnp.concatenate([own, own], axis=0)
    row, col = lax.axis_index("rows"), lax.axis_index("cols")
    slot, mask = row, jnp.zeros((8, 128), jnp.bool_)
    for k, (c, j, at) in enumerate(RELAYS):
        slot = slot + jnp.where(col == c, 32 * k, 0)
        spot = (sublane((8, 128)) % 4 == j) & (lane((8, 128)) // 64 == at // 64)
        mask = mask | (spot & (jnp.full((8, 128), col, jnp.int32) == c))
    move = 0
    for first, count, offset in SLOTS:
        move = move + jnp.where((slot >= first) & (slot < first + count), 4 * offset, 0)
    for k in range(64):
        upper = passed[pl.ds(40 + 16 * k - move, 8), :]
        lower = passed[pl.ds(48 + 16 * k - move, 8), :]
        block = jnp.concatenate([jnp.where(mask, upper, own), jnp.where(mask, lower, own)], axis=0)
        send_ref[16 * k : 16 * k + 16, :] = block.astype(BF)


def flat_kernel(next_ref, core_ref, one_ref, two_ref):
    shift = ring_shift()
    for k, ref in enumerate((core_ref, one_ref, two_ref)):
        store_flat(ref, from_ring(next_ref[k], shift))


def finish_kernel(
    got_ref, outp_ref, old_ref, utp_ref, u_ref, ot_ref, take_ref, over_ref,
    out_ref, grad_ref, table, half, result, got, pixels, tiles, qs, sems,
):
    gather_table(got_ref, take_ref, over_ref, table)
    cube = table[...].astype(BF)
    even = dot(cube[:, 0:64], ot_ref[...]).astype(BF)
    odd = dot(cube[:, 64:128], ot_ref[...]).astype(BF)
    for t in range(27):
        half[t, 0:32, :] = even[32 * t : 32 * t + 32]
        half[t, 32:64, :] = odd[32 * t : 32 * t + 32]
    u = u_ref[...]

    def store(a):
        part = pl.ds(3 * a, 3)
        return pltpu.make_async_copy(result.at[part], out_ref.at[part], sems.at[a])

    for a in range(9):
        for t in range(3 * a, 3 * a + 3):
            result[t] = dot(u, half[t]).astype(BF)
        store(a).start()

    for g in range(4):
        got[256 * g : 256 * g + 256, :] = got_ref[256 * g : 256 * g + 256, :].astype(F32)
    for k, (c, j, at) in enumerate(RELAYS):
        rows = got[pl.ds(4 * c + j, 32, stride=32), :]
        pixels[32 * k : 32 * k + 32, 0:128] = jnp.where(lane((32, 128)) // 64 == at // 64, rows, 0.0)
    spread = (sublane((128, 256)) % 64 == lane((128, 256)) % 64).astype(BF)
    pixels[...] = dot(pixels[:, 0:128].astype(BF), spread)
    row, col = lax.axis_index("rows"), lax.axis_index("cols")
    zero = jnp.zeros((8, 256), F32)

    def inside(flag, v):
        return jnp.where(jnp.full((8, 256), flag.astype(jnp.int32), jnp.int32) > 0, v, zero)

    def spot(k):
        return jnp.broadcast_to(pixels[k : k + 1, :], (8, 256))

    for f in range(FRAMES):
        for y in range(8):
            if y == 0:
                tile, left, right = pixels[24 + 8 * f : 32 + 8 * f, :], spot(93 + f), spot(90 + f)
            elif y == 7:
                tile, left, right = pixels[8 * f : 8 * f + 8, :], spot(87 + f), spot(84 + f)
            else:
                at = 48 * f + 8 * (y - 1)
                tile = outp_ref[at : at + 8, :]
                left, right = spot(66 + 6 * f + y - 1), spot(48 + 6 * f + y - 1)
            tile = shifted(tile, inside(col > 0, left), inside(col < 7, right), (64, 128), 256)
            if y == 0:
                tile = inside(row > 0, tile)
            elif y == 7:
                tile = inside(row < 31, tile)
            tiles[f, y] = tile
    stack_rows(tiles, qs)
    total = jnp.zeros((CELLS, 64), F32)
    for a in range(3):
        for b in range(3):
            rows = qs[2 - b, 48 * (2 - a) : 48 * (2 - a) + CELLS, :]
            for c in range(3):
                t = 9 * a + 3 * b + c
                part = old_ref[32 * t : 32 * t + 32, :]
                cube = jnp.concatenate([part[:, 0:64], part[:, 64:128]], axis=0)
                piece = rows[:, 64 * (2 - c) : 64 * (2 - c) + 64]
                total = total + dot_nt(piece, cube)
    grad_ref[...] = dot(total.astype(BF), utp_ref[...]).astype(BF)
    for a in range(9):
        store(a).wait()


def call(kernel, args, outs, scratch, flops=10**7):
    def spec(far):
        return pl.BlockSpec(memory_space=pltpu.HBM if far else pltpu.VMEM)

    return pl.pallas_call(
        kernel,
        out_shape=[jax.ShapeDtypeStruct(shape, dtype) for shape, dtype, _ in outs],
        in_specs=[spec(far) for _, far in args],
        out_specs=[spec(far) for _, _, far in outs],
        scratch_shapes=scratch,
        compiler_params=pltpu.CompilerParams(vmem_limit_bytes=32 << 20),
        cost_estimate=pl.CostEstimate(flops=flops, bytes_accessed=10**5, transcendentals=0),
    )(*[pltpu.with_memory_space_constraint(arg, pltpu.HBM) if far else arg for arg, far in args])


def near(*args):
    return [(arg, False) for arg in args]


def far(*args):
    return [(arg, True) for arg in args]


def both_ways(high, low, axis):
    count = lax.axis_size(axis)
    forward = [(i, i + 1) for i in range(count - 1)]
    backward = [(i + 1, i) for i in range(count - 1)]
    return lax.ppermute(high, axis, forward), lax.ppermute(low, axis, backward)


def exchange(x):
    return lax.all_to_all(x, AXES, 0, 0, tiled=True)


def body(frames_in, cotangent, core, moment_one, moment_two, u_in, u_out):
    take, give, over = ring_tables()
    take, give, over = jnp.asarray(take, BF), jnp.asarray(give, BF), jnp.asarray(over, F32)
    vm, dma = pltpu.VMEM, pltpu.SemaphoreType.DMA
    edge = (FRAMES, 8, 256)

    send, first, last, inner = call(
        start_kernel,
        far(core, frames_in),
        [((1024, 128), BF, False), (edge, BF, False), (edge, BF, False), ((FRAMES, ROWS, COLS, 256), BF, False)],
        [vm((OWN,), F32), vm((8, 128), F32), dma((4,))],
    )
    above, below = both_ways(last, first, "rows")
    got = exchange(send)
    own, wide, utp, u, ring, ot, cot, take, give, over = call(
        fetch_kernel,
        near(inner.reshape(CELLS, 256)) + far(
            u_in.T, u_out.T, cotangent.reshape(CELLS, 256), core, moment_one, moment_two, take, give, over,
        ),
        [
            ((CELLS, 256), F32, False), ((256, 256), BF, False), ((64, 256), BF, False), ((256, 64), BF, False),
            ((3, 4, 128), F32, False), ((64, 256), BF, False), ((CELLS, 256), BF, False),
            ((216, 512), BF, False), ((512, 240), BF, False), ((256, 128), F32, False),
        ],
        [
            vm((64, 256), BF), [vm((OWN,), F32) for _ in range(3)], vm((8, 128), F32),
            dma((9,)),
        ],
    )
    low, high = call(
        sides_kernel,
        near(inner, above, below),
        [((SIDE, 256), BF, False)] * 2,
        [vm((SIDE, 256), F32)] * 2,
    )
    left, right = both_ways(high, low, "cols")
    (q,) = call(
        rank_kernel,
        near(own, wide, above.reshape(SIDE, 256), below.reshape(SIDE, 256), left, right),
        [((3, 240, 256), BF, False)],
        [vm((FRAMES, 8, 8, 256), F32), vm((2, SIDE, 256), F32)],
    )
    send, table, outp = call(
        forward_kernel,
        near(got, q, cot, ot, take, give, over),
        [((1024, 128), BF, False), ((TABLE, 128), BF, False), ((CELLS, 256), F32, False)],
        [vm((TABLE, 128), F32), vm((TABLE, 128), F32), vm((CELLS, 128), F32), vm((96, 128), F32)],
    )
    got = exchange(send)
    send, latest = call(
        adam_kernel,
        near(got, ring),
        [((1024, 128), BF, False), ((3, 4, 128), F32, False)],
        [vm((1104, 128), F32)],
    )
    got = exchange(send)
    core_next, one_next, two_next = call(flat_kernel, near(latest), [((OWN,), F32, False)] * 3, [])
    got, core_next, one_next, two_next = lax.optimization_barrier((got, core_next, one_next, two_next))
    kernel_next, frames_grad = call(
        finish_kernel,
        near(got, outp, table, utp, u, ot, take, over),
        [((27, 256, 256), BF, True), ((CELLS, 256), BF, False)],
        [
            vm((TABLE, 128), F32), vm((27, 64, 256), BF), vm((27, 256, 256), BF), vm((1024, 128), F32),
            vm((96, 256), F32), vm((FRAMES, 8, 8, 256), F32), vm((3, 240, 256), BF), dma((9,)),
        ],
    )
    frames_grad = frames_grad.reshape(FRAMES, ROWS, COLS, 256)
    return frames_grad, core_next, one_next, two_next, kernel_next


def solution(mesh):
    in_specs = (
        P(None, "rows", "cols", None),
        P(None, "rows", "cols", None),
        P(AXES),
        P(AXES),
        P(AXES),
        P(),
        P(),
    )
    out_specs = (
        P(None, "rows", "cols", None),
        P(AXES),
        P(AXES),
        P(AXES),
        P(),
    )
    return jax.shard_map(body, mesh=mesh, in_specs=in_specs, out_specs=out_specs, check_vma=False)
```

```python
import jax
import jax.numpy as jnp
import numpy as np
from jax import lax
from jax.experimental import pallas as pl
from jax.experimental.pallas import tpu as pltpu
from jax.sharding import PartitionSpec as P

beta_one = 0.9
beta_two = 0.999
learn_rate = 0.06
epsilon = 1e-08
fix_one = 1.0 - 0.9**10
fix_two = 1.0 - 0.999**10

BF = jnp.bfloat16
F32 = jnp.float32
AXES = ("rows", "cols")

OWN = 432
FRAMES, ROWS, COLS = 3, 6, 8
CELLS = FRAMES * ROWS * COLS
SIDE = FRAMES * 8
TABLE = 864


RELAYS = ((7, 0, 0), (4, 0, 0), (3, 3, 64))
SLOTS = ((0, 24, -8), (24, 24, 8), (48, 18, -1), (66, 18, 1), (84, 3, -9), (87, 3, -7), (90, 3, 7), (93, 3, 9))


def ring_tables():
    take = np.zeros((216, 512), np.float32)
    give = np.zeros((512, 240), np.float32)
    over = np.zeros((256, 128), np.float32)
    for r in range(8):
        for c in range(8):
            first = 27 * r + 27 * c // 8
            col = 32 * r + 4 * c
            for j in range(4):
                take[first + j, col + j] = 1
                give[col + j, first + j] = 1
            wrapped = 48 * c % 128 + OWN - 512
            if wrapped > 0:
                take[first + 4, 256 + col] = 1
                give[256 + col, first + 4] = 1
                over[col, :wrapped] = 1
        for k, (c, j, at) in enumerate(RELAYS):
            col = 32 * r + 4 * c + j
            give[256 + col, 216 + 8 * k + r] = 1
            over[col, at : at + 64] = 1
    return take, give, over


def dot(a, b):
    return jnp.dot(a, b, preferred_element_type=F32)


def dot_nt(a, b):
    return lax.dot_general(a, b, (((1,), (1,)), ((), ())), preferred_element_type=F32)


def dot_tn(a, b):
    return lax.dot_general(a, b, (((0,), (0,)), ((), ())), preferred_element_type=F32)


def lane(shape):
    return lax.broadcasted_iota(jnp.int32, shape, 1)


def sublane(shape):
    return lax.broadcasted_iota(jnp.int32, shape, 0)


def ring_shift():
    return lax.rem(lax.axis_index("cols") * 48, 128)


def to_ring(v, shift):
    turned = pltpu.roll(v, shift, axis=1)
    above = jnp.concatenate([turned[3:4], turned[0:3]], axis=0)
    return jnp.where(lane(v.shape) >= shift, turned, above)


def from_ring(v, shift):
    turned = pltpu.roll(v, lax.rem(128 - shift, 128), axis=1)
    below = jnp.concatenate([turned[1:4], turned[0:1]], axis=0)
    return jnp.where(lane(v.shape) < 128 - shift, turned, below)


def in_ring(shift):
    place = sublane((4, 128)) * 128 + lane((4, 128)) - shift
    place = jnp.where(place < 0, place + 512, place)
    return place < OWN


def load_flat(ref, scratch):
    scratch[...] = jnp.zeros_like(scratch)
    for k in range(3):
        scratch[k, :] = ref[pl.ds(128 * k, 128)]
    scratch[3, 0 : OWN - 384] = ref[pl.ds(384, OWN - 384)]
    return scratch[0:4, :]


def store_flat(ref, v):
    for k in range(3):
        ref[pl.ds(128 * k, 128)] = v[k]
    ref[pl.ds(384, OWN - 384)] = v[3, 0 : OWN - 384]


def fetch(pairs, sems):
    copies = [pltpu.make_async_copy(src, dst, sems.at[k]) for k, (src, dst) in enumerate(pairs)]
    for copy in copies:
        copy.start()
    return copies


def even_first(axis, first, last):
    even = jnp.full(first.shape, lax.rem(lax.axis_index(axis), 2), jnp.int32) == 0
    return jnp.where(even, last, first), jnp.where(even, first, last)


def columns_kernel(x_ref, inner_ref, one_ref, two_ref, low, high, sems):
    fetch(((x_ref, inner_ref),), sems)[0].wait()
    for f in range(FRAMES):
        for y in range(ROWS):
            tile = inner_ref[f, y].astype(F32)
            k = ROWS * f + y
            low[k : k + 1, :] = tile[0:1, :]
            high[k : k + 1, :] = tile[7:8, :]
    one, two = even_first("cols", low[...], high[...])
    one_ref[...] = one.astype(BF)
    two_ref[...] = two.astype(BF)


def start_kernel(core_ref, send_ref, own, flat, sems):
    fetch(((core_ref, own),), sems)[0].wait()
    v = to_ring(load_flat(own, flat), ring_shift())
    block = jnp.concatenate([v, v, v, v], axis=0).astype(BF)
    for k in range(64):
        send_ref[16 * k : 16 * k + 16, :] = block


def rows_kernel(inner_ref, one_ref, two_ref, left_ref, right_ref, up_ref, down_ref, first, last):
    right, left = even_first("cols", two_ref[...].astype(F32), one_ref[...].astype(F32))
    left_ref[...] = left
    right_ref[...] = right
    first[...] = jnp.zeros_like(first)
    last[...] = jnp.zeros_like(last)
    for f in range(FRAMES):
        for y, rows in ((0, first), (ROWS - 1, last)):
            k = ROWS * f + y
            rows[16 * f : 16 * f + 8, :] = inner_ref[f, y].astype(F32)
            rows[16 * f + 8 : 16 * f + 9, :] = left_ref[k : k + 1, :]
            rows[16 * f + 9 : 16 * f + 10, :] = right_ref[k : k + 1, :]
    one, two = even_first("rows", first[...], last[...])
    up_ref[...] = one.astype(BF)
    down_ref[...] = two.astype(BF)


def shifted(tile, left, right, bounds, period):
    at = lane(tile.shape) % period
    row = sublane(tile.shape)
    back = jnp.where(row == 0, left, pltpu.roll(tile, 1, axis=0))
    ahead = jnp.where(row == 7, right, pltpu.roll(tile, 7, axis=0))
    return jnp.where(at < bounds[0], back, jnp.where(at < bounds[1], tile, ahead))


def fetch_kernel(
    x_ref, ut_ref, ot_ref, cot_ref, core_ref, one_ref, two_ref, take_ref, give_ref, over_ref,
    own_ref, wide_ref, utp_ref, u_ref, ring_ref, ot_out, cot_out, take_out, give_out, over_out,
    ut, owns, flat, sems,
):
    copies = fetch(
        (
            (ut_ref, ut), (core_ref, owns[0]), (one_ref, owns[1]), (two_ref, owns[2]),
            (take_ref, take_out), (give_ref, give_out), (over_ref, over_out), (ot_ref, ot_out), (cot_ref, cot_out),
        ),
        sems,
    )
    row = sublane((256, 64))
    at = row % 128
    pick = (lane((256, 64)) == (at % 32) * 2 + row // 128) & (at < 96)
    half_row = sublane((64, 64))
    half_pick = lane((64, 64)) == (half_row % 32) * 2 + half_row // 32
    copies[0].wait()
    wide = dot(pick.astype(BF), ut[...]).astype(BF)
    wide_ref[...] = wide
    utp = dot(half_pick.astype(BF), ut[...])
    utp_ref[...] = utp.astype(BF)
    u_ref[...] = utp.T.astype(BF)
    own_ref[...] = dot_nt(x_ref[...], wide).astype(BF).astype(F32)
    shift = ring_shift()
    for k in range(3):
        copies[1 + k].wait()
        ring_ref[k] = to_ring(load_flat(owns[k], flat), shift)
    for k in range(4, 9):
        copies[k].wait()


def stack_rows(tiles, out_ref):
    for b in range(3):
        out_ref[b, 0:48, :] = jnp.zeros((48, 256), BF)
        out_ref[b, 192:240, :] = jnp.zeros((48, 256), BF)
        for f in range(FRAMES):
            rows = tiles[f, b : b + ROWS].reshape(48, 256)
            out_ref[b, 48 * f + 48 : 48 * f + 96, :] = rows.astype(BF)


def rank_kernel(own_ref, wide_ref, one_ref, two_ref, left_ref, right_ref, q_ref, tiles, edge, rims):
    wide = wide_ref[...]

    def project(v):
        return dot_nt(v.astype(BF), wide).astype(BF).astype(F32)

    below, above = even_first("rows", project(two_ref[...]), project(one_ref[...]))
    rims[0] = above
    rims[1] = below
    edge[0] = project(left_ref[...])
    edge[1] = project(right_ref[...])
    for f in range(FRAMES):
        for y in range(8):
            if y in (0, 7):
                rim = rims.at[y // 7]
                at = 16 * f
                tile, left, right = rim[at : at + 8, :], rim[at + 8 : at + 9, :], rim[at + 9 : at + 10, :]
            else:
                k = ROWS * f + y - 1
                tile = own_ref[8 * k : 8 * k + 8, :]
                left, right = edge[0, k : k + 1, :], edge[1, k : k + 1, :]
            left = jnp.broadcast_to(left, (8, 256))
            right = jnp.broadcast_to(right, (8, 256))
            tiles[f, y] = shifted(tile, left, right, (32, 64), 128)
    stack_rows(tiles, q_ref)


def gather_table(got_ref, take_ref, over_ref, table_ref):
    over = over_ref[...] > 0
    take = take_ref[...]
    for g in range(4):
        block = got_ref[256 * g : 256 * g + 256, :]
        none = jnp.zeros_like(block)
        both = jnp.concatenate(
            [jnp.where(over, none, block), jnp.where(over, block, none)], axis=0
        )
        table_ref[216 * g : 216 * g + 216, :] = dot(take, both)


def forward_kernel(
    got_ref, q_ref, cot_ref, ot_ref, take_ref, give_ref, over_ref,
    send_ref, table_out, outp_ref, table, grads, border, pixels,
):
    gather_table(got_ref, take_ref, over_ref, table)
    table_out[...] = table[...].astype(BF)
    even = jnp.zeros((CELLS, 128), F32)
    odd = jnp.zeros((CELLS, 128), F32)
    for a in range(3):
        for b in range(3):
            k = 3 * a + b
            weights = table_out[96 * k : 96 * k + 96, :]
            rows = q_ref[b, 48 * a : 48 * a + CELLS, :]
            even = even + dot(rows[:, 0:96], weights)
            odd = odd + dot(rows[:, 128:224], weights)
    mid = (even[:, 0:64] + odd[:, 64:128]).astype(BF)
    pre = dot(mid, ot_ref[...])
    sig = jax.nn.sigmoid(pre)
    slope = (cot_ref[...].astype(F32) * sig * (1.0 + pre * (1.0 - sig))).astype(BF)
    ot = ot_ref[...]
    out_t = dot_nt(ot, slope).astype(BF)
    wide = jnp.concatenate([ot, ot, ot, ot], axis=0)
    outp = dot_nt(slope, wide).astype(BF).astype(F32)
    outp_ref[...] = outp
    border[...] = outp[:, 0:128]
    for f in range(FRAMES):
        pixels[8 * f : 8 * f + 8, :] = border[48 * f : 48 * f + 8, :]
        pixels[24 + 8 * f : 32 + 8 * f, :] = border[48 * f + 40 : 48 * f + 48, :]
    pixels[48:66, :] = border[pl.ds(0, 18, stride=8), :]
    pixels[66:84, :] = border[pl.ds(7, 18, stride=8), :]
    for k, cell in enumerate((0, 7, 40, 47)):
        pixels[84 + 3 * k : 87 + 3 * k, :] = border[pl.ds(cell, 3, stride=48), :]
    for a in range(3):
        for b in range(3):
            k = 3 * a + b
            part = dot(out_t, q_ref[b, 48 * a : 48 * a + CELLS, :])
            stack = jnp.concatenate([part[:, 0:128], part[:, 128:256]], axis=0)
            grads[96 * k : 96 * k + 96, :] = stack.T[0:96, :]
    over = over_ref[...] > 0
    give = give_ref[...]
    for g in range(4):
        source = [grads[216 * g : 216 * g + 216, :]]
        for k in range(3):
            source.append(pixels[32 * k + 8 * g : 32 * k + 8 * g + 8, :])
        part = dot(give, jnp.concatenate(source, axis=0).astype(BF))
        send_ref[256 * g : 256 * g + 256, :] = jnp.where(over, part[256:512], part[0:256]).astype(BF)


def adam_kernel(got_ref, ring_ref, send_ref, next_ref, passed):
    total = jnp.zeros((8, 128), F32)
    passed[0:40, :] = jnp.zeros((40, 128), F32)
    passed[1064:1104, :] = jnp.zeros((40, 128), F32)
    for g in range(8):
        part = got_ref[128 * g : 128 * g + 128, :].astype(F32)
        passed[128 * g + 40 : 128 * g + 168, :] = part
        total = total + part.reshape(16, 8, 128).sum(axis=0)
    grad = (total[0:4] + total[4:8]) * (1.0 / 192.0)
    core, one, two = ring_ref[0], ring_ref[1], ring_ref[2]
    one = beta_one * one + (1.0 - beta_one) * grad
    two = beta_two * two + (1.0 - beta_two) * grad * grad
    core = core - learn_rate * (one / fix_one) / (jnp.sqrt(two / fix_two) + epsilon)
    next_ref[0] = core
    next_ref[1] = one
    next_ref[2] = two
    own = jnp.where(in_ring(ring_shift()), core, 0.0)
    own = jnp.concatenate([own, own], axis=0)
    row, col = lax.axis_index("rows"), lax.axis_index("cols")
    slot, mask = row, jnp.zeros((8, 128), jnp.bool_)
    for k, (c, j, at) in enumerate(RELAYS):
        slot = slot + jnp.where(col == c, 32 * k, 0)
        spot = (sublane((8, 128)) % 4 == j) & (lane((8, 128)) // 64 == at // 64)
        mask = mask | (spot & (jnp.full((8, 128), col, jnp.int32) == c))
    move = 0
    for first, count, offset in SLOTS:
        move = move + jnp.where((slot >= first) & (slot < first + count), 4 * offset, 0)
    for k in range(64):
        upper = passed[pl.ds(40 + 16 * k - move, 8), :]
        lower = passed[pl.ds(48 + 16 * k - move, 8), :]
        block = jnp.concatenate([jnp.where(mask, upper, own), jnp.where(mask, lower, own)], axis=0)
        send_ref[16 * k : 16 * k + 16, :] = block.astype(BF)


def flat_kernel(next_ref, core_ref, one_ref, two_ref):
    shift = ring_shift()
    for k, ref in enumerate((core_ref, one_ref, two_ref)):
        store_flat(ref, from_ring(next_ref[k], shift))


def finish_kernel(
    got_ref, outp_ref, old_ref, utp_ref, u_ref, ot_ref, take_ref, over_ref,
    out_ref, grad_ref, table, half, result, got, pixels, tiles, qs, sems,
):
    gather_table(got_ref, take_ref, over_ref, table)
    cube = table[...].astype(BF)
    even = dot(cube[:, 0:64], ot_ref[...]).astype(BF)
    odd = dot(cube[:, 64:128], ot_ref[...]).astype(BF)
    for t in range(27):
        half[t, 0:32, :] = even[32 * t : 32 * t + 32]
        half[t, 32:64, :] = odd[32 * t : 32 * t + 32]
    u = u_ref[...]

    def store(a):
        part = pl.ds(3 * a, 3)
        return pltpu.make_async_copy(result.at[part], out_ref.at[part], sems.at[a])

    for a in range(9):
        for t in range(3 * a, 3 * a + 3):
            result[t] = dot(u, half[t]).astype(BF)
        store(a).start()

    for g in range(4):
        got[256 * g : 256 * g + 256, :] = got_ref[256 * g : 256 * g + 256, :].astype(F32)
    for k, (c, j, at) in enumerate(RELAYS):
        rows = got[pl.ds(4 * c + j, 32, stride=32), :]
        pixels[32 * k : 32 * k + 32, 0:128] = jnp.where(lane((32, 128)) // 64 == at // 64, rows, 0.0)
    spread = (sublane((128, 256)) % 64 == lane((128, 256)) % 64).astype(BF)
    pixels[...] = dot(pixels[:, 0:128].astype(BF), spread)
    row, col = lax.axis_index("rows"), lax.axis_index("cols")
    zero = jnp.zeros((8, 256), F32)

    def inside(flag, v):
        return jnp.where(jnp.full((8, 256), flag.astype(jnp.int32), jnp.int32) > 0, v, zero)

    def spot(k):
        return jnp.broadcast_to(pixels[k : k + 1, :], (8, 256))

    for f in range(FRAMES):
        for y in range(8):
            if y == 0:
                tile, left, right = pixels[24 + 8 * f : 32 + 8 * f, :], spot(93 + f), spot(90 + f)
            elif y == 7:
                tile, left, right = pixels[8 * f : 8 * f + 8, :], spot(87 + f), spot(84 + f)
            else:
                at = 48 * f + 8 * (y - 1)
                tile = outp_ref[at : at + 8, :]
                left, right = spot(66 + 6 * f + y - 1), spot(48 + 6 * f + y - 1)
            tile = shifted(tile, inside(col > 0, left), inside(col < 7, right), (64, 128), 256)
            if y == 0:
                tile = inside(row > 0, tile)
            elif y == 7:
                tile = inside(row < 31, tile)
            tiles[f, y] = tile
    stack_rows(tiles, qs)
    total = jnp.zeros((CELLS, 64), F32)
    for a in range(3):
        for b in range(3):
            rows = qs[2 - b, 48 * (2 - a) : 48 * (2 - a) + CELLS, :]
            for c in range(3):
                t = 9 * a + 3 * b + c
                part = old_ref[32 * t : 32 * t + 32, :]
                cube = jnp.concatenate([part[:, 0:64], part[:, 64:128]], axis=0)
                piece = rows[:, 64 * (2 - c) : 64 * (2 - c) + 64]
                total = total + dot_nt(piece, cube)
    grad_ref[...] = dot(total.astype(BF), utp_ref[...]).astype(BF)
    for a in range(9):
        store(a).wait()


def call(kernel, args, outs, scratch, flops=10**7):
    def spec(far):
        return pl.BlockSpec(memory_space=pltpu.HBM if far else pltpu.VMEM)

    return pl.pallas_call(
        kernel,
        out_shape=[jax.ShapeDtypeStruct(shape, dtype) for shape, dtype, _ in outs],
        in_specs=[spec(far) for _, far in args],
        out_specs=[spec(far) for _, _, far in outs],
        scratch_shapes=scratch,
        compiler_params=pltpu.CompilerParams(vmem_limit_bytes=32 << 20),
        cost_estimate=pl.CostEstimate(flops=flops, bytes_accessed=10**5, transcendentals=0),
    )(*[pltpu.with_memory_space_constraint(arg, pltpu.HBM) if far else arg for arg, far in args])


def near(*args):
    return [(arg, False) for arg in args]


def far(*args):
    return [(arg, True) for arg in args]


def swap(one, two, axis):
    count = lax.axis_size(axis)
    pairs = [[(i, i + 1) for i in range(k, count - 1, 2)] for k in range(2)]
    return tuple(
        lax.ppermute(x, axis, forward + [(b, a) for a, b in forward]) for x, forward in zip((one, two), pairs)
    )


def exchange(x):
    return lax.all_to_all(x, AXES, 0, 0, tiled=True)


def body(frames_in, cotangent, core, moment_one, moment_two, u_in, u_out):
    take, give, over = ring_tables()
    take, give, over = jnp.asarray(take, BF), jnp.asarray(give, BF), jnp.asarray(over, F32)
    vm, dma = pltpu.VMEM, pltpu.SemaphoreType.DMA
    side = (FRAMES * ROWS, 256)
    rim = (FRAMES * 16, 256)

    inner, one, two = call(
        columns_kernel,
        far(frames_in),
        [((FRAMES, ROWS, COLS, 256), BF, False), (side, BF, False), (side, BF, False)],
        [vm(side, F32), vm(side, F32), dma((1,))],
    )
    one, two = swap(one, two, "cols")
    (send,) = call(
        start_kernel,
        far(core),
        [((1024, 128), BF, False)],
        [vm((OWN,), F32), vm((8, 128), F32), dma((1,))],
    )
    send, one, two = lax.optimization_barrier((send, one, two))
    got = exchange(send)
    own, wide, utp, u, ring, ot, cot, take, give, over = call(
        fetch_kernel,
        near(inner.reshape(CELLS, 256)) + far(
            u_in.T, u_out.T, cotangent.reshape(CELLS, 256), core, moment_one, moment_two, take, give, over,
        ),
        [
            ((CELLS, 256), F32, False), ((256, 256), BF, False), ((64, 256), BF, False), ((256, 64), BF, False),
            ((3, 4, 128), F32, False), ((64, 256), BF, False), ((CELLS, 256), BF, False),
            ((216, 512), BF, False), ((512, 240), BF, False), ((256, 128), F32, False),
        ],
        [
            vm((64, 256), BF), [vm((OWN,), F32) for _ in range(3)], vm((8, 128), F32),
            dma((9,)),
        ],
    )
    left, right, one, two = call(
        rows_kernel,
        near(inner, one, two),
        [(side, F32, False), (side, F32, False), (rim, BF, False), (rim, BF, False)],
        [vm(rim, F32), vm(rim, F32)],
    )
    one, two = swap(one, two, "rows")
    (q,) = call(
        rank_kernel,
        near(own, wide, one, two, left, right),
        [((3, 240, 256), BF, False)],
        [vm((FRAMES, 8, 8, 256), F32), vm((2, 18, 256), F32), vm((2, 48, 256), F32)],
    )
    send, table, outp = call(
        forward_kernel,
        near(got, q, cot, ot, take, give, over),
        [((1024, 128), BF, False), ((TABLE, 128), BF, False), ((CELLS, 256), F32, False)],
        [vm((TABLE, 128), F32), vm((TABLE, 128), F32), vm((CELLS, 128), F32), vm((96, 128), F32)],
    )
    got = exchange(send)
    send, latest = call(
        adam_kernel,
        near(got, ring),
        [((1024, 128), BF, False), ((3, 4, 128), F32, False)],
        [vm((1104, 128), F32)],
    )
    got = exchange(send)
    core_next, one_next, two_next = call(flat_kernel, near(latest), [((OWN,), F32, False)] * 3, [])
    got, core_next, one_next, two_next = lax.optimization_barrier((got, core_next, one_next, two_next))
    kernel_next, frames_grad = call(
        finish_kernel,
        near(got, outp, table, utp, u, ot, take, over),
        [((27, 256, 256), BF, True), ((CELLS, 256), BF, False)],
        [
            vm((TABLE, 128), F32), vm((27, 64, 256), BF), vm((27, 256, 256), BF), vm((1024, 128), F32),
            vm((96, 256), F32), vm((FRAMES, 8, 8, 256), F32), vm((3, 240, 256), BF), dma((9,)),
        ],
    )
    frames_grad = frames_grad.reshape(FRAMES, ROWS, COLS, 256)
    return frames_grad, core_next, one_next, two_next, kernel_next


def solution(mesh):
    in_specs = (
        P(None, "rows", "cols", None),
        P(None, "rows", "cols", None),
        P(AXES),
        P(AXES),
        P(AXES),
        P(),
        P(),
    )
    out_specs = (
        P(None, "rows", "cols", None),
        P(AXES),
        P(AXES),
        P(AXES),
        P(),
    )
    return jax.shard_map(body, mesh=mesh, in_specs=in_specs, out_specs=out_specs, check_vma=False)
```

```python
import jax
import jax.numpy as jnp
import numpy as np
from jax import lax
from jax.experimental import pallas as pl
from jax.experimental.pallas import tpu as pltpu
from jax.sharding import PartitionSpec as P

beta_one = 0.9
beta_two = 0.999
learn_rate = 0.06
epsilon = 1e-08
fix_one = 1.0 - 0.9**10
fix_two = 1.0 - 0.999**10

BF = jnp.bfloat16
F32 = jnp.float32
AXES = ("rows", "cols")

OWN = 432
FRAMES, ROWS, COLS = 3, 6, 8
CELLS = FRAMES * ROWS * COLS
SIDE = FRAMES * 8
TABLE = 864


RELAYS = ((7, 0, 0), (4, 0, 0), (3, 3, 64))
SLOTS = ((0, 24, -8), (24, 24, 8), (48, 18, -1), (66, 18, 1), (84, 3, -9), (87, 3, -7), (90, 3, 7), (93, 3, 9))


def ring_tables():
    take = np.zeros((216, 512), np.float32)
    give = np.zeros((512, 240), np.float32)
    over = np.zeros((256, 128), np.float32)
    for r in range(8):
        for c in range(8):
            first = 27 * r + 27 * c // 8
            col = 32 * r + 4 * c
            for j in range(4):
                take[first + j, col + j] = 1
                give[col + j, first + j] = 1
            wrapped = 48 * c % 128 + OWN - 512
            if wrapped > 0:
                take[first + 4, 256 + col] = 1
                give[256 + col, first + 4] = 1
                over[col, :wrapped] = 1
        for k, (c, j, at) in enumerate(RELAYS):
            col = 32 * r + 4 * c + j
            give[256 + col, 216 + 8 * k + r] = 1
            over[col, at : at + 64] = 1
    return take, give, over


def dot(a, b):
    return jnp.dot(a, b, preferred_element_type=F32)


def dot_nt(a, b):
    return lax.dot_general(a, b, (((1,), (1,)), ((), ())), preferred_element_type=F32)


def dot_tn(a, b):
    return lax.dot_general(a, b, (((0,), (0,)), ((), ())), preferred_element_type=F32)


def lane(shape):
    return lax.broadcasted_iota(jnp.int32, shape, 1)


def sublane(shape):
    return lax.broadcasted_iota(jnp.int32, shape, 0)


def ring_shift():
    return lax.rem(lax.axis_index("cols") * 48, 128)


def to_ring(v, shift):
    turned = pltpu.roll(v, shift, axis=1)
    above = jnp.concatenate([turned[3:4], turned[0:3]], axis=0)
    return jnp.where(lane(v.shape) >= shift, turned, above)


def from_ring(v, shift):
    turned = pltpu.roll(v, lax.rem(128 - shift, 128), axis=1)
    below = jnp.concatenate([turned[1:4], turned[0:1]], axis=0)
    return jnp.where(lane(v.shape) < 128 - shift, turned, below)


def in_ring(shift):
    place = sublane((4, 128)) * 128 + lane((4, 128)) - shift
    place = jnp.where(place < 0, place + 512, place)
    return place < OWN


def load_flat(ref, scratch):
    scratch[...] = jnp.zeros_like(scratch)
    for k in range(3):
        scratch[k, :] = ref[pl.ds(128 * k, 128)]
    scratch[3, 0 : OWN - 384] = ref[pl.ds(384, OWN - 384)]
    return scratch[0:4, :]


def store_flat(ref, v):
    for k in range(3):
        ref[pl.ds(128 * k, 128)] = v[k]
    ref[pl.ds(384, OWN - 384)] = v[3, 0 : OWN - 384]


def fetch(pairs, sems):
    copies = [pltpu.make_async_copy(src, dst, sems.at[k]) for k, (src, dst) in enumerate(pairs)]
    for copy in copies:
        copy.start()
    return copies


def even_first(axis, first, last):
    even = jnp.full(first.shape, lax.rem(lax.axis_index(axis), 2), jnp.int32) == 0
    return jnp.where(even, last, first), jnp.where(even, first, last)


def start_kernel(core_ref, x_ref, send_ref, one_ref, two_ref, inner_ref, own, flat, sems):
    copies = fetch(((x_ref, inner_ref), (core_ref, own)), sems)
    copies[0].wait()
    for f in range(FRAMES):
        first, last = inner_ref[f, 0].astype(F32), inner_ref[f, ROWS - 1].astype(F32)
        one, two = even_first("rows", first, last)
        one_ref[f] = one.astype(BF)
        two_ref[f] = two.astype(BF)
    copies[1].wait()
    v = to_ring(load_flat(own, flat), ring_shift())
    block = jnp.concatenate([v, v, v, v], axis=0).astype(BF)
    for k in range(64):
        send_ref[16 * k : 16 * k + 16, :] = block


def columns_kernel(inner_ref, one_ref, two_ref, above_ref, below_ref, left_ref, right_ref, low, high):
    for f in range(FRAMES):
        below, above = even_first("rows", two_ref[f].astype(F32), one_ref[f].astype(F32))
        above_ref[8 * f : 8 * f + 8, :] = above
        below_ref[8 * f : 8 * f + 8, :] = below
        for y in range(8):
            tile = above if y == 0 else below if y == 7 else inner_ref[f, y - 1].astype(F32)
            low[8 * f + y : 8 * f + y + 1, :] = tile[0:1, :]
            high[8 * f + y : 8 * f + y + 1, :] = tile[7:8, :]
    one, two = even_first("cols", low[...], high[...])
    left_ref[...] = one.astype(BF)
    right_ref[...] = two.astype(BF)


def shifted(tile, left, right, bounds, period):
    at = lane(tile.shape) % period
    row = sublane(tile.shape)
    back = jnp.where(row == 0, left, pltpu.roll(tile, 1, axis=0))
    ahead = jnp.where(row == 7, right, pltpu.roll(tile, 7, axis=0))
    return jnp.where(at < bounds[0], back, jnp.where(at < bounds[1], tile, ahead))


def fetch_kernel(
    x_ref, ut_ref, ot_ref, cot_ref, core_ref, one_ref, two_ref, take_ref, give_ref, over_ref,
    own_ref, wide_ref, utp_ref, u_ref, ring_ref, ot_out, cot_out, take_out, give_out, over_out,
    ut, owns, flat, sems,
):
    copies = fetch(
        (
            (ut_ref, ut), (core_ref, owns[0]), (one_ref, owns[1]), (two_ref, owns[2]),
            (take_ref, take_out), (give_ref, give_out), (over_ref, over_out), (ot_ref, ot_out), (cot_ref, cot_out),
        ),
        sems,
    )
    row = sublane((256, 64))
    at = row % 128
    pick = (lane((256, 64)) == (at % 32) * 2 + row // 128) & (at < 96)
    half_row = sublane((64, 64))
    half_pick = lane((64, 64)) == (half_row % 32) * 2 + half_row // 32
    copies[0].wait()
    wide = dot(pick.astype(BF), ut[...]).astype(BF)
    wide_ref[...] = wide
    utp = dot(half_pick.astype(BF), ut[...])
    utp_ref[...] = utp.astype(BF)
    u_ref[...] = utp.T.astype(BF)
    own_ref[...] = dot_nt(x_ref[...], wide).astype(BF).astype(F32)
    shift = ring_shift()
    for k in range(3):
        copies[1 + k].wait()
        ring_ref[k] = to_ring(load_flat(owns[k], flat), shift)
    for k in range(4, 9):
        copies[k].wait()


def stack_rows(tiles, out_ref):
    for b in range(3):
        out_ref[b, 0:48, :] = jnp.zeros((48, 256), BF)
        out_ref[b, 192:240, :] = jnp.zeros((48, 256), BF)
        for f in range(FRAMES):
            rows = tiles[f, b : b + ROWS].reshape(48, 256)
            out_ref[b, 48 * f + 48 : 48 * f + 96, :] = rows.astype(BF)


def rank_kernel(own_ref, wide_ref, above_ref, below_ref, one_ref, two_ref, q_ref, tiles, edge, rims):
    wide = wide_ref[...]

    def project(v):
        return dot_nt(v.astype(BF), wide).astype(BF).astype(F32)

    rims[0] = project(above_ref[...])
    rims[1] = project(below_ref[...])
    right, left = even_first("cols", project(two_ref[...]), project(one_ref[...]))
    edge[0] = left
    edge[1] = right
    for f in range(FRAMES):
        for y in range(8):
            k = 8 * f + y
            if y in (0, 7):
                tile = rims[y // 7, 8 * f : 8 * f + 8, :]
            else:
                at = 48 * f + 8 * (y - 1)
                tile = own_ref[at : at + 8, :]
            left = jnp.broadcast_to(edge[0, k : k + 1, :], (8, 256))
            right = jnp.broadcast_to(edge[1, k : k + 1, :], (8, 256))
            tiles[f, y] = shifted(tile, left, right, (32, 64), 128)
    stack_rows(tiles, q_ref)


def gather_table(got_ref, take_ref, over_ref, table_ref):
    over = over_ref[...] > 0
    take = take_ref[...]
    for g in range(4):
        block = got_ref[256 * g : 256 * g + 256, :]
        none = jnp.zeros_like(block)
        both = jnp.concatenate(
            [jnp.where(over, none, block), jnp.where(over, block, none)], axis=0
        )
        table_ref[216 * g : 216 * g + 216, :] = dot(take, both)


def forward_kernel(
    got_ref, q_ref, cot_ref, ot_ref, take_ref, give_ref, over_ref,
    send_ref, table_out, outp_ref, table, grads, border, pixels,
):
    gather_table(got_ref, take_ref, over_ref, table)
    table_out[...] = table[...].astype(BF)
    even = jnp.zeros((CELLS, 128), F32)
    odd = jnp.zeros((CELLS, 128), F32)
    for a in range(3):
        for b in range(3):
            k = 3 * a + b
            weights = table_out[96 * k : 96 * k + 96, :]
            rows = q_ref[b, 48 * a : 48 * a + CELLS, :]
            even = even + dot(rows[:, 0:96], weights)
            odd = odd + dot(rows[:, 128:224], weights)
    mid = (even[:, 0:64] + odd[:, 64:128]).astype(BF)
    pre = dot(mid, ot_ref[...])
    sig = jax.nn.sigmoid(pre)
    slope = (cot_ref[...].astype(F32) * sig * (1.0 + pre * (1.0 - sig))).astype(BF)
    ot = ot_ref[...]
    out_t = dot_nt(ot, slope).astype(BF)
    wide = jnp.concatenate([ot, ot, ot, ot], axis=0)
    outp = dot_nt(slope, wide).astype(BF).astype(F32)
    outp_ref[...] = outp
    border[...] = outp[:, 0:128]
    for f in range(FRAMES):
        pixels[8 * f : 8 * f + 8, :] = border[48 * f : 48 * f + 8, :]
        pixels[24 + 8 * f : 32 + 8 * f, :] = border[48 * f + 40 : 48 * f + 48, :]
    pixels[48:66, :] = border[pl.ds(0, 18, stride=8), :]
    pixels[66:84, :] = border[pl.ds(7, 18, stride=8), :]
    for k, cell in enumerate((0, 7, 40, 47)):
        pixels[84 + 3 * k : 87 + 3 * k, :] = border[pl.ds(cell, 3, stride=48), :]
    for a in range(3):
        for b in range(3):
            k = 3 * a + b
            part = dot(out_t, q_ref[b, 48 * a : 48 * a + CELLS, :])
            stack = jnp.concatenate([part[:, 0:128], part[:, 128:256]], axis=0)
            grads[96 * k : 96 * k + 96, :] = stack.T[0:96, :]
    over = over_ref[...] > 0
    give = give_ref[...]
    for g in range(4):
        source = [grads[216 * g : 216 * g + 216, :]]
        for k in range(3):
            source.append(pixels[32 * k + 8 * g : 32 * k + 8 * g + 8, :])
        part = dot(give, jnp.concatenate(source, axis=0).astype(BF))
        send_ref[256 * g : 256 * g + 256, :] = jnp.where(over, part[256:512], part[0:256]).astype(BF)


def adam_kernel(got_ref, ring_ref, send_ref, next_ref, passed):
    total = jnp.zeros((8, 128), F32)
    passed[0:40, :] = jnp.zeros((40, 128), F32)
    passed[1064:1104, :] = jnp.zeros((40, 128), F32)
    for g in range(8):
        part = got_ref[128 * g : 128 * g + 128, :].astype(F32)
        passed[128 * g + 40 : 128 * g + 168, :] = part
        total = total + part.reshape(16, 8, 128).sum(axis=0)
    grad = (total[0:4] + total[4:8]) * (1.0 / 192.0)
    core, one, two = ring_ref[0], ring_ref[1], ring_ref[2]
    one = beta_one * one + (1.0 - beta_one) * grad
    two = beta_two * two + (1.0 - beta_two) * grad * grad
    core = core - learn_rate * (one / fix_one) / (jnp.sqrt(two / fix_two) + epsilon)
    next_ref[0] = core
    next_ref[1] = one
    next_ref[2] = two
    own = jnp.where(in_ring(ring_shift()), core, 0.0)
    own = jnp.concatenate([own, own], axis=0)
    row, col = lax.axis_index("rows"), lax.axis_index("cols")
    slot, mask = row, jnp.zeros((8, 128), jnp.bool_)
    for k, (c, j, at) in enumerate(RELAYS):
        slot = slot + jnp.where(col == c, 32 * k, 0)
        spot = (sublane((8, 128)) % 4 == j) & (lane((8, 128)) // 64 == at // 64)
        mask = mask | (spot & (jnp.full((8, 128), col, jnp.int32) == c))
    move = 0
    for first, count, offset in SLOTS:
        move = move + jnp.where((slot >= first) & (slot < first + count), 4 * offset, 0)
    for k in range(64):
        upper = passed[pl.ds(40 + 16 * k - move, 8), :]
        lower = passed[pl.ds(48 + 16 * k - move, 8), :]
        block = jnp.concatenate([jnp.where(mask, upper, own), jnp.where(mask, lower, own)], axis=0)
        send_ref[16 * k : 16 * k + 16, :] = block.astype(BF)


def flat_kernel(next_ref, core_ref, one_ref, two_ref):
    shift = ring_shift()
    for k, ref in enumerate((core_ref, one_ref, two_ref)):
        store_flat(ref, from_ring(next_ref[k], shift))


def finish_kernel(
    got_ref, outp_ref, old_ref, utp_ref, u_ref, ot_ref, take_ref, over_ref,
    out_ref, grad_ref, table, half, result, got, pixels, tiles, qs, sems,
):
    gather_table(got_ref, take_ref, over_ref, table)
    cube = table[...].astype(BF)
    even = dot(cube[:, 0:64], ot_ref[...]).astype(BF)
    odd = dot(cube[:, 64:128], ot_ref[...]).astype(BF)
    for t in range(27):
        half[t, 0:32, :] = even[32 * t : 32 * t + 32]
        half[t, 32:64, :] = odd[32 * t : 32 * t + 32]
    u = u_ref[...]

    def store(a):
        part = pl.ds(3 * a, 3)
        return pltpu.make_async_copy(result.at[part], out_ref.at[part], sems.at[a])

    for a in range(9):
        for t in range(3 * a, 3 * a + 3):
            result[t] = dot(u, half[t]).astype(BF)
        store(a).start()

    for g in range(4):
        got[256 * g : 256 * g + 256, :] = got_ref[256 * g : 256 * g + 256, :].astype(F32)
    for k, (c, j, at) in enumerate(RELAYS):
        rows = got[pl.ds(4 * c + j, 32, stride=32), :]
        pixels[32 * k : 32 * k + 32, 0:128] = jnp.where(lane((32, 128)) // 64 == at // 64, rows, 0.0)
    spread = (sublane((128, 256)) % 64 == lane((128, 256)) % 64).astype(BF)
    pixels[...] = dot(pixels[:, 0:128].astype(BF), spread)
    row, col = lax.axis_index("rows"), lax.axis_index("cols")
    zero = jnp.zeros((8, 256), F32)

    def inside(flag, v):
        return jnp.where(jnp.full((8, 256), flag.astype(jnp.int32), jnp.int32) > 0, v, zero)

    def spot(k):
        return jnp.broadcast_to(pixels[k : k + 1, :], (8, 256))

    for f in range(FRAMES):
        for y in range(8):
            if y == 0:
                tile, left, right = pixels[24 + 8 * f : 32 + 8 * f, :], spot(93 + f), spot(90 + f)
            elif y == 7:
                tile, left, right = pixels[8 * f : 8 * f + 8, :], spot(87 + f), spot(84 + f)
            else:
                at = 48 * f + 8 * (y - 1)
                tile = outp_ref[at : at + 8, :]
                left, right = spot(66 + 6 * f + y - 1), spot(48 + 6 * f + y - 1)
            tile = shifted(tile, inside(col > 0, left), inside(col < 7, right), (64, 128), 256)
            if y == 0:
                tile = inside(row > 0, tile)
            elif y == 7:
                tile = inside(row < 31, tile)
            tiles[f, y] = tile
    stack_rows(tiles, qs)
    total = jnp.zeros((CELLS, 64), F32)
    for a in range(3):
        for b in range(3):
            rows = qs[2 - b, 48 * (2 - a) : 48 * (2 - a) + CELLS, :]
            for c in range(3):
                t = 9 * a + 3 * b + c
                part = old_ref[32 * t : 32 * t + 32, :]
                cube = jnp.concatenate([part[:, 0:64], part[:, 64:128]], axis=0)
                piece = rows[:, 64 * (2 - c) : 64 * (2 - c) + 64]
                total = total + dot_nt(piece, cube)
    grad_ref[...] = dot(total.astype(BF), utp_ref[...]).astype(BF)
    for a in range(9):
        store(a).wait()


def call(kernel, args, outs, scratch, flops=10**7):
    def spec(far):
        return pl.BlockSpec(memory_space=pltpu.HBM if far else pltpu.VMEM)

    return pl.pallas_call(
        kernel,
        out_shape=[jax.ShapeDtypeStruct(shape, dtype) for shape, dtype, _ in outs],
        in_specs=[spec(far) for _, far in args],
        out_specs=[spec(far) for _, _, far in outs],
        scratch_shapes=scratch,
        compiler_params=pltpu.CompilerParams(vmem_limit_bytes=32 << 20),
        cost_estimate=pl.CostEstimate(flops=flops, bytes_accessed=10**5, transcendentals=0),
    )(*[pltpu.with_memory_space_constraint(arg, pltpu.HBM) if far else arg for arg, far in args])


def near(*args):
    return [(arg, False) for arg in args]


def far(*args):
    return [(arg, True) for arg in args]


def swap(one, two, axis):
    count = lax.axis_size(axis)
    pairs = [[(i, i + 1) for i in range(k, count - 1, 2)] for k in range(2)]
    return tuple(
        lax.ppermute(x, axis, forward + [(b, a) for a, b in forward]) for x, forward in zip((one, two), pairs)
    )


def exchange(x):
    return lax.all_to_all(x, AXES, 0, 0, tiled=True)


def body(frames_in, cotangent, core, moment_one, moment_two, u_in, u_out):
    take, give, over = ring_tables()
    take, give, over = jnp.asarray(take, BF), jnp.asarray(give, BF), jnp.asarray(over, F32)
    vm, dma = pltpu.VMEM, pltpu.SemaphoreType.DMA
    rim = (FRAMES * 8, 256)
    row = (FRAMES, 8, 256)

    send, one, two, inner = call(
        start_kernel,
        far(core, frames_in),
        [((1024, 128), BF, False), (row, BF, False), (row, BF, False), ((FRAMES, ROWS, COLS, 256), BF, False)],
        [vm((OWN,), F32), vm((8, 128), F32), dma((2,))],
    )
    one, two = swap(one, two, "rows")
    got = exchange(send)
    own, wide, utp, u, ring, ot, cot, take, give, over = call(
        fetch_kernel,
        near(inner.reshape(CELLS, 256)) + far(
            u_in.T, u_out.T, cotangent.reshape(CELLS, 256), core, moment_one, moment_two, take, give, over,
        ),
        [
            ((CELLS, 256), F32, False), ((256, 256), BF, False), ((64, 256), BF, False), ((256, 64), BF, False),
            ((3, 4, 128), F32, False), ((64, 256), BF, False), ((CELLS, 256), BF, False),
            ((216, 512), BF, False), ((512, 240), BF, False), ((256, 128), F32, False),
        ],
        [
            vm((64, 256), BF), [vm((OWN,), F32) for _ in range(3)], vm((8, 128), F32),
            dma((9,)),
        ],
    )
    above, below, one, two = call(
        columns_kernel,
        near(inner, one, two),
        [(rim, F32, False), (rim, F32, False), (rim, BF, False), (rim, BF, False)],
        [vm(rim, F32), vm(rim, F32)],
        flops=10000000000,
    )
    one, two = swap(one, two, "cols")
    (q,) = call(
        rank_kernel,
        near(own, wide, above, below, one, two),
        [((3, 240, 256), BF, False)],
        [vm((FRAMES, 8, 8, 256), F32), vm((2, 24, 256), F32), vm((2, 24, 256), F32)],
    )
    send, table, outp = call(
        forward_kernel,
        near(got, q, cot, ot, take, give, over),
        [((1024, 128), BF, False), ((TABLE, 128), BF, False), ((CELLS, 256), F32, False)],
        [vm((TABLE, 128), F32), vm((TABLE, 128), F32), vm((CELLS, 128), F32), vm((96, 128), F32)],
    )
    got = exchange(send)
    send, latest = call(
        adam_kernel,
        near(got, ring),
        [((1024, 128), BF, False), ((3, 4, 128), F32, False)],
        [vm((1104, 128), F32)],
    )
    got = exchange(send)
    core_next, one_next, two_next = call(flat_kernel, near(latest), [((OWN,), F32, False)] * 3, [])
    got, core_next, one_next, two_next = lax.optimization_barrier((got, core_next, one_next, two_next))
    kernel_next, frames_grad = call(
        finish_kernel,
        near(got, outp, table, utp, u, ot, take, over),
        [((27, 256, 256), BF, True), ((CELLS, 256), BF, False)],
        [
            vm((TABLE, 128), F32), vm((27, 64, 256), BF), vm((27, 256, 256), BF), vm((1024, 128), F32),
            vm((96, 256), F32), vm((FRAMES, 8, 8, 256), F32), vm((3, 240, 256), BF), dma((9,)),
        ],
    )
    frames_grad = frames_grad.reshape(FRAMES, ROWS, COLS, 256)
    return frames_grad, core_next, one_next, two_next, kernel_next


def solution(mesh):
    in_specs = (
        P(None, "rows", "cols", None),
        P(None, "rows", "cols", None),
        P(AXES),
        P(AXES),
        P(AXES),
        P(),
        P(),
    )
    out_specs = (
        P(None, "rows", "cols", None),
        P(AXES),
        P(AXES),
        P(AXES),
        P(),
    )
    return jax.shard_map(body, mesh=mesh, in_specs=in_specs, out_specs=out_specs, check_vma=False)
```

```python
import jax
import jax.numpy as jnp
import numpy as np
from jax import lax
from jax.experimental import pallas as pl
from jax.experimental.pallas import tpu as pltpu
from jax.sharding import PartitionSpec as P

beta_one = 0.9
beta_two = 0.999
learn_rate = 0.06
epsilon = 1e-08
fix_one = 1.0 - 0.9**10
fix_two = 1.0 - 0.999**10

BF = jnp.bfloat16
F32 = jnp.float32
AXES = ("rows", "cols")

OWN = 432
FRAMES, ROWS, COLS = 3, 6, 8
CELLS = FRAMES * ROWS * COLS
SIDE = FRAMES * 8
TABLE = 864


RELAYS = ((7, 0, 0), (4, 0, 0), (3, 3, 64))
SLOTS = ((0, 24, -8), (24, 24, 8), (48, 18, -1), (66, 18, 1), (84, 3, -9), (87, 3, -7), (90, 3, 7), (93, 3, 9))


def ring_tables():
    take = np.zeros((216, 512), np.float32)
    give = np.zeros((512, 240), np.float32)
    over = np.zeros((256, 128), np.float32)
    for r in range(8):
        for c in range(8):
            first = 27 * r + 27 * c // 8
            col = 32 * r + 4 * c
            for j in range(4):
                take[first + j, col + j] = 1
                give[col + j, first + j] = 1
            wrapped = 48 * c % 128 + OWN - 512
            if wrapped > 0:
                take[first + 4, 256 + col] = 1
                give[256 + col, first + 4] = 1
                over[col, :wrapped] = 1
        for k, (c, j, at) in enumerate(RELAYS):
            col = 32 * r + 4 * c + j
            give[256 + col, 216 + 8 * k + r] = 1
            over[col, at : at + 64] = 1
    return take, give, over


def dot(a, b):
    return jnp.dot(a, b, preferred_element_type=F32)


def dot_nt(a, b):
    return lax.dot_general(a, b, (((1,), (1,)), ((), ())), preferred_element_type=F32)


def dot_tn(a, b):
    return lax.dot_general(a, b, (((0,), (0,)), ((), ())), preferred_element_type=F32)


def lane(shape):
    return lax.broadcasted_iota(jnp.int32, shape, 1)


def sublane(shape):
    return lax.broadcasted_iota(jnp.int32, shape, 0)


def ring_shift():
    return lax.rem(lax.axis_index("cols") * 48, 128)


def to_ring(v, shift):
    turned = pltpu.roll(v, shift, axis=1)
    above = jnp.concatenate([turned[3:4], turned[0:3]], axis=0)
    return jnp.where(lane(v.shape) >= shift, turned, above)


def from_ring(v, shift):
    turned = pltpu.roll(v, lax.rem(128 - shift, 128), axis=1)
    below = jnp.concatenate([turned[1:4], turned[0:1]], axis=0)
    return jnp.where(lane(v.shape) < 128 - shift, turned, below)


def in_ring(shift):
    place = sublane((4, 128)) * 128 + lane((4, 128)) - shift
    place = jnp.where(place < 0, place + 512, place)
    return place < OWN


def load_flat(ref, scratch):
    scratch[...] = jnp.zeros_like(scratch)
    for k in range(3):
        scratch[k, :] = ref[pl.ds(128 * k, 128)]
    scratch[3, 0 : OWN - 384] = ref[pl.ds(384, OWN - 384)]
    return scratch[0:4, :]


def store_flat(ref, v):
    for k in range(3):
        ref[pl.ds(128 * k, 128)] = v[k]
    ref[pl.ds(384, OWN - 384)] = v[3, 0 : OWN - 384]


def fetch(pairs, sems):
    copies = [pltpu.make_async_copy(src, dst, sems.at[k]) for k, (src, dst) in enumerate(pairs)]
    for copy in copies:
        copy.start()
    return copies


def even_first(axis, first, last):
    even = jnp.full(first.shape, lax.rem(lax.axis_index(axis), 2), jnp.int32) == 0
    return jnp.where(even, last, first), jnp.where(even, first, last)


def start_kernel(core_ref, x_ref, send_ref, one_ref, two_ref, inner_ref, own, flat, low, high, sems):
    copies = fetch(((x_ref, inner_ref), (core_ref, own)), sems)
    copies[1].wait()
    v = to_ring(load_flat(own, flat), ring_shift())
    block = jnp.concatenate([v, v, v, v], axis=0).astype(BF)
    for k in range(64):
        send_ref[16 * k : 16 * k + 16, :] = block
    copies[0].wait()
    for f in range(FRAMES):
        for y in range(ROWS):
            tile = inner_ref[f, y].astype(F32)
            k = ROWS * f + y
            low[k : k + 1, :] = tile[0:1, :]
            high[k : k + 1, :] = tile[7:8, :]
    one, two = even_first("cols", low[...], high[...])
    one_ref[...] = one.astype(BF)
    two_ref[...] = two.astype(BF)


def rows_kernel(inner_ref, one_ref, two_ref, left_ref, right_ref, up_ref, down_ref, first, last):
    right, left = even_first("cols", two_ref[...].astype(F32), one_ref[...].astype(F32))
    left_ref[...] = left
    right_ref[...] = right
    first[...] = jnp.zeros_like(first)
    last[...] = jnp.zeros_like(last)
    for f in range(FRAMES):
        for y, rows in ((0, first), (ROWS - 1, last)):
            k = ROWS * f + y
            rows[16 * f : 16 * f + 8, :] = inner_ref[f, y].astype(F32)
            rows[16 * f + 8 : 16 * f + 9, :] = left_ref[k : k + 1, :]
            rows[16 * f + 9 : 16 * f + 10, :] = right_ref[k : k + 1, :]
    one, two = even_first("rows", first[...], last[...])
    up_ref[...] = one.astype(BF)
    down_ref[...] = two.astype(BF)


def shifted(tile, left, right, bounds, period):
    at = lane(tile.shape) % period
    row = sublane(tile.shape)
    back = jnp.where(row == 0, left, pltpu.roll(tile, 1, axis=0))
    ahead = jnp.where(row == 7, right, pltpu.roll(tile, 7, axis=0))
    return jnp.where(at < bounds[0], back, jnp.where(at < bounds[1], tile, ahead))


def fetch_kernel(
    x_ref, ut_ref, ot_ref, cot_ref, core_ref, one_ref, two_ref, take_ref, give_ref, over_ref,
    own_ref, wide_ref, utp_ref, u_ref, ring_ref, ot_out, cot_out, take_out, give_out, over_out,
    ut, owns, flat, sems,
):
    copies = fetch(
        (
            (ut_ref, ut), (core_ref, owns[0]), (one_ref, owns[1]), (two_ref, owns[2]),
            (take_ref, take_out), (give_ref, give_out), (over_ref, over_out), (ot_ref, ot_out), (cot_ref, cot_out),
        ),
        sems,
    )
    row = sublane((256, 64))
    at = row % 128
    pick = (lane((256, 64)) == (at % 32) * 2 + row // 128) & (at < 96)
    half_row = sublane((64, 64))
    half_pick = lane((64, 64)) == (half_row % 32) * 2 + half_row // 32
    copies[0].wait()
    wide = dot(pick.astype(BF), ut[...]).astype(BF)
    wide_ref[...] = wide
    utp = dot(half_pick.astype(BF), ut[...])
    utp_ref[...] = utp.astype(BF)
    u_ref[...] = utp.T.astype(BF)
    own_ref[...] = dot_nt(x_ref[...], wide).astype(BF).astype(F32)
    shift = ring_shift()
    for k in range(3):
        copies[1 + k].wait()
        ring_ref[k] = to_ring(load_flat(owns[k], flat), shift)
    for k in range(4, 9):
        copies[k].wait()


def stack_rows(tiles, out_ref):
    for b in range(3):
        out_ref[b, 0:48, :] = jnp.zeros((48, 256), BF)
        out_ref[b, 192:240, :] = jnp.zeros((48, 256), BF)
        for f in range(FRAMES):
            rows = tiles[f, b : b + ROWS].reshape(48, 256)
            out_ref[b, 48 * f + 48 : 48 * f + 96, :] = rows.astype(BF)


def rank_kernel(own_ref, wide_ref, one_ref, two_ref, left_ref, right_ref, q_ref, tiles, edge, rims):
    wide = wide_ref[...]

    def project(v):
        return dot_nt(v.astype(BF), wide).astype(BF).astype(F32)

    below, above = even_first("rows", project(two_ref[...]), project(one_ref[...]))
    rims[0] = above
    rims[1] = below
    edge[0] = project(left_ref[...])
    edge[1] = project(right_ref[...])
    for f in range(FRAMES):
        for y in range(8):
            if y in (0, 7):
                rim = rims.at[y // 7]
                at = 16 * f
                tile, left, right = rim[at : at + 8, :], rim[at + 8 : at + 9, :], rim[at + 9 : at + 10, :]
            else:
                k = ROWS * f + y - 1
                tile = own_ref[8 * k : 8 * k + 8, :]
                left, right = edge[0, k : k + 1, :], edge[1, k : k + 1, :]
            left = jnp.broadcast_to(left, (8, 256))
            right = jnp.broadcast_to(right, (8, 256))
            tiles[f, y] = shifted(tile, left, right, (32, 64), 128)
    stack_rows(tiles, q_ref)


def gather_table(got_ref, take_ref, over_ref, table_ref):
    over = over_ref[...] > 0
    take = take_ref[...]
    for g in range(4):
        block = got_ref[256 * g : 256 * g + 256, :]
        none = jnp.zeros_like(block)
        both = jnp.concatenate(
            [jnp.where(over, none, block), jnp.where(over, block, none)], axis=0
        )
        table_ref[216 * g : 216 * g + 216, :] = dot(take, both)


def forward_kernel(
    got_ref, q_ref, cot_ref, ot_ref, take_ref, give_ref, over_ref,
    send_ref, table_out, outp_ref, table, grads, border, pixels,
):
    gather_table(got_ref, take_ref, over_ref, table)
    table_out[...] = table[...].astype(BF)
    even = jnp.zeros((CELLS, 128), F32)
    odd = jnp.zeros((CELLS, 128), F32)
    for a in range(3):
        for b in range(3):
            k = 3 * a + b
            weights = table_out[96 * k : 96 * k + 96, :]
            rows = q_ref[b, 48 * a : 48 * a + CELLS, :]
            even = even + dot(rows[:, 0:96], weights)
            odd = odd + dot(rows[:, 128:224], weights)
    mid = (even[:, 0:64] + odd[:, 64:128]).astype(BF)
    pre = dot(mid, ot_ref[...])
    sig = jax.nn.sigmoid(pre)
    slope = (cot_ref[...].astype(F32) * sig * (1.0 + pre * (1.0 - sig))).astype(BF)
    ot = ot_ref[...]
    out_t = dot_nt(ot, slope).astype(BF)
    wide = jnp.concatenate([ot, ot, ot, ot], axis=0)
    outp = dot_nt(slope, wide).astype(BF).astype(F32)
    outp_ref[...] = outp
    border[...] = outp[:, 0:128]
    for f in range(FRAMES):
        pixels[8 * f : 8 * f + 8, :] = border[48 * f : 48 * f + 8, :]
        pixels[24 + 8 * f : 32 + 8 * f, :] = border[48 * f + 40 : 48 * f + 48, :]
    pixels[48:66, :] = border[pl.ds(0, 18, stride=8), :]
    pixels[66:84, :] = border[pl.ds(7, 18, stride=8), :]
    for k, cell in enumerate((0, 7, 40, 47)):
        pixels[84 + 3 * k : 87 + 3 * k, :] = border[pl.ds(cell, 3, stride=48), :]
    for a in range(3):
        for b in range(3):
            k = 3 * a + b
            part = dot(out_t, q_ref[b, 48 * a : 48 * a + CELLS, :])
            stack = jnp.concatenate([part[:, 0:128], part[:, 128:256]], axis=0)
            grads[96 * k : 96 * k + 96, :] = stack.T[0:96, :]
    over = over_ref[...] > 0
    give = give_ref[...]
    for g in range(4):
        source = [grads[216 * g : 216 * g + 216, :]]
        for k in range(3):
            source.append(pixels[32 * k + 8 * g : 32 * k + 8 * g + 8, :])
        part = dot(give, jnp.concatenate(source, axis=0).astype(BF))
        send_ref[256 * g : 256 * g + 256, :] = jnp.where(over, part[256:512], part[0:256]).astype(BF)


def adam_kernel(got_ref, ring_ref, send_ref, next_ref, passed):
    total = jnp.zeros((8, 128), F32)
    passed[0:40, :] = jnp.zeros((40, 128), F32)
    passed[1064:1104, :] = jnp.zeros((40, 128), F32)
    for g in range(8):
        part = got_ref[128 * g : 128 * g + 128, :].astype(F32)
        passed[128 * g + 40 : 128 * g + 168, :] = part
        total = total + part.reshape(16, 8, 128).sum(axis=0)
    grad = (total[0:4] + total[4:8]) * (1.0 / 192.0)
    core, one, two = ring_ref[0], ring_ref[1], ring_ref[2]
    one = beta_one * one + (1.0 - beta_one) * grad
    two = beta_two * two + (1.0 - beta_two) * grad * grad
    core = core - learn_rate * (one / fix_one) / (jnp.sqrt(two / fix_two) + epsilon)
    next_ref[0] = core
    next_ref[1] = one
    next_ref[2] = two
    own = jnp.where(in_ring(ring_shift()), core, 0.0)
    own = jnp.concatenate([own, own], axis=0)
    row, col = lax.axis_index("rows"), lax.axis_index("cols")
    slot, mask = row, jnp.zeros((8, 128), jnp.bool_)
    for k, (c, j, at) in enumerate(RELAYS):
        slot = slot + jnp.where(col == c, 32 * k, 0)
        spot = (sublane((8, 128)) % 4 == j) & (lane((8, 128)) // 64 == at // 64)
        mask = mask | (spot & (jnp.full((8, 128), col, jnp.int32) == c))
    move = 0
    for first, count, offset in SLOTS:
        move = move + jnp.where((slot >= first) & (slot < first + count), 4 * offset, 0)
    for k in range(64):
        upper = passed[pl.ds(40 + 16 * k - move, 8), :]
        lower = passed[pl.ds(48 + 16 * k - move, 8), :]
        block = jnp.concatenate([jnp.where(mask, upper, own), jnp.where(mask, lower, own)], axis=0)
        send_ref[16 * k : 16 * k + 16, :] = block.astype(BF)


def flat_kernel(next_ref, core_ref, one_ref, two_ref):
    shift = ring_shift()
    for k, ref in enumerate((core_ref, one_ref, two_ref)):
        store_flat(ref, from_ring(next_ref[k], shift))


def turn_kernel(table_ref, back_ref):
    for k in range(9):
        for c in range(3):
            t = 3 * k + c
            part = table_ref[32 * t : 32 * t + 32, :].astype(F32).T
            cube = jnp.concatenate([part[0:64], part[64:128]], axis=1)
            back_ref[k, 64 * (2 - c) : 64 * (2 - c) + 64, :] = cube.astype(BF)


def finish_kernel(
    got_ref, outp_ref, back_ref, utp_ref, u_ref, ot_ref, take_ref, over_ref,
    out_ref, grad_ref, table, half, result, got, pixels, tiles, qs, sems,
):
    gather_table(got_ref, take_ref, over_ref, table)
    cube = table[...].astype(BF)
    even = dot(cube[:, 0:64], ot_ref[...]).astype(BF)
    odd = dot(cube[:, 64:128], ot_ref[...]).astype(BF)
    for t in range(27):
        half[t, 0:32, :] = even[32 * t : 32 * t + 32]
        half[t, 32:64, :] = odd[32 * t : 32 * t + 32]
    u = u_ref[...]

    def store(a):
        part = pl.ds(3 * a, 3)
        return pltpu.make_async_copy(result.at[part], out_ref.at[part], sems.at[a])

    for a in range(9):
        for t in range(3 * a, 3 * a + 3):
            result[t] = dot(u, half[t]).astype(BF)
        store(a).start()

    for g in range(4):
        got[256 * g : 256 * g + 256, :] = got_ref[256 * g : 256 * g + 256, :].astype(F32)
    for k, (c, j, at) in enumerate(RELAYS):
        rows = got[pl.ds(4 * c + j, 32, stride=32), :]
        pixels[32 * k : 32 * k + 32, 0:128] = jnp.where(lane((32, 128)) // 64 == at // 64, rows, 0.0)
    spread = (sublane((128, 256)) % 64 == lane((128, 256)) % 64).astype(BF)
    pixels[...] = dot(pixels[:, 0:128].astype(BF), spread)
    row, col = lax.axis_index("rows"), lax.axis_index("cols")
    zero = jnp.zeros((8, 256), F32)

    def inside(flag, v):
        return jnp.where(jnp.full((8, 256), flag.astype(jnp.int32), jnp.int32) > 0, v, zero)

    def spot(k):
        return jnp.broadcast_to(pixels[k : k + 1, :], (8, 256))

    for f in range(FRAMES):
        for y in range(8):
            if y == 0:
                tile, left, right = pixels[24 + 8 * f : 32 + 8 * f, :], spot(93 + f), spot(90 + f)
            elif y == 7:
                tile, left, right = pixels[8 * f : 8 * f + 8, :], spot(87 + f), spot(84 + f)
            else:
                at = 48 * f + 8 * (y - 1)
                tile = outp_ref[at : at + 8, :]
                left, right = spot(66 + 6 * f + y - 1), spot(48 + 6 * f + y - 1)
            tile = shifted(tile, inside(col > 0, left), inside(col < 7, right), (64, 128), 256)
            if y == 0:
                tile = inside(row > 0, tile)
            elif y == 7:
                tile = inside(row < 31, tile)
            tiles[f, y] = tile
    stack_rows(tiles, qs)
    total = jnp.zeros((CELLS, 64), F32)
    for a in range(3):
        for b in range(3):
            rows = qs[2 - b, 48 * (2 - a) : 48 * (2 - a) + CELLS, :]
            total = total + dot(rows[:, 0:192], back_ref[3 * a + b])
    grad_ref[...] = dot(total.astype(BF), utp_ref[...]).astype(BF)
    for a in range(9):
        store(a).wait()


def call(kernel, args, outs, scratch, flops=10**7):
    def spec(far):
        return pl.BlockSpec(memory_space=pltpu.HBM if far else pltpu.VMEM)

    return pl.pallas_call(
        kernel,
        out_shape=[jax.ShapeDtypeStruct(shape, dtype) for shape, dtype, _ in outs],
        in_specs=[spec(far) for _, far in args],
        out_specs=[spec(far) for _, _, far in outs],
        scratch_shapes=scratch,
        compiler_params=pltpu.CompilerParams(vmem_limit_bytes=32 << 20),
        cost_estimate=pl.CostEstimate(flops=flops, bytes_accessed=10**5, transcendentals=0),
    )(*[pltpu.with_memory_space_constraint(arg, pltpu.HBM) if far else arg for arg, far in args])


def near(*args):
    return [(arg, False) for arg in args]


def far(*args):
    return [(arg, True) for arg in args]


def swap(one, two, axis):
    count = lax.axis_size(axis)
    pairs = [[(i, i + 1) for i in range(k, count - 1, 2)] for k in range(2)]
    two, one = (
        lax.ppermute(x, axis, forward + [(b, a) for a, b in forward]) for x, forward in ((two, pairs[1]), (one, pairs[0]))
    )
    return one, two


def exchange(x):
    return lax.all_to_all(x, AXES, 0, 0, tiled=True)


def body(frames_in, cotangent, core, moment_one, moment_two, u_in, u_out):
    take, give, over = ring_tables()
    take, give, over = jnp.asarray(take, BF), jnp.asarray(give, BF), jnp.asarray(over, F32)
    vm, dma = pltpu.VMEM, pltpu.SemaphoreType.DMA
    side = (FRAMES * ROWS, 256)
    rim = (FRAMES * 16, 256)

    send, one, two, inner = call(
        start_kernel,
        far(core, frames_in),
        [((1024, 128), BF, False), (side, BF, False), (side, BF, False), ((FRAMES, ROWS, COLS, 256), BF, False)],
        [vm((OWN,), F32), vm((8, 128), F32), vm(side, F32), vm(side, F32), dma((2,))],
    )
    one, two = swap(one, two, "cols")
    got = exchange(send)
    own, wide, utp, u, ring, ot, cot, take, give, over = call(
        fetch_kernel,
        near(inner.reshape(CELLS, 256)) + far(
            u_in.T, u_out.T, cotangent.reshape(CELLS, 256), core, moment_one, moment_two, take, give, over,
        ),
        [
            ((CELLS, 256), F32, False), ((256, 256), BF, False), ((64, 256), BF, False), ((256, 64), BF, False),
            ((3, 4, 128), F32, False), ((64, 256), BF, False), ((CELLS, 256), BF, False),
            ((216, 512), BF, False), ((512, 240), BF, False), ((256, 128), F32, False),
        ],
        [
            vm((64, 256), BF), [vm((OWN,), F32) for _ in range(3)], vm((8, 128), F32),
            dma((9,)),
        ],
    )
    left, right, one, two = call(
        rows_kernel,
        near(inner, one, two),
        [(side, F32, False), (side, F32, False), (rim, BF, False), (rim, BF, False)],
        [vm(rim, F32), vm(rim, F32)],
        flops=10**10,
    )
    one, two = swap(one, two, "rows")
    (q,) = call(
        rank_kernel,
        near(own, wide, one, two, left, right),
        [((3, 240, 256), BF, False)],
        [vm((FRAMES, 8, 8, 256), F32), vm((2, 18, 256), F32), vm((2, 48, 256), F32)],
    )
    send, table, outp = call(
        forward_kernel,
        near(got, q, cot, ot, take, give, over),
        [((1024, 128), BF, False), ((TABLE, 128), BF, False), ((CELLS, 256), F32, False)],
        [vm((TABLE, 128), F32), vm((TABLE, 128), F32), vm((CELLS, 128), F32), vm((96, 128), F32)],
    )
    got = exchange(send)
    (back,) = call(turn_kernel, near(table), [((9, 192, 64), BF, False)], [])
    got, back = lax.optimization_barrier((got, back))
    send, latest = call(
        adam_kernel,
        near(got, ring),
        [((1024, 128), BF, False), ((3, 4, 128), F32, False)],
        [vm((1104, 128), F32)],
    )
    got = exchange(send)
    core_next, one_next, two_next = call(flat_kernel, near(latest), [((OWN,), F32, False)] * 3, [])
    got, core_next, one_next, two_next = lax.optimization_barrier((got, core_next, one_next, two_next))
    kernel_next, frames_grad = call(
        finish_kernel,
        near(got, outp, back, utp, u, ot, take, over),
        [((27, 256, 256), BF, True), ((CELLS, 256), BF, False)],
        [
            vm((TABLE, 128), F32), vm((27, 64, 256), BF), vm((27, 256, 256), BF), vm((1024, 128), F32),
            vm((96, 256), F32), vm((FRAMES, 8, 8, 256), F32), vm((3, 240, 256), BF), dma((9,)),
        ],
    )
    frames_grad = frames_grad.reshape(FRAMES, ROWS, COLS, 256)
    return frames_grad, core_next, one_next, two_next, kernel_next


def solution(mesh):
    in_specs = (
        P(None, "rows", "cols", None),
        P(None, "rows", "cols", None),
        P(AXES),
        P(AXES),
        P(AXES),
        P(),
        P(),
    )
    out_specs = (
        P(None, "rows", "cols", None),
        P(AXES),
        P(AXES),
        P(AXES),
        P(),
    )
    return jax.shard_map(body, mesh=mesh, in_specs=in_specs, out_specs=out_specs, check_vma=False)
```

```python
import jax
import jax.numpy as jnp
import numpy as np
from jax import lax
from jax.experimental import pallas as pl
from jax.experimental.pallas import tpu as pltpu
from jax.sharding import PartitionSpec as P

beta_one = 0.9
beta_two = 0.999
learn_rate = 0.06
epsilon = 1e-08
fix_one = 1.0 - 0.9**10
fix_two = 1.0 - 0.999**10

BF = jnp.bfloat16
F32 = jnp.float32
AXES = ("rows", "cols")

OWN = 432
FRAMES, ROWS, COLS = 3, 6, 8
CELLS = FRAMES * ROWS * COLS
SIDE = FRAMES * 8
TABLE = 864


RELAYS = ((7, 0, 0), (4, 0, 0), (3, 3, 64), (0, 3, 64), (2, 0, 16), (5, 0, 32))
SLOTS = (
    (0, 24, -1, 0), (24, 24, 1, 0), (48, 18, 0, -1), (66, 18, 0, 1),
    (84, 3, -1, -1), (87, 3, -1, 1), (90, 3, 1, -1), (93, 3, 1, 1),
)


def ring_tables():
    take = np.zeros((216, 512), np.float32)
    give = np.zeros((512, 216), np.float32)
    kind = np.zeros((256, 128), np.float32)
    for r in range(8):
        for c in range(8):
            first = 27 * r + 27 * c // 8
            col = 128 * (r % 2) + 32 * (r // 2) + 4 * c
            for j in range(4):
                take[first + j, col + j] = 1
                give[col + j, first + j] = 1
            wrapped = 48 * c % 128 + OWN - 512
            if wrapped > 0:
                take[first + 4, 256 + col] = 1
                give[256 + col, first + 4] = 1
                kind[col, :wrapped] = 1
        for c, j, at in RELAYS:
            kind[128 * (r % 2) + 32 * (r // 2) + 4 * c + j, at : at + 64] = 2
    return take, give, kind


def dot(a, b):
    return jnp.dot(a, b, preferred_element_type=F32)


def dot_nt(a, b):
    return lax.dot_general(a, b, (((1,), (1,)), ((), ())), preferred_element_type=F32)


def dot_tn(a, b):
    return lax.dot_general(a, b, (((0,), (0,)), ((), ())), preferred_element_type=F32)


def lane(shape):
    return lax.broadcasted_iota(jnp.int32, shape, 1)


def sublane(shape):
    return lax.broadcasted_iota(jnp.int32, shape, 0)


def ring_shift():
    return lax.rem(lax.axis_index("cols") * 48, 128)


def to_ring(v, shift):
    turned = pltpu.roll(v, shift, axis=1)
    above = jnp.concatenate([turned[3:4], turned[0:3]], axis=0)
    return jnp.where(lane(v.shape) >= shift, turned, above)


def from_ring(v, shift):
    turned = pltpu.roll(v, lax.rem(128 - shift, 128), axis=1)
    below = jnp.concatenate([turned[1:4], turned[0:1]], axis=0)
    return jnp.where(lane(v.shape) < 128 - shift, turned, below)


def in_ring(shift):
    place = sublane((4, 128)) * 128 + lane((4, 128)) - shift
    place = jnp.where(place < 0, place + 512, place)
    return place < OWN


def load_flat(ref, scratch):
    scratch[...] = jnp.zeros_like(scratch)
    for k in range(3):
        scratch[k, :] = ref[pl.ds(128 * k, 128)]
    scratch[3, 0 : OWN - 384] = ref[pl.ds(384, OWN - 384)]
    return scratch[0:4, :]


def store_flat(ref, v):
    for k in range(3):
        ref[pl.ds(128 * k, 128)] = v[k]
    ref[pl.ds(384, OWN - 384)] = v[3, 0 : OWN - 384]


def fetch(pairs, sems):
    copies = [pltpu.make_async_copy(src, dst, sems.at[k]) for k, (src, dst) in enumerate(pairs)]
    for copy in copies:
        copy.start()
    return copies


def even_first(axis, first, last):
    even = jnp.full(first.shape, lax.rem(lax.axis_index(axis), 2), jnp.int32) == 0
    return jnp.where(even, last, first), jnp.where(even, first, last)


def start_kernel(core_ref, x_ref, send_ref, one_ref, two_ref, inner_ref, own, flat, block, low, high, sems):
    copies = fetch(((core_ref, own), (x_ref, inner_ref)), sems)
    copies[0].wait()
    v = to_ring(load_flat(own, flat), ring_shift())
    rows = jnp.concatenate([v, v, v, v], axis=0).astype(BF)
    for k in range(8):
        block[16 * k : 16 * k + 16, :] = rows
    sends = fetch([(block, send_ref.at[pl.ds(128 * k, 128)]) for k in range(4)], sems.at[pl.ds(2, 4)])
    copies[1].wait()
    for f in range(FRAMES):
        for y in range(ROWS):
            tile = inner_ref[f, y].astype(F32)
            k = ROWS * f + y
            low[k : k + 1, :] = tile[0:1, :]
            high[k : k + 1, :] = tile[7:8, :]
    one, two = even_first("cols", low[...], high[...])
    one_ref[...] = one.astype(BF)
    two_ref[...] = two.astype(BF)
    for copy in sends:
        copy.wait()


def rows_kernel(inner_ref, one_ref, two_ref, left_ref, right_ref, up_ref, down_ref, first, last):
    right, left = even_first("cols", two_ref[...].astype(F32), one_ref[...].astype(F32))
    left_ref[...] = left
    right_ref[...] = right
    first[...] = jnp.zeros_like(first)
    last[...] = jnp.zeros_like(last)
    for f in range(FRAMES):
        for y, rows in ((0, first), (ROWS - 1, last)):
            k = ROWS * f + y
            rows[16 * f : 16 * f + 8, :] = inner_ref[f, y].astype(F32)
            rows[16 * f + 8 : 16 * f + 9, :] = left_ref[k : k + 1, :]
            rows[16 * f + 9 : 16 * f + 10, :] = right_ref[k : k + 1, :]
    one, two = even_first("rows", first[...], last[...])
    up_ref[...] = one.astype(BF)
    down_ref[...] = two.astype(BF)


def shifted(tile, left, right, bounds, period):
    at = lane(tile.shape) % period
    row = sublane(tile.shape)
    back = jnp.where(row == 0, left, pltpu.roll(tile, 1, axis=0))
    ahead = jnp.where(row == 7, right, pltpu.roll(tile, 7, axis=0))
    return jnp.where(at < bounds[0], back, jnp.where(at < bounds[1], tile, ahead))


def fetch_kernel(
    x_ref, ut_ref, ot_ref, cot_ref, core_ref, one_ref, two_ref, take_ref, give_ref, kind_ref,
    own_ref, wide_ref, utp_ref, u_ref, ring_ref, ot_out, cot_out, take_out, give_out, kind_out,
    ut, owns, flat, sems,
):
    copies = fetch(
        (
            (ut_ref, ut), (core_ref, owns[0]), (one_ref, owns[1]), (two_ref, owns[2]),
            (take_ref, take_out), (give_ref, give_out), (kind_ref, kind_out), (ot_ref, ot_out), (cot_ref, cot_out),
        ),
        sems,
    )
    row = sublane((256, 64))
    at = row % 128
    pick = (lane((256, 64)) == (at % 32) * 2 + row // 128) & (at < 96)
    half_row = sublane((64, 64))
    half_pick = lane((64, 64)) == (half_row % 32) * 2 + half_row // 32
    copies[0].wait()
    wide = dot(pick.astype(BF), ut[...]).astype(BF)
    wide_ref[...] = wide
    utp = dot(half_pick.astype(BF), ut[...])
    utp_ref[...] = utp.astype(BF)
    u_ref[...] = utp.T.astype(BF)
    own_ref[...] = dot_nt(x_ref[...], wide).astype(BF).astype(F32)
    shift = ring_shift()
    for k in range(3):
        copies[1 + k].wait()
        ring_ref[k] = to_ring(load_flat(owns[k], flat), shift)
    for k in range(4, 9):
        copies[k].wait()


def stack_rows(tiles, out_ref):
    for b in range(3):
        out_ref[b, 0:48, :] = jnp.zeros((48, 256), BF)
        out_ref[b, 192:240, :] = jnp.zeros((48, 256), BF)
        for f in range(FRAMES):
            rows = tiles[f, b : b + ROWS].reshape(48, 256)
            out_ref[b, 48 * f + 48 : 48 * f + 96, :] = rows.astype(BF)


def rank_kernel(own_ref, wide_ref, one_ref, two_ref, left_ref, right_ref, q_ref, tiles, edge, rims):
    wide = wide_ref[...]

    def project(v):
        return dot_nt(v.astype(BF), wide).astype(BF).astype(F32)

    below, above = even_first("rows", project(two_ref[...]), project(one_ref[...]))
    rims[0] = above
    rims[1] = below
    edge[0] = project(left_ref[...])
    edge[1] = project(right_ref[...])
    for f in range(FRAMES):
        for y in range(8):
            if y in (0, 7):
                rim = rims.at[y // 7]
                at = 16 * f
                tile, left, right = rim[at : at + 8, :], rim[at + 8 : at + 9, :], rim[at + 9 : at + 10, :]
            else:
                k = ROWS * f + y - 1
                tile = own_ref[8 * k : 8 * k + 8, :]
                left, right = edge[0, k : k + 1, :], edge[1, k : k + 1, :]
            left = jnp.broadcast_to(left, (8, 256))
            right = jnp.broadcast_to(right, (8, 256))
            tiles[f, y] = shifted(tile, left, right, (32, 64), 128)
    stack_rows(tiles, q_ref)


def gather_table(got_ref, take_ref, kind_ref, table_ref):
    kind = kind_ref[...]
    take = take_ref[...]
    for g in range(4):
        block = jnp.concatenate([got_ref[512 * k + 128 * g : 512 * k + 128 * g + 128, :] for k in range(2)], axis=0)
        none = jnp.zeros_like(block)
        both = jnp.concatenate(
            [jnp.where(kind == 0, block, none), jnp.where(kind == 1, block, none)], axis=0
        )
        table_ref[216 * g : 216 * g + 216, :] = dot(take, both)


def inside(lanes, at):
    return (lanes >= at) & (lanes < at + 64)


def forward_kernel(
    got_ref, q_ref, cot_ref, ot_ref, take_ref, give_ref, kind_ref,
    send_ref, table_out, outp_ref, table, grads, border, pixels, blocks,
):
    gather_table(got_ref, take_ref, kind_ref, table)
    table_out[...] = table[...].astype(BF)
    even = jnp.zeros((CELLS, 128), F32)
    odd = jnp.zeros((CELLS, 128), F32)
    for a in range(3):
        for b in range(3):
            k = 3 * a + b
            weights = table_out[96 * k : 96 * k + 96, :]
            rows = q_ref[b, 48 * a : 48 * a + CELLS, :]
            even = even + dot(rows[:, 0:96], weights)
            odd = odd + dot(rows[:, 128:224], weights)
    mid = (even[:, 0:64] + odd[:, 64:128]).astype(BF)
    pre = dot(mid, ot_ref[...])
    sig = jax.nn.sigmoid(pre)
    slope = (cot_ref[...].astype(F32) * sig * (1.0 + pre * (1.0 - sig))).astype(BF)
    ot = ot_ref[...]
    out_t = dot_nt(ot, slope).astype(BF)
    wide = jnp.concatenate([ot, ot, ot, ot], axis=0)
    outp = dot_nt(slope, wide).astype(BF).astype(F32)
    outp_ref[...] = outp
    border[...] = outp[:, 0:128]
    for f in range(FRAMES):
        pixels[8 * f : 8 * f + 8, :] = border[48 * f : 48 * f + 8, :]
        pixels[24 + 8 * f : 32 + 8 * f, :] = border[48 * f + 40 : 48 * f + 48, :]
    pixels[48:66, :] = border[pl.ds(0, 18, stride=8), :]
    pixels[66:84, :] = border[pl.ds(7, 18, stride=8), :]
    for k, cell in enumerate((0, 7, 40, 47)):
        pixels[84 + 3 * k : 87 + 3 * k, :] = border[pl.ds(cell, 3, stride=48), :]
    for a in range(3):
        for b in range(3):
            k = 3 * a + b
            part = dot(out_t, q_ref[b, 48 * a : 48 * a + CELLS, :])
            stack = jnp.concatenate([part[:, 0:128], part[:, 128:256]], axis=0)
            grads[96 * k : 96 * k + 96, :] = stack.T[0:96, :]
    wrapped = kind_ref[...] == 1
    give = give_ref[...]
    for g in range(4):
        part = dot(give, grads[216 * g : 216 * g + 216, :].astype(BF))
        part = jnp.where(wrapped, part[256:512], part[0:256])
        for k in range(2):
            blocks[512 * k + 128 * g : 512 * k + 128 * g + 128, :] = part[128 * k : 128 * k + 128]
    lanes = lane((16, 128))
    for a, (c, j, at) in enumerate(RELAYS):
        for k in range(2):
            first = 32 * (a % 3) + 16 * k
            pixel = pixels[first : first + 16, :]
            if at % 64:
                pixel = pltpu.roll(pixel, at, axis=1)
            spot = pl.ds(512 * k + 4 * c + j, 16, stride=32)
            blocks[spot, :] = jnp.where(inside(lanes, at), pixel, blocks[spot, :])
    for g in range(4):
        send_ref[256 * g : 256 * g + 256, :] = blocks[256 * g : 256 * g + 256, :].astype(BF)


def adam_kernel(got_ref, ring_ref, send_ref, next_ref, passed):
    total = jnp.zeros((8, 128), F32)
    passed[0:40, :] = jnp.zeros((40, 128), F32)
    passed[1064:1104, :] = jnp.zeros((40, 128), F32)
    for g in range(8):
        part = got_ref[128 * g : 128 * g + 128, :].astype(F32)
        passed[128 * g + 40 : 128 * g + 168, :] = part
        total = total + part.reshape(16, 8, 128).sum(axis=0)
    grad = (total[0:4] + total[4:8]) * (1.0 / 192.0)
    core, one, two = ring_ref[0], ring_ref[1], ring_ref[2]
    one = beta_one * one + (1.0 - beta_one) * grad
    two = beta_two * two + (1.0 - beta_two) * grad * grad
    core = core - learn_rate * (one / fix_one) / (jnp.sqrt(two / fix_two) + epsilon)
    next_ref[0] = core
    next_ref[1] = one
    next_ref[2] = two
    own = jnp.where(in_ring(ring_shift()), core, 0.0)
    own = jnp.concatenate([own, own], axis=0)
    row, col = lax.axis_index("rows"), lax.axis_index("cols")
    slot = 16 * lax.rem(row, 2) + lax.div(row, 2)
    parity, mask = 0, jnp.zeros((8, 128), jnp.bool_)
    for a, (c, j, at) in enumerate(RELAYS):
        slot = slot + jnp.where(col == c, 32 * (a % 3), 0)
        parity = parity + jnp.where(col == c, a // 3, 0)
        spot = (sublane((8, 128)) % 4 == j) & inside(lane((8, 128)), at)
        mask = mask | (spot & (jnp.full((8, 128), col, jnp.int32) == c))
    up, right = 0, 0
    for first, count, rows, cols in SLOTS:
        here = (slot >= first) & (slot < first + count)
        up = up + jnp.where(here, rows, 0)
        right = right + jnp.where(here, cols, 0)
    source = lax.rem(parity - up + 2, 2)
    chips = lax.div(source + up - parity + 2, 2) - 1
    start = 40 + 512 * source - 4 * (8 * chips + right)
    for k in range(32):
        upper = passed[pl.ds(start + 16 * k, 8), :]
        lower = passed[pl.ds(start + 16 * k + 8, 8), :]
        block = jnp.concatenate([jnp.where(mask, upper, own), jnp.where(mask, lower, own)], axis=0)
        send_ref[16 * k : 16 * k + 16, :] = block.astype(BF)


def flat_kernel(next_ref, core_ref, one_ref, two_ref):
    shift = ring_shift()
    for k, ref in enumerate((core_ref, one_ref, two_ref)):
        store_flat(ref, from_ring(next_ref[k], shift))


def turn_kernel(table_ref, back_ref):
    for k in range(9):
        for c in range(3):
            t = 3 * k + c
            part = table_ref[32 * t : 32 * t + 32, :].astype(F32).T
            cube = jnp.concatenate([part[0:64], part[64:128]], axis=1)
            back_ref[k, 64 * (2 - c) : 64 * (2 - c) + 64, :] = cube.astype(BF)


def finish_kernel(
    got_ref, outp_ref, back_ref, utp_ref, u_ref, ot_ref, take_ref, kind_ref,
    out_ref, grad_ref, table, half, result, got, pixels, tiles, qs, sems,
):
    gather_table(got_ref, take_ref, kind_ref, table)
    cube = table[...].astype(BF)
    even = dot(cube[:, 0:64], ot_ref[...]).astype(BF)
    odd = dot(cube[:, 64:128], ot_ref[...]).astype(BF)
    for t in range(27):
        half[t, 0:32, :] = even[32 * t : 32 * t + 32]
        half[t, 32:64, :] = odd[32 * t : 32 * t + 32]
    u = u_ref[...]

    def store(a):
        part = pl.ds(3 * a, 3)
        return pltpu.make_async_copy(result.at[part], out_ref.at[part], sems.at[a])

    for a in range(9):
        for t in range(3 * a, 3 * a + 3):
            result[t] = dot(u, half[t]).astype(BF)
        store(a).start()

    for g in range(4):
        got[256 * g : 256 * g + 256, :] = got_ref[256 * g : 256 * g + 256, :].astype(F32)
    row, col = lax.axis_index("rows"), lax.axis_index("cols")
    lanes = lane((16, 128))
    for q in range(3):
        for k in range(2):
            found = []
            for c, j, at in (RELAYS[q], RELAYS[q + 3]):
                pixel = got[pl.ds(512 * k + 4 * c + j, 16, stride=32), :]
                found.append(pltpu.roll(pixel, 128 - at, axis=1) if at else pixel)
            odd = jnp.full((16, 128), lax.rem(row, 2), jnp.int32) > 0
            first = 32 * q + 16 * k
            pixels[first : first + 16, 0:128] = jnp.where(odd, found[1], found[0])
    spread = (sublane((64, 256)) == lane((64, 256)) % 64).astype(BF)
    pixels[...] = dot(pixels[:, 0:64].astype(BF), spread)
    zero = jnp.zeros((8, 256), F32)

    def kept(flag, v):
        return jnp.where(jnp.full((8, 256), flag.astype(jnp.int32), jnp.int32) > 0, v, zero)

    def spot(k):
        return jnp.broadcast_to(pixels[k : k + 1, :], (8, 256))

    for f in range(FRAMES):
        for y in range(8):
            if y == 0:
                tile, left, right = pixels[24 + 8 * f : 32 + 8 * f, :], spot(93 + f), spot(90 + f)
            elif y == 7:
                tile, left, right = pixels[8 * f : 8 * f + 8, :], spot(87 + f), spot(84 + f)
            else:
                at = 48 * f + 8 * (y - 1)
                tile = outp_ref[at : at + 8, :]
                left, right = spot(66 + 6 * f + y - 1), spot(48 + 6 * f + y - 1)
            tile = shifted(tile, kept(col > 0, left), kept(col < 7, right), (64, 128), 256)
            if y == 0:
                tile = kept(row > 0, tile)
            elif y == 7:
                tile = kept(row < 31, tile)
            tiles[f, y] = tile
    stack_rows(tiles, qs)
    total = jnp.zeros((CELLS, 64), F32)
    for a in range(3):
        for b in range(3):
            rows = qs[2 - b, 48 * (2 - a) : 48 * (2 - a) + CELLS, :]
            total = total + dot(rows[:, 0:192], back_ref[3 * a + b])
    grad_ref[...] = dot(total.astype(BF), utp_ref[...]).astype(BF)
    for a in range(9):
        store(a).wait()


def call(kernel, args, outs, scratch, flops=10**7):
    def spec(far):
        return pl.BlockSpec(memory_space=pltpu.HBM if far else pltpu.VMEM)

    return pl.pallas_call(
        kernel,
        out_shape=[jax.ShapeDtypeStruct(shape, dtype) for shape, dtype, _ in outs],
        in_specs=[spec(far) for _, far in args],
        out_specs=[spec(far) for _, _, far in outs],
        scratch_shapes=scratch,
        compiler_params=pltpu.CompilerParams(vmem_limit_bytes=32 << 20),
        cost_estimate=pl.CostEstimate(flops=flops, bytes_accessed=10**5, transcendentals=0),
    )(*[pltpu.with_memory_space_constraint(arg, pltpu.HBM) if far else arg for arg, far in args])


def near(*args):
    return [(arg, False) for arg in args]


def far(*args):
    return [(arg, True) for arg in args]


def swap(one, two, axis):
    count = lax.axis_size(axis)
    pairs = [[(i, i + 1) for i in range(k, count - 1, 2)] for k in range(2)]
    two, one = (
        lax.ppermute(x, axis, forward + [(b, a) for a, b in forward]) for x, forward in ((two, pairs[1]), (one, pairs[0]))
    )
    return one, two


def device(k, chip, col):
    return 8 * (2 * chip + k) + col


ORDER = [[device(k, chip, col) for chip in range(16) for col in range(8)] for k in range(2)]


def exchange(x):
    return lax.all_to_all(x, AXES, 0, 0, tiled=True, axis_index_groups=[ORDER[0] + ORDER[1]])


def exchange_half(x):
    return lax.all_to_all(x, AXES, 0, 0, tiled=True, axis_index_groups=ORDER)


def in_chip(x):
    chips = [[2 * chip, 2 * chip + 1] for chip in range(16)]
    return lax.all_gather(x, "rows", axis=0, tiled=True, axis_index_groups=chips)


def body(frames_in, cotangent, core, moment_one, moment_two, u_in, u_out):
    take, give, kind = ring_tables()
    take, give, kind = jnp.asarray(take, BF), jnp.asarray(give, BF), jnp.asarray(kind, F32)
    vm, dma = pltpu.VMEM, pltpu.SemaphoreType.DMA
    side = (FRAMES * ROWS, 256)
    rim = (FRAMES * 16, 256)

    send, one, two, inner = call(
        start_kernel,
        far(core, frames_in),
        [((512, 128), BF, True), (side, BF, False), (side, BF, False), ((FRAMES, ROWS, COLS, 256), BF, False)],
        [vm((OWN,), F32), vm((8, 128), F32), vm((128, 128), BF), vm(side, F32), vm(side, F32), dma((6,))],
    )
    one, two = swap(one, two, "cols")
    got = in_chip(exchange_half(send))
    own, wide, utp, u, ring, ot, cot, take, give, kind = call(
        fetch_kernel,
        near(inner.reshape(CELLS, 256)) + far(
            u_in.T, u_out.T, cotangent.reshape(CELLS, 256), core, moment_one, moment_two, take, give, kind,
        ),
        [
            ((CELLS, 256), F32, False), ((256, 256), BF, False), ((64, 256), BF, False), ((256, 64), BF, False),
            ((3, 4, 128), F32, False), ((64, 256), BF, False), ((CELLS, 256), BF, False),
            ((216, 512), BF, False), ((512, 216), BF, False), ((256, 128), F32, False),
        ],
        [
            vm((64, 256), BF), [vm((OWN,), F32) for _ in range(3)], vm((8, 128), F32),
            dma((9,)),
        ],
    )
    left, right, one, two = call(
        rows_kernel,
        near(inner, one, two),
        [(side, F32, False), (side, F32, False), (rim, BF, False), (rim, BF, False)],
        [vm(rim, F32), vm(rim, F32)],
        flops=10**10,
    )
    one, two = swap(one, two, "rows")
    (q,) = call(
        rank_kernel,
        near(own, wide, one, two, left, right),
        [((3, 240, 256), BF, False)],
        [vm((FRAMES, 8, 8, 256), F32), vm((2, 18, 256), F32), vm((2, 48, 256), F32)],
    )
    send, table, outp = call(
        forward_kernel,
        near(got, q, cot, ot, take, give, kind),
        [((1024, 128), BF, False), ((TABLE, 128), BF, False), ((CELLS, 256), F32, False)],
        [vm((TABLE, 128), F32), vm((TABLE, 128), F32), vm((CELLS, 128), F32), vm((96, 128), F32), vm((1024, 128), F32)],
    )
    got = exchange(send)
    send, latest = call(
        adam_kernel,
        near(got, ring),
        [((512, 128), BF, False), ((3, 4, 128), F32, False)],
        [vm((1104, 128), F32)],
    )
    got = exchange_half(send)
    (back,) = call(turn_kernel, near(table), [((9, 192, 64), BF, False)], [])
    core_next, one_next, two_next = call(flat_kernel, near(latest), [((OWN,), F32, False)] * 3, [])
    got, back, core_next, one_next, two_next = lax.optimization_barrier((got, back, core_next, one_next, two_next))
    got = in_chip(got)
    kernel_next, frames_grad = call(
        finish_kernel,
        near(got, outp, back, utp, u, ot, take, kind),
        [((27, 256, 256), BF, True), ((CELLS, 256), BF, False)],
        [
            vm((TABLE, 128), F32), vm((27, 64, 256), BF), vm((27, 256, 256), BF), vm((1024, 128), F32),
            vm((96, 256), F32), vm((FRAMES, 8, 8, 256), F32), vm((3, 240, 256), BF), dma((9,)),
        ],
    )
    frames_grad = frames_grad.reshape(FRAMES, ROWS, COLS, 256)
    return frames_grad, core_next, one_next, two_next, kernel_next


def solution(mesh):
    in_specs = (
        P(None, "rows", "cols", None),
        P(None, "rows", "cols", None),
        P(AXES),
        P(AXES),
        P(AXES),
        P(),
        P(),
    )
    out_specs = (
        P(None, "rows", "cols", None),
        P(AXES),
        P(AXES),
        P(AXES),
        P(),
    )
    return jax.shard_map(body, mesh=mesh, in_specs=in_specs, out_specs=out_specs, check_vma=False)
```

```python
import jax
import jax.numpy as jnp
import numpy as np
from jax import lax
from jax.experimental import pallas as pl
from jax.experimental.pallas import tpu as pltpu
from jax.sharding import PartitionSpec as P

beta_one = 0.9
beta_two = 0.999
learn_rate = 0.06
epsilon = 1e-08
fix_one = 1.0 - 0.9**10
fix_two = 1.0 - 0.999**10

BF = jnp.bfloat16
F32 = jnp.float32
AXES = ("rows", "cols")

OWN = 432
FRAMES, ROWS, COLS = 3, 6, 8
CELLS = FRAMES * ROWS * COLS
SIDE = FRAMES * 8
TABLE = 864


RELAYS = ((7, 0, 0), (4, 0, 0), (3, 3, 64), (0, 3, 64), (2, 0, 16), (5, 0, 32))
SLOTS = (
    (0, 24, -1, 0), (24, 24, 1, 0), (48, 18, 0, -1), (66, 18, 0, 1),
    (84, 3, -1, -1), (87, 3, -1, 1), (90, 3, 1, -1), (93, 3, 1, 1),
)


def ring_tables():
    take = np.zeros((216, 512), np.float32)
    give = np.zeros((512, 216), np.float32)
    kind = np.zeros((256, 128), np.float32)
    for r in range(8):
        for c in range(8):
            first = 27 * r + 27 * c // 8
            col = 128 * (r % 2) + 32 * (r // 2) + 4 * c
            for j in range(4):
                take[first + j, col + j] = 1
                give[col + j, first + j] = 1
            wrapped = 48 * c % 128 + OWN - 512
            if wrapped > 0:
                take[first + 4, 256 + col] = 1
                give[256 + col, first + 4] = 1
                kind[col, :wrapped] = 1
        for c, j, at in RELAYS:
            kind[128 * (r % 2) + 32 * (r // 2) + 4 * c + j, at : at + 64] = 2
    return take, give, kind


def dot(a, b):
    return jnp.dot(a, b, preferred_element_type=F32)


def dot_nt(a, b):
    return lax.dot_general(a, b, (((1,), (1,)), ((), ())), preferred_element_type=F32)


def dot_tn(a, b):
    return lax.dot_general(a, b, (((0,), (0,)), ((), ())), preferred_element_type=F32)


def lane(shape):
    return lax.broadcasted_iota(jnp.int32, shape, 1)


def sublane(shape):
    return lax.broadcasted_iota(jnp.int32, shape, 0)


def ring_shift():
    return lax.rem(lax.axis_index("cols") * 48, 128)


def to_ring(v, shift):
    turned = pltpu.roll(v, shift, axis=1)
    above = jnp.concatenate([turned[3:4], turned[0:3]], axis=0)
    return jnp.where(lane(v.shape) >= shift, turned, above)


def from_ring(v, shift):
    turned = pltpu.roll(v, lax.rem(128 - shift, 128), axis=1)
    below = jnp.concatenate([turned[1:4], turned[0:1]], axis=0)
    return jnp.where(lane(v.shape) < 128 - shift, turned, below)


def in_ring(shift):
    place = sublane((4, 128)) * 128 + lane((4, 128)) - shift
    place = jnp.where(place < 0, place + 512, place)
    return place < OWN


def load_flat(ref, scratch):
    scratch[...] = jnp.zeros_like(scratch)
    for k in range(3):
        scratch[k, :] = ref[pl.ds(128 * k, 128)]
    scratch[3, 0 : OWN - 384] = ref[pl.ds(384, OWN - 384)]
    return scratch[0:4, :]


def store_flat(ref, v):
    for k in range(3):
        ref[pl.ds(128 * k, 128)] = v[k]
    ref[pl.ds(384, OWN - 384)] = v[3, 0 : OWN - 384]


def fetch(pairs, sems):
    copies = [pltpu.make_async_copy(src, dst, sems.at[k]) for k, (src, dst) in enumerate(pairs)]
    for copy in copies:
        copy.start()
    return copies


def even_first(axis, first, last):
    even = jnp.full(first.shape, lax.rem(lax.axis_index(axis), 2), jnp.int32) == 0
    return jnp.where(even, last, first), jnp.where(even, first, last)


def start_kernel(core_ref, x_ref, send_ref, one_ref, two_ref, inner_ref, own, flat, block, low, high, sems):
    copies = fetch(((core_ref, own), (x_ref, inner_ref)), sems)
    copies[0].wait()
    v = to_ring(load_flat(own, flat), ring_shift())
    rows = jnp.concatenate([v, v, v, v], axis=0).astype(BF)
    for k in range(8):
        block[16 * k : 16 * k + 16, :] = rows
    sends = fetch([(block, send_ref.at[pl.ds(128 * k, 128)]) for k in range(4)], sems.at[pl.ds(2, 4)])
    copies[1].wait()
    for f in range(FRAMES):
        for y in range(ROWS):
            tile = inner_ref[f, y].astype(F32)
            k = ROWS * f + y
            low[k : k + 1, :] = tile[0:1, :]
            high[k : k + 1, :] = tile[7:8, :]
    one, two = even_first("cols", low[...], high[...])
    one_ref[...] = one.astype(BF)
    two_ref[...] = two.astype(BF)
    for copy in sends:
        copy.wait()


def rows_kernel(inner_ref, one_ref, two_ref, left_ref, right_ref, up_ref, down_ref, first, last):
    right, left = even_first("cols", two_ref[...].astype(F32), one_ref[...].astype(F32))
    left_ref[...] = left
    right_ref[...] = right
    first[...] = jnp.zeros_like(first)
    last[...] = jnp.zeros_like(last)
    for f in range(FRAMES):
        for y, rows in ((0, first), (ROWS - 1, last)):
            k = ROWS * f + y
            rows[16 * f : 16 * f + 8, :] = inner_ref[f, y].astype(F32)
            rows[16 * f + 8 : 16 * f + 9, :] = left_ref[k : k + 1, :]
            rows[16 * f + 9 : 16 * f + 10, :] = right_ref[k : k + 1, :]
    one, two = even_first("rows", first[...], last[...])
    up_ref[...] = one.astype(BF)
    down_ref[...] = two.astype(BF)


def shifted(tile, left, right, bounds, period):
    at = lane(tile.shape) % period
    row = sublane(tile.shape)
    back = jnp.where(row == 0, left, pltpu.roll(tile, 1, axis=0))
    ahead = jnp.where(row == 7, right, pltpu.roll(tile, 7, axis=0))
    return jnp.where(at < bounds[0], back, jnp.where(at < bounds[1], tile, ahead))


def fetch_kernel(
    _, x_ref, ut_ref, ot_ref, cot_ref, core_ref, one_ref, two_ref, take_ref, give_ref, kind_ref,
    own_ref, wide_ref, utp_ref, u_ref, ring_ref, ot_out, cot_out, take_out, give_out, kind_out,
    ut, owns, flat, sems,
):
    copies = fetch(
        (
            (ut_ref, ut), (core_ref, owns[0]), (one_ref, owns[1]), (two_ref, owns[2]),
            (take_ref, take_out), (give_ref, give_out), (kind_ref, kind_out), (ot_ref, ot_out), (cot_ref, cot_out),
        ),
        sems,
    )
    row = sublane((256, 64))
    at = row % 128
    pick = (lane((256, 64)) == (at % 32) * 2 + row // 128) & (at < 96)
    half_row = sublane((64, 64))
    half_pick = lane((64, 64)) == (half_row % 32) * 2 + half_row // 32
    copies[0].wait()
    wide = dot(pick.astype(BF), ut[...]).astype(BF)
    wide_ref[...] = wide
    utp = dot(half_pick.astype(BF), ut[...])
    utp_ref[...] = utp.astype(BF)
    u_ref[...] = utp.T.astype(BF)
    own_ref[...] = dot_nt(x_ref[...], wide).astype(BF).astype(F32)
    shift = ring_shift()
    for k in range(3):
        copies[1 + k].wait()
        ring_ref[k] = to_ring(load_flat(owns[k], flat), shift)
    for k in range(4, 9):
        copies[k].wait()


def stack_rows(tiles, out_ref):
    for b in range(3):
        out_ref[b, 0:48, :] = jnp.zeros((48, 256), BF)
        out_ref[b, 192:240, :] = jnp.zeros((48, 256), BF)
        for f in range(FRAMES):
            rows = tiles[f, b : b + ROWS].reshape(48, 256)
            out_ref[b, 48 * f + 48 : 48 * f + 96, :] = rows.astype(BF)


def rank_kernel(own_ref, wide_ref, one_ref, two_ref, left_ref, right_ref, q_ref, tiles, edge, rims):
    wide = wide_ref[...]

    def project(v):
        return dot_nt(v.astype(BF), wide).astype(BF).astype(F32)

    below, above = even_first("rows", project(two_ref[...]), project(one_ref[...]))
    rims[0] = above
    rims[1] = below
    edge[0] = project(left_ref[...])
    edge[1] = project(right_ref[...])
    for f in range(FRAMES):
        for y in range(8):
            if y in (0, 7):
                rim = rims.at[y // 7]
                at = 16 * f
                tile, left, right = rim[at : at + 8, :], rim[at + 8 : at + 9, :], rim[at + 9 : at + 10, :]
            else:
                k = ROWS * f + y - 1
                tile = own_ref[8 * k : 8 * k + 8, :]
                left, right = edge[0, k : k + 1, :], edge[1, k : k + 1, :]
            left = jnp.broadcast_to(left, (8, 256))
            right = jnp.broadcast_to(right, (8, 256))
            tiles[f, y] = shifted(tile, left, right, (32, 64), 128)
    stack_rows(tiles, q_ref)


def core_index(shape):
    return jnp.full(shape, lax.rem(lax.axis_index("rows"), 2), jnp.int32)


def gather_table(mine_ref, other_ref, take_ref, kind_ref, table_ref):
    kind = kind_ref[...]
    take = take_ref[...]
    first = core_index((128, 128)) == 0
    for g in range(4):
        mine, other = mine_ref[128 * g : 128 * g + 128, :], other_ref[128 * g : 128 * g + 128, :]
        block = jnp.concatenate([jnp.where(first, mine, other), jnp.where(first, other, mine)], axis=0)
        none = jnp.zeros_like(block)
        both = jnp.concatenate(
            [jnp.where(kind == 0, block, none), jnp.where(kind == 1, block, none)], axis=0
        )
        table_ref[216 * g : 216 * g + 216, :] = dot(take, both)


def inside(lanes, at):
    return (lanes >= at) & (lanes < at + 64)


def forward_kernel(
    mine_ref, other_ref, q_ref, cot_ref, ot_ref, take_ref, give_ref, kind_ref,
    keep_ref, send_ref, table_out, outp_ref, table, grads, border, pixels, blocks,
):
    gather_table(mine_ref, other_ref, take_ref, kind_ref, table)
    table_out[...] = table[...].astype(BF)
    even = jnp.zeros((CELLS, 128), F32)
    odd = jnp.zeros((CELLS, 128), F32)
    for a in range(3):
        for b in range(3):
            k = 3 * a + b
            weights = table_out[96 * k : 96 * k + 96, :]
            rows = q_ref[b, 48 * a : 48 * a + CELLS, :]
            even = even + dot(rows[:, 0:96], weights)
            odd = odd + dot(rows[:, 128:224], weights)
    mid = (even[:, 0:64] + odd[:, 64:128]).astype(BF)
    pre = dot(mid, ot_ref[...])
    sig = jax.nn.sigmoid(pre)
    slope = (cot_ref[...].astype(F32) * sig * (1.0 + pre * (1.0 - sig))).astype(BF)
    ot = ot_ref[...]
    out_t = dot_nt(ot, slope).astype(BF)
    wide = jnp.concatenate([ot, ot, ot, ot], axis=0)
    outp = dot_nt(slope, wide).astype(BF).astype(F32)
    outp_ref[...] = outp
    border[...] = outp[:, 0:128]
    for f in range(FRAMES):
        pixels[8 * f : 8 * f + 8, :] = border[48 * f : 48 * f + 8, :]
        pixels[24 + 8 * f : 32 + 8 * f, :] = border[48 * f + 40 : 48 * f + 48, :]
    pixels[48:66, :] = border[pl.ds(0, 18, stride=8), :]
    pixels[66:84, :] = border[pl.ds(7, 18, stride=8), :]
    for k, cell in enumerate((0, 7, 40, 47)):
        pixels[84 + 3 * k : 87 + 3 * k, :] = border[pl.ds(cell, 3, stride=48), :]
    for a in range(3):
        for b in range(3):
            k = 3 * a + b
            part = dot(out_t, q_ref[b, 48 * a : 48 * a + CELLS, :])
            stack = jnp.concatenate([part[:, 0:128], part[:, 128:256]], axis=0)
            grads[96 * k : 96 * k + 96, :] = stack.T[0:96, :]
    wrapped = kind_ref[...] == 1
    give = give_ref[...]
    for g in range(4):
        part = dot(give, grads[216 * g : 216 * g + 216, :].astype(BF))
        part = jnp.where(wrapped, part[256:512], part[0:256])
        for k in range(2):
            blocks[512 * k + 128 * g : 512 * k + 128 * g + 128, :] = part[128 * k : 128 * k + 128]
    lanes = lane((16, 128))
    for a, (c, j, at) in enumerate(RELAYS):
        for k in range(2):
            first = 32 * (a % 3) + 16 * k
            slot = sublane((16, 128)) + first
            odd = core_index((16, 128)) + ((slot < 48) | (slot >= 84)).astype(jnp.int32) == 1
            pixel = jnp.where(odd if a >= 3 else ~odd, pixels[first : first + 16, :], 0.0)
            if at % 64:
                pixel = pltpu.roll(pixel, at, axis=1)
            spot = pl.ds(512 * k + 4 * c + j, 16, stride=32)
            blocks[spot, :] = jnp.where(inside(lanes, at), pixel, blocks[spot, :])
    first = core_index((128, 128)) == 0
    for g in range(4):
        part = pl.ds(128 * g, 128)
        low, high = blocks[part, :], blocks[pl.ds(512 + 128 * g, 128), :]
        keep_ref[part, :] = jnp.where(first, low, high)
        send_ref[part, :] = jnp.where(first, high, low).astype(BF)


def add_kernel(keep_ref, got_ref, send_ref):
    send_ref[...] = (keep_ref[...] + got_ref[...].astype(F32)).astype(BF)


def adam_kernel(got_ref, ring_ref, send_ref, next_ref, passed):
    total = jnp.zeros((8, 128), F32)
    passed[0:40, :] = jnp.zeros((40, 128), F32)
    passed[552:592, :] = jnp.zeros((40, 128), F32)
    for g in range(4):
        part = got_ref[128 * g : 128 * g + 128, :].astype(F32)
        passed[128 * g + 40 : 128 * g + 168, :] = part
        total = total + part.reshape(16, 8, 128).sum(axis=0)
    grad = (total[0:4] + total[4:8]) * (1.0 / 192.0)
    core, one, two = ring_ref[0], ring_ref[1], ring_ref[2]
    one = beta_one * one + (1.0 - beta_one) * grad
    two = beta_two * two + (1.0 - beta_two) * grad * grad
    core = core - learn_rate * (one / fix_one) / (jnp.sqrt(two / fix_two) + epsilon)
    next_ref[0] = core
    next_ref[1] = one
    next_ref[2] = two
    own = jnp.where(in_ring(ring_shift()), core, 0.0)
    own = jnp.concatenate([own, own], axis=0)
    row, col = lax.axis_index("rows"), lax.axis_index("cols")
    slot = 16 * lax.rem(row, 2) + lax.div(row, 2)
    parity, mask = 0, jnp.zeros((8, 128), jnp.bool_)
    for a, (c, j, at) in enumerate(RELAYS):
        slot = slot + jnp.where(col == c, 32 * (a % 3), 0)
        parity = parity + jnp.where(col == c, a // 3, 0)
        spot = (sublane((8, 128)) % 4 == j) & inside(lane((8, 128)), at)
        mask = mask | (spot & (jnp.full((8, 128), col, jnp.int32) == c))
    up, right = 0, 0
    for first, count, rows, cols in SLOTS:
        here = (slot >= first) & (slot < first + count)
        up = up + jnp.where(here, rows, 0)
        right = right + jnp.where(here, cols, 0)
    source = lax.rem(parity - up + 2, 2)
    chips = lax.div(source + up - parity + 2, 2) - 1
    start = 40 - 4 * (8 * chips + right)
    for k in range(32):
        upper = passed[pl.ds(start + 16 * k, 8), :]
        lower = passed[pl.ds(start + 16 * k + 8, 8), :]
        block = jnp.concatenate([jnp.where(mask, upper, own), jnp.where(mask, lower, own)], axis=0)
        send_ref[16 * k : 16 * k + 16, :] = block.astype(BF)


def flat_kernel(next_ref, core_ref, one_ref, two_ref):
    shift = ring_shift()
    for k, ref in enumerate((core_ref, one_ref, two_ref)):
        store_flat(ref, from_ring(next_ref[k], shift))


def turn_kernel(table_ref, back_ref):
    for k in range(9):
        for c in range(3):
            t = 3 * k + c
            part = table_ref[32 * t : 32 * t + 32, :].astype(F32).T
            cube = jnp.concatenate([part[0:64], part[64:128]], axis=1)
            back_ref[k, 64 * (2 - c) : 64 * (2 - c) + 64, :] = cube.astype(BF)


def finish_kernel(
    mine_ref, other_ref, outp_ref, back_ref, utp_ref, u_ref, ot_ref, take_ref, kind_ref,
    out_ref, grad_ref, table, half, result, got, pixels, tiles, qs, sems,
):
    gather_table(mine_ref, other_ref, take_ref, kind_ref, table)
    cube = table[...].astype(BF)
    even = dot(cube[:, 0:64], ot_ref[...]).astype(BF)
    odd = dot(cube[:, 64:128], ot_ref[...]).astype(BF)
    for t in range(27):
        half[t, 0:32, :] = even[32 * t : 32 * t + 32]
        half[t, 32:64, :] = odd[32 * t : 32 * t + 32]
    u = u_ref[...]

    def store(a):
        part = pl.ds(3 * a, 3)
        return pltpu.make_async_copy(result.at[part], out_ref.at[part], sems.at[a])

    for a in range(9):
        for t in range(3 * a, 3 * a + 3):
            result[t] = dot(u, half[t]).astype(BF)
        store(a).start()

    first = core_index((128, 128)) == 0
    for g in range(4):
        part = pl.ds(128 * g, 128)
        mine, other = mine_ref[part, :], other_ref[part, :]
        got[part, :] = jnp.where(first, mine, other).astype(F32)
        got[pl.ds(512 + 128 * g, 128), :] = jnp.where(first, other, mine).astype(F32)
    row, col = lax.axis_index("rows"), lax.axis_index("cols")
    lanes = lane((16, 128))
    for q in range(3):
        for k in range(2):
            found = []
            for c, j, at in (RELAYS[q], RELAYS[q + 3]):
                pixel = got[pl.ds(512 * k + 4 * c + j, 16, stride=32), :]
                found.append(pltpu.roll(pixel, 128 - at, axis=1) if at else pixel)
            odd = jnp.full((16, 128), lax.rem(row, 2), jnp.int32) > 0
            first = 32 * q + 16 * k
            pixels[first : first + 16, 0:128] = jnp.where(odd, found[1], found[0])
    spread = (sublane((64, 256)) == lane((64, 256)) % 64).astype(BF)
    pixels[...] = dot(pixels[:, 0:64].astype(BF), spread)
    zero = jnp.zeros((8, 256), F32)

    def kept(flag, v):
        return jnp.where(jnp.full((8, 256), flag.astype(jnp.int32), jnp.int32) > 0, v, zero)

    def spot(k):
        return jnp.broadcast_to(pixels[k : k + 1, :], (8, 256))

    for f in range(FRAMES):
        for y in range(8):
            if y == 0:
                tile, left, right = pixels[24 + 8 * f : 32 + 8 * f, :], spot(93 + f), spot(90 + f)
            elif y == 7:
                tile, left, right = pixels[8 * f : 8 * f + 8, :], spot(87 + f), spot(84 + f)
            else:
                at = 48 * f + 8 * (y - 1)
                tile = outp_ref[at : at + 8, :]
                left, right = spot(66 + 6 * f + y - 1), spot(48 + 6 * f + y - 1)
            tile = shifted(tile, kept(col > 0, left), kept(col < 7, right), (64, 128), 256)
            if y == 0:
                tile = kept(row > 0, tile)
            elif y == 7:
                tile = kept(row < 31, tile)
            tiles[f, y] = tile
    stack_rows(tiles, qs)
    total = jnp.zeros((CELLS, 64), F32)
    for a in range(3):
        for b in range(3):
            rows = qs[2 - b, 48 * (2 - a) : 48 * (2 - a) + CELLS, :]
            total = total + dot(rows[:, 0:192], back_ref[3 * a + b])
    grad_ref[...] = dot(total.astype(BF), utp_ref[...]).astype(BF)
    for a in range(9):
        store(a).wait()


def call(kernel, args, outs, scratch, flops=10**7):
    def spec(far):
        return pl.BlockSpec(memory_space=pltpu.HBM if far else pltpu.VMEM)

    return pl.pallas_call(
        kernel,
        out_shape=[jax.ShapeDtypeStruct(shape, dtype) for shape, dtype, _ in outs],
        in_specs=[spec(far) for _, far in args],
        out_specs=[spec(far) for _, _, far in outs],
        scratch_shapes=scratch,
        compiler_params=pltpu.CompilerParams(vmem_limit_bytes=32 << 20),
        cost_estimate=pl.CostEstimate(flops=flops, bytes_accessed=10**5, transcendentals=0),
    )(*[pltpu.with_memory_space_constraint(arg, pltpu.HBM) if far else arg for arg, far in args])


def near(*args):
    return [(arg, False) for arg in args]


def far(*args):
    return [(arg, True) for arg in args]


def swap(one, two, axis):
    count = lax.axis_size(axis)
    pairs = [[(i, i + 1) for i in range(k, count - 1, 2)] for k in range(2)]
    two, one = (
        lax.ppermute(x, axis, forward + [(b, a) for a, b in forward]) for x, forward in ((two, pairs[1]), (one, pairs[0]))
    )
    return one, two


def device(k, chip, col):
    return 8 * (2 * chip + k) + col


ORDER = [[device(k, chip, col) for chip in range(16) for col in range(8)] for k in range(2)]


def exchange(x):
    return lax.all_to_all(x, AXES, 0, 0, tiled=True, axis_index_groups=ORDER)


def in_chip(x):
    return lax.ppermute(x, "rows", [(r, r ^ 1) for r in range(32)])


def body(frames_in, cotangent, core, moment_one, moment_two, u_in, u_out):
    take, give, kind = ring_tables()
    take, give, kind = jnp.asarray(take, BF), jnp.asarray(give, BF), jnp.asarray(kind, F32)
    vm, dma = pltpu.VMEM, pltpu.SemaphoreType.DMA
    side = (FRAMES * ROWS, 256)
    rim = (FRAMES * 16, 256)

    send, one, two, inner = call(
        start_kernel,
        far(core, frames_in),
        [((512, 128), BF, True), (side, BF, False), (side, BF, False), ((FRAMES, ROWS, COLS, 256), BF, False)],
        [vm((OWN,), F32), vm((8, 128), F32), vm((128, 128), BF), vm(side, F32), vm(side, F32), dma((6,))],
    )
    one, two = swap(one, two, "cols")
    mine = exchange(send)
    left, right, one, two = call(
        rows_kernel,
        near(inner, one, two),
        [(side, F32, False), (side, F32, False), (rim, BF, False), (rim, BF, False)],
        [vm(rim, F32), vm(rim, F32)],
        flops=10**10,
    )
    own, wide, utp, u, ring, ot, cot, take, give, kind = call(
        fetch_kernel,
        near(left, inner.reshape(CELLS, 256)) + far(
            u_in.T, u_out.T, cotangent.reshape(CELLS, 256), core, moment_one, moment_two, take, give, kind,
        ),
        [
            ((CELLS, 256), F32, False), ((256, 256), BF, False), ((64, 256), BF, False), ((256, 64), BF, False),
            ((3, 4, 128), F32, False), ((64, 256), BF, False), ((CELLS, 256), BF, False),
            ((216, 512), BF, False), ((512, 216), BF, False), ((256, 128), F32, False),
        ],
        [
            vm((64, 256), BF), [vm((OWN,), F32) for _ in range(3)], vm((8, 128), F32),
            dma((9,)),
        ],
        flops=10000000000,
    )
    mine, _ = lax.optimization_barrier((mine, ring))
    other = in_chip(mine)
    one, two = swap(one, two, "rows")
    (q,) = call(
        rank_kernel,
        near(own, wide, one, two, left, right),
        [((3, 240, 256), BF, False)],
        [vm((FRAMES, 8, 8, 256), F32), vm((2, 18, 256), F32), vm((2, 48, 256), F32)],
        flops=10000000000,
    )
    keep, send, table, outp = call(
        forward_kernel,
        near(mine, other, q, cot, ot, take, give, kind),
        [
            ((512, 128), F32, False), ((512, 128), BF, False), ((TABLE, 128), BF, False), ((CELLS, 256), F32, False),
        ],
        [vm((TABLE, 128), F32), vm((TABLE, 128), F32), vm((CELLS, 128), F32), vm((96, 128), F32), vm((1024, 128), F32)],
    )
    (send,) = call(add_kernel, near(keep, in_chip(send)), [((512, 128), BF, False)], [])
    got = exchange(send)
    send, latest = call(
        adam_kernel,
        near(got, ring),
        [((512, 128), BF, False), ((3, 4, 128), F32, False)],
        [vm((592, 128), F32)],
    )
    mine = exchange(send)
    (back,) = call(turn_kernel, near(table), [((9, 192, 64), BF, False)], [])
    core_next, one_next, two_next = call(flat_kernel, near(latest), [((OWN,), F32, False)] * 3, [])
    mine, back, core_next, one_next, two_next = lax.optimization_barrier((mine, back, core_next, one_next, two_next))
    other = in_chip(mine)
    kernel_next, frames_grad = call(
        finish_kernel,
        near(mine, other, outp, back, utp, u, ot, take, kind),
        [((27, 256, 256), BF, True), ((CELLS, 256), BF, False)],
        [
            vm((TABLE, 128), F32), vm((27, 64, 256), BF), vm((27, 256, 256), BF), vm((1024, 128), F32),
            vm((96, 256), F32), vm((FRAMES, 8, 8, 256), F32), vm((3, 240, 256), BF), dma((9,)),
        ],
    )
    frames_grad = frames_grad.reshape(FRAMES, ROWS, COLS, 256)
    return frames_grad, core_next, one_next, two_next, kernel_next


def solution(mesh):
    in_specs = (
        P(None, "rows", "cols", None),
        P(None, "rows", "cols", None),
        P(AXES),
        P(AXES),
        P(AXES),
        P(),
        P(),
    )
    out_specs = (
        P(None, "rows", "cols", None),
        P(AXES),
        P(AXES),
        P(AXES),
        P(),
    )
    return jax.shard_map(body, mesh=mesh, in_specs=in_specs, out_specs=out_specs, check_vma=False)
```

```python
import jax
import jax.numpy as jnp
import numpy as np
from jax import lax
from jax.experimental import pallas as pl
from jax.experimental.pallas import tpu as pltpu
from jax.sharding import PartitionSpec as P

beta_one = 0.9
beta_two = 0.999
learn_rate = 0.06
epsilon = 1e-08
fix_one = 1.0 - 0.9**10
fix_two = 1.0 - 0.999**10

BF = jnp.bfloat16
F32 = jnp.float32
AXES = ("rows", "cols")

OWN = 432
FRAMES, ROWS, COLS = 3, 6, 8
CELLS = FRAMES * ROWS * COLS
SIDE = FRAMES * 8
TABLE = 864


RELAYS = ((7, 0, 0), (4, 0, 0), (3, 3, 64), (0, 3, 64), (2, 0, 16), (5, 0, 32))
SLOTS = (
    (0, 24, -1, 0), (24, 24, 1, 0), (48, 18, 0, -1), (66, 18, 0, 1),
    (84, 3, -1, -1), (87, 3, -1, 1), (90, 3, 1, -1), (93, 3, 1, 1),
)


def ring_tables():
    take = np.zeros((216, 512), np.float32)
    give = np.zeros((2, 256, 216), np.float32)
    kind = np.zeros((256, 128), np.float32)
    for r in range(8):
        for c in range(8):
            first = 27 * r + 27 * c // 8
            col = 128 * (r % 2) + 32 * (r // 2) + 4 * c
            for j in range(4):
                take[first + j, col + j] = 1
                give[r % 2, col % 128 + j, first + j] = 1
            wrapped = 48 * c % 128 + OWN - 512
            if wrapped > 0:
                take[first + 4, 256 + col] = 1
                give[r % 2, 128 + col % 128, first + 4] = 1
                kind[col, :wrapped] = 1
        for c, j, at in RELAYS:
            kind[128 * (r % 2) + 32 * (r // 2) + 4 * c + j, at : at + 64] = 2
    return take, give, kind


def dot(a, b):
    return jnp.dot(a, b, preferred_element_type=F32)


def dot_nt(a, b):
    return lax.dot_general(a, b, (((1,), (1,)), ((), ())), preferred_element_type=F32)


def dot_tn(a, b):
    return lax.dot_general(a, b, (((0,), (0,)), ((), ())), preferred_element_type=F32)


def lane(shape):
    return lax.broadcasted_iota(jnp.int32, shape, 1)


def sublane(shape):
    return lax.broadcasted_iota(jnp.int32, shape, 0)


def ring_shift():
    return lax.rem(lax.axis_index("cols") * 48, 128)


def to_ring(v, shift):
    turned = pltpu.roll(v, shift, axis=1)
    above = jnp.concatenate([turned[3:4], turned[0:3]], axis=0)
    return jnp.where(lane(v.shape) >= shift, turned, above)


def from_ring(v, shift):
    turned = pltpu.roll(v, lax.rem(128 - shift, 128), axis=1)
    below = jnp.concatenate([turned[1:4], turned[0:1]], axis=0)
    return jnp.where(lane(v.shape) < 128 - shift, turned, below)


def in_ring(shift):
    place = sublane((4, 128)) * 128 + lane((4, 128)) - shift
    place = jnp.where(place < 0, place + 512, place)
    return place < OWN


def load_flat(ref, scratch):
    scratch[...] = jnp.zeros_like(scratch)
    for k in range(3):
        scratch[k, :] = ref[pl.ds(128 * k, 128)]
    scratch[3, 0 : OWN - 384] = ref[pl.ds(384, OWN - 384)]
    return scratch[0:4, :]


def store_flat(ref, v):
    for k in range(3):
        ref[pl.ds(128 * k, 128)] = v[k]
    ref[pl.ds(384, OWN - 384)] = v[3, 0 : OWN - 384]


def fetch(pairs, sems):
    copies = [pltpu.make_async_copy(src, dst, sems.at[k]) for k, (src, dst) in enumerate(pairs)]
    for copy in copies:
        copy.start()
    return copies


def even_first(axis, first, last):
    even = jnp.full(first.shape, lax.rem(lax.axis_index(axis), 2), jnp.int32) == 0
    return jnp.where(even, last, first), jnp.where(even, first, last)


def start_kernel(core_ref, x_ref, send_ref, one_ref, two_ref, inner_ref, own, flat, block, low, high, sems):
    copies = fetch(((core_ref, own), (x_ref, inner_ref)), sems)
    copies[0].wait()
    v = to_ring(load_flat(own, flat), ring_shift())
    rows = jnp.concatenate([v, v, v, v], axis=0).astype(BF)
    for k in range(8):
        block[16 * k : 16 * k + 16, :] = rows
    sends = fetch([(block, send_ref.at[pl.ds(128 * k, 128)]) for k in range(4)], sems.at[pl.ds(2, 4)])
    copies[1].wait()
    for f in range(FRAMES):
        for y in range(ROWS):
            tile = inner_ref[f, y].astype(F32)
            k = ROWS * f + y
            low[k : k + 1, :] = tile[0:1, :]
            high[k : k + 1, :] = tile[7:8, :]
    one, two = even_first("cols", low[...], high[...])
    one_ref[...] = one.astype(BF)
    two_ref[...] = two.astype(BF)
    for copy in sends:
        copy.wait()


def rows_kernel(inner_ref, one_ref, two_ref, left_ref, right_ref, up_ref, down_ref, first, last):
    right, left = even_first("cols", two_ref[...].astype(F32), one_ref[...].astype(F32))
    left_ref[...] = left
    right_ref[...] = right
    first[...] = jnp.zeros_like(first)
    last[...] = jnp.zeros_like(last)
    for f in range(FRAMES):
        for y, rows in ((0, first), (ROWS - 1, last)):
            k = ROWS * f + y
            rows[16 * f : 16 * f + 8, :] = inner_ref[f, y].astype(F32)
            rows[16 * f + 8 : 16 * f + 9, :] = left_ref[k : k + 1, :]
            rows[16 * f + 9 : 16 * f + 10, :] = right_ref[k : k + 1, :]
    one, two = even_first("rows", first[...], last[...])
    up_ref[...] = one.astype(BF)
    down_ref[...] = two.astype(BF)


def shifted(tile, left, right, bounds, period):
    at = lane(tile.shape) % period
    row = sublane(tile.shape)
    back = jnp.where(row == 0, left, pltpu.roll(tile, 1, axis=0))
    ahead = jnp.where(row == 7, right, pltpu.roll(tile, 7, axis=0))
    return jnp.where(at < bounds[0], back, jnp.where(at < bounds[1], tile, ahead))


def fetch_kernel(
    _, x_ref, ut_ref, ot_ref, cot_ref, core_ref, one_ref, two_ref, take_ref, give_ref, kind_ref,
    own_ref, wide_ref, utp_ref, u_ref, ring_ref, ot_out, cot_out, take_out, give_out, kind_out,
    ut, owns, flat, sems,
):
    copies = fetch(
        (
            (ut_ref, ut), (core_ref, owns[0]), (one_ref, owns[1]), (two_ref, owns[2]),
            (take_ref, take_out), (give_ref, give_out), (kind_ref, kind_out), (ot_ref, ot_out), (cot_ref, cot_out),
        ),
        sems,
    )
    row = sublane((256, 64))
    at = row % 128
    pick = (lane((256, 64)) == (at % 32) * 2 + row // 128) & (at < 96)
    half_row = sublane((64, 64))
    half_pick = lane((64, 64)) == (half_row % 32) * 2 + half_row // 32
    copies[0].wait()
    wide = dot(pick.astype(BF), ut[...]).astype(BF)
    wide_ref[...] = wide
    utp = dot(half_pick.astype(BF), ut[...])
    utp_ref[...] = utp.astype(BF)
    u_ref[...] = utp.T.astype(BF)
    own_ref[...] = dot_nt(x_ref[...], wide).astype(BF).astype(F32)
    shift = ring_shift()
    for k in range(3):
        copies[1 + k].wait()
        ring_ref[k] = to_ring(load_flat(owns[k], flat), shift)
    for k in range(4, 9):
        copies[k].wait()


def stack_rows(tiles, out_ref):
    for b in range(3):
        out_ref[b, 0:48, :] = jnp.zeros((48, 256), BF)
        out_ref[b, 192:240, :] = jnp.zeros((48, 256), BF)
        for f in range(FRAMES):
            rows = tiles[f, b : b + ROWS].reshape(48, 256)
            out_ref[b, 48 * f + 48 : 48 * f + 96, :] = rows.astype(BF)


def rank_kernel(own_ref, wide_ref, one_ref, two_ref, left_ref, right_ref, q_ref, tiles, edge, rims):
    wide = wide_ref[...]

    def project(v):
        return dot_nt(v.astype(BF), wide).astype(BF).astype(F32)

    below, above = even_first("rows", project(two_ref[...]), project(one_ref[...]))
    rims[0] = above
    rims[1] = below
    edge[0] = project(left_ref[...])
    edge[1] = project(right_ref[...])
    for f in range(FRAMES):
        for y in range(8):
            if y in (0, 7):
                rim = rims.at[y // 7]
                at = 16 * f
                tile, left, right = rim[at : at + 8, :], rim[at + 8 : at + 9, :], rim[at + 9 : at + 10, :]
            else:
                k = ROWS * f + y - 1
                tile = own_ref[8 * k : 8 * k + 8, :]
                left, right = edge[0, k : k + 1, :], edge[1, k : k + 1, :]
            left = jnp.broadcast_to(left, (8, 256))
            right = jnp.broadcast_to(right, (8, 256))
            tiles[f, y] = shifted(tile, left, right, (32, 64), 128)
    stack_rows(tiles, q_ref)


def core_index(shape):
    return jnp.full(shape, lax.rem(lax.axis_index("rows"), 2), jnp.int32)


def gather_table(mine_ref, other_ref, take_ref, kind_ref, table_ref):
    kind = kind_ref[...]
    take = take_ref[...]
    first = core_index((128, 128)) == 0
    for g in range(4):
        mine, other = mine_ref[128 * g : 128 * g + 128, :], other_ref[128 * g : 128 * g + 128, :]
        block = jnp.concatenate([jnp.where(first, mine, other), jnp.where(first, other, mine)], axis=0)
        none = jnp.zeros_like(block)
        both = jnp.concatenate(
            [jnp.where(kind == 0, block, none), jnp.where(kind == 1, block, none)], axis=0
        )
        table_ref[216 * g : 216 * g + 216, :] = dot(take, both)


def inside(lanes, at):
    return (lanes >= at) & (lanes < at + 64)


def gradient_blocks(half, grads, pixels, give_ref, kind_ref, blocks):
    wrapped = kind_ref[0:128, :] == 1
    for g in range(4):
        source = grads[216 * g : 216 * g + 216, :].astype(BF)
        part = dot(give_ref[half], source)
        blocks[128 * g : 128 * g + 128, :] = jnp.where(wrapped, part[128:256], part[0:128])
    lanes = lane((16, 128))
    row = lax.axis_index("rows")
    for a, (c, j, at) in enumerate(RELAYS):
        slot = sublane((16, 128)) + 16 * a
        across = ((slot < 48) | (slot >= 84)).astype(jnp.int32)
        goes = lax.rem(jnp.full((16, 128), row + half, jnp.int32) + across, 2) == 0
        pixel = jnp.where(goes, pixels[16 * a : 16 * a + 16, :], 0.0)
        if at % 64:
            pixel = pltpu.roll(pixel, at, axis=1)
        spot = pl.ds(4 * c + j, 16, stride=32)
        blocks[spot, :] = jnp.where(inside(lanes, at), pixel, blocks[spot, :])


def forward_kernel(
    mine_ref, other_ref, q_ref, cot_ref, ot_ref, take_ref, give_ref, kind_ref,
    send_ref, grads, pixels, table_out, outp_ref, table, border, blocks,
):
    gather_table(mine_ref, other_ref, take_ref, kind_ref, table)
    table_out[...] = table[...].astype(BF)
    even = jnp.zeros((CELLS, 128), F32)
    odd = jnp.zeros((CELLS, 128), F32)
    for a in range(3):
        for b in range(3):
            k = 3 * a + b
            weights = table_out[96 * k : 96 * k + 96, :]
            rows = q_ref[b, 48 * a : 48 * a + CELLS, :]
            even = even + dot(rows[:, 0:96], weights)
            odd = odd + dot(rows[:, 128:224], weights)
    mid = (even[:, 0:64] + odd[:, 64:128]).astype(BF)
    pre = dot(mid, ot_ref[...])
    sig = jax.nn.sigmoid(pre)
    slope = (cot_ref[...].astype(F32) * sig * (1.0 + pre * (1.0 - sig))).astype(BF)
    ot = ot_ref[...]
    out_t = dot_nt(ot, slope).astype(BF)
    wide = jnp.concatenate([ot, ot, ot, ot], axis=0)
    outp = dot_nt(slope, wide).astype(BF).astype(F32)
    outp_ref[...] = outp
    border[...] = outp[:, 0:128]
    for f in range(FRAMES):
        pixels[8 * f : 8 * f + 8, :] = border[48 * f : 48 * f + 8, :]
        pixels[24 + 8 * f : 32 + 8 * f, :] = border[48 * f + 40 : 48 * f + 48, :]
    pixels[48:66, :] = border[pl.ds(0, 18, stride=8), :]
    pixels[66:84, :] = border[pl.ds(7, 18, stride=8), :]
    for k, cell in enumerate((0, 7, 40, 47)):
        pixels[84 + 3 * k : 87 + 3 * k, :] = border[pl.ds(cell, 3, stride=48), :]
    for a in range(3):
        for b in range(3):
            k = 3 * a + b
            part = dot(out_t, q_ref[b, 48 * a : 48 * a + CELLS, :])
            stack = jnp.concatenate([part[:, 0:128], part[:, 128:256]], axis=0)
            grads[96 * k : 96 * k + 96, :] = stack.T[0:96, :]
    gradient_blocks(1 - lax.rem(lax.axis_index("rows"), 2), grads, pixels, give_ref, kind_ref, blocks)
    send_ref[...] = blocks[...].astype(BF)


def keep_kernel(grads, pixels, give_ref, kind_ref, keep_ref):
    gradient_blocks(lax.rem(lax.axis_index("rows"), 2), grads, pixels, give_ref, kind_ref, keep_ref)


def add_kernel(keep_ref, got_ref, send_ref):
    send_ref[...] = (keep_ref[...] + got_ref[...].astype(F32)).astype(BF)


def adam_kernel(got_ref, ring_ref, send_ref, next_ref, passed):
    total = jnp.zeros((8, 128), F32)
    passed[0:40, :] = jnp.zeros((40, 128), F32)
    passed[552:592, :] = jnp.zeros((40, 128), F32)
    for g in range(4):
        part = got_ref[128 * g : 128 * g + 128, :].astype(F32)
        passed[128 * g + 40 : 128 * g + 168, :] = part
        total = total + part.reshape(16, 8, 128).sum(axis=0)
    grad = (total[0:4] + total[4:8]) * (1.0 / 192.0)
    core, one, two = ring_ref[0], ring_ref[1], ring_ref[2]
    one = beta_one * one + (1.0 - beta_one) * grad
    two = beta_two * two + (1.0 - beta_two) * grad * grad
    core = core - learn_rate * (one / fix_one) / (jnp.sqrt(two / fix_two) + epsilon)
    next_ref[0] = core
    next_ref[1] = one
    next_ref[2] = two
    own = jnp.where(in_ring(ring_shift()), core, 0.0)
    own = jnp.concatenate([own, own], axis=0)
    row, col = lax.axis_index("rows"), lax.axis_index("cols")
    slot, parity, mask = lax.div(row, 2), lax.rem(row, 2), jnp.zeros((8, 128), jnp.bool_)
    for a, (c, j, at) in enumerate(RELAYS):
        slot = slot + jnp.where(col == c, 16 * a, 0)
        spot = (sublane((8, 128)) % 4 == j) & inside(lane((8, 128)), at)
        mask = mask | (spot & (jnp.full((8, 128), col, jnp.int32) == c))
    up, right = 0, 0
    for first, count, rows, cols in SLOTS:
        here = (slot >= first) & (slot < first + count)
        up = up + jnp.where(here, rows, 0)
        right = right + jnp.where(here, cols, 0)
    source = lax.rem(parity - up + 2, 2)
    chips = lax.div(source + up - parity + 2, 2) - 1
    start = 40 - 4 * (8 * chips + right)
    for k in range(32):
        upper = passed[pl.ds(start + 16 * k, 8), :]
        lower = passed[pl.ds(start + 16 * k + 8, 8), :]
        block = jnp.concatenate([jnp.where(mask, upper, own), jnp.where(mask, lower, own)], axis=0)
        send_ref[16 * k : 16 * k + 16, :] = block.astype(BF)


def flat_kernel(next_ref, core_ref, one_ref, two_ref):
    shift = ring_shift()
    for k, ref in enumerate((core_ref, one_ref, two_ref)):
        store_flat(ref, from_ring(next_ref[k], shift))


def turn_kernel(table_ref, back_ref):
    for k in range(9):
        for c in range(3):
            t = 3 * k + c
            part = table_ref[32 * t : 32 * t + 32, :].astype(F32).T
            cube = jnp.concatenate([part[0:64], part[64:128]], axis=1)
            back_ref[k, 64 * (2 - c) : 64 * (2 - c) + 64, :] = cube.astype(BF)


def backward_kernel(mine_ref, outp_ref, back_ref, utp_ref, grad_ref, got, pixels, tiles, qs):
    row, col = lax.axis_index("rows"), lax.axis_index("cols")
    got[...] = mine_ref[...].astype(F32)
    for a, (c, j, at) in enumerate(RELAYS):
        pixel = got[pl.ds(4 * c + j, 16, stride=32), :]
        pixels[16 * a : 16 * a + 16, 0:128] = pltpu.roll(pixel, 128 - at, axis=1) if at else pixel
    spread = (sublane((64, 256)) == lane((64, 256)) % 64).astype(BF)
    pixels[...] = dot(pixels[:, 0:64].astype(BF), spread)
    zero = jnp.zeros((8, 256), F32)

    def kept(flag, v):
        return jnp.where(jnp.full((8, 256), flag.astype(jnp.int32), jnp.int32) > 0, v, zero)

    def spot(k):
        return jnp.broadcast_to(pixels[k : k + 1, :], (8, 256))

    for f in range(FRAMES):
        for y in range(8):
            if y == 0:
                tile, left, right = pixels[24 + 8 * f : 32 + 8 * f, :], spot(93 + f), spot(90 + f)
            elif y == 7:
                tile, left, right = pixels[8 * f : 8 * f + 8, :], spot(87 + f), spot(84 + f)
            else:
                at = 48 * f + 8 * (y - 1)
                tile = outp_ref[at : at + 8, :]
                left, right = spot(66 + 6 * f + y - 1), spot(48 + 6 * f + y - 1)
            tile = shifted(tile, kept(col > 0, left), kept(col < 7, right), (64, 128), 256)
            if y == 0:
                tile = kept(row > 0, tile)
            elif y == 7:
                tile = kept(row < 31, tile)
            tiles[f, y] = tile
    stack_rows(tiles, qs)
    total = jnp.zeros((CELLS, 64), F32)
    for a in range(3):
        for b in range(3):
            rows = qs[2 - b, 48 * (2 - a) : 48 * (2 - a) + CELLS, :]
            total = total + dot(rows[:, 0:192], back_ref[3 * a + b])
    grad_ref[...] = dot(total.astype(BF), utp_ref[...]).astype(BF)

def build_kernel(mine_ref, other_ref, u_ref, ot_ref, take_ref, kind_ref, out_ref, table, half, result, sems):
    gather_table(mine_ref, other_ref, take_ref, kind_ref, table)
    cube = table[...].astype(BF)
    even = dot(cube[:, 0:64], ot_ref[...]).astype(BF)
    odd = dot(cube[:, 64:128], ot_ref[...]).astype(BF)
    for t in range(27):
        half[t, 0:32, :] = even[32 * t : 32 * t + 32]
        half[t, 32:64, :] = odd[32 * t : 32 * t + 32]
    u = u_ref[...]

    def store(a):
        part = pl.ds(3 * a, 3)
        return pltpu.make_async_copy(result.at[part], out_ref.at[part], sems.at[a])

    for a in range(9):
        for t in range(3 * a, 3 * a + 3):
            result[t] = dot(u, half[t]).astype(BF)
        store(a).start()
    for a in range(9):
        store(a).wait()


def call(kernel, args, outs, scratch, flops=10**7):
    def spec(far):
        return pl.BlockSpec(memory_space=pltpu.HBM if far else pltpu.VMEM)

    return pl.pallas_call(
        kernel,
        out_shape=[jax.ShapeDtypeStruct(shape, dtype) for shape, dtype, _ in outs],
        in_specs=[spec(far) for _, far in args],
        out_specs=[spec(far) for _, _, far in outs],
        scratch_shapes=scratch,
        compiler_params=pltpu.CompilerParams(vmem_limit_bytes=32 << 20),
        cost_estimate=pl.CostEstimate(flops=flops, bytes_accessed=10**5, transcendentals=0),
    )(*[pltpu.with_memory_space_constraint(arg, pltpu.HBM) if far else arg for arg, far in args])


def near(*args):
    return [(arg, False) for arg in args]


def far(*args):
    return [(arg, True) for arg in args]


def swap(one, two, axis):
    count = lax.axis_size(axis)
    pairs = [[(i, i + 1) for i in range(k, count - 1, 2)] for k in range(2)]
    two, one = (
        lax.ppermute(x, axis, forward + [(b, a) for a, b in forward]) for x, forward in ((two, pairs[1]), (one, pairs[0]))
    )
    return one, two


def device(k, chip, col):
    return 8 * (2 * chip + k) + col


ORDER = [[device(k, chip, col) for chip in range(16) for col in range(8)] for k in range(2)]


def exchange(x):
    return lax.all_to_all(x, AXES, 0, 0, tiled=True, axis_index_groups=ORDER)


def in_chip(x):
    return lax.ppermute(x, "rows", [(r, r ^ 1) for r in range(32)])


def body(frames_in, cotangent, core, moment_one, moment_two, u_in, u_out):
    take, give, kind = ring_tables()
    take, give, kind = jnp.asarray(take, BF), jnp.asarray(give, BF), jnp.asarray(kind, F32)
    vm, dma = pltpu.VMEM, pltpu.SemaphoreType.DMA
    side = (FRAMES * ROWS, 256)
    rim = (FRAMES * 16, 256)

    send, one, two, inner = call(
        start_kernel,
        far(core, frames_in),
        [((512, 128), BF, True), (side, BF, False), (side, BF, False), ((FRAMES, ROWS, COLS, 256), BF, False)],
        [vm((OWN,), F32), vm((8, 128), F32), vm((128, 128), BF), vm(side, F32), vm(side, F32), dma((6,))],
    )
    one, two = swap(one, two, "cols")
    mine = exchange(send)
    left, right, one, two = call(
        rows_kernel,
        near(inner, one, two),
        [(side, F32, False), (side, F32, False), (rim, BF, False), (rim, BF, False)],
        [vm(rim, F32), vm(rim, F32)],
        flops=10**10,
    )
    own, wide, utp, u, ring, ot, cot, take, give, kind = call(
        fetch_kernel,
        near(left, inner.reshape(CELLS, 256)) + far(
            u_in.T, u_out.T, cotangent.reshape(CELLS, 256), core, moment_one, moment_two, take, give, kind,
        ),
        [
            ((CELLS, 256), F32, False), ((256, 256), BF, False), ((64, 256), BF, False), ((256, 64), BF, False),
            ((3, 4, 128), F32, False), ((64, 256), BF, False), ((CELLS, 256), BF, False),
            ((216, 512), BF, False), ((2, 256, 216), BF, False), ((256, 128), F32, False),
        ],
        [
            vm((64, 256), BF), [vm((OWN,), F32) for _ in range(3)], vm((8, 128), F32),
            dma((9,)),
        ],
        flops=10000000000,
    )
    mine, _ = lax.optimization_barrier((mine, ring))
    other = in_chip(mine)
    one, two = swap(one, two, "rows")
    (q,) = call(
        rank_kernel,
        near(own, wide, one, two, left, right),
        [((3, 240, 256), BF, False)],
        [vm((FRAMES, 8, 8, 256), F32), vm((2, 18, 256), F32), vm((2, 48, 256), F32)],
        flops=10000000000,
    )
    send, grads, pixels, table, outp = call(
        forward_kernel,
        near(mine, other, q, cot, ot, take, give, kind),
        [
            ((512, 128), BF, False), ((TABLE, 128), F32, False), ((96, 128), F32, False), ((TABLE, 128), BF, False),
            ((CELLS, 256), F32, False),
        ],
        [vm((TABLE, 128), F32), vm((CELLS, 128), F32), vm((512, 128), F32)],
    )
    got = in_chip(send)
    (keep,) = call(keep_kernel, near(grads, pixels, give, kind), [((512, 128), F32, False)], [], flops=10**9)
    (send,) = call(add_kernel, near(keep, got), [((512, 128), BF, False)], [])
    got = exchange(send)
    send, latest = call(
        adam_kernel,
        near(got, ring),
        [((512, 128), BF, False), ((3, 4, 128), F32, False)],
        [vm((592, 128), F32)],
    )
    mine = exchange(send)
    (back,) = call(turn_kernel, near(table), [((9, 192, 64), BF, False)], [])
    core_next, one_next, two_next = call(flat_kernel, near(latest), [((OWN,), F32, False)] * 3, [])
    mine, back, core_next, one_next, two_next = lax.optimization_barrier((mine, back, core_next, one_next, two_next))
    other = in_chip(mine)
    (frames_grad,) = call(
        backward_kernel,
        near(mine, outp, back, utp),
        [((CELLS, 256), BF, False)],
        [vm((512, 128), F32), vm((96, 256), F32), vm((FRAMES, 8, 8, 256), F32), vm((3, 240, 256), BF)],
        flops=10**9,
    )
    other, frames_grad = lax.optimization_barrier((other, frames_grad))
    (kernel_next,) = call(
        build_kernel,
        near(mine, other, u, ot, take, kind),
        [((27, 256, 256), BF, True)],
        [vm((TABLE, 128), F32), vm((27, 64, 256), BF), vm((27, 256, 256), BF), dma((9,))],
    )
    frames_grad = frames_grad.reshape(FRAMES, ROWS, COLS, 256)
    return frames_grad, core_next, one_next, two_next, kernel_next


def solution(mesh):
    in_specs = (
        P(None, "rows", "cols", None),
        P(None, "rows", "cols", None),
        P(AXES),
        P(AXES),
        P(AXES),
        P(),
        P(),
    )
    out_specs = (
        P(None, "rows", "cols", None),
        P(AXES),
        P(AXES),
        P(AXES),
        P(),
    )
    return jax.shard_map(body, mesh=mesh, in_specs=in_specs, out_specs=out_specs, check_vma=False)
```

```python
import jax
import jax.numpy as jnp
import numpy as np
from jax import lax
from jax.experimental import pallas as pl
from jax.experimental.pallas import tpu as pltpu
from jax.sharding import PartitionSpec as P

beta_one = 0.9
beta_two = 0.999
learn_rate = 0.06
epsilon = 1e-08
fix_one = 1.0 - 0.9**10
fix_two = 1.0 - 0.999**10

BF = jnp.bfloat16
F32 = jnp.float32
AXES = ("rows", "cols")

OWN = 432
FRAMES, ROWS, COLS = 3, 6, 8
CELLS = FRAMES * ROWS * COLS
SIDE = FRAMES * 8
TABLE = 864


RELAYS = ((7, 0, 0), (4, 0, 0), (3, 3, 64), (0, 3, 64), (2, 0, 16), (5, 0, 32))
SLOTS = (
    (0, 24, -1, 0), (24, 24, 1, 0), (48, 18, 0, -1), (66, 18, 0, 1),
    (84, 3, -1, -1), (87, 3, -1, 1), (90, 3, 1, -1), (93, 3, 1, 1),
)


def ring_tables():
    take = np.zeros((216, 512), np.float32)
    give = np.zeros((2, 256, 216), np.float32)
    kind = np.zeros((256, 128), np.float32)
    for r in range(8):
        for c in range(8):
            first = 27 * r + 27 * c // 8
            col = 128 * (r % 2) + 32 * (r // 2) + 4 * c
            for j in range(4):
                take[first + j, col + j] = 1
                give[r % 2, col % 128 + j, first + j] = 1
            wrapped = 48 * c % 128 + OWN - 512
            if wrapped > 0:
                take[first + 4, 256 + col] = 1
                give[r % 2, 128 + col % 128, first + 4] = 1
                kind[col, :wrapped] = 1
        for c, j, at in RELAYS:
            kind[128 * (r % 2) + 32 * (r // 2) + 4 * c + j, at : at + 64] = 2
    return take, give, kind


def dot(a, b):
    return jnp.dot(a, b, preferred_element_type=F32)


def dot_nt(a, b):
    return lax.dot_general(a, b, (((1,), (1,)), ((), ())), preferred_element_type=F32)


def dot_tn(a, b):
    return lax.dot_general(a, b, (((0,), (0,)), ((), ())), preferred_element_type=F32)


def lane(shape):
    return lax.broadcasted_iota(jnp.int32, shape, 1)


def sublane(shape):
    return lax.broadcasted_iota(jnp.int32, shape, 0)


def ring_shift():
    return lax.rem(lax.axis_index("cols") * 48, 128)


def to_ring(v, shift):
    turned = pltpu.roll(v, shift, axis=1)
    above = jnp.concatenate([turned[3:4], turned[0:3]], axis=0)
    return jnp.where(lane(v.shape) >= shift, turned, above)


def from_ring(v, shift):
    turned = pltpu.roll(v, lax.rem(128 - shift, 128), axis=1)
    below = jnp.concatenate([turned[1:4], turned[0:1]], axis=0)
    return jnp.where(lane(v.shape) < 128 - shift, turned, below)


def in_ring(shift):
    place = sublane((4, 128)) * 128 + lane((4, 128)) - shift
    place = jnp.where(place < 0, place + 512, place)
    return place < OWN


def load_flat(ref, scratch):
    scratch[...] = jnp.zeros_like(scratch)
    for k in range(3):
        scratch[k, :] = ref[pl.ds(128 * k, 128)]
    scratch[3, 0 : OWN - 384] = ref[pl.ds(384, OWN - 384)]
    return scratch[0:4, :]


def store_flat(ref, v):
    for k in range(3):
        ref[pl.ds(128 * k, 128)] = v[k]
    ref[pl.ds(384, OWN - 384)] = v[3, 0 : OWN - 384]


def fetch(pairs, sems):
    copies = [pltpu.make_async_copy(src, dst, sems.at[k]) for k, (src, dst) in enumerate(pairs)]
    for copy in copies:
        copy.start()
    return copies


def even_first(axis, first, last):
    even = jnp.full(first.shape, lax.rem(lax.axis_index(axis), 2), jnp.int32) == 0
    return jnp.where(even, last, first), jnp.where(even, first, last)


def start_kernel(core_ref, x_ref, send_ref, one_ref, two_ref, inner_ref, own, flat, block, low, high, sems):
    copies = fetch(((core_ref, own), (x_ref, inner_ref)), sems)
    copies[0].wait()
    v = to_ring(load_flat(own, flat), ring_shift())
    rows = jnp.concatenate([v, v, v, v], axis=0).astype(BF)
    for k in range(8):
        block[16 * k : 16 * k + 16, :] = rows
    sends = fetch([(block, send_ref.at[pl.ds(128 * k, 128)]) for k in range(4)], sems.at[pl.ds(2, 4)])
    copies[1].wait()
    for f in range(FRAMES):
        for y in range(ROWS):
            tile = inner_ref[f, y].astype(F32)
            k = ROWS * f + y
            low[k : k + 1, :] = tile[0:1, :]
            high[k : k + 1, :] = tile[7:8, :]
    one, two = even_first("cols", low[...], high[...])
    one_ref[...] = one.astype(BF)
    two_ref[...] = two.astype(BF)
    for copy in sends:
        copy.wait()


def rows_kernel(inner_ref, two_ref, one_ref, left_ref, right_ref, up_ref, down_ref, first, last):
    right, left = even_first("cols", two_ref[...].astype(F32), one_ref[...].astype(F32))
    left_ref[...] = left
    right_ref[...] = right
    first[...] = jnp.zeros_like(first)
    last[...] = jnp.zeros_like(last)
    for f in range(FRAMES):
        for y, rows in ((0, first), (ROWS - 1, last)):
            k = ROWS * f + y
            rows[16 * f : 16 * f + 8, :] = inner_ref[f, y].astype(F32)
            rows[16 * f + 8 : 16 * f + 9, :] = left_ref[k : k + 1, :]
            rows[16 * f + 9 : 16 * f + 10, :] = right_ref[k : k + 1, :]
    one, two = even_first("rows", first[...], last[...])
    up_ref[...] = one.astype(BF)
    down_ref[...] = two.astype(BF)


def shifted(tile, left, right, bounds, period):
    at = lane(tile.shape) % period
    row = sublane(tile.shape)
    back = jnp.where(row == 0, left, pltpu.roll(tile, 1, axis=0))
    ahead = jnp.where(row == 7, right, pltpu.roll(tile, 7, axis=0))
    return jnp.where(at < bounds[0], back, jnp.where(at < bounds[1], tile, ahead))


def fetch_kernel(
    _, x_ref, ut_ref, ot_ref, cot_ref, core_ref, one_ref, two_ref, take_ref, give_ref, kind_ref,
    own_ref, wide_ref, utp_ref, u_ref, ring_ref, ot_out, cot_out, take_out, give_out, kind_out,
    ut, owns, flat, sems,
):
    copies = fetch(
        (
            (ut_ref, ut), (core_ref, owns[0]), (one_ref, owns[1]), (two_ref, owns[2]),
            (take_ref, take_out), (give_ref, give_out), (kind_ref, kind_out), (ot_ref, ot_out), (cot_ref, cot_out),
        ),
        sems,
    )
    row = sublane((256, 64))
    at = row % 128
    pick = (lane((256, 64)) == (at % 32) * 2 + row // 128) & (at < 96)
    half_row = sublane((64, 64))
    half_pick = lane((64, 64)) == (half_row % 32) * 2 + half_row // 32
    copies[0].wait()
    wide = dot(pick.astype(BF), ut[...]).astype(BF)
    wide_ref[...] = wide
    utp = dot(half_pick.astype(BF), ut[...])
    utp_ref[...] = utp.astype(BF)
    u_ref[...] = utp.T.astype(BF)
    own_ref[...] = dot_nt(x_ref[...], wide).astype(BF).astype(F32)
    shift = ring_shift()
    for k in range(3):
        copies[1 + k].wait()
        ring_ref[k] = to_ring(load_flat(owns[k], flat), shift)
    for k in range(4, 9):
        copies[k].wait()


def stack_rows(tiles, out_ref):
    for b in range(3):
        out_ref[b, 0:48, :] = jnp.zeros((48, 256), BF)
        out_ref[b, 192:240, :] = jnp.zeros((48, 256), BF)
        for f in range(FRAMES):
            rows = tiles[f, b : b + ROWS].reshape(48, 256)
            out_ref[b, 48 * f + 48 : 48 * f + 96, :] = rows.astype(BF)


def rank_kernel(own_ref, wide_ref, two_ref, one_ref, left_ref, right_ref, q_ref, tiles, edge, rims):
    wide = wide_ref[...]

    def project(v):
        return dot_nt(v.astype(BF), wide).astype(BF).astype(F32)

    below, above = even_first("rows", project(two_ref[...]), project(one_ref[...]))
    rims[0] = above
    rims[1] = below
    edge[0] = project(left_ref[...])
    edge[1] = project(right_ref[...])
    for f in range(FRAMES):
        for y in range(8):
            if y in (0, 7):
                rim = rims.at[y // 7]
                at = 16 * f
                tile, left, right = rim[at : at + 8, :], rim[at + 8 : at + 9, :], rim[at + 9 : at + 10, :]
            else:
                k = ROWS * f + y - 1
                tile = own_ref[8 * k : 8 * k + 8, :]
                left, right = edge[0, k : k + 1, :], edge[1, k : k + 1, :]
            left = jnp.broadcast_to(left, (8, 256))
            right = jnp.broadcast_to(right, (8, 256))
            tiles[f, y] = shifted(tile, left, right, (32, 64), 128)
    stack_rows(tiles, q_ref)


def core_index(shape):
    return jnp.full(shape, lax.rem(lax.axis_index("rows"), 2), jnp.int32)


def gather_table(mine_ref, other_ref, take_ref, kind_ref, table_ref):
    kind = kind_ref[...]
    take = take_ref[...]
    first = core_index((128, 128)) == 0
    for g in range(4):
        mine, other = mine_ref[128 * g : 128 * g + 128, :], other_ref[128 * g : 128 * g + 128, :]
        block = jnp.concatenate([jnp.where(first, mine, other), jnp.where(first, other, mine)], axis=0)
        none = jnp.zeros_like(block)
        both = jnp.concatenate(
            [jnp.where(kind == 0, block, none), jnp.where(kind == 1, block, none)], axis=0
        )
        table_ref[216 * g : 216 * g + 216, :] = dot(take, both)


def inside(lanes, at):
    return (lanes >= at) & (lanes < at + 64)


def gradient_blocks(half, grads, pixels, give_ref, kind_ref, blocks):
    wrapped = kind_ref[0:128, :] == 1
    for g in range(4):
        source = grads[216 * g : 216 * g + 216, :].astype(BF)
        part = dot(give_ref[half], source)
        blocks[128 * g : 128 * g + 128, :] = jnp.where(wrapped, part[128:256], part[0:128])
    lanes = lane((16, 128))
    row = lax.axis_index("rows")
    for a, (c, j, at) in enumerate(RELAYS):
        slot = sublane((16, 128)) + 16 * a
        across = ((slot < 48) | (slot >= 84)).astype(jnp.int32)
        goes = lax.rem(jnp.full((16, 128), row + half, jnp.int32) + across, 2) == 0
        pixel = jnp.where(goes, pixels[16 * a : 16 * a + 16, :], 0.0)
        if at % 64:
            pixel = pltpu.roll(pixel, at, axis=1)
        spot = pl.ds(4 * c + j, 16, stride=32)
        blocks[spot, :] = jnp.where(inside(lanes, at), pixel, blocks[spot, :])


def forward_kernel(
    mine_ref, other_ref, q_ref, cot_ref, ot_ref, take_ref, give_ref, kind_ref,
    send_ref, grads, pixels, table_out, outp_ref, table, border, blocks,
):
    gather_table(mine_ref, other_ref, take_ref, kind_ref, table)
    table_out[...] = table[...].astype(BF)
    even = jnp.zeros((CELLS, 128), F32)
    odd = jnp.zeros((CELLS, 128), F32)
    for a in range(3):
        for b in range(3):
            k = 3 * a + b
            weights = table_out[96 * k : 96 * k + 96, :]
            rows = q_ref[b, 48 * a : 48 * a + CELLS, :]
            even = even + dot(rows[:, 0:96], weights)
            odd = odd + dot(rows[:, 128:224], weights)
    mid = (even[:, 0:64] + odd[:, 64:128]).astype(BF)
    pre = dot(mid, ot_ref[...])
    sig = jax.nn.sigmoid(pre)
    slope = (cot_ref[...].astype(F32) * sig * (1.0 + pre * (1.0 - sig))).astype(BF)
    ot = ot_ref[...]
    out_t = dot_nt(ot, slope).astype(BF)
    wide = jnp.concatenate([ot, ot, ot, ot], axis=0)
    outp = dot_nt(slope, wide).astype(BF).astype(F32)
    outp_ref[...] = outp
    border[...] = outp[:, 0:128]
    for f in range(FRAMES):
        pixels[8 * f : 8 * f + 8, :] = border[48 * f : 48 * f + 8, :]
        pixels[24 + 8 * f : 32 + 8 * f, :] = border[48 * f + 40 : 48 * f + 48, :]
    pixels[48:66, :] = border[pl.ds(0, 18, stride=8), :]
    pixels[66:84, :] = border[pl.ds(7, 18, stride=8), :]
    for k, cell in enumerate((0, 7, 40, 47)):
        pixels[84 + 3 * k : 87 + 3 * k, :] = border[pl.ds(cell, 3, stride=48), :]
    for a in range(3):
        for b in range(3):
            k = 3 * a + b
            part = dot(out_t, q_ref[b, 48 * a : 48 * a + CELLS, :])
            stack = jnp.concatenate([part[:, 0:128], part[:, 128:256]], axis=0)
            grads[96 * k : 96 * k + 96, :] = stack.T[0:96, :]
    gradient_blocks(1 - lax.rem(lax.axis_index("rows"), 2), grads, pixels, give_ref, kind_ref, blocks)
    send_ref[...] = blocks[...].astype(BF)


def keep_kernel(grads, pixels, give_ref, kind_ref, keep_ref):
    gradient_blocks(lax.rem(lax.axis_index("rows"), 2), grads, pixels, give_ref, kind_ref, keep_ref)


def add_kernel(keep_ref, got_ref, send_ref):
    send_ref[...] = (keep_ref[...] + got_ref[...].astype(F32)).astype(BF)


def adam_kernel(got_ref, ring_ref, send_ref, next_ref, passed):
    total = jnp.zeros((8, 128), F32)
    passed[0:40, :] = jnp.zeros((40, 128), F32)
    passed[552:592, :] = jnp.zeros((40, 128), F32)
    for g in range(4):
        part = got_ref[128 * g : 128 * g + 128, :].astype(F32)
        passed[128 * g + 40 : 128 * g + 168, :] = part
        total = total + part.reshape(16, 8, 128).sum(axis=0)
    grad = (total[0:4] + total[4:8]) * (1.0 / 192.0)
    core, one, two = ring_ref[0], ring_ref[1], ring_ref[2]
    one = beta_one * one + (1.0 - beta_one) * grad
    two = beta_two * two + (1.0 - beta_two) * grad * grad
    core = core - learn_rate * (one / fix_one) / (jnp.sqrt(two / fix_two) + epsilon)
    next_ref[0] = core
    next_ref[1] = one
    next_ref[2] = two
    own = jnp.where(in_ring(ring_shift()), core, 0.0)
    own = jnp.concatenate([own, own], axis=0)
    row, col = lax.axis_index("rows"), lax.axis_index("cols")
    slot, parity, mask = lax.div(row, 2), lax.rem(row, 2), jnp.zeros((8, 128), jnp.bool_)
    for a, (c, j, at) in enumerate(RELAYS):
        slot = slot + jnp.where(col == c, 16 * a, 0)
        spot = (sublane((8, 128)) % 4 == j) & inside(lane((8, 128)), at)
        mask = mask | (spot & (jnp.full((8, 128), col, jnp.int32) == c))
    up, right = 0, 0
    for first, count, rows, cols in SLOTS:
        here = (slot >= first) & (slot < first + count)
        up = up + jnp.where(here, rows, 0)
        right = right + jnp.where(here, cols, 0)
    source = lax.rem(parity - up + 2, 2)
    chips = lax.div(source + up - parity + 2, 2) - 1
    start = 40 - 4 * (8 * chips + right)
    for k in range(32):
        upper = passed[pl.ds(start + 16 * k, 8), :]
        lower = passed[pl.ds(start + 16 * k + 8, 8), :]
        block = jnp.concatenate([jnp.where(mask, upper, own), jnp.where(mask, lower, own)], axis=0)
        send_ref[16 * k : 16 * k + 16, :] = block.astype(BF)


def flat_kernel(next_ref, core_ref, one_ref, two_ref):
    shift = ring_shift()
    for k, ref in enumerate((core_ref, one_ref, two_ref)):
        store_flat(ref, from_ring(next_ref[k], shift))


def turn_kernel(table_ref, back_ref):
    for k in range(9):
        for c in range(3):
            t = 3 * k + c
            part = table_ref[32 * t : 32 * t + 32, :].astype(F32).T
            cube = jnp.concatenate([part[0:64], part[64:128]], axis=1)
            back_ref[k, 64 * (2 - c) : 64 * (2 - c) + 64, :] = cube.astype(BF)


def backward_kernel(mine_ref, outp_ref, back_ref, utp_ref, grad_ref, got, pixels, tiles, qs):
    row, col = lax.axis_index("rows"), lax.axis_index("cols")
    got[...] = mine_ref[...].astype(F32)
    for a, (c, j, at) in enumerate(RELAYS):
        pixel = got[pl.ds(4 * c + j, 16, stride=32), :]
        pixels[16 * a : 16 * a + 16, 0:128] = pltpu.roll(pixel, 128 - at, axis=1) if at else pixel
    spread = (sublane((64, 256)) == lane((64, 256)) % 64).astype(BF)
    pixels[...] = dot(pixels[:, 0:64].astype(BF), spread)
    zero = jnp.zeros((8, 256), F32)

    def kept(flag, v):
        return jnp.where(jnp.full((8, 256), flag.astype(jnp.int32), jnp.int32) > 0, v, zero)

    def spot(k):
        return jnp.broadcast_to(pixels[k : k + 1, :], (8, 256))

    for f in range(FRAMES):
        for y in range(8):
            if y == 0:
                tile, left, right = pixels[24 + 8 * f : 32 + 8 * f, :], spot(93 + f), spot(90 + f)
            elif y == 7:
                tile, left, right = pixels[8 * f : 8 * f + 8, :], spot(87 + f), spot(84 + f)
            else:
                at = 48 * f + 8 * (y - 1)
                tile = outp_ref[at : at + 8, :]
                left, right = spot(66 + 6 * f + y - 1), spot(48 + 6 * f + y - 1)
            tile = shifted(tile, kept(col > 0, left), kept(col < 7, right), (64, 128), 256)
            if y == 0:
                tile = kept(row > 0, tile)
            elif y == 7:
                tile = kept(row < 31, tile)
            tiles[f, y] = tile
    stack_rows(tiles, qs)
    total = jnp.zeros((CELLS, 64), F32)
    for a in range(3):
        for b in range(3):
            rows = qs[2 - b, 48 * (2 - a) : 48 * (2 - a) + CELLS, :]
            total = total + dot(rows[:, 0:192], back_ref[3 * a + b])
    grad_ref[...] = dot(total.astype(BF), utp_ref[...]).astype(BF)

def build_kernel(mine_ref, other_ref, u_ref, ot_ref, take_ref, kind_ref, out_ref, table, half, result, sems):
    gather_table(mine_ref, other_ref, take_ref, kind_ref, table)
    cube = table[...].astype(BF)
    even = dot(cube[:, 0:64], ot_ref[...]).astype(BF)
    odd = dot(cube[:, 64:128], ot_ref[...]).astype(BF)
    for t in range(27):
        half[t, 0:32, :] = even[32 * t : 32 * t + 32]
        half[t, 32:64, :] = odd[32 * t : 32 * t + 32]
    u = u_ref[...]

    def store(a):
        part = pl.ds(3 * a, 3)
        return pltpu.make_async_copy(result.at[part], out_ref.at[part], sems.at[a])

    for a in range(9):
        for t in range(3 * a, 3 * a + 3):
            result[t] = dot(u, half[t]).astype(BF)
        store(a).start()
    for a in range(9):
        store(a).wait()


def call(kernel, args, outs, scratch, flops=10**7):
    def spec(far):
        return pl.BlockSpec(memory_space=pltpu.HBM if far else pltpu.VMEM)

    return pl.pallas_call(
        kernel,
        out_shape=[jax.ShapeDtypeStruct(shape, dtype) for shape, dtype, _ in outs],
        in_specs=[spec(far) for _, far in args],
        out_specs=[spec(far) for _, _, far in outs],
        scratch_shapes=scratch,
        compiler_params=pltpu.CompilerParams(vmem_limit_bytes=32 << 20),
        cost_estimate=pl.CostEstimate(flops=flops, bytes_accessed=10**5, transcendentals=0),
    )(*[pltpu.with_memory_space_constraint(arg, pltpu.HBM) if far else arg for arg, far in args])


def near(*args):
    return [(arg, False) for arg in args]


def far(*args):
    return [(arg, True) for arg in args]


def swap(one, two, axis):
    count = lax.axis_size(axis)
    pairs = [[(i, i + 1) for i in range(k, count - 1, 2)] for k in range(2)]
    two, one = (
        lax.ppermute(x, axis, forward + [(b, a) for a, b in forward]) for x, forward in ((two, pairs[1]), (one, pairs[0]))
    )
    return one, two


def device(k, chip, col):
    return 8 * (2 * chip + k) + col


ORDER = [[device(k, chip, col) for chip in range(16) for col in range(8)] for k in range(2)]


def exchange(x):
    return lax.all_to_all(x, AXES, 0, 0, tiled=True, axis_index_groups=ORDER)


def in_chip(x):
    return lax.ppermute(x, "rows", [(r, r ^ 1) for r in range(32)])


def body(frames_in, cotangent, core, moment_one, moment_two, u_in, u_out):
    take, give, kind = ring_tables()
    take, give, kind = jnp.asarray(take, BF), jnp.asarray(give, BF), jnp.asarray(kind, F32)
    vm, dma = pltpu.VMEM, pltpu.SemaphoreType.DMA
    side = (FRAMES * ROWS, 256)
    rim = (FRAMES * 16, 256)

    send, one, two, inner = call(
        start_kernel,
        far(core, frames_in),
        [((512, 128), BF, True), (side, BF, False), (side, BF, False), ((FRAMES, ROWS, COLS, 256), BF, False)],
        [vm((OWN,), F32), vm((8, 128), F32), vm((128, 128), BF), vm(side, F32), vm(side, F32), dma((6,))],
    )
    one, two = swap(one, two, "cols")
    mine = exchange(send)
    left, right, one, two = call(
        rows_kernel,
        near(inner, two, one),
        [(side, F32, False), (side, F32, False), (rim, BF, False), (rim, BF, False)],
        [vm(rim, F32), vm(rim, F32)],
        flops=10**10,
    )
    own, wide, utp, u, ring, ot, cot, take, give, kind = call(
        fetch_kernel,
        near(left, inner.reshape(CELLS, 256)) + far(
            u_in.T, u_out.T, cotangent.reshape(CELLS, 256), core, moment_one, moment_two, take, give, kind,
        ),
        [
            ((CELLS, 256), F32, False), ((256, 256), BF, False), ((64, 256), BF, False), ((256, 64), BF, False),
            ((3, 4, 128), F32, False), ((64, 256), BF, False), ((CELLS, 256), BF, False),
            ((216, 512), BF, False), ((2, 256, 216), BF, False), ((256, 128), F32, False),
        ],
        [
            vm((64, 256), BF), [vm((OWN,), F32) for _ in range(3)], vm((8, 128), F32),
            dma((9,)),
        ],
        flops=10000000000,
    )
    mine, _ = lax.optimization_barrier((mine, ring))
    other = in_chip(mine)
    one, two = swap(one, two, "rows")
    (q,) = call(
        rank_kernel,
        near(own, wide, two, one, left, right),
        [((3, 240, 256), BF, False)],
        [vm((FRAMES, 8, 8, 256), F32), vm((2, 18, 256), F32), vm((2, 48, 256), F32)],
        flops=10000000000,
    )
    send, grads, pixels, table, outp = call(
        forward_kernel,
        near(mine, other, q, cot, ot, take, give, kind),
        [
            ((512, 128), BF, False), ((TABLE, 128), F32, False), ((96, 128), F32, False), ((TABLE, 128), BF, False),
            ((CELLS, 256), F32, False),
        ],
        [vm((TABLE, 128), F32), vm((CELLS, 128), F32), vm((512, 128), F32)],
    )
    got = in_chip(send)
    (keep,) = call(keep_kernel, near(grads, pixels, give, kind), [((512, 128), F32, False)], [], flops=10**9)
    (send,) = call(add_kernel, near(keep, got), [((512, 128), BF, False)], [])
    got = exchange(send)
    send, latest = call(
        adam_kernel,
        near(got, ring),
        [((512, 128), BF, False), ((3, 4, 128), F32, False)],
        [vm((592, 128), F32)],
    )
    mine = exchange(send)
    (back,) = call(turn_kernel, near(table), [((9, 192, 64), BF, False)], [])
    core_next, one_next, two_next = call(flat_kernel, near(latest), [((OWN,), F32, False)] * 3, [])
    mine, back, core_next, one_next, two_next = lax.optimization_barrier((mine, back, core_next, one_next, two_next))
    other = in_chip(mine)
    (frames_grad,) = call(
        backward_kernel,
        near(mine, outp, back, utp),
        [((CELLS, 256), BF, False)],
        [vm((512, 128), F32), vm((96, 256), F32), vm((FRAMES, 8, 8, 256), F32), vm((3, 240, 256), BF)],
        flops=10**9,
    )
    other, frames_grad = lax.optimization_barrier((other, frames_grad))
    (kernel_next,) = call(
        build_kernel,
        near(mine, other, u, ot, take, kind),
        [((27, 256, 256), BF, True)],
        [vm((TABLE, 128), F32), vm((27, 64, 256), BF), vm((27, 256, 256), BF), dma((9,))],
    )
    frames_grad = frames_grad.reshape(FRAMES, ROWS, COLS, 256)
    return frames_grad, core_next, one_next, two_next, kernel_next


def solution(mesh):
    in_specs = (
        P(None, "rows", "cols", None),
        P(None, "rows", "cols", None),
        P(AXES),
        P(AXES),
        P(AXES),
        P(),
        P(),
    )
    out_specs = (
        P(None, "rows", "cols", None),
        P(AXES),
        P(AXES),
        P(AXES),
        P(),
    )
    return jax.shard_map(body, mesh=mesh, in_specs=in_specs, out_specs=out_specs, check_vma=False)
```

```python
import jax
import jax.numpy as jnp
import numpy as np
from jax import lax
from jax.experimental import pallas as pl
from jax.experimental.pallas import tpu as pltpu
from jax.sharding import PartitionSpec as P

beta_one = 0.9
beta_two = 0.999
learn_rate = 0.06
epsilon = 1e-08
fix_one = 1.0 - 0.9**10
fix_two = 1.0 - 0.999**10

BF = jnp.bfloat16
F32 = jnp.float32
AXES = ("rows", "cols")

OWN = 432
FRAMES, ROWS, COLS = 3, 6, 8
CELLS = FRAMES * ROWS * COLS
SIDE = FRAMES * 8
TABLE = 864


RELAYS = ((7, 0, 0), (4, 0, 0), (3, 3, 64), (0, 3, 64), (2, 0, 16), (5, 0, 32))
SLOTS = (
    (0, 24, -1, 0), (24, 24, 1, 0), (48, 18, 0, -1), (66, 18, 0, 1),
    (84, 3, -1, -1), (87, 3, -1, 1), (90, 3, 1, -1), (93, 3, 1, 1),
)


def ring_tables():
    take = np.zeros((216, 512), np.float32)
    give = np.zeros((2, 256, 216), np.float32)
    kind = np.zeros((256, 128), np.float32)
    for r in range(8):
        for c in range(8):
            first = 27 * r + 27 * c // 8
            col = 128 * (r % 2) + 32 * (r // 2) + 4 * c
            for j in range(4):
                take[first + j, col + j] = 1
                give[r % 2, col % 128 + j, first + j] = 1
            wrapped = 48 * c % 128 + OWN - 512
            if wrapped > 0:
                take[first + 4, 256 + col] = 1
                give[r % 2, 128 + col % 128, first + 4] = 1
                kind[col, :wrapped] = 1
        for c, j, at in RELAYS:
            kind[128 * (r % 2) + 32 * (r // 2) + 4 * c + j, at : at + 64] = 2
    return take, give, kind


def dot(a, b):
    return jnp.dot(a, b, preferred_element_type=F32)


def dot_nt(a, b):
    return lax.dot_general(a, b, (((1,), (1,)), ((), ())), preferred_element_type=F32)


def dot_tn(a, b):
    return lax.dot_general(a, b, (((0,), (0,)), ((), ())), preferred_element_type=F32)


def lane(shape):
    return lax.broadcasted_iota(jnp.int32, shape, 1)


def sublane(shape):
    return lax.broadcasted_iota(jnp.int32, shape, 0)


def ring_shift():
    return lax.rem(lax.axis_index("cols") * 48, 128)


def to_ring(v, shift):
    turned = pltpu.roll(v, shift, axis=1)
    above = jnp.concatenate([turned[3:4], turned[0:3]], axis=0)
    return jnp.where(lane(v.shape) >= shift, turned, above)


def from_ring(v, shift):
    turned = pltpu.roll(v, lax.rem(128 - shift, 128), axis=1)
    below = jnp.concatenate([turned[1:4], turned[0:1]], axis=0)
    return jnp.where(lane(v.shape) < 128 - shift, turned, below)


def in_ring(shift):
    place = sublane((4, 128)) * 128 + lane((4, 128)) - shift
    place = jnp.where(place < 0, place + 512, place)
    return place < OWN


def load_flat(ref, scratch):
    scratch[...] = jnp.zeros_like(scratch)
    for k in range(3):
        scratch[k, :] = ref[pl.ds(128 * k, 128)]
    scratch[3, 0 : OWN - 384] = ref[pl.ds(384, OWN - 384)]
    return scratch[0:4, :]


def store_flat(ref, v):
    for k in range(3):
        ref[pl.ds(128 * k, 128)] = v[k]
    ref[pl.ds(384, OWN - 384)] = v[3, 0 : OWN - 384]


def fetch(pairs, sems):
    copies = [pltpu.make_async_copy(src, dst, sems.at[k]) for k, (src, dst) in enumerate(pairs)]
    for copy in copies:
        copy.start()
    return copies


def even_first(axis, first, last):
    even = jnp.full(first.shape, lax.rem(lax.axis_index(axis), 2), jnp.int32) == 0
    return jnp.where(even, last, first), jnp.where(even, first, last)


def start_kernel(
    core_ref, x_ref, one_ref, two_ref, ut_ref, ot_ref, cot_ref, take_ref, give_ref, kind_ref,
    send_ref, near_ref, far_ref, inner_ref, ring_ref, one_out, two_out, ut_out, ot_out, cot_out, take_out, give_out, kind_out,
    own, flat, block, low, high, sems,
):
    copies = fetch(
        (
            (core_ref, own), (x_ref, inner_ref), (one_ref, one_out), (two_ref, two_out), (ut_ref, ut_out),
            (ot_ref, ot_out), (take_ref, take_out), (kind_ref, kind_out), (give_ref, give_out), (cot_ref, cot_out),
        ),
        sems,
    )
    copies[0].wait()
    v = to_ring(load_flat(own, flat), ring_shift())
    ring_ref[...] = v
    rows = jnp.concatenate([v, v, v, v], axis=0).astype(BF)
    for k in range(8):
        block[16 * k : 16 * k + 16, :] = rows
    sends = fetch([(block, send_ref.at[pl.ds(128 * k, 128)]) for k in range(4)], sems.at[pl.ds(10, 4)])
    copies[1].wait()
    for f in range(FRAMES):
        for y in range(ROWS):
            tile = inner_ref[f, y].astype(F32)
            k = ROWS * f + y
            low[k : k + 1, :] = tile[0:1, :]
            high[k : k + 1, :] = tile[7:8, :]
    one, two = even_first("cols", low[...], high[...])
    near_ref[...] = one.astype(BF)
    far_ref[...] = two.astype(BF)
    for copy in copies[2:] + sends:
        copy.wait()


def rows_kernel(inner_ref, two_ref, one_ref, left_ref, right_ref, up_ref, down_ref, first, last):
    right, left = even_first("cols", two_ref[...].astype(F32), one_ref[...].astype(F32))
    left_ref[...] = left
    right_ref[...] = right
    first[...] = jnp.zeros_like(first)
    last[...] = jnp.zeros_like(last)
    for f in range(FRAMES):
        for y, rows in ((0, first), (ROWS - 1, last)):
            k = ROWS * f + y
            rows[16 * f : 16 * f + 8, :] = inner_ref[f, y].astype(F32)
            rows[16 * f + 8 : 16 * f + 9, :] = left_ref[k : k + 1, :]
            rows[16 * f + 9 : 16 * f + 10, :] = right_ref[k : k + 1, :]
    one, two = even_first("rows", first[...], last[...])
    up_ref[...] = one.astype(BF)
    down_ref[...] = two.astype(BF)


def shifted(tile, left, right, bounds, period):
    at = lane(tile.shape) % period
    row = sublane(tile.shape)
    back = jnp.where(row == 0, left, pltpu.roll(tile, 1, axis=0))
    ahead = jnp.where(row == 7, right, pltpu.roll(tile, 7, axis=0))
    return jnp.where(at < bounds[0], back, jnp.where(at < bounds[1], tile, ahead))


def prepare_kernel(_, x_ref, ut_ref, one_ref, two_ref, own_ref, wide_ref, utp_ref, u_ref, ring_ref, flat):
    row = sublane((256, 64))
    at = row % 128
    pick = (lane((256, 64)) == (at % 32) * 2 + row // 128) & (at < 96)
    half_row = sublane((64, 64))
    half_pick = lane((64, 64)) == (half_row % 32) * 2 + half_row // 32
    wide = dot(pick.astype(BF), ut_ref[...]).astype(BF)
    wide_ref[...] = wide
    utp = dot(half_pick.astype(BF), ut_ref[...])
    utp_ref[...] = utp.astype(BF)
    u_ref[...] = utp.T.astype(BF)
    own_ref[...] = dot_nt(x_ref[...], wide).astype(BF).astype(F32)
    shift = ring_shift()
    ring_ref[0] = to_ring(load_flat(one_ref, flat), shift)
    ring_ref[1] = to_ring(load_flat(two_ref, flat), shift)


def stack_rows(tiles, out_ref):
    for b in range(3):
        out_ref[b, 0:48, :] = jnp.zeros((48, 256), BF)
        out_ref[b, 192:240, :] = jnp.zeros((48, 256), BF)
        for f in range(FRAMES):
            rows = tiles[f, b : b + ROWS].reshape(48, 256)
            out_ref[b, 48 * f + 48 : 48 * f + 96, :] = rows.astype(BF)


def rank_kernel(_, own_ref, wide_ref, two_ref, one_ref, left_ref, right_ref, q_ref, tiles, edge, rims):
    wide = wide_ref[...]

    def project(v):
        return dot_nt(v.astype(BF), wide).astype(BF).astype(F32)

    below, above = even_first("rows", project(two_ref[...]), project(one_ref[...]))
    rims[0] = above
    rims[1] = below
    edge[0] = project(left_ref[...])
    edge[1] = project(right_ref[...])
    for f in range(FRAMES):
        for y in range(8):
            if y in (0, 7):
                rim = rims.at[y // 7]
                at = 16 * f
                tile, left, right = rim[at : at + 8, :], rim[at + 8 : at + 9, :], rim[at + 9 : at + 10, :]
            else:
                k = ROWS * f + y - 1
                tile = own_ref[8 * k : 8 * k + 8, :]
                left, right = edge[0, k : k + 1, :], edge[1, k : k + 1, :]
            left = jnp.broadcast_to(left, (8, 256))
            right = jnp.broadcast_to(right, (8, 256))
            tiles[f, y] = shifted(tile, left, right, (32, 64), 128)
    stack_rows(tiles, q_ref)


def core_index(shape):
    return jnp.full(shape, lax.rem(lax.axis_index("rows"), 2), jnp.int32)


def gather_table(mine_ref, other_ref, take_ref, kind_ref, table_ref):
    kind = kind_ref[...]
    take = take_ref[...]
    first = core_index((128, 128)) == 0
    for g in range(4):
        mine, other = mine_ref[128 * g : 128 * g + 128, :], other_ref[128 * g : 128 * g + 128, :]
        block = jnp.concatenate([jnp.where(first, mine, other), jnp.where(first, other, mine)], axis=0)
        none = jnp.zeros_like(block)
        both = jnp.concatenate(
            [jnp.where(kind == 0, block, none), jnp.where(kind == 1, block, none)], axis=0
        )
        table_ref[216 * g : 216 * g + 216, :] = dot(take, both)


def inside(lanes, at):
    return (lanes >= at) & (lanes < at + 64)


def gradient_blocks(half, grads, pixels, give_ref, kind_ref, blocks):
    wrapped = kind_ref[0:128, :] == 1
    for g in range(4):
        source = grads[216 * g : 216 * g + 216, :].astype(BF)
        part = dot(give_ref[half], source)
        blocks[128 * g : 128 * g + 128, :] = jnp.where(wrapped, part[128:256], part[0:128])
    lanes = lane((16, 128))
    row = lax.axis_index("rows")
    for a, (c, j, at) in enumerate(RELAYS):
        slot = sublane((16, 128)) + 16 * a
        across = ((slot < 48) | (slot >= 84)).astype(jnp.int32)
        goes = lax.rem(jnp.full((16, 128), row + half, jnp.int32) + across, 2) == 0
        pixel = jnp.where(goes, pixels[16 * a : 16 * a + 16, :], 0.0)
        if at % 64:
            pixel = pltpu.roll(pixel, at, axis=1)
        spot = pl.ds(4 * c + j, 16, stride=32)
        blocks[spot, :] = jnp.where(inside(lanes, at), pixel, blocks[spot, :])


def table_kernel(mine_ref, other_ref, take_ref, kind_ref, table_out, table):
    gather_table(mine_ref, other_ref, take_ref, kind_ref, table)
    table_out[...] = table[...].astype(BF)


def forward_kernel(
    table_ref, q_ref, cot_ref, ot_ref, give_ref, kind_ref, send_ref, grads, pixels, outp_ref, border, blocks
):
    even = jnp.zeros((CELLS, 128), F32)
    odd = jnp.zeros((CELLS, 128), F32)
    for a in range(3):
        for b in range(3):
            k = 3 * a + b
            weights = table_ref[96 * k : 96 * k + 96, :]
            rows = q_ref[b, 48 * a : 48 * a + CELLS, :]
            even = even + dot(rows[:, 0:96], weights)
            odd = odd + dot(rows[:, 128:224], weights)
    mid = (even[:, 0:64] + odd[:, 64:128]).astype(BF)
    pre = dot(mid, ot_ref[...])
    sig = jax.nn.sigmoid(pre)
    slope = (cot_ref[...].astype(F32) * sig * (1.0 + pre * (1.0 - sig))).astype(BF)
    ot = ot_ref[...]
    out_t = dot_nt(ot, slope).astype(BF)
    wide = jnp.concatenate([ot, ot, ot, ot], axis=0)
    outp = dot_nt(slope, wide).astype(BF).astype(F32)
    outp_ref[...] = outp
    border[...] = outp[:, 0:128]
    for f in range(FRAMES):
        pixels[8 * f : 8 * f + 8, :] = border[48 * f : 48 * f + 8, :]
        pixels[24 + 8 * f : 32 + 8 * f, :] = border[48 * f + 40 : 48 * f + 48, :]
    pixels[48:66, :] = border[pl.ds(0, 18, stride=8), :]
    pixels[66:84, :] = border[pl.ds(7, 18, stride=8), :]
    for k, cell in enumerate((0, 7, 40, 47)):
        pixels[84 + 3 * k : 87 + 3 * k, :] = border[pl.ds(cell, 3, stride=48), :]
    for a in range(3):
        for b in range(3):
            k = 3 * a + b
            part = dot(out_t, q_ref[b, 48 * a : 48 * a + CELLS, :])
            stack = jnp.concatenate([part[:, 0:128], part[:, 128:256]], axis=0)
            grads[96 * k : 96 * k + 96, :] = stack.T[0:96, :]
    gradient_blocks(1 - lax.rem(lax.axis_index("rows"), 2), grads, pixels, give_ref, kind_ref, blocks)
    send_ref[...] = blocks[...].astype(BF)


def keep_kernel(grads, pixels, give_ref, kind_ref, keep_ref):
    gradient_blocks(lax.rem(lax.axis_index("rows"), 2), grads, pixels, give_ref, kind_ref, keep_ref)


def add_kernel(keep_ref, got_ref, send_ref):
    send_ref[...] = (keep_ref[...] + got_ref[...].astype(F32)).astype(BF)


def adam_kernel(got_ref, core_ref, ring_ref, send_ref, next_ref, passed):
    total = jnp.zeros((8, 128), F32)
    passed[0:40, :] = jnp.zeros((40, 128), F32)
    passed[552:592, :] = jnp.zeros((40, 128), F32)
    for g in range(4):
        part = got_ref[128 * g : 128 * g + 128, :].astype(F32)
        passed[128 * g + 40 : 128 * g + 168, :] = part
        total = total + part.reshape(16, 8, 128).sum(axis=0)
    grad = (total[0:4] + total[4:8]) * (1.0 / 192.0)
    core, one, two = core_ref[...], ring_ref[0], ring_ref[1]
    one = beta_one * one + (1.0 - beta_one) * grad
    two = beta_two * two + (1.0 - beta_two) * grad * grad
    core = core - learn_rate * (one / fix_one) / (jnp.sqrt(two / fix_two) + epsilon)
    next_ref[0] = core
    next_ref[1] = one
    next_ref[2] = two
    own = jnp.where(in_ring(ring_shift()), core, 0.0)
    own = jnp.concatenate([own, own], axis=0)
    row, col = lax.axis_index("rows"), lax.axis_index("cols")
    slot, parity, mask = lax.div(row, 2), lax.rem(row, 2), jnp.zeros((8, 128), jnp.bool_)
    for a, (c, j, at) in enumerate(RELAYS):
        slot = slot + jnp.where(col == c, 16 * a, 0)
        spot = (sublane((8, 128)) % 4 == j) & inside(lane((8, 128)), at)
        mask = mask | (spot & (jnp.full((8, 128), col, jnp.int32) == c))
    up, right = 0, 0
    for first, count, rows, cols in SLOTS:
        here = (slot >= first) & (slot < first + count)
        up = up + jnp.where(here, rows, 0)
        right = right + jnp.where(here, cols, 0)
    source = lax.rem(parity - up + 2, 2)
    chips = lax.div(source + up - parity + 2, 2) - 1
    start = 40 - 4 * (8 * chips + right)
    for k in range(32):
        upper = passed[pl.ds(start + 16 * k, 8), :]
        lower = passed[pl.ds(start + 16 * k + 8, 8), :]
        block = jnp.concatenate([jnp.where(mask, upper, own), jnp.where(mask, lower, own)], axis=0)
        send_ref[16 * k : 16 * k + 16, :] = block.astype(BF)


def flat_kernel(next_ref, core_ref, one_ref, two_ref):
    shift = ring_shift()
    for k, ref in enumerate((core_ref, one_ref, two_ref)):
        store_flat(ref, from_ring(next_ref[k], shift))


def turn_kernel(table_ref, back_ref):
    for k in range(9):
        for c in range(3):
            t = 3 * k + c
            part = table_ref[32 * t : 32 * t + 32, :].astype(F32).T
            cube = jnp.concatenate([part[0:64], part[64:128]], axis=1)
            back_ref[k, 64 * (2 - c) : 64 * (2 - c) + 64, :] = cube.astype(BF)


def backward_kernel(mine_ref, outp_ref, back_ref, utp_ref, grad_ref, got, pixels, tiles, qs):
    row, col = lax.axis_index("rows"), lax.axis_index("cols")
    got[...] = mine_ref[...].astype(F32)
    for a, (c, j, at) in enumerate(RELAYS):
        pixel = got[pl.ds(4 * c + j, 16, stride=32), :]
        pixels[16 * a : 16 * a + 16, 0:128] = pltpu.roll(pixel, 128 - at, axis=1) if at else pixel
    spread = (sublane((64, 256)) == lane((64, 256)) % 64).astype(BF)
    pixels[...] = dot(pixels[:, 0:64].astype(BF), spread)
    zero = jnp.zeros((8, 256), F32)

    def kept(flag, v):
        return jnp.where(jnp.full((8, 256), flag.astype(jnp.int32), jnp.int32) > 0, v, zero)

    def spot(k):
        return jnp.broadcast_to(pixels[k : k + 1, :], (8, 256))

    for f in range(FRAMES):
        for y in range(8):
            if y == 0:
                tile, left, right = pixels[24 + 8 * f : 32 + 8 * f, :], spot(93 + f), spot(90 + f)
            elif y == 7:
                tile, left, right = pixels[8 * f : 8 * f + 8, :], spot(87 + f), spot(84 + f)
            else:
                at = 48 * f + 8 * (y - 1)
                tile = outp_ref[at : at + 8, :]
                left, right = spot(66 + 6 * f + y - 1), spot(48 + 6 * f + y - 1)
            tile = shifted(tile, kept(col > 0, left), kept(col < 7, right), (64, 128), 256)
            if y == 0:
                tile = kept(row > 0, tile)
            elif y == 7:
                tile = kept(row < 31, tile)
            tiles[f, y] = tile
    stack_rows(tiles, qs)
    total = jnp.zeros((CELLS, 64), F32)
    for a in range(3):
        for b in range(3):
            rows = qs[2 - b, 48 * (2 - a) : 48 * (2 - a) + CELLS, :]
            total = total + dot(rows[:, 0:192], back_ref[3 * a + b])
    grad_ref[...] = dot(total.astype(BF), utp_ref[...]).astype(BF)

def build_kernel(mine_ref, other_ref, u_ref, ot_ref, take_ref, kind_ref, out_ref, table, half, result, sems):
    gather_table(mine_ref, other_ref, take_ref, kind_ref, table)
    cube = table[...].astype(BF)
    even = dot(cube[:, 0:64], ot_ref[...]).astype(BF)
    odd = dot(cube[:, 64:128], ot_ref[...]).astype(BF)
    for t in range(27):
        half[t, 0:32, :] = even[32 * t : 32 * t + 32]
        half[t, 32:64, :] = odd[32 * t : 32 * t + 32]
    u = u_ref[...]

    def store(a):
        part = pl.ds(3 * a, 3)
        return pltpu.make_async_copy(result.at[part], out_ref.at[part], sems.at[a])

    for a in range(9):
        for t in range(3 * a, 3 * a + 3):
            result[t] = dot(u, half[t]).astype(BF)
        store(a).start()
    for a in range(9):
        store(a).wait()


def call(kernel, args, outs, scratch, flops=10**7):
    def spec(far):
        return pl.BlockSpec(memory_space=pltpu.HBM if far else pltpu.VMEM)

    return pl.pallas_call(
        kernel,
        out_shape=[jax.ShapeDtypeStruct(shape, dtype) for shape, dtype, _ in outs],
        in_specs=[spec(far) for _, far in args],
        out_specs=[spec(far) for _, _, far in outs],
        scratch_shapes=scratch,
        compiler_params=pltpu.CompilerParams(vmem_limit_bytes=32 << 20),
        cost_estimate=pl.CostEstimate(flops=flops, bytes_accessed=10**5, transcendentals=0),
    )(*[pltpu.with_memory_space_constraint(arg, pltpu.HBM) if far else arg for arg, far in args])


def near(*args):
    return [(arg, False) for arg in args]


def far(*args):
    return [(arg, True) for arg in args]


def swap(one, two, axis):
    count = lax.axis_size(axis)
    pairs = [[(i, i + 1) for i in range(k, count - 1, 2)] for k in range(2)]
    two, one = (
        lax.ppermute(x, axis, forward + [(b, a) for a, b in forward]) for x, forward in ((two, pairs[1]), (one, pairs[0]))
    )
    return one, two


def device(k, chip, col):
    return 8 * (2 * chip + k) + col


ORDER = [[device(k, chip, col) for chip in range(16) for col in range(8)] for k in range(2)]


def exchange(x):
    return lax.all_to_all(x, AXES, 0, 0, tiled=True, axis_index_groups=ORDER)


def in_chip(x):
    return lax.ppermute(x, "rows", [(r, r ^ 1) for r in range(32)])


def body(frames_in, cotangent, core, moment_one, moment_two, u_in, u_out):
    take, give, kind = ring_tables()
    take, give, kind = jnp.asarray(take, BF), jnp.asarray(give, BF), jnp.asarray(kind, F32)
    vm, dma = pltpu.VMEM, pltpu.SemaphoreType.DMA
    side = (FRAMES * ROWS, 256)
    rim = (FRAMES * 16, 256)

    send, one, two, inner, core_ring, m_one, m_two, ut, ot, cot, take, give, kind = call(
        start_kernel,
        far(
            core, frames_in, moment_one, moment_two, u_in.T, u_out.T, cotangent.reshape(CELLS, 256), take, give, kind,
        ),
        [
            ((512, 128), BF, True), (side, BF, False), (side, BF, False), ((FRAMES, ROWS, COLS, 256), BF, False),
            ((4, 128), F32, False), ((OWN,), F32, False), ((OWN,), F32, False), ((64, 256), BF, False),
            ((64, 256), BF, False), ((CELLS, 256), BF, False), ((216, 512), BF, False), ((2, 256, 216), BF, False),
            ((256, 128), F32, False),
        ],
        [vm((OWN,), F32), vm((8, 128), F32), vm((128, 128), BF), vm(side, F32), vm(side, F32), dma((14,))],
    )
    one, two = swap(one, two, "cols")
    mine = exchange(send)
    left, right, one, two = call(
        rows_kernel,
        near(inner, two, one),
        [(side, F32, False), (side, F32, False), (rim, BF, False), (rim, BF, False)],
        [vm(rim, F32), vm(rim, F32)],
        flops=10**10,
    )
    own, wide, utp, u, ring = call(
        prepare_kernel,
        near(left, inner.reshape(CELLS, 256), ut, m_one, m_two),
        [
            ((CELLS, 256), F32, False), ((256, 256), BF, False), ((64, 256), BF, False), ((256, 64), BF, False),
            ((2, 4, 128), F32, False),
        ],
        [vm((8, 128), F32)],
        flops=10**10,
    )
    mine, _ = lax.optimization_barrier((mine, left))
    other = in_chip(mine)
    (table,) = call(
        table_kernel,
        near(mine, other, take, kind),
        [((TABLE, 128), BF, False)],
        [vm((TABLE, 128), F32)],
        flops=10000000000,
    )
    one, two = swap(one, two, "rows")
    (q,) = call(
        rank_kernel,
        near(table, own, wide, two, one, left, right),
        [((3, 240, 256), BF, False)],
        [vm((FRAMES, 8, 8, 256), F32), vm((2, 18, 256), F32), vm((2, 48, 256), F32)],
        flops=10000000,
    )
    send, grads, pixels, outp = call(
        forward_kernel,
        near(table, q, cot, ot, give, kind),
        [((512, 128), BF, False), ((TABLE, 128), F32, False), ((96, 128), F32, False), ((CELLS, 256), F32, False)],
        [vm((CELLS, 128), F32), vm((512, 128), F32)],
    )
    got = in_chip(send)
    (keep,) = call(keep_kernel, near(grads, pixels, give, kind), [((512, 128), F32, False)], [], flops=10**9)
    (send,) = call(add_kernel, near(keep, got), [((512, 128), BF, False)], [])
    got = exchange(send)
    send, latest = call(
        adam_kernel,
        near(got, core_ring, ring),
        [((512, 128), BF, False), ((3, 4, 128), F32, False)],
        [vm((592, 128), F32)],
    )
    mine = exchange(send)
    (back,) = call(turn_kernel, near(table), [((9, 192, 64), BF, False)], [])
    core_next, one_next, two_next = call(flat_kernel, near(latest), [((OWN,), F32, False)] * 3, [])
    mine, back, core_next, one_next, two_next = lax.optimization_barrier((mine, back, core_next, one_next, two_next))
    other = in_chip(mine)
    (frames_grad,) = call(
        backward_kernel,
        near(mine, outp, back, utp),
        [((CELLS, 256), BF, False)],
        [vm((512, 128), F32), vm((96, 256), F32), vm((FRAMES, 8, 8, 256), F32), vm((3, 240, 256), BF)],
        flops=10**9,
    )
    other, frames_grad = lax.optimization_barrier((other, frames_grad))
    (kernel_next,) = call(
        build_kernel,
        near(mine, other, u, ot, take, kind),
        [((27, 256, 256), BF, True)],
        [vm((TABLE, 128), F32), vm((27, 64, 256), BF), vm((27, 256, 256), BF), dma((9,))],
    )
    frames_grad = frames_grad.reshape(FRAMES, ROWS, COLS, 256)
    return frames_grad, core_next, one_next, two_next, kernel_next


def solution(mesh):
    in_specs = (
        P(None, "rows", "cols", None),
        P(None, "rows", "cols", None),
        P(AXES),
        P(AXES),
        P(AXES),
        P(),
        P(),
    )
    out_specs = (
        P(None, "rows", "cols", None),
        P(AXES),
        P(AXES),
        P(AXES),
        P(),
    )
    return jax.shard_map(body, mesh=mesh, in_specs=in_specs, out_specs=out_specs, check_vma=False)
```

```python
import jax
import jax.numpy as jnp
import numpy as np
from jax import lax
from jax.experimental import pallas as pl
from jax.experimental.pallas import tpu as pltpu
from jax.sharding import PartitionSpec as P

beta_one = 0.9
beta_two = 0.999
learn_rate = 0.06
epsilon = 1e-08
fix_one = 1.0 - 0.9**10
fix_two = 1.0 - 0.999**10

BF = jnp.bfloat16
F32 = jnp.float32
AXES = ("rows", "cols")

OWN = 432
FRAMES, ROWS, COLS = 3, 6, 8
CELLS = FRAMES * ROWS * COLS
SIDE = FRAMES * 8
TABLE = 864


RELAYS = ((7, 0, 0), (4, 0, 0), (3, 3, 64), (0, 3, 64), (2, 0, 16), (5, 0, 32))
SLOTS = (
    (0, 24, -1, 0), (24, 24, 1, 0), (48, 18, 0, -1), (66, 18, 0, 1),
    (84, 3, -1, -1), (87, 3, -1, 1), (90, 3, 1, -1), (93, 3, 1, 1),
)


def ring_tables():
    take = np.zeros((216, 512), np.float32)
    give = np.zeros((2, 256, 216), np.float32)
    kind = np.zeros((256, 128), np.float32)
    for r in range(8):
        for c in range(8):
            first = 27 * r + 27 * c // 8
            col = 128 * (r % 2) + 32 * (r // 2) + 4 * c
            for j in range(4):
                take[first + j, col + j] = 1
                give[r % 2, col % 128 + j, first + j] = 1
            wrapped = 48 * c % 128 + OWN - 512
            if wrapped > 0:
                take[first + 4, 256 + col] = 1
                give[r % 2, 128 + col % 128, first + 4] = 1
                kind[col, :wrapped] = 1
        for c, j, at in RELAYS:
            kind[128 * (r % 2) + 32 * (r // 2) + 4 * c + j, at : at + 64] = 2
    return take, give, kind


def dot(a, b):
    return jnp.dot(a, b, preferred_element_type=F32)


def dot_nt(a, b):
    return lax.dot_general(a, b, (((1,), (1,)), ((), ())), preferred_element_type=F32)


def dot_tn(a, b):
    return lax.dot_general(a, b, (((0,), (0,)), ((), ())), preferred_element_type=F32)


def lane(shape):
    return lax.broadcasted_iota(jnp.int32, shape, 1)


def sublane(shape):
    return lax.broadcasted_iota(jnp.int32, shape, 0)


def ring_shift():
    return lax.rem(lax.axis_index("cols") * 48, 128)


def to_ring(v, shift):
    turned = pltpu.roll(v, shift, axis=1)
    above = jnp.concatenate([turned[3:4], turned[0:3]], axis=0)
    return jnp.where(lane(v.shape) >= shift, turned, above)


def from_ring(v, shift):
    turned = pltpu.roll(v, lax.rem(128 - shift, 128), axis=1)
    below = jnp.concatenate([turned[1:4], turned[0:1]], axis=0)
    return jnp.where(lane(v.shape) < 128 - shift, turned, below)


def in_ring(shift):
    place = sublane((4, 128)) * 128 + lane((4, 128)) - shift
    place = jnp.where(place < 0, place + 512, place)
    return place < OWN


def load_flat(ref, scratch):
    scratch[...] = jnp.zeros_like(scratch)
    for k in range(3):
        scratch[k, :] = ref[pl.ds(128 * k, 128)]
    scratch[3, 0 : OWN - 384] = ref[pl.ds(384, OWN - 384)]
    return scratch[0:4, :]


def store_flat(ref, v):
    for k in range(3):
        ref[pl.ds(128 * k, 128)] = v[k]
    ref[pl.ds(384, OWN - 384)] = v[3, 0 : OWN - 384]


def fetch(pairs, sems):
    copies = [pltpu.make_async_copy(src, dst, sems.at[k]) for k, (src, dst) in enumerate(pairs)]
    for copy in copies:
        copy.start()
    return copies


def even_first(axis, first, last):
    even = jnp.full(first.shape, lax.rem(lax.axis_index(axis), 2), jnp.int32) == 0
    return jnp.where(even, last, first), jnp.where(even, first, last)


def start_kernel(
    core_ref, x_ref, one_ref, two_ref, ut_ref, ot_ref, cot_ref, take_ref, give_ref, kind_ref,
    send_ref, near_ref, far_ref, inner_ref, ring_ref, one_out, two_out, ut_out, ot_out, cot_out, take_out, give_out, kind_out,
    own, flat, block, low, high, sems,
):
    copies = fetch(
        (
            (core_ref, own), (x_ref, inner_ref), (one_ref, one_out), (two_ref, two_out), (ut_ref, ut_out),
            (ot_ref, ot_out), (take_ref, take_out), (kind_ref, kind_out), (give_ref, give_out), (cot_ref, cot_out),
        ),
        sems,
    )
    copies[0].wait()
    v = to_ring(load_flat(own, flat), ring_shift())
    ring_ref[...] = v
    rows = jnp.concatenate([v, v, v, v], axis=0).astype(BF)
    for k in range(8):
        block[16 * k : 16 * k + 16, :] = rows
    sends = fetch([(block, send_ref.at[pl.ds(128 * k, 128)]) for k in range(4)], sems.at[pl.ds(10, 4)])
    copies[1].wait()
    for f in range(FRAMES):
        for y in range(ROWS):
            tile = inner_ref[f, y].astype(F32)
            k = ROWS * f + y
            low[k : k + 1, :] = tile[0:1, :]
            high[k : k + 1, :] = tile[7:8, :]
    one, two = even_first("cols", low[...], high[...])
    near_ref[...] = one.astype(BF)
    far_ref[...] = two.astype(BF)
    for copy in copies[2:] + sends:
        copy.wait()


def rows_kernel(inner_ref, two_ref, one_ref, left_ref, right_ref, up_ref, down_ref, first, last):
    right, left = even_first("cols", two_ref[...].astype(F32), one_ref[...].astype(F32))
    left_ref[...] = left
    right_ref[...] = right
    first[...] = jnp.zeros_like(first)
    last[...] = jnp.zeros_like(last)
    for f in range(FRAMES):
        for y, rows in ((0, first), (ROWS - 1, last)):
            k = ROWS * f + y
            rows[16 * f : 16 * f + 8, :] = inner_ref[f, y].astype(F32)
            rows[16 * f + 8 : 16 * f + 9, :] = left_ref[k : k + 1, :]
            rows[16 * f + 9 : 16 * f + 10, :] = right_ref[k : k + 1, :]
    one, two = even_first("rows", first[...], last[...])
    up_ref[...] = one.astype(BF)
    down_ref[...] = two.astype(BF)


def shifted(tile, left, right, bounds, period):
    at = lane(tile.shape) % period
    row = sublane(tile.shape)
    back = jnp.where(row == 0, left, pltpu.roll(tile, 1, axis=0))
    ahead = jnp.where(row == 7, right, pltpu.roll(tile, 7, axis=0))
    return jnp.where(at < bounds[0], back, jnp.where(at < bounds[1], tile, ahead))


def prepare_kernel(_, x_ref, ut_ref, one_ref, two_ref, own_ref, wide_ref, utp_ref, u_ref, ring_ref, flat):
    row = sublane((256, 64))
    at = row % 128
    pick = (lane((256, 64)) == (at % 32) * 2 + row // 128) & (at < 96)
    half_row = sublane((64, 64))
    half_pick = lane((64, 64)) == (half_row % 32) * 2 + half_row // 32
    wide = dot(pick.astype(BF), ut_ref[...]).astype(BF)
    wide_ref[...] = wide
    utp = dot(half_pick.astype(BF), ut_ref[...])
    utp_ref[...] = utp.astype(BF)
    u_ref[...] = utp.T.astype(BF)
    own_ref[...] = dot_nt(x_ref[...], wide).astype(BF).astype(F32)
    shift = ring_shift()
    ring_ref[0] = to_ring(load_flat(one_ref, flat), shift)
    ring_ref[1] = to_ring(load_flat(two_ref, flat), shift)


def stack_rows(tiles, out_ref):
    for b in range(3):
        out_ref[b, 0:48, :] = jnp.zeros((48, 256), BF)
        out_ref[b, 192:240, :] = jnp.zeros((48, 256), BF)
        for f in range(FRAMES):
            rows = tiles[f, b : b + ROWS].reshape(48, 256)
            out_ref[b, 48 * f + 48 : 48 * f + 96, :] = rows.astype(BF)


def rank_kernel(_, own_ref, wide_ref, two_ref, one_ref, left_ref, right_ref, q_ref, tiles, edge, rims):
    wide = wide_ref[...]

    def project(v):
        return dot_nt(v.astype(BF), wide).astype(BF).astype(F32)

    below, above = even_first("rows", project(two_ref[...]), project(one_ref[...]))
    rims[0] = above
    rims[1] = below
    edge[0] = project(left_ref[...])
    edge[1] = project(right_ref[...])
    for f in range(FRAMES):
        for y in range(8):
            if y in (0, 7):
                rim = rims.at[y // 7]
                at = 16 * f
                tile, left, right = rim[at : at + 8, :], rim[at + 8 : at + 9, :], rim[at + 9 : at + 10, :]
            else:
                k = ROWS * f + y - 1
                tile = own_ref[8 * k : 8 * k + 8, :]
                left, right = edge[0, k : k + 1, :], edge[1, k : k + 1, :]
            left = jnp.broadcast_to(left, (8, 256))
            right = jnp.broadcast_to(right, (8, 256))
            tiles[f, y] = shifted(tile, left, right, (32, 64), 128)
    stack_rows(tiles, q_ref)


def core_index(shape):
    return jnp.full(shape, lax.rem(lax.axis_index("rows"), 2), jnp.int32)


def gather_rows(g, mine_ref, other_ref, take_ref, kind_ref, table_ref):
    kind = kind_ref[...]
    first = core_index((128, 128)) == 0
    mine, other = mine_ref[128 * g : 128 * g + 128, :], other_ref[128 * g : 128 * g + 128, :]
    block = jnp.concatenate([jnp.where(first, mine, other), jnp.where(first, other, mine)], axis=0)
    none = jnp.zeros_like(block)
    both = jnp.concatenate([jnp.where(kind == 0, block, none), jnp.where(kind == 1, block, none)], axis=0)
    table_ref[216 * g : 216 * g + 216, :] = dot(take_ref[...], both)


def inside(lanes, at):
    return (lanes >= at) & (lanes < at + 64)


def gradient_blocks(half, grads, pixels, give_ref, kind_ref, blocks):
    wrapped = kind_ref[0:128, :] == 1
    for g in range(4):
        source = grads[216 * g : 216 * g + 216, :].astype(BF)
        part = dot(give_ref[half], source)
        blocks[128 * g : 128 * g + 128, :] = jnp.where(wrapped, part[128:256], part[0:128])
    lanes = lane((16, 128))
    row = lax.axis_index("rows")
    for a, (c, j, at) in enumerate(RELAYS):
        slot = sublane((16, 128)) + 16 * a
        across = ((slot < 48) | (slot >= 84)).astype(jnp.int32)
        goes = lax.rem(jnp.full((16, 128), row + half, jnp.int32) + across, 2) == 0
        pixel = jnp.where(goes, pixels[16 * a : 16 * a + 16, :], 0.0)
        if at % 64:
            pixel = pltpu.roll(pixel, at, axis=1)
        spot = pl.ds(4 * c + j, 16, stride=32)
        blocks[spot, :] = jnp.where(inside(lanes, at), pixel, blocks[spot, :])


def table_kernel(mine_ref, other_ref, take_ref, kind_ref, table_out, table):
    for g in range(4):
        gather_rows(g, mine_ref, other_ref, take_ref, kind_ref, table)
    table_out[...] = table[...].astype(BF)


def forward_kernel(
    table_ref, q_ref, cot_ref, ot_ref, give_ref, kind_ref, send_ref, grads, pixels, outp_ref, border, blocks
):
    even = jnp.zeros((CELLS, 128), F32)
    odd = jnp.zeros((CELLS, 128), F32)
    for a in range(3):
        for b in range(3):
            k = 3 * a + b
            weights = table_ref[96 * k : 96 * k + 96, :]
            rows = q_ref[b, 48 * a : 48 * a + CELLS, :]
            even = even + dot(rows[:, 0:96], weights)
            odd = odd + dot(rows[:, 128:224], weights)
    mid = (even[:, 0:64] + odd[:, 64:128]).astype(BF)
    pre = dot(mid, ot_ref[...])
    sig = jax.nn.sigmoid(pre)
    slope = (cot_ref[...].astype(F32) * sig * (1.0 + pre * (1.0 - sig))).astype(BF)
    ot = ot_ref[...]
    out_t = dot_nt(ot, slope).astype(BF)
    wide = jnp.concatenate([ot, ot, ot, ot], axis=0)
    outp = dot_nt(slope, wide).astype(BF).astype(F32)
    outp_ref[...] = outp
    border[...] = outp[:, 0:128]
    for f in range(FRAMES):
        pixels[8 * f : 8 * f + 8, :] = border[48 * f : 48 * f + 8, :]
        pixels[24 + 8 * f : 32 + 8 * f, :] = border[48 * f + 40 : 48 * f + 48, :]
    pixels[48:66, :] = border[pl.ds(0, 18, stride=8), :]
    pixels[66:84, :] = border[pl.ds(7, 18, stride=8), :]
    for k, cell in enumerate((0, 7, 40, 47)):
        pixels[84 + 3 * k : 87 + 3 * k, :] = border[pl.ds(cell, 3, stride=48), :]
    for a in range(3):
        for b in range(3):
            k = 3 * a + b
            part = dot(out_t, q_ref[b, 48 * a : 48 * a + CELLS, :])
            stack = jnp.concatenate([part[:, 0:128], part[:, 128:256]], axis=0)
            grads[96 * k : 96 * k + 96, :] = stack.T[0:96, :]
    gradient_blocks(1 - lax.rem(lax.axis_index("rows"), 2), grads, pixels, give_ref, kind_ref, blocks)
    send_ref[...] = blocks[...].astype(BF)


def keep_kernel(grads, pixels, give_ref, kind_ref, keep_ref):
    gradient_blocks(lax.rem(lax.axis_index("rows"), 2), grads, pixels, give_ref, kind_ref, keep_ref)


def add_kernel(keep_ref, got_ref, send_ref):
    send_ref[...] = (keep_ref[...] + got_ref[...].astype(F32)).astype(BF)


def adam_kernel(got_ref, core_ref, ring_ref, send_ref, next_ref, passed, blocks, sems):
    total = jnp.zeros((8, 128), F32)
    passed[0:40, :] = jnp.zeros((40, 128), F32)
    passed[552:592, :] = jnp.zeros((40, 128), F32)
    for g in range(4):
        part = got_ref[128 * g : 128 * g + 128, :].astype(F32)
        passed[128 * g + 40 : 128 * g + 168, :] = part
        total = total + part.reshape(16, 8, 128).sum(axis=0)
    grad = (total[0:4] + total[4:8]) * (1.0 / 192.0)
    core, one, two = core_ref[...], ring_ref[0], ring_ref[1]
    one = beta_one * one + (1.0 - beta_one) * grad
    two = beta_two * two + (1.0 - beta_two) * grad * grad
    core = core - learn_rate * (one / fix_one) / (jnp.sqrt(two / fix_two) + epsilon)
    next_ref[0] = core
    next_ref[1] = one
    next_ref[2] = two
    own = jnp.where(in_ring(ring_shift()), core, 0.0)
    own = jnp.concatenate([own, own], axis=0)
    row, col = lax.axis_index("rows"), lax.axis_index("cols")
    slot, parity, mask = lax.div(row, 2), lax.rem(row, 2), jnp.zeros((8, 128), jnp.bool_)
    for a, (c, j, at) in enumerate(RELAYS):
        slot = slot + jnp.where(col == c, 16 * a, 0)
        spot = (sublane((8, 128)) % 4 == j) & inside(lane((8, 128)), at)
        mask = mask | (spot & (jnp.full((8, 128), col, jnp.int32) == c))
    up, right = 0, 0
    for first, count, rows, cols in SLOTS:
        here = (slot >= first) & (slot < first + count)
        up = up + jnp.where(here, rows, 0)
        right = right + jnp.where(here, cols, 0)
    source = lax.rem(parity - up + 2, 2)
    chips = lax.div(source + up - parity + 2, 2) - 1
    start, copies = 40 - 4 * (8 * chips + right), []
    for k in range(32):
        upper = passed[pl.ds(start + 16 * k, 8), :]
        lower = passed[pl.ds(start + 16 * k + 8, 8), :]
        block = jnp.concatenate([jnp.where(mask, upper, own), jnp.where(mask, lower, own)], axis=0)
        blocks[16 * k : 16 * k + 16, :] = block.astype(BF)
        if k % 8 == 7:
            part = pl.ds(16 * k - 112, 128)
            copies += fetch(((blocks.at[part], send_ref.at[part]),), sems.at[pl.ds(k // 8, 1)])
    for copy in copies:
        copy.wait()


def flat_kernel(next_ref, core_ref, one_ref, two_ref):
    shift = ring_shift()
    for k, ref in enumerate((core_ref, one_ref, two_ref)):
        store_flat(ref, from_ring(next_ref[k], shift))


def turn_kernel(table_ref, back_ref):
    for k in range(9):
        for c in range(3):
            t = 3 * k + c
            part = table_ref[32 * t : 32 * t + 32, :].astype(F32).T
            cube = jnp.concatenate([part[0:64], part[64:128]], axis=1)
            back_ref[k, 64 * (2 - c) : 64 * (2 - c) + 64, :] = cube.astype(BF)


def backward_kernel(mine_ref, outp_ref, back_ref, utp_ref, grad_ref, got, pixels, tiles, qs):
    row, col = lax.axis_index("rows"), lax.axis_index("cols")
    got[...] = mine_ref[...].astype(F32)
    for a, (c, j, at) in enumerate(RELAYS):
        pixel = got[pl.ds(4 * c + j, 16, stride=32), :]
        pixels[16 * a : 16 * a + 16, 0:128] = pltpu.roll(pixel, 128 - at, axis=1) if at else pixel
    spread = (sublane((64, 256)) == lane((64, 256)) % 64).astype(BF)
    pixels[...] = dot(pixels[:, 0:64].astype(BF), spread)
    zero = jnp.zeros((8, 256), F32)

    def kept(flag, v):
        return jnp.where(jnp.full((8, 256), flag.astype(jnp.int32), jnp.int32) > 0, v, zero)

    def spot(k):
        return jnp.broadcast_to(pixels[k : k + 1, :], (8, 256))

    for f in range(FRAMES):
        for y in range(8):
            if y == 0:
                tile, left, right = pixels[24 + 8 * f : 32 + 8 * f, :], spot(93 + f), spot(90 + f)
            elif y == 7:
                tile, left, right = pixels[8 * f : 8 * f + 8, :], spot(87 + f), spot(84 + f)
            else:
                at = 48 * f + 8 * (y - 1)
                tile = outp_ref[at : at + 8, :]
                left, right = spot(66 + 6 * f + y - 1), spot(48 + 6 * f + y - 1)
            tile = shifted(tile, kept(col > 0, left), kept(col < 7, right), (64, 128), 256)
            if y == 0:
                tile = kept(row > 0, tile)
            elif y == 7:
                tile = kept(row < 31, tile)
            tiles[f, y] = tile
    stack_rows(tiles, qs)
    total = jnp.zeros((CELLS, 64), F32)
    for a in range(3):
        for b in range(3):
            rows = qs[2 - b, 48 * (2 - a) : 48 * (2 - a) + CELLS, :]
            total = total + dot(rows[:, 0:192], back_ref[3 * a + b])
    grad_ref[...] = dot(total.astype(BF), utp_ref[...]).astype(BF)

def build_kernel(mine_ref, other_ref, u_ref, ot_ref, take_ref, kind_ref, out_ref, table, half, result, sems):
    u, ot = u_ref[...], ot_ref[...]
    copies = []
    for g, (start, end) in enumerate(((0, 6), (6, 13), (13, 20), (20, 27))):
        gather_rows(g, mine_ref, other_ref, take_ref, kind_ref, table)
        cube = table[32 * start : 32 * end, :].astype(BF)
        even = dot(cube[:, 0:64], ot).astype(BF)
        odd = dot(cube[:, 64:128], ot).astype(BF)
        for t in range(start, end):
            at = 32 * (t - start)
            half[t, 0:32, :] = even[at : at + 32]
            half[t, 32:64, :] = odd[at : at + 32]
            result[t] = dot(u, half[t]).astype(BF)
            copies.append(pltpu.make_async_copy(result.at[t], out_ref.at[t], sems.at[t]))
            copies[-1].start()
    for copy in copies:
        copy.wait()


def call(kernel, args, outs, scratch, flops=10**7):
    def spec(far):
        return pl.BlockSpec(memory_space=pltpu.HBM if far else pltpu.VMEM)

    return pl.pallas_call(
        kernel,
        out_shape=[jax.ShapeDtypeStruct(shape, dtype) for shape, dtype, _ in outs],
        in_specs=[spec(far) for _, far in args],
        out_specs=[spec(far) for _, _, far in outs],
        scratch_shapes=scratch,
        compiler_params=pltpu.CompilerParams(vmem_limit_bytes=32 << 20),
        cost_estimate=pl.CostEstimate(flops=flops, bytes_accessed=10**5, transcendentals=0),
    )(*[pltpu.with_memory_space_constraint(arg, pltpu.HBM) if far else arg for arg, far in args])


def near(*args):
    return [(arg, False) for arg in args]


def far(*args):
    return [(arg, True) for arg in args]


def swap(one, two, axis):
    count = lax.axis_size(axis)
    pairs = [[(i, i + 1) for i in range(k, count - 1, 2)] for k in range(2)]
    two, one = (
        lax.ppermute(x, axis, forward + [(b, a) for a, b in forward]) for x, forward in ((two, pairs[1]), (one, pairs[0]))
    )
    return one, two


def device(k, chip, col):
    return 8 * (2 * chip + k) + col


ORDER = [[device(k, chip, col) for chip in range(16) for col in range(8)] for k in range(2)]


def exchange(x):
    return lax.all_to_all(x, AXES, 0, 0, tiled=True, axis_index_groups=ORDER)


def in_chip(x):
    return lax.ppermute(x, "rows", [(r, r ^ 1) for r in range(32)])


def body(frames_in, cotangent, core, moment_one, moment_two, u_in, u_out):
    take, give, kind = ring_tables()
    take, give, kind = jnp.asarray(take, BF), jnp.asarray(give, BF), jnp.asarray(kind, F32)
    vm, dma = pltpu.VMEM, pltpu.SemaphoreType.DMA
    side = (FRAMES * ROWS, 256)
    rim = (FRAMES * 16, 256)

    send, one, two, inner, core_ring, m_one, m_two, ut, ot, cot, take, give, kind = call(
        start_kernel,
        far(
            core, frames_in, moment_one, moment_two, u_in.T, u_out.T, cotangent.reshape(CELLS, 256), take, give, kind,
        ),
        [
            ((512, 128), BF, True), (side, BF, False), (side, BF, False), ((FRAMES, ROWS, COLS, 256), BF, False),
            ((4, 128), F32, False), ((OWN,), F32, False), ((OWN,), F32, False), ((64, 256), BF, False),
            ((64, 256), BF, False), ((CELLS, 256), BF, False), ((216, 512), BF, False), ((2, 256, 216), BF, False),
            ((256, 128), F32, False),
        ],
        [vm((OWN,), F32), vm((8, 128), F32), vm((128, 128), BF), vm(side, F32), vm(side, F32), dma((14,))],
    )
    one, two = swap(one, two, "cols")
    mine = exchange(send)
    left, right, one, two = call(
        rows_kernel,
        near(inner, two, one),
        [(side, F32, False), (side, F32, False), (rim, BF, False), (rim, BF, False)],
        [vm(rim, F32), vm(rim, F32)],
        flops=10**10,
    )
    own, wide, utp, u, ring = call(
        prepare_kernel,
        near(left, inner.reshape(CELLS, 256), ut, m_one, m_two),
        [
            ((CELLS, 256), F32, False), ((256, 256), BF, False), ((64, 256), BF, False), ((256, 64), BF, False),
            ((2, 4, 128), F32, False),
        ],
        [vm((8, 128), F32)],
        flops=10**10,
    )
    mine, _ = lax.optimization_barrier((mine, left))
    other = in_chip(mine)
    (table,) = call(
        table_kernel,
        near(mine, other, take, kind),
        [((TABLE, 128), BF, False)],
        [vm((TABLE, 128), F32)],
        flops=10000000000,
    )
    one, two = swap(one, two, "rows")
    (q,) = call(
        rank_kernel,
        near(table, own, wide, two, one, left, right),
        [((3, 240, 256), BF, False)],
        [vm((FRAMES, 8, 8, 256), F32), vm((2, 18, 256), F32), vm((2, 48, 256), F32)],
        flops=10000000,
    )
    send, grads, pixels, outp = call(
        forward_kernel,
        near(table, q, cot, ot, give, kind),
        [((512, 128), BF, False), ((TABLE, 128), F32, False), ((96, 128), F32, False), ((CELLS, 256), F32, False)],
        [vm((CELLS, 128), F32), vm((512, 128), F32)],
    )
    got = in_chip(send)
    (keep,) = call(keep_kernel, near(grads, pixels, give, kind), [((512, 128), F32, False)], [], flops=10**9)
    (send,) = call(add_kernel, near(keep, got), [((512, 128), BF, False)], [])
    got = exchange(send)
    send, latest = call(
        adam_kernel,
        near(got, core_ring, ring),
        [((512, 128), BF, True), ((3, 4, 128), F32, False)],
        [vm((592, 128), F32), vm((512, 128), BF), dma((4,))],
    )
    mine = exchange(send)
    (back,) = call(turn_kernel, near(table), [((9, 192, 64), BF, False)], [])
    core_next, one_next, two_next = call(flat_kernel, near(latest), [((OWN,), F32, False)] * 3, [])
    mine, back, core_next, one_next, two_next = lax.optimization_barrier((mine, back, core_next, one_next, two_next))
    other = in_chip(mine)
    (frames_grad,) = call(
        backward_kernel,
        near(mine, outp, back, utp),
        [((CELLS, 256), BF, False)],
        [vm((512, 128), F32), vm((96, 256), F32), vm((FRAMES, 8, 8, 256), F32), vm((3, 240, 256), BF)],
        flops=10**9,
    )
    other, frames_grad = lax.optimization_barrier((other, frames_grad))
    (kernel_next,) = call(
        build_kernel,
        near(mine, other, u, ot, take, kind),
        [((27, 256, 256), BF, True)],
        [vm((TABLE, 128), F32), vm((27, 64, 256), BF), vm((27, 256, 256), BF), dma((27,))],
    )
    frames_grad = frames_grad.reshape(FRAMES, ROWS, COLS, 256)
    return frames_grad, core_next, one_next, two_next, kernel_next


def solution(mesh):
    in_specs = (
        P(None, "rows", "cols", None),
        P(None, "rows", "cols", None),
        P(AXES),
        P(AXES),
        P(AXES),
        P(),
        P(),
    )
    out_specs = (
        P(None, "rows", "cols", None),
        P(AXES),
        P(AXES),
        P(AXES),
        P(),
    )
    return jax.shard_map(body, mesh=mesh, in_specs=in_specs, out_specs=out_specs, check_vma=False)
```

```python
import jax
import jax.numpy as jnp
import numpy as np
from jax import lax
from jax.experimental import pallas as pl
from jax.experimental.pallas import tpu as pltpu
from jax.sharding import PartitionSpec as P

beta_one = 0.9
beta_two = 0.999
learn_rate = 0.06
epsilon = 1e-08
fix_one = 1.0 - 0.9**10
fix_two = 1.0 - 0.999**10

BF = jnp.bfloat16
F32 = jnp.float32
AXES = ("rows", "cols")

OWN = 432
FRAMES, ROWS, COLS = 3, 6, 8
CELLS = FRAMES * ROWS * COLS
SIDE = FRAMES * 8
TABLE = 864


RELAYS = ((7, 0, 0), (4, 0, 0), (3, 3, 64), (0, 3, 64), (2, 0, 16), (5, 0, 32))
SLOTS = (
    (0, 24, -1, 0), (24, 24, 1, 0), (48, 18, 0, -1), (66, 18, 0, 1),
    (84, 3, -1, -1), (87, 3, -1, 1), (90, 3, 1, -1), (93, 3, 1, 1),
)


def ring_tables():
    take = np.zeros((216, 512), np.float32)
    give = np.zeros((2, 256, 216), np.float32)
    kind = np.zeros((256, 128), np.float32)
    for r in range(8):
        for c in range(8):
            first = 27 * r + 27 * c // 8
            col = 128 * (r % 2) + 32 * (r // 2) + 4 * c
            for j in range(4):
                take[first + j, col + j] = 1
                give[r % 2, col % 128 + j, first + j] = 1
            wrapped = 48 * c % 128 + OWN - 512
            if wrapped > 0:
                take[first + 4, 256 + col] = 1
                give[r % 2, 128 + col % 128, first + 4] = 1
                kind[col, :wrapped] = 1
        for c, j, at in RELAYS:
            kind[128 * (r % 2) + 32 * (r // 2) + 4 * c + j, at : at + 64] = 2
    return take, give, kind


def dot(a, b):
    return jnp.dot(a, b, preferred_element_type=F32)


def dot_nt(a, b):
    return lax.dot_general(a, b, (((1,), (1,)), ((), ())), preferred_element_type=F32)


def dot_tn(a, b):
    return lax.dot_general(a, b, (((0,), (0,)), ((), ())), preferred_element_type=F32)


def lane(shape):
    return lax.broadcasted_iota(jnp.int32, shape, 1)


def sublane(shape):
    return lax.broadcasted_iota(jnp.int32, shape, 0)


def ring_shift():
    return lax.rem(lax.axis_index("cols") * 48, 128)


def to_ring(v, shift):
    turned = pltpu.roll(v, shift, axis=1)
    above = jnp.concatenate([turned[3:4], turned[0:3]], axis=0)
    return jnp.where(lane(v.shape) >= shift, turned, above)


def from_ring(v, shift):
    turned = pltpu.roll(v, lax.rem(128 - shift, 128), axis=1)
    below = jnp.concatenate([turned[1:4], turned[0:1]], axis=0)
    return jnp.where(lane(v.shape) < 128 - shift, turned, below)


def in_ring(shift):
    place = sublane((4, 128)) * 128 + lane((4, 128)) - shift
    place = jnp.where(place < 0, place + 512, place)
    return place < OWN


def load_flat(ref, scratch):
    scratch[...] = jnp.zeros_like(scratch)
    for k in range(3):
        scratch[k, :] = ref[pl.ds(128 * k, 128)]
    scratch[3, 0 : OWN - 384] = ref[pl.ds(384, OWN - 384)]
    return scratch[0:4, :]


def store_flat(ref, v):
    for k in range(3):
        ref[pl.ds(128 * k, 128)] = v[k]
    ref[pl.ds(384, OWN - 384)] = v[3, 0 : OWN - 384]


def fetch(pairs, sems):
    copies = [pltpu.make_async_copy(src, dst, sems.at[k]) for k, (src, dst) in enumerate(pairs)]
    for copy in copies:
        copy.start()
    return copies


def even_first(axis, first, last):
    even = jnp.full(first.shape, lax.rem(lax.axis_index(axis), 2), jnp.int32) == 0
    return jnp.where(even, last, first), jnp.where(even, first, last)


def start_kernel(
    core_ref, x_ref, one_ref, two_ref, ut_ref, ot_ref, cot_ref, take_ref, give_ref, kind_ref,
    send_ref, near_ref, far_ref, inner_ref, ring_ref, one_out, two_out, ut_out, ot_out, cot_out, take_out, give_out, kind_out,
    own, flat, block, sems,
):
    copies = fetch(
        (
            (core_ref, own), (x_ref, inner_ref), (one_ref, one_out), (two_ref, two_out), (ut_ref, ut_out),
            (ot_ref, ot_out), (take_ref, take_out), (kind_ref, kind_out), (give_ref, give_out), (cot_ref, cot_out),
        ),
        sems,
    )
    copies[0].wait()
    v = to_ring(load_flat(own, flat), ring_shift())
    ring_ref[...] = v
    rows = jnp.concatenate([v, v, v, v], axis=0).astype(BF)
    for k in range(8):
        block[16 * k : 16 * k + 16, :] = rows
    sends = fetch([(block, send_ref.at[pl.ds(128 * k, 128)]) for k in range(4)], sems.at[pl.ds(10, 4)])
    copies[1].wait()
    for f in range(FRAMES):
        first, last = inner_ref[f, 0].astype(F32), inner_ref[f, ROWS - 1].astype(F32)
        one, two = even_first("rows", first, last)
        near_ref[f] = one.astype(BF)
        far_ref[f] = two.astype(BF)
    for copy in copies[2:] + sends:
        copy.wait()


def columns_kernel(inner_ref, two_ref, one_ref, above_ref, below_ref, left_ref, right_ref, low, high):
    for f in range(FRAMES):
        below, above = even_first("rows", two_ref[f].astype(F32), one_ref[f].astype(F32))
        above_ref[8 * f : 8 * f + 8, :] = above
        below_ref[8 * f : 8 * f + 8, :] = below
        for y in range(8):
            tile = above if y == 0 else below if y == 7 else inner_ref[f, y - 1].astype(F32)
            low[8 * f + y : 8 * f + y + 1, :] = tile[0:1, :]
            high[8 * f + y : 8 * f + y + 1, :] = tile[7:8, :]
    one, two = even_first("cols", low[...], high[...])
    left_ref[...] = one.astype(BF)
    right_ref[...] = two.astype(BF)


def shifted(tile, left, right, bounds, period):
    at = lane(tile.shape) % period
    row = sublane(tile.shape)
    back = jnp.where(row == 0, left, pltpu.roll(tile, 1, axis=0))
    ahead = jnp.where(row == 7, right, pltpu.roll(tile, 7, axis=0))
    return jnp.where(at < bounds[0], back, jnp.where(at < bounds[1], tile, ahead))


def prepare_kernel(_, x_ref, ut_ref, one_ref, two_ref, own_ref, wide_ref, utp_ref, u_ref, ring_ref, flat):
    row = sublane((256, 64))
    at = row % 128
    pick = (lane((256, 64)) == (at % 32) * 2 + row // 128) & (at < 96)
    half_row = sublane((64, 64))
    half_pick = lane((64, 64)) == (half_row % 32) * 2 + half_row // 32
    wide = dot(pick.astype(BF), ut_ref[...]).astype(BF)
    wide_ref[...] = wide
    utp = dot(half_pick.astype(BF), ut_ref[...])
    utp_ref[...] = utp.astype(BF)
    u_ref[...] = utp.T.astype(BF)
    own_ref[...] = dot_nt(x_ref[...], wide).astype(BF).astype(F32)
    shift = ring_shift()
    ring_ref[0] = to_ring(load_flat(one_ref, flat), shift)
    ring_ref[1] = to_ring(load_flat(two_ref, flat), shift)


def stack_rows(tiles, out_ref):
    for b in range(3):
        out_ref[b, 0:48, :] = jnp.zeros((48, 256), BF)
        out_ref[b, 192:240, :] = jnp.zeros((48, 256), BF)
        for f in range(FRAMES):
            rows = tiles[f, b : b + ROWS].reshape(48, 256)
            out_ref[b, 48 * f + 48 : 48 * f + 96, :] = rows.astype(BF)


def rank_kernel(_, own_ref, wide_ref, above_ref, below_ref, two_ref, one_ref, q_ref, tiles, edge, rims):
    wide = wide_ref[...]

    def project(v):
        return dot_nt(v.astype(BF), wide).astype(BF).astype(F32)

    rims[0] = project(above_ref[...])
    rims[1] = project(below_ref[...])
    right, left = even_first("cols", project(two_ref[...]), project(one_ref[...]))
    edge[0] = left
    edge[1] = right
    for f in range(FRAMES):
        for y in range(8):
            k = 8 * f + y
            if y in (0, 7):
                tile = rims[y // 7, 8 * f : 8 * f + 8, :]
            else:
                at = 48 * f + 8 * (y - 1)
                tile = own_ref[at : at + 8, :]
            left = jnp.broadcast_to(edge[0, k : k + 1, :], (8, 256))
            right = jnp.broadcast_to(edge[1, k : k + 1, :], (8, 256))
            tiles[f, y] = shifted(tile, left, right, (32, 64), 128)
    stack_rows(tiles, q_ref)


def core_index(shape):
    return jnp.full(shape, lax.rem(lax.axis_index("rows"), 2), jnp.int32)


def gather_table(mine_ref, other_ref, take_ref, kind_ref, table_ref):
    kind = kind_ref[...]
    take = take_ref[...]
    first = core_index((128, 128)) == 0
    for g in range(4):
        mine, other = mine_ref[128 * g : 128 * g + 128, :], other_ref[128 * g : 128 * g + 128, :]
        block = jnp.concatenate([jnp.where(first, mine, other), jnp.where(first, other, mine)], axis=0)
        none = jnp.zeros_like(block)
        both = jnp.concatenate(
            [jnp.where(kind == 0, block, none), jnp.where(kind == 1, block, none)], axis=0
        )
        table_ref[216 * g : 216 * g + 216, :] = dot(take, both)


def inside(lanes, at):
    return (lanes >= at) & (lanes < at + 64)


def gradient_blocks(half, grads, pixels, give_ref, kind_ref, blocks):
    wrapped = kind_ref[0:128, :] == 1
    for g in range(4):
        source = grads[216 * g : 216 * g + 216, :].astype(BF)
        part = dot(give_ref[half], source)
        blocks[128 * g : 128 * g + 128, :] = jnp.where(wrapped, part[128:256], part[0:128])
    lanes = lane((16, 128))
    row = lax.axis_index("rows")
    for a, (c, j, at) in enumerate(RELAYS):
        slot = sublane((16, 128)) + 16 * a
        across = ((slot < 48) | (slot >= 84)).astype(jnp.int32)
        goes = lax.rem(jnp.full((16, 128), row + half, jnp.int32) + across, 2) == 0
        pixel = jnp.where(goes, pixels[16 * a : 16 * a + 16, :], 0.0)
        if at % 64:
            pixel = pltpu.roll(pixel, at, axis=1)
        spot = pl.ds(4 * c + j, 16, stride=32)
        blocks[spot, :] = jnp.where(inside(lanes, at), pixel, blocks[spot, :])


def table_kernel(mine_ref, other_ref, take_ref, kind_ref, table_out, table):
    gather_table(mine_ref, other_ref, take_ref, kind_ref, table)
    table_out[...] = table[...].astype(BF)


def forward_kernel(
    table_ref, q_ref, cot_ref, ot_ref, give_ref, kind_ref, send_ref, grads, pixels, outp_ref, border, blocks
):
    even = jnp.zeros((CELLS, 128), F32)
    odd = jnp.zeros((CELLS, 128), F32)
    for a in range(3):
        for b in range(3):
            k = 3 * a + b
            weights = table_ref[96 * k : 96 * k + 96, :]
            rows = q_ref[b, 48 * a : 48 * a + CELLS, :]
            even = even + dot(rows[:, 0:96], weights)
            odd = odd + dot(rows[:, 128:224], weights)
    mid = (even[:, 0:64] + odd[:, 64:128]).astype(BF)
    pre = dot(mid, ot_ref[...])
    sig = jax.nn.sigmoid(pre)
    slope = (cot_ref[...].astype(F32) * sig * (1.0 + pre * (1.0 - sig))).astype(BF)
    ot = ot_ref[...]
    out_t = dot_nt(ot, slope).astype(BF)
    wide = jnp.concatenate([ot, ot, ot, ot], axis=0)
    outp = dot_nt(slope, wide).astype(BF).astype(F32)
    outp_ref[...] = outp
    border[...] = outp[:, 0:128]
    for f in range(FRAMES):
        pixels[8 * f : 8 * f + 8, :] = border[48 * f : 48 * f + 8, :]
        pixels[24 + 8 * f : 32 + 8 * f, :] = border[48 * f + 40 : 48 * f + 48, :]
    pixels[48:66, :] = border[pl.ds(0, 18, stride=8), :]
    pixels[66:84, :] = border[pl.ds(7, 18, stride=8), :]
    for k, cell in enumerate((0, 7, 40, 47)):
        pixels[84 + 3 * k : 87 + 3 * k, :] = border[pl.ds(cell, 3, stride=48), :]
    for a in range(3):
        for b in range(3):
            k = 3 * a + b
            part = dot(out_t, q_ref[b, 48 * a : 48 * a + CELLS, :])
            stack = jnp.concatenate([part[:, 0:128], part[:, 128:256]], axis=0)
            grads[96 * k : 96 * k + 96, :] = stack.T[0:96, :]
    gradient_blocks(1 - lax.rem(lax.axis_index("rows"), 2), grads, pixels, give_ref, kind_ref, blocks)
    send_ref[...] = blocks[...].astype(BF)


def keep_kernel(grads, pixels, give_ref, kind_ref, keep_ref):
    gradient_blocks(lax.rem(lax.axis_index("rows"), 2), grads, pixels, give_ref, kind_ref, keep_ref)


def add_kernel(keep_ref, got_ref, send_ref):
    send_ref[...] = (keep_ref[...] + got_ref[...].astype(F32)).astype(BF)


def adam_kernel(got_ref, core_ref, ring_ref, send_ref, next_ref, passed):
    total = jnp.zeros((8, 128), F32)
    passed[0:40, :] = jnp.zeros((40, 128), F32)
    passed[552:592, :] = jnp.zeros((40, 128), F32)
    for g in range(4):
        part = got_ref[128 * g : 128 * g + 128, :].astype(F32)
        passed[128 * g + 40 : 128 * g + 168, :] = part
        total = total + part.reshape(16, 8, 128).sum(axis=0)
    grad = (total[0:4] + total[4:8]) * (1.0 / 192.0)
    core, one, two = core_ref[...], ring_ref[0], ring_ref[1]
    one = beta_one * one + (1.0 - beta_one) * grad
    two = beta_two * two + (1.0 - beta_two) * grad * grad
    core = core - learn_rate * (one / fix_one) / (jnp.sqrt(two / fix_two) + epsilon)
    next_ref[0] = core
    next_ref[1] = one
    next_ref[2] = two
    own = jnp.where(in_ring(ring_shift()), core, 0.0)
    own = jnp.concatenate([own, own], axis=0)
    row, col = lax.axis_index("rows"), lax.axis_index("cols")
    slot, parity, mask = lax.div(row, 2), lax.rem(row, 2), jnp.zeros((8, 128), jnp.bool_)
    for a, (c, j, at) in enumerate(RELAYS):
        slot = slot + jnp.where(col == c, 16 * a, 0)
        spot = (sublane((8, 128)) % 4 == j) & inside(lane((8, 128)), at)
        mask = mask | (spot & (jnp.full((8, 128), col, jnp.int32) == c))
    up, right = 0, 0
    for first, count, rows, cols in SLOTS:
        here = (slot >= first) & (slot < first + count)
        up = up + jnp.where(here, rows, 0)
        right = right + jnp.where(here, cols, 0)
    source = lax.rem(parity - up + 2, 2)
    chips = lax.div(source + up - parity + 2, 2) - 1
    start = 40 - 4 * (8 * chips + right)
    for k in range(32):
        upper = passed[pl.ds(start + 16 * k, 8), :]
        lower = passed[pl.ds(start + 16 * k + 8, 8), :]
        block = jnp.concatenate([jnp.where(mask, upper, own), jnp.where(mask, lower, own)], axis=0)
        send_ref[16 * k : 16 * k + 16, :] = block.astype(BF)


def flat_kernel(next_ref, core_ref, one_ref, two_ref):
    shift = ring_shift()
    for k, ref in enumerate((core_ref, one_ref, two_ref)):
        store_flat(ref, from_ring(next_ref[k], shift))


def turn_kernel(table_ref, back_ref):
    for k in range(9):
        for c in range(3):
            t = 3 * k + c
            part = table_ref[32 * t : 32 * t + 32, :].astype(F32).T
            cube = jnp.concatenate([part[0:64], part[64:128]], axis=1)
            back_ref[k, 64 * (2 - c) : 64 * (2 - c) + 64, :] = cube.astype(BF)


def backward_kernel(mine_ref, outp_ref, back_ref, utp_ref, grad_ref, got, pixels, tiles, qs):
    row, col = lax.axis_index("rows"), lax.axis_index("cols")
    got[...] = mine_ref[...].astype(F32)
    for a, (c, j, at) in enumerate(RELAYS):
        pixel = got[pl.ds(4 * c + j, 16, stride=32), :]
        pixels[16 * a : 16 * a + 16, 0:128] = pltpu.roll(pixel, 128 - at, axis=1) if at else pixel
    spread = (sublane((64, 256)) == lane((64, 256)) % 64).astype(BF)
    pixels[...] = dot(pixels[:, 0:64].astype(BF), spread)
    zero = jnp.zeros((8, 256), F32)

    def kept(flag, v):
        return jnp.where(jnp.full((8, 256), flag.astype(jnp.int32), jnp.int32) > 0, v, zero)

    def spot(k):
        return jnp.broadcast_to(pixels[k : k + 1, :], (8, 256))

    for f in range(FRAMES):
        for y in range(8):
            if y == 0:
                tile, left, right = pixels[24 + 8 * f : 32 + 8 * f, :], spot(93 + f), spot(90 + f)
            elif y == 7:
                tile, left, right = pixels[8 * f : 8 * f + 8, :], spot(87 + f), spot(84 + f)
            else:
                at = 48 * f + 8 * (y - 1)
                tile = outp_ref[at : at + 8, :]
                left, right = spot(66 + 6 * f + y - 1), spot(48 + 6 * f + y - 1)
            tile = shifted(tile, kept(col > 0, left), kept(col < 7, right), (64, 128), 256)
            if y == 0:
                tile = kept(row > 0, tile)
            elif y == 7:
                tile = kept(row < 31, tile)
            tiles[f, y] = tile
    stack_rows(tiles, qs)
    total = jnp.zeros((CELLS, 64), F32)
    for a in range(3):
        for b in range(3):
            rows = qs[2 - b, 48 * (2 - a) : 48 * (2 - a) + CELLS, :]
            total = total + dot(rows[:, 0:192], back_ref[3 * a + b])
    grad_ref[...] = dot(total.astype(BF), utp_ref[...]).astype(BF)

def build_kernel(mine_ref, other_ref, u_ref, ot_ref, take_ref, kind_ref, out_ref, table, half, result, sems):
    gather_table(mine_ref, other_ref, take_ref, kind_ref, table)
    cube = table[...].astype(BF)
    even = dot(cube[:, 0:64], ot_ref[...]).astype(BF)
    odd = dot(cube[:, 64:128], ot_ref[...]).astype(BF)
    for t in range(27):
        half[t, 0:32, :] = even[32 * t : 32 * t + 32]
        half[t, 32:64, :] = odd[32 * t : 32 * t + 32]
    u = u_ref[...]

    def store(a):
        part = pl.ds(3 * a, 3)
        return pltpu.make_async_copy(result.at[part], out_ref.at[part], sems.at[a])

    for a in range(9):
        for t in range(3 * a, 3 * a + 3):
            result[t] = dot(u, half[t]).astype(BF)
        store(a).start()
    for a in range(9):
        store(a).wait()


def call(kernel, args, outs, scratch, flops=10**7):
    def spec(far):
        return pl.BlockSpec(memory_space=pltpu.HBM if far else pltpu.VMEM)

    return pl.pallas_call(
        kernel,
        out_shape=[jax.ShapeDtypeStruct(shape, dtype) for shape, dtype, _ in outs],
        in_specs=[spec(far) for _, far in args],
        out_specs=[spec(far) for _, _, far in outs],
        scratch_shapes=scratch,
        compiler_params=pltpu.CompilerParams(vmem_limit_bytes=32 << 20),
        cost_estimate=pl.CostEstimate(flops=flops, bytes_accessed=10**5, transcendentals=0),
    )(*[pltpu.with_memory_space_constraint(arg, pltpu.HBM) if far else arg for arg, far in args])


def near(*args):
    return [(arg, False) for arg in args]


def far(*args):
    return [(arg, True) for arg in args]


def swap(one, two, axis):
    count = lax.axis_size(axis)
    pairs = [[(i, i + 1) for i in range(k, count - 1, 2)] for k in range(2)]
    two, one = (
        lax.ppermute(x, axis, forward + [(b, a) for a, b in forward]) for x, forward in ((two, pairs[1]), (one, pairs[0]))
    )
    return one, two


def device(k, chip, col):
    return 8 * (2 * chip + k) + col


ORDER = [[device(k, chip, col) for chip in range(16) for col in range(8)] for k in range(2)]


def exchange(x):
    return lax.all_to_all(x, AXES, 0, 0, tiled=True, axis_index_groups=ORDER)


def in_chip(x):
    return lax.ppermute(x, "rows", [(r, r ^ 1) for r in range(32)])


def body(frames_in, cotangent, core, moment_one, moment_two, u_in, u_out):
    take, give, kind = ring_tables()
    take, give, kind = jnp.asarray(take, BF), jnp.asarray(give, BF), jnp.asarray(kind, F32)
    vm, dma = pltpu.VMEM, pltpu.SemaphoreType.DMA
    rim = (FRAMES * 8, 256)
    row = (FRAMES, 8, 256)

    send, one, two, inner, core_ring, m_one, m_two, ut, ot, cot, take, give, kind = call(
        start_kernel,
        far(
            core, frames_in, moment_one, moment_two, u_in.T, u_out.T, cotangent.reshape(CELLS, 256), take, give, kind,
        ),
        [
            ((512, 128), BF, True), (row, BF, False), (row, BF, False), ((FRAMES, ROWS, COLS, 256), BF, False),
            ((4, 128), F32, False), ((OWN,), F32, False), ((OWN,), F32, False), ((64, 256), BF, False),
            ((64, 256), BF, False), ((CELLS, 256), BF, False), ((216, 512), BF, False), ((2, 256, 216), BF, False),
            ((256, 128), F32, False),
        ],
        [vm((OWN,), F32), vm((8, 128), F32), vm((128, 128), BF), dma((14,))],
    )
    one, two = swap(one, two, "rows")
    mine = exchange(send)
    above, below, one, two = call(
        columns_kernel,
        near(inner, two, one),
        [(rim, F32, False), (rim, F32, False), (rim, BF, False), (rim, BF, False)],
        [vm(rim, F32), vm(rim, F32)],
        flops=10**10,
    )
    own, wide, utp, u, ring = call(
        prepare_kernel,
        near(above, inner.reshape(CELLS, 256), ut, m_one, m_two),
        [
            ((CELLS, 256), F32, False), ((256, 256), BF, False), ((64, 256), BF, False), ((256, 64), BF, False),
            ((2, 4, 128), F32, False),
        ],
        [vm((8, 128), F32)],
        flops=10**10,
    )
    mine, _ = lax.optimization_barrier((mine, above))
    other = in_chip(mine)
    (table,) = call(
        table_kernel,
        near(mine, other, take, kind),
        [((TABLE, 128), BF, False)],
        [vm((TABLE, 128), F32)],
        flops=10000000000,
    )
    one, two = swap(one, two, "cols")
    (q,) = call(
        rank_kernel,
        near(table, own, wide, above, below, two, one),
        [((3, 240, 256), BF, False)],
        [vm((FRAMES, 8, 8, 256), F32), vm((2, 24, 256), F32), vm((2, 24, 256), F32)],
        flops=10000000,
    )
    send, grads, pixels, outp = call(
        forward_kernel,
        near(table, q, cot, ot, give, kind),
        [((512, 128), BF, False), ((TABLE, 128), F32, False), ((96, 128), F32, False), ((CELLS, 256), F32, False)],
        [vm((CELLS, 128), F32), vm((512, 128), F32)],
    )
    got = in_chip(send)
    (keep,) = call(keep_kernel, near(grads, pixels, give, kind), [((512, 128), F32, False)], [], flops=10**9)
    (send,) = call(add_kernel, near(keep, got), [((512, 128), BF, False)], [])
    got = exchange(send)
    send, latest = call(
        adam_kernel,
        near(got, core_ring, ring),
        [((512, 128), BF, False), ((3, 4, 128), F32, False)],
        [vm((592, 128), F32)],
    )
    mine = exchange(send)
    (back,) = call(turn_kernel, near(table), [((9, 192, 64), BF, False)], [])
    core_next, one_next, two_next = call(flat_kernel, near(latest), [((OWN,), F32, False)] * 3, [])
    mine, back, core_next, one_next, two_next = lax.optimization_barrier((mine, back, core_next, one_next, two_next))
    other = in_chip(mine)
    (frames_grad,) = call(
        backward_kernel,
        near(mine, outp, back, utp),
        [((CELLS, 256), BF, False)],
        [vm((512, 128), F32), vm((96, 256), F32), vm((FRAMES, 8, 8, 256), F32), vm((3, 240, 256), BF)],
        flops=10**9,
    )
    other, frames_grad = lax.optimization_barrier((other, frames_grad))
    (kernel_next,) = call(
        build_kernel,
        near(mine, other, u, ot, take, kind),
        [((27, 256, 256), BF, True)],
        [vm((TABLE, 128), F32), vm((27, 64, 256), BF), vm((27, 256, 256), BF), dma((9,))],
    )
    frames_grad = frames_grad.reshape(FRAMES, ROWS, COLS, 256)
    return frames_grad, core_next, one_next, two_next, kernel_next


def solution(mesh):
    in_specs = (
        P(None, "rows", "cols", None),
        P(None, "rows", "cols", None),
        P(AXES),
        P(AXES),
        P(AXES),
        P(),
        P(),
    )
    out_specs = (
        P(None, "rows", "cols", None),
        P(AXES),
        P(AXES),
        P(AXES),
        P(),
    )
    return jax.shard_map(body, mesh=mesh, in_specs=in_specs, out_specs=out_specs, check_vma=False)
```

```python
import jax
import jax.numpy as jnp
import numpy as np
from jax import lax
from jax.experimental import pallas as pl
from jax.experimental.pallas import tpu as pltpu
from jax.sharding import PartitionSpec as P

beta_one = 0.9
beta_two = 0.999
learn_rate = 0.06
epsilon = 1e-08
fix_one = 1.0 - 0.9**10
fix_two = 1.0 - 0.999**10

BF = jnp.bfloat16
F32 = jnp.float32
AXES = ("rows", "cols")

OWN = 432
FRAMES, ROWS, COLS = 3, 6, 8
CELLS = FRAMES * ROWS * COLS
SIDE = FRAMES * 8
TABLE = 864


RELAYS = ((7, 0, 0), (4, 0, 0), (3, 3, 64), (0, 3, 64), (2, 0, 16), (5, 0, 32))
SLOTS = (
    (0, 24, -1, 0), (24, 24, 1, 0), (48, 18, 0, -1), (66, 18, 0, 1),
    (84, 3, -1, -1), (87, 3, -1, 1), (90, 3, 1, -1), (93, 3, 1, 1),
)


def ring_tables():
    take = np.zeros((216, 512), np.float32)
    give = np.zeros((2, 256, 216), np.float32)
    kind = np.zeros((256, 128), np.float32)
    for r in range(8):
        for c in range(8):
            first = 27 * r + 27 * c // 8
            col = 128 * (r % 2) + 32 * (r // 2) + 4 * c
            for j in range(4):
                take[first + j, col + j] = 1
                give[r % 2, col % 128 + j, first + j] = 1
            wrapped = 48 * c % 128 + OWN - 512
            if wrapped > 0:
                take[first + 4, 256 + col] = 1
                give[r % 2, 128 + col % 128, first + 4] = 1
                kind[col, :wrapped] = 1
        for c, j, at in RELAYS:
            kind[128 * (r % 2) + 32 * (r // 2) + 4 * c + j, at : at + 64] = 2
    return take, give, kind


def dot(a, b):
    return jnp.dot(a, b, preferred_element_type=F32)


def dot_nt(a, b):
    return lax.dot_general(a, b, (((1,), (1,)), ((), ())), preferred_element_type=F32)


def dot_tn(a, b):
    return lax.dot_general(a, b, (((0,), (0,)), ((), ())), preferred_element_type=F32)


def lane(shape):
    return lax.broadcasted_iota(jnp.int32, shape, 1)


def sublane(shape):
    return lax.broadcasted_iota(jnp.int32, shape, 0)


def ring_shift():
    return lax.rem(lax.axis_index("cols") * 48, 128)


def to_ring(v, shift):
    turned = pltpu.roll(v, shift, axis=1)
    above = jnp.concatenate([turned[3:4], turned[0:3]], axis=0)
    return jnp.where(lane(v.shape) >= shift, turned, above)


def from_ring(v, shift):
    turned = pltpu.roll(v, lax.rem(128 - shift, 128), axis=1)
    below = jnp.concatenate([turned[1:4], turned[0:1]], axis=0)
    return jnp.where(lane(v.shape) < 128 - shift, turned, below)


def in_ring(shift):
    place = sublane((4, 128)) * 128 + lane((4, 128)) - shift
    place = jnp.where(place < 0, place + 512, place)
    return place < OWN


def load_flat(ref, scratch):
    scratch[...] = jnp.zeros_like(scratch)
    for k in range(3):
        scratch[k, :] = ref[pl.ds(128 * k, 128)]
    scratch[3, 0 : OWN - 384] = ref[pl.ds(384, OWN - 384)]
    return scratch[0:4, :]


def store_flat(ref, v):
    for k in range(3):
        ref[pl.ds(128 * k, 128)] = v[k]
    ref[pl.ds(384, OWN - 384)] = v[3, 0 : OWN - 384]


def fetch(pairs, sems):
    copies = [pltpu.make_async_copy(src, dst, sems.at[k]) for k, (src, dst) in enumerate(pairs)]
    for copy in copies:
        copy.start()
    return copies


def even_first(axis, first, last):
    even = jnp.full(first.shape, lax.rem(lax.axis_index(axis), 2), jnp.int32) == 0
    return jnp.where(even, last, first), jnp.where(even, first, last)


def start_kernel(
    core_ref, x_ref, one_ref, two_ref, ut_ref, ot_ref, cot_ref, take_ref, give_ref, kind_ref,
    send_ref, near_ref, far_ref, inner_ref, ring_ref, one_out, two_out, ut_out, ot_out, cot_out, take_out, give_out, kind_out,
    own, flat, block, sems,
):
    copies = fetch(
        (
            (core_ref, own), (x_ref, inner_ref), (one_ref, one_out), (two_ref, two_out), (ut_ref, ut_out),
            (ot_ref, ot_out), (take_ref, take_out), (kind_ref, kind_out), (give_ref, give_out), (cot_ref, cot_out),
        ),
        sems,
    )
    copies[0].wait()
    v = to_ring(load_flat(own, flat), ring_shift())
    ring_ref[...] = v
    rows = jnp.concatenate([v, v, v, v], axis=0).astype(BF)
    for k in range(8):
        block[16 * k : 16 * k + 16, :] = rows
    sends = fetch([(block, send_ref.at[pl.ds(128 * k, 128)]) for k in range(4)], sems.at[pl.ds(10, 4)])
    copies[1].wait()
    for f in range(FRAMES):
        first, last = inner_ref[f, 0].astype(F32), inner_ref[f, ROWS - 1].astype(F32)
        one, two = even_first("rows", first, last)
        near_ref[f] = one.astype(BF)
        far_ref[f] = two.astype(BF)
    for copy in copies[2:] + sends:
        copy.wait()


def columns_kernel(inner_ref, two_ref, one_ref, above_ref, below_ref, left_ref, right_ref, low, high):
    for f in range(FRAMES):
        below, above = even_first("rows", two_ref[f].astype(F32), one_ref[f].astype(F32))
        above_ref[8 * f : 8 * f + 8, :] = above
        below_ref[8 * f : 8 * f + 8, :] = below
        for y in range(8):
            tile = above if y == 0 else below if y == 7 else inner_ref[f, y - 1].astype(F32)
            low[8 * f + y : 8 * f + y + 1, :] = tile[0:1, :]
            high[8 * f + y : 8 * f + y + 1, :] = tile[7:8, :]
    one, two = even_first("cols", low[...], high[...])
    left_ref[...] = one.astype(BF)
    right_ref[...] = two.astype(BF)


def shifted(tile, left, right, bounds, period):
    at = lane(tile.shape) % period
    row = sublane(tile.shape)
    back = jnp.where(row == 0, left, pltpu.roll(tile, 1, axis=0))
    ahead = jnp.where(row == 7, right, pltpu.roll(tile, 7, axis=0))
    return jnp.where(at < bounds[0], back, jnp.where(at < bounds[1], tile, ahead))


def prepare_kernel(_, x_ref, ut_ref, one_ref, two_ref, own_ref, wide_ref, utp_ref, u_ref, ring_ref, flat):
    row = sublane((256, 64))
    at = row % 128
    pick = (lane((256, 64)) == (at % 32) * 2 + row // 128) & (at < 96)
    half_row = sublane((64, 64))
    half_pick = lane((64, 64)) == (half_row % 32) * 2 + half_row // 32
    wide = dot(pick.astype(BF), ut_ref[...]).astype(BF)
    wide_ref[...] = wide
    utp = dot(half_pick.astype(BF), ut_ref[...])
    utp_ref[...] = utp.astype(BF)
    u_ref[...] = utp.T.astype(BF)
    own_ref[...] = dot_nt(x_ref[...], wide).astype(BF).astype(F32)
    shift = ring_shift()
    ring_ref[0] = to_ring(load_flat(one_ref, flat), shift)
    ring_ref[1] = to_ring(load_flat(two_ref, flat), shift)


def stack_rows(tiles, out_ref):
    for b in range(3):
        out_ref[b, 0:48, :] = jnp.zeros((48, 256), BF)
        out_ref[b, 192:240, :] = jnp.zeros((48, 256), BF)
        for f in range(FRAMES):
            rows = tiles[f, b : b + ROWS].reshape(48, 256)
            out_ref[b, 48 * f + 48 : 48 * f + 96, :] = rows.astype(BF)


def rank_kernel(_, own_ref, wide_ref, above_ref, below_ref, two_ref, one_ref, q_ref, tiles, edge, rims):
    wide = wide_ref[...]

    def project(v):
        return dot_nt(v.astype(BF), wide).astype(BF).astype(F32)

    rims[0] = project(above_ref[...])
    rims[1] = project(below_ref[...])
    right, left = even_first("cols", project(two_ref[...]), project(one_ref[...]))
    edge[0] = left
    edge[1] = right
    for f in range(FRAMES):
        for y in range(8):
            k = 8 * f + y
            if y in (0, 7):
                tile = rims[y // 7, 8 * f : 8 * f + 8, :]
            else:
                at = 48 * f + 8 * (y - 1)
                tile = own_ref[at : at + 8, :]
            left = jnp.broadcast_to(edge[0, k : k + 1, :], (8, 256))
            right = jnp.broadcast_to(edge[1, k : k + 1, :], (8, 256))
            tiles[f, y] = shifted(tile, left, right, (32, 64), 128)
    stack_rows(tiles, q_ref)


def core_index(shape):
    return jnp.full(shape, lax.rem(lax.axis_index("rows"), 2), jnp.int32)


def gather_table(mine_ref, other_ref, take_ref, kind_ref, table_ref):
    kind = kind_ref[...]
    take = take_ref[...]
    first = core_index((128, 128)) == 0
    for g in range(4):
        mine, other = mine_ref[128 * g : 128 * g + 128, :], other_ref[128 * g : 128 * g + 128, :]
        block = jnp.concatenate([jnp.where(first, mine, other), jnp.where(first, other, mine)], axis=0)
        none = jnp.zeros_like(block)
        both = jnp.concatenate(
            [jnp.where(kind == 0, block, none), jnp.where(kind == 1, block, none)], axis=0
        )
        table_ref[216 * g : 216 * g + 216, :] = dot(take, both)


def inside(lanes, at):
    return (lanes >= at) & (lanes < at + 64)


def gradient_blocks(half, grads, pixels, give_ref, kind_ref, blocks):
    wrapped = kind_ref[0:128, :] == 1
    for g in range(4):
        source = grads[216 * g : 216 * g + 216, :].astype(BF)
        part = dot(give_ref[half], source)
        blocks[128 * g : 128 * g + 128, :] = jnp.where(wrapped, part[128:256], part[0:128])
    lanes = lane((16, 128))
    row = lax.axis_index("rows")
    for a, (c, j, at) in enumerate(RELAYS):
        slot = sublane((16, 128)) + 16 * a
        across = ((slot < 48) | (slot >= 84)).astype(jnp.int32)
        goes = lax.rem(jnp.full((16, 128), row + half, jnp.int32) + across, 2) == 0
        pixel = jnp.where(goes, pixels[16 * a : 16 * a + 16, :], 0.0)
        if at % 64:
            pixel = pltpu.roll(pixel, at, axis=1)
        spot = pl.ds(4 * c + j, 16, stride=32)
        blocks[spot, :] = jnp.where(inside(lanes, at), pixel, blocks[spot, :])


def table_kernel(mine_ref, other_ref, take_ref, kind_ref, table_out, weights_ref, table):
    gather_table(mine_ref, other_ref, take_ref, kind_ref, table)
    table_out[...] = table[...].astype(BF)
    none = jnp.zeros((32, 64), BF)
    for k in range(9):
        part = table[96 * k : 96 * k + 96, :]
        weights_ref[k, 0:96, :] = part[:, 0:64].astype(BF)
        weights_ref[k, 96:128, :] = none
        weights_ref[k, 128:224, :] = part[:, 64:128].astype(BF)
        weights_ref[k, 224:256, :] = none


def forward_kernel(
    weights_ref, q_ref, cot_ref, ot_ref, give_ref, kind_ref, send_ref, grads, pixels, outp_ref, border, blocks
):
    total = jnp.zeros((CELLS, 64), F32)
    for a in range(3):
        for b in range(3):
            total = total + dot(q_ref[b, 48 * a : 48 * a + CELLS, :], weights_ref[3 * a + b])
    mid = total.astype(BF)
    pre = dot(mid, ot_ref[...])
    sig = jax.nn.sigmoid(pre)
    slope = (cot_ref[...].astype(F32) * sig * (1.0 + pre * (1.0 - sig))).astype(BF)
    ot = ot_ref[...]
    out_t = dot_nt(ot, slope).astype(BF)
    wide = jnp.concatenate([ot, ot, ot, ot], axis=0)
    outp = dot_nt(slope, wide).astype(BF).astype(F32)
    outp_ref[...] = outp
    border[...] = outp[:, 0:128]
    for f in range(FRAMES):
        pixels[8 * f : 8 * f + 8, :] = border[48 * f : 48 * f + 8, :]
        pixels[24 + 8 * f : 32 + 8 * f, :] = border[48 * f + 40 : 48 * f + 48, :]
    pixels[48:66, :] = border[pl.ds(0, 18, stride=8), :]
    pixels[66:84, :] = border[pl.ds(7, 18, stride=8), :]
    for k, cell in enumerate((0, 7, 40, 47)):
        pixels[84 + 3 * k : 87 + 3 * k, :] = border[pl.ds(cell, 3, stride=48), :]
    for a in range(3):
        for b in range(3):
            k = 3 * a + b
            part = dot(out_t, q_ref[b, 48 * a : 48 * a + CELLS, :])
            stack = jnp.concatenate([part[:, 0:128], part[:, 128:256]], axis=0)
            grads[96 * k : 96 * k + 96, :] = stack.T[0:96, :]
    gradient_blocks(1 - lax.rem(lax.axis_index("rows"), 2), grads, pixels, give_ref, kind_ref, blocks)
    send_ref[...] = blocks[...].astype(BF)


def keep_kernel(grads, pixels, give_ref, kind_ref, keep_ref):
    gradient_blocks(lax.rem(lax.axis_index("rows"), 2), grads, pixels, give_ref, kind_ref, keep_ref)


def add_kernel(keep_ref, got_ref, send_ref):
    send_ref[...] = (keep_ref[...] + got_ref[...].astype(F32)).astype(BF)


def adam_kernel(got_ref, core_ref, ring_ref, send_ref, next_ref, passed):
    total = jnp.zeros((8, 128), F32)
    passed[0:40, :] = jnp.zeros((40, 128), F32)
    passed[552:592, :] = jnp.zeros((40, 128), F32)
    for g in range(4):
        part = got_ref[128 * g : 128 * g + 128, :].astype(F32)
        passed[128 * g + 40 : 128 * g + 168, :] = part
        total = total + part.reshape(16, 8, 128).sum(axis=0)
    grad = (total[0:4] + total[4:8]) * (1.0 / 192.0)
    core, one, two = core_ref[...], ring_ref[0], ring_ref[1]
    one = beta_one * one + (1.0 - beta_one) * grad
    two = beta_two * two + (1.0 - beta_two) * grad * grad
    core = core - learn_rate * (one / fix_one) / (jnp.sqrt(two / fix_two) + epsilon)
    next_ref[0] = core
    next_ref[1] = one
    next_ref[2] = two
    own = jnp.where(in_ring(ring_shift()), core, 0.0)
    own = jnp.concatenate([own, own], axis=0)
    row, col = lax.axis_index("rows"), lax.axis_index("cols")
    slot, parity, mask = lax.div(row, 2), lax.rem(row, 2), jnp.zeros((8, 128), jnp.bool_)
    for a, (c, j, at) in enumerate(RELAYS):
        slot = slot + jnp.where(col == c, 16 * a, 0)
        spot = (sublane((8, 128)) % 4 == j) & inside(lane((8, 128)), at)
        mask = mask | (spot & (jnp.full((8, 128), col, jnp.int32) == c))
    up, right = 0, 0
    for first, count, rows, cols in SLOTS:
        here = (slot >= first) & (slot < first + count)
        up = up + jnp.where(here, rows, 0)
        right = right + jnp.where(here, cols, 0)
    source = lax.rem(parity - up + 2, 2)
    chips = lax.div(source + up - parity + 2, 2) - 1
    start = 40 - 4 * (8 * chips + right)
    for k in range(32):
        upper = passed[pl.ds(start + 16 * k, 8), :]
        lower = passed[pl.ds(start + 16 * k + 8, 8), :]
        block = jnp.concatenate([jnp.where(mask, upper, own), jnp.where(mask, lower, own)], axis=0)
        send_ref[16 * k : 16 * k + 16, :] = block.astype(BF)


def flat_kernel(next_ref, core_ref, one_ref, two_ref):
    shift = ring_shift()
    for k, ref in enumerate((core_ref, one_ref, two_ref)):
        store_flat(ref, from_ring(next_ref[k], shift))


def turn_kernel(table_ref, back_ref):
    for k in range(9):
        for c in range(3):
            t = 3 * k + c
            part = table_ref[32 * t : 32 * t + 32, :].astype(F32).T
            cube = jnp.concatenate([part[0:64], part[64:128]], axis=1)
            back_ref[k, 64 * (2 - c) : 64 * (2 - c) + 64, :] = cube.astype(BF)


def backward_kernel(mine_ref, outp_ref, back_ref, utp_ref, grad_ref, got, pixels, tiles, qs):
    row, col = lax.axis_index("rows"), lax.axis_index("cols")
    got[...] = mine_ref[...].astype(F32)
    for a, (c, j, at) in enumerate(RELAYS):
        pixel = got[pl.ds(4 * c + j, 16, stride=32), :]
        pixels[16 * a : 16 * a + 16, 0:128] = pltpu.roll(pixel, 128 - at, axis=1) if at else pixel
    spread = (sublane((64, 256)) == lane((64, 256)) % 64).astype(BF)
    pixels[...] = dot(pixels[:, 0:64].astype(BF), spread)
    zero = jnp.zeros((8, 256), F32)

    def kept(flag, v):
        return jnp.where(jnp.full((8, 256), flag.astype(jnp.int32), jnp.int32) > 0, v, zero)

    def spot(k):
        return jnp.broadcast_to(pixels[k : k + 1, :], (8, 256))

    for f in range(FRAMES):
        for y in range(8):
            if y == 0:
                tile, left, right = pixels[24 + 8 * f : 32 + 8 * f, :], spot(93 + f), spot(90 + f)
            elif y == 7:
                tile, left, right = pixels[8 * f : 8 * f + 8, :], spot(87 + f), spot(84 + f)
            else:
                at = 48 * f + 8 * (y - 1)
                tile = outp_ref[at : at + 8, :]
                left, right = spot(66 + 6 * f + y - 1), spot(48 + 6 * f + y - 1)
            tile = shifted(tile, kept(col > 0, left), kept(col < 7, right), (64, 128), 256)
            if y == 0:
                tile = kept(row > 0, tile)
            elif y == 7:
                tile = kept(row < 31, tile)
            tiles[f, y] = tile
    stack_rows(tiles, qs)
    total = jnp.zeros((CELLS, 64), F32)
    for a in range(3):
        for b in range(3):
            rows = qs[2 - b, 48 * (2 - a) : 48 * (2 - a) + CELLS, :]
            total = total + dot(rows[:, 0:192], back_ref[3 * a + b])
    grad_ref[...] = dot(total.astype(BF), utp_ref[...]).astype(BF)

def build_kernel(mine_ref, other_ref, u_ref, ot_ref, take_ref, kind_ref, out_ref, table, half, result, sems):
    gather_table(mine_ref, other_ref, take_ref, kind_ref, table)
    cube = table[...].astype(BF)
    even = dot(cube[:, 0:64], ot_ref[...]).astype(BF)
    odd = dot(cube[:, 64:128], ot_ref[...]).astype(BF)
    for t in range(27):
        half[t, 0:32, :] = even[32 * t : 32 * t + 32]
        half[t, 32:64, :] = odd[32 * t : 32 * t + 32]
    u = u_ref[...]

    def store(a):
        part = pl.ds(3 * a, 3)
        return pltpu.make_async_copy(result.at[part], out_ref.at[part], sems.at[a])

    for a in range(9):
        for t in range(3 * a, 3 * a + 3):
            result[t] = dot(u, half[t]).astype(BF)
        store(a).start()
    for a in range(9):
        store(a).wait()


def call(kernel, args, outs, scratch, flops=10**7):
    def spec(far):
        return pl.BlockSpec(memory_space=pltpu.HBM if far else pltpu.VMEM)

    return pl.pallas_call(
        kernel,
        out_shape=[jax.ShapeDtypeStruct(shape, dtype) for shape, dtype, _ in outs],
        in_specs=[spec(far) for _, far in args],
        out_specs=[spec(far) for _, _, far in outs],
        scratch_shapes=scratch,
        compiler_params=pltpu.CompilerParams(vmem_limit_bytes=32 << 20),
        cost_estimate=pl.CostEstimate(flops=flops, bytes_accessed=10**5, transcendentals=0),
    )(*[pltpu.with_memory_space_constraint(arg, pltpu.HBM) if far else arg for arg, far in args])


def near(*args):
    return [(arg, False) for arg in args]


def far(*args):
    return [(arg, True) for arg in args]


def swap(one, two, axis):
    count = lax.axis_size(axis)
    pairs = [[(i, i + 1) for i in range(k, count - 1, 2)] for k in range(2)]
    two, one = (
        lax.ppermute(x, axis, forward + [(b, a) for a, b in forward]) for x, forward in ((two, pairs[1]), (one, pairs[0]))
    )
    return one, two


def device(k, chip, col):
    return 8 * (2 * chip + k) + col


ORDER = [[device(k, chip, col) for chip in range(16) for col in range(8)] for k in range(2)]


def exchange(x):
    return lax.all_to_all(x, AXES, 0, 0, tiled=True, axis_index_groups=ORDER)


def in_chip(x):
    return lax.ppermute(x, "rows", [(r, r ^ 1) for r in range(32)])


def body(frames_in, cotangent, core, moment_one, moment_two, u_in, u_out):
    take, give, kind = ring_tables()
    take, give, kind = jnp.asarray(take, BF), jnp.asarray(give, BF), jnp.asarray(kind, F32)
    vm, dma = pltpu.VMEM, pltpu.SemaphoreType.DMA
    rim = (FRAMES * 8, 256)
    row = (FRAMES, 8, 256)

    send, one, two, inner, core_ring, m_one, m_two, ut, ot, cot, take, give, kind = call(
        start_kernel,
        far(
            core, frames_in, moment_one, moment_two, u_in.T, u_out.T, cotangent.reshape(CELLS, 256), take, give, kind,
        ),
        [
            ((512, 128), BF, True), (row, BF, False), (row, BF, False), ((FRAMES, ROWS, COLS, 256), BF, False),
            ((4, 128), F32, False), ((OWN,), F32, False), ((OWN,), F32, False), ((64, 256), BF, False),
            ((64, 256), BF, False), ((CELLS, 256), BF, False), ((216, 512), BF, False), ((2, 256, 216), BF, False),
            ((256, 128), F32, False),
        ],
        [vm((OWN,), F32), vm((8, 128), F32), vm((128, 128), BF), dma((14,))],
    )
    one, two = swap(one, two, "rows")
    mine = exchange(send)
    above, below, one, two = call(
        columns_kernel,
        near(inner, two, one),
        [(rim, F32, False), (rim, F32, False), (rim, BF, False), (rim, BF, False)],
        [vm(rim, F32), vm(rim, F32)],
        flops=10**10,
    )
    own, wide, utp, u, ring = call(
        prepare_kernel,
        near(above, inner.reshape(CELLS, 256), ut, m_one, m_two),
        [
            ((CELLS, 256), F32, False), ((256, 256), BF, False), ((64, 256), BF, False), ((256, 64), BF, False),
            ((2, 4, 128), F32, False),
        ],
        [vm((8, 128), F32)],
        flops=10**10,
    )
    mine, _ = lax.optimization_barrier((mine, above))
    other = in_chip(mine)
    table, weights = call(
        table_kernel,
        near(mine, other, take, kind),
        [((TABLE, 128), BF, False), ((9, 256, 64), BF, False)],
        [vm((TABLE, 128), F32)],
        flops=10000000000,
    )
    one, two = swap(one, two, "cols")
    (q,) = call(
        rank_kernel,
        near(table, own, wide, above, below, two, one),
        [((3, 240, 256), BF, False)],
        [vm((FRAMES, 8, 8, 256), F32), vm((2, 24, 256), F32), vm((2, 24, 256), F32)],
        flops=10000000,
    )
    send, grads, pixels, outp = call(
        forward_kernel,
        near(weights, q, cot, ot, give, kind),
        [((512, 128), BF, False), ((TABLE, 128), F32, False), ((96, 128), F32, False), ((CELLS, 256), F32, False)],
        [vm((CELLS, 128), F32), vm((512, 128), F32)],
    )
    got = in_chip(send)
    (keep,) = call(keep_kernel, near(grads, pixels, give, kind), [((512, 128), F32, False)], [], flops=10**9)
    (send,) = call(add_kernel, near(keep, got), [((512, 128), BF, False)], [])
    got = exchange(send)
    send, latest = call(
        adam_kernel,
        near(got, core_ring, ring),
        [((512, 128), BF, False), ((3, 4, 128), F32, False)],
        [vm((592, 128), F32)],
    )
    mine = exchange(send)
    (back,) = call(turn_kernel, near(table), [((9, 192, 64), BF, False)], [])
    core_next, one_next, two_next = call(flat_kernel, near(latest), [((OWN,), F32, False)] * 3, [])
    mine, back, core_next, one_next, two_next = lax.optimization_barrier((mine, back, core_next, one_next, two_next))
    other = in_chip(mine)
    (frames_grad,) = call(
        backward_kernel,
        near(mine, outp, back, utp),
        [((CELLS, 256), BF, False)],
        [vm((512, 128), F32), vm((96, 256), F32), vm((FRAMES, 8, 8, 256), F32), vm((3, 240, 256), BF)],
        flops=10**9,
    )
    other, frames_grad = lax.optimization_barrier((other, frames_grad))
    (kernel_next,) = call(
        build_kernel,
        near(mine, other, u, ot, take, kind),
        [((27, 256, 256), BF, True)],
        [vm((TABLE, 128), F32), vm((27, 64, 256), BF), vm((27, 256, 256), BF), dma((9,))],
    )
    frames_grad = frames_grad.reshape(FRAMES, ROWS, COLS, 256)
    return frames_grad, core_next, one_next, two_next, kernel_next


def solution(mesh):
    in_specs = (
        P(None, "rows", "cols", None),
        P(None, "rows", "cols", None),
        P(AXES),
        P(AXES),
        P(AXES),
        P(),
        P(),
    )
    out_specs = (
        P(None, "rows", "cols", None),
        P(AXES),
        P(AXES),
        P(AXES),
        P(),
    )
    return jax.shard_map(body, mesh=mesh, in_specs=in_specs, out_specs=out_specs, check_vma=False)
```

```python
import jax
import jax.numpy as jnp
import numpy as np
from jax import lax
from jax.experimental import pallas as pl
from jax.experimental.pallas import tpu as pltpu
from jax.sharding import PartitionSpec as P

beta_one = 0.9
beta_two = 0.999
learn_rate = 0.06
epsilon = 1e-08
fix_one = 1.0 - 0.9**10
fix_two = 1.0 - 0.999**10

BF = jnp.bfloat16
F32 = jnp.float32
AXES = ("rows", "cols")

OWN = 432
FRAMES, ROWS, COLS = 3, 6, 8
CELLS = FRAMES * ROWS * COLS
SIDE = FRAMES * 8
TABLE = 864


RELAYS = ((7, 0, 0), (4, 0, 0), (3, 3, 64), (0, 3, 64), (2, 0, 16), (5, 0, 32))
SLOTS = (
    (0, 24, -1, 0), (24, 24, 1, 0), (48, 18, 0, -1), (66, 18, 0, 1),
    (84, 3, -1, -1), (87, 3, -1, 1), (90, 3, 1, -1), (93, 3, 1, 1),
)


def ring_tables():
    take = np.zeros((216, 512), np.float32)
    give = np.zeros((2, 256, 216), np.float32)
    kind = np.zeros((256, 128), np.float32)
    for r in range(8):
        for c in range(8):
            first = 27 * r + 27 * c // 8
            col = 128 * (r % 2) + 32 * (r // 2) + 4 * c
            for j in range(4):
                take[first + j, col + j] = 1
                give[r % 2, col % 128 + j, first + j] = 1
            wrapped = 48 * c % 128 + OWN - 512
            if wrapped > 0:
                take[first + 4, 256 + col] = 1
                give[r % 2, 128 + col % 128, first + 4] = 1
                kind[col, :wrapped] = 1
        for c, j, at in RELAYS:
            kind[128 * (r % 2) + 32 * (r // 2) + 4 * c + j, at : at + 64] = 2
    return take, give, kind


def dot(a, b):
    return jnp.dot(a, b, preferred_element_type=F32)


def dot_nt(a, b):
    return lax.dot_general(a, b, (((1,), (1,)), ((), ())), preferred_element_type=F32)


def dot_tn(a, b):
    return lax.dot_general(a, b, (((0,), (0,)), ((), ())), preferred_element_type=F32)


def lane(shape):
    return lax.broadcasted_iota(jnp.int32, shape, 1)


def sublane(shape):
    return lax.broadcasted_iota(jnp.int32, shape, 0)


def ring_shift():
    return lax.rem(lax.axis_index("cols") * 48, 128)


def to_ring(v, shift):
    turned = pltpu.roll(v, shift, axis=1)
    above = jnp.concatenate([turned[3:4], turned[0:3]], axis=0)
    return jnp.where(lane(v.shape) >= shift, turned, above)


def from_ring(v, shift):
    turned = pltpu.roll(v, lax.rem(128 - shift, 128), axis=1)
    below = jnp.concatenate([turned[1:4], turned[0:1]], axis=0)
    return jnp.where(lane(v.shape) < 128 - shift, turned, below)


def in_ring(shift):
    place = sublane((4, 128)) * 128 + lane((4, 128)) - shift
    place = jnp.where(place < 0, place + 512, place)
    return place < OWN


def load_flat(ref, scratch):
    scratch[...] = jnp.zeros_like(scratch)
    for k in range(3):
        scratch[k, :] = ref[pl.ds(128 * k, 128)]
    scratch[3, 0 : OWN - 384] = ref[pl.ds(384, OWN - 384)]
    return scratch[0:4, :]


def store_flat(ref, v):
    for k in range(3):
        ref[pl.ds(128 * k, 128)] = v[k]
    ref[pl.ds(384, OWN - 384)] = v[3, 0 : OWN - 384]


def fetch(pairs, sems):
    copies = [pltpu.make_async_copy(src, dst, sems.at[k]) for k, (src, dst) in enumerate(pairs)]
    for copy in copies:
        copy.start()
    return copies


def even_first(axis, first, last):
    even = jnp.full(first.shape, lax.rem(lax.axis_index(axis), 2), jnp.int32) == 0
    return jnp.where(even, last, first), jnp.where(even, first, last)


def start_kernel(
    core_ref, x_ref, one_ref, two_ref, ut_ref, ot_ref, cot_ref, take_ref, give_ref, kind_ref,
    send_ref, near_ref, far_ref, inner_ref, ring_ref, one_out, two_out, ut_out, ot_out, cot_out, take_out, give_out, kind_out,
    own, flat, block, sems,
):
    copies = fetch(
        (
            (core_ref, own), (x_ref, inner_ref), (one_ref, one_out), (two_ref, two_out), (ut_ref, ut_out),
            (ot_ref, ot_out), (take_ref, take_out), (kind_ref, kind_out), (give_ref, give_out), (cot_ref, cot_out),
        ),
        sems,
    )
    copies[0].wait()
    v = to_ring(load_flat(own, flat), ring_shift())
    ring_ref[...] = v
    rows = jnp.concatenate([v, v, v, v], axis=0).astype(BF)
    for k in range(8):
        block[16 * k : 16 * k + 16, :] = rows
    sends = fetch([(block, send_ref.at[pl.ds(128 * k, 128)]) for k in range(4)], sems.at[pl.ds(10, 4)])
    copies[1].wait()
    for f in range(FRAMES):
        first, last = inner_ref[f, 0].astype(F32), inner_ref[f, ROWS - 1].astype(F32)
        one, two = even_first("rows", first, last)
        near_ref[f] = one.astype(BF)
        far_ref[f] = two.astype(BF)
    for copy in copies[2:] + sends:
        copy.wait()


def columns_kernel(inner_ref, two_ref, one_ref, above_ref, below_ref, left_ref, right_ref, low, high):
    for f in range(FRAMES):
        below, above = even_first("rows", two_ref[f].astype(F32), one_ref[f].astype(F32))
        above_ref[8 * f : 8 * f + 8, :] = above
        below_ref[8 * f : 8 * f + 8, :] = below
        for y in range(8):
            tile = above if y == 0 else below if y == 7 else inner_ref[f, y - 1].astype(F32)
            low[8 * f + y : 8 * f + y + 1, :] = tile[0:1, :]
            high[8 * f + y : 8 * f + y + 1, :] = tile[7:8, :]
    one, two = even_first("cols", low[...], high[...])
    left_ref[...] = one.astype(BF)
    right_ref[...] = two.astype(BF)


def shifted(tile, left, right, bounds, period):
    at = lane(tile.shape) % period
    row = sublane(tile.shape)
    back = jnp.where(row == 0, left, pltpu.roll(tile, 1, axis=0))
    ahead = jnp.where(row == 7, right, pltpu.roll(tile, 7, axis=0))
    return jnp.where(at < bounds[0], back, jnp.where(at < bounds[1], tile, ahead))


def prepare_kernel(_, x_ref, ut_ref, one_ref, two_ref, own_ref, wide_ref, utp_ref, u_ref, ring_ref, flat):
    row = sublane((256, 64))
    at = row % 128
    pick = (lane((256, 64)) == (at % 32) * 2 + row // 128) & (at < 96)
    half_row = sublane((64, 64))
    half_pick = lane((64, 64)) == (half_row % 32) * 2 + half_row // 32
    wide = dot(pick.astype(BF), ut_ref[...]).astype(BF)
    wide_ref[...] = wide
    utp = dot(half_pick.astype(BF), ut_ref[...])
    utp_ref[...] = utp.astype(BF)
    u_ref[...] = utp.T.astype(BF)
    own_ref[...] = dot_nt(x_ref[...], wide).astype(BF).astype(F32)
    shift = ring_shift()
    ring_ref[0] = to_ring(load_flat(one_ref, flat), shift)
    ring_ref[1] = to_ring(load_flat(two_ref, flat), shift)


def stack_rows(tiles, out_ref):
    for b in range(3):
        out_ref[b, 0:48, :] = jnp.zeros((48, 256), BF)
        out_ref[b, 192:240, :] = jnp.zeros((48, 256), BF)
        for f in range(FRAMES):
            rows = tiles[f, b : b + ROWS].reshape(48, 256)
            out_ref[b, 48 * f + 48 : 48 * f + 96, :] = rows.astype(BF)


def stack_inputs(own_ref, wide_ref, above_ref, below_ref, two_ref, one_ref, q_ref, tiles, edge, rims):
    wide = wide_ref[...]

    def project(v):
        return dot_nt(v.astype(BF), wide).astype(BF).astype(F32)

    rims[0] = project(above_ref[...])
    rims[1] = project(below_ref[...])
    right, left = even_first("cols", project(two_ref[...]), project(one_ref[...]))
    edge[0] = left
    edge[1] = right
    for f in range(FRAMES):
        for y in range(8):
            k = 8 * f + y
            if y in (0, 7):
                tile = rims[y // 7, 8 * f : 8 * f + 8, :]
            else:
                at = 48 * f + 8 * (y - 1)
                tile = own_ref[at : at + 8, :]
            left = jnp.broadcast_to(edge[0, k : k + 1, :], (8, 256))
            right = jnp.broadcast_to(edge[1, k : k + 1, :], (8, 256))
            tiles[f, y] = shifted(tile, left, right, (32, 64), 128)
    stack_rows(tiles, q_ref)


def core_index(shape):
    return jnp.full(shape, lax.rem(lax.axis_index("rows"), 2), jnp.int32)


def gather_table(mine_ref, other_ref, take_ref, kind_ref, table_ref):
    kind = kind_ref[...]
    take = take_ref[...]
    first = core_index((128, 128)) == 0
    for g in range(4):
        mine, other = mine_ref[128 * g : 128 * g + 128, :], other_ref[128 * g : 128 * g + 128, :]
        block = jnp.concatenate([jnp.where(first, mine, other), jnp.where(first, other, mine)], axis=0)
        none = jnp.zeros_like(block)
        both = jnp.concatenate(
            [jnp.where(kind == 0, block, none), jnp.where(kind == 1, block, none)], axis=0
        )
        table_ref[216 * g : 216 * g + 216, :] = dot(take, both)


def inside(lanes, at):
    return (lanes >= at) & (lanes < at + 64)


def gradient_blocks(half, grads, pixels, give_ref, kind_ref, blocks):
    wrapped = kind_ref[0:128, :] == 1
    for g in range(4):
        source = grads[216 * g : 216 * g + 216, :].astype(BF)
        part = dot(give_ref[half], source)
        blocks[128 * g : 128 * g + 128, :] = jnp.where(wrapped, part[128:256], part[0:128])
    lanes = lane((16, 128))
    row = lax.axis_index("rows")
    for a, (c, j, at) in enumerate(RELAYS):
        slot = sublane((16, 128)) + 16 * a
        across = ((slot < 48) | (slot >= 84)).astype(jnp.int32)
        goes = lax.rem(jnp.full((16, 128), row + half, jnp.int32) + across, 2) == 0
        pixel = jnp.where(goes, pixels[16 * a : 16 * a + 16, :], 0.0)
        if at % 64:
            pixel = pltpu.roll(pixel, at, axis=1)
        spot = pl.ds(4 * c + j, 16, stride=32)
        blocks[spot, :] = jnp.where(inside(lanes, at), pixel, blocks[spot, :])


def table_kernel(mine_ref, other_ref, take_ref, kind_ref, table_out, weights_ref, table):
    gather_table(mine_ref, other_ref, take_ref, kind_ref, table)
    table_out[...] = table[...].astype(BF)
    none = jnp.zeros((32, 64), BF)
    for k in range(9):
        part = table[96 * k : 96 * k + 96, :]
        weights_ref[k, 0:96, :] = part[:, 0:64].astype(BF)
        weights_ref[k, 96:128, :] = none
        weights_ref[k, 128:224, :] = part[:, 64:128].astype(BF)
        weights_ref[k, 224:256, :] = none


def forward_kernel(
    own_ref, wide_ref, above_ref, below_ref, two_ref, one_ref, weights_ref, cot_ref, ot_ref, give_ref, kind_ref,
    send_ref, grads, pixels, outp_ref, border, blocks, q_ref, tiles, edge, rims,
):
    stack_inputs(own_ref, wide_ref, above_ref, below_ref, two_ref, one_ref, q_ref, tiles, edge, rims)
    total = jnp.zeros((CELLS, 64), F32)
    for a in range(3):
        for b in range(3):
            total = total + dot(q_ref[b, 48 * a : 48 * a + CELLS, :], weights_ref[3 * a + b])
    mid = total.astype(BF)
    pre = dot(mid, ot_ref[...])
    sig = jax.nn.sigmoid(pre)
    slope = (cot_ref[...].astype(F32) * sig * (1.0 + pre * (1.0 - sig))).astype(BF)
    ot = ot_ref[...]
    out_t = dot_nt(ot, slope).astype(BF)
    wide = jnp.concatenate([ot, ot, ot, ot], axis=0)
    outp = dot_nt(slope, wide).astype(BF).astype(F32)
    outp_ref[...] = outp
    border[...] = outp[:, 0:128]
    for f in range(FRAMES):
        pixels[8 * f : 8 * f + 8, :] = border[48 * f : 48 * f + 8, :]
        pixels[24 + 8 * f : 32 + 8 * f, :] = border[48 * f + 40 : 48 * f + 48, :]
    pixels[48:66, :] = border[pl.ds(0, 18, stride=8), :]
    pixels[66:84, :] = border[pl.ds(7, 18, stride=8), :]
    for k, cell in enumerate((0, 7, 40, 47)):
        pixels[84 + 3 * k : 87 + 3 * k, :] = border[pl.ds(cell, 3, stride=48), :]
    for a in range(3):
        for b in range(3):
            k = 3 * a + b
            part = dot(out_t, q_ref[b, 48 * a : 48 * a + CELLS, :])
            stack = jnp.concatenate([part[:, 0:128], part[:, 128:256]], axis=0)
            grads[96 * k : 96 * k + 96, :] = stack.T[0:96, :]
    gradient_blocks(1 - lax.rem(lax.axis_index("rows"), 2), grads, pixels, give_ref, kind_ref, blocks)
    send_ref[...] = blocks[...].astype(BF)


def keep_kernel(grads, pixels, give_ref, kind_ref, keep_ref):
    gradient_blocks(lax.rem(lax.axis_index("rows"), 2), grads, pixels, give_ref, kind_ref, keep_ref)


def add_kernel(keep_ref, got_ref, send_ref):
    send_ref[...] = (keep_ref[...] + got_ref[...].astype(F32)).astype(BF)


def adam_kernel(got_ref, core_ref, ring_ref, send_ref, next_ref, passed):
    total = jnp.zeros((8, 128), F32)
    passed[0:40, :] = jnp.zeros((40, 128), F32)
    passed[552:592, :] = jnp.zeros((40, 128), F32)
    for g in range(4):
        part = got_ref[128 * g : 128 * g + 128, :].astype(F32)
        passed[128 * g + 40 : 128 * g + 168, :] = part
        total = total + part.reshape(16, 8, 128).sum(axis=0)
    grad = (total[0:4] + total[4:8]) * (1.0 / 192.0)
    core, one, two = core_ref[...], ring_ref[0], ring_ref[1]
    one = beta_one * one + (1.0 - beta_one) * grad
    two = beta_two * two + (1.0 - beta_two) * grad * grad
    core = core - learn_rate * (one / fix_one) / (jnp.sqrt(two / fix_two) + epsilon)
    next_ref[0] = core
    next_ref[1] = one
    next_ref[2] = two
    own = jnp.where(in_ring(ring_shift()), core, 0.0)
    own = jnp.concatenate([own, own], axis=0)
    row, col = lax.axis_index("rows"), lax.axis_index("cols")
    slot, parity, mask = lax.div(row, 2), lax.rem(row, 2), jnp.zeros((8, 128), jnp.bool_)
    for a, (c, j, at) in enumerate(RELAYS):
        slot = slot + jnp.where(col == c, 16 * a, 0)
        spot = (sublane((8, 128)) % 4 == j) & inside(lane((8, 128)), at)
        mask = mask | (spot & (jnp.full((8, 128), col, jnp.int32) == c))
    up, right = 0, 0
    for first, count, rows, cols in SLOTS:
        here = (slot >= first) & (slot < first + count)
        up = up + jnp.where(here, rows, 0)
        right = right + jnp.where(here, cols, 0)
    source = lax.rem(parity - up + 2, 2)
    chips = lax.div(source + up - parity + 2, 2) - 1
    start = 40 - 4 * (8 * chips + right)
    for k in range(32):
        upper = passed[pl.ds(start + 16 * k, 8), :]
        lower = passed[pl.ds(start + 16 * k + 8, 8), :]
        block = jnp.concatenate([jnp.where(mask, upper, own), jnp.where(mask, lower, own)], axis=0)
        send_ref[16 * k : 16 * k + 16, :] = block.astype(BF)


def flat_kernel(next_ref, core_ref, one_ref, two_ref):
    shift = ring_shift()
    for k, ref in enumerate((core_ref, one_ref, two_ref)):
        store_flat(ref, from_ring(next_ref[k], shift))


def turn_kernel(table_ref, back_ref):
    for k in range(9):
        for c in range(3):
            t = 3 * k + c
            part = table_ref[32 * t : 32 * t + 32, :].astype(F32).T
            cube = jnp.concatenate([part[0:64], part[64:128]], axis=1)
            back_ref[k, 64 * (2 - c) : 64 * (2 - c) + 64, :] = cube.astype(BF)


def backward_kernel(mine_ref, outp_ref, back_ref, utp_ref, grad_ref, got, pixels, tiles, qs):
    row, col = lax.axis_index("rows"), lax.axis_index("cols")
    got[...] = mine_ref[...].astype(F32)
    for a, (c, j, at) in enumerate(RELAYS):
        pixel = got[pl.ds(4 * c + j, 16, stride=32), :]
        pixels[16 * a : 16 * a + 16, 0:128] = pltpu.roll(pixel, 128 - at, axis=1) if at else pixel
    spread = (sublane((64, 256)) == lane((64, 256)) % 64).astype(BF)
    pixels[...] = dot(pixels[:, 0:64].astype(BF), spread)
    zero = jnp.zeros((8, 256), F32)

    def kept(flag, v):
        return jnp.where(jnp.full((8, 256), flag.astype(jnp.int32), jnp.int32) > 0, v, zero)

    def spot(k):
        return jnp.broadcast_to(pixels[k : k + 1, :], (8, 256))

    for f in range(FRAMES):
        for y in range(8):
            if y == 0:
                tile, left, right = pixels[24 + 8 * f : 32 + 8 * f, :], spot(93 + f), spot(90 + f)
            elif y == 7:
                tile, left, right = pixels[8 * f : 8 * f + 8, :], spot(87 + f), spot(84 + f)
            else:
                at = 48 * f + 8 * (y - 1)
                tile = outp_ref[at : at + 8, :]
                left, right = spot(66 + 6 * f + y - 1), spot(48 + 6 * f + y - 1)
            tile = shifted(tile, kept(col > 0, left), kept(col < 7, right), (64, 128), 256)
            if y == 0:
                tile = kept(row > 0, tile)
            elif y == 7:
                tile = kept(row < 31, tile)
            tiles[f, y] = tile
    stack_rows(tiles, qs)
    total = jnp.zeros((CELLS, 64), F32)
    for a in range(3):
        for b in range(3):
            rows = qs[2 - b, 48 * (2 - a) : 48 * (2 - a) + CELLS, :]
            total = total + dot(rows[:, 0:192], back_ref[3 * a + b])
    grad_ref[...] = dot(total.astype(BF), utp_ref[...]).astype(BF)

def build_kernel(mine_ref, other_ref, u_ref, ot_ref, take_ref, kind_ref, out_ref, table, half, result, sems):
    gather_table(mine_ref, other_ref, take_ref, kind_ref, table)
    cube = table[...].astype(BF)
    even = dot(cube[:, 0:64], ot_ref[...]).astype(BF)
    odd = dot(cube[:, 64:128], ot_ref[...]).astype(BF)
    for t in range(27):
        half[t, 0:32, :] = even[32 * t : 32 * t + 32]
        half[t, 32:64, :] = odd[32 * t : 32 * t + 32]
    u = u_ref[...]

    def store(a):
        part = pl.ds(3 * a, 3)
        return pltpu.make_async_copy(result.at[part], out_ref.at[part], sems.at[a])

    for a in range(9):
        for t in range(3 * a, 3 * a + 3):
            result[t] = dot(u, half[t]).astype(BF)
        store(a).start()
    for a in range(9):
        store(a).wait()


def call(kernel, args, outs, scratch, flops=10**7):
    def spec(far):
        return pl.BlockSpec(memory_space=pltpu.HBM if far else pltpu.VMEM)

    return pl.pallas_call(
        kernel,
        out_shape=[jax.ShapeDtypeStruct(shape, dtype) for shape, dtype, _ in outs],
        in_specs=[spec(far) for _, far in args],
        out_specs=[spec(far) for _, _, far in outs],
        scratch_shapes=scratch,
        compiler_params=pltpu.CompilerParams(vmem_limit_bytes=32 << 20),
        cost_estimate=pl.CostEstimate(flops=flops, bytes_accessed=10**5, transcendentals=0),
    )(*[pltpu.with_memory_space_constraint(arg, pltpu.HBM) if far else arg for arg, far in args])


def near(*args):
    return [(arg, False) for arg in args]


def far(*args):
    return [(arg, True) for arg in args]


def swap(one, two, axis):
    count = lax.axis_size(axis)
    pairs = [[(i, i + 1) for i in range(k, count - 1, 2)] for k in range(2)]
    two, one = (
        lax.ppermute(x, axis, forward + [(b, a) for a, b in forward]) for x, forward in ((two, pairs[1]), (one, pairs[0]))
    )
    return one, two


def device(k, chip, col):
    return 8 * (2 * chip + k) + col


ORDER = [[device(k, chip, col) for chip in range(16) for col in range(8)] for k in range(2)]


def exchange(x):
    return lax.all_to_all(x, AXES, 0, 0, tiled=True, axis_index_groups=ORDER)


def in_chip(x):
    return lax.ppermute(x, "rows", [(r, r ^ 1) for r in range(32)])


def body(frames_in, cotangent, core, moment_one, moment_two, u_in, u_out):
    take, give, kind = ring_tables()
    take, give, kind = jnp.asarray(take, BF), jnp.asarray(give, BF), jnp.asarray(kind, F32)
    vm, dma = pltpu.VMEM, pltpu.SemaphoreType.DMA
    rim = (FRAMES * 8, 256)
    row = (FRAMES, 8, 256)

    send, one, two, inner, core_ring, m_one, m_two, ut, ot, cot, take, give, kind = call(
        start_kernel,
        far(
            core, frames_in, moment_one, moment_two, u_in.T, u_out.T, cotangent.reshape(CELLS, 256), take, give, kind,
        ),
        [
            ((512, 128), BF, True), (row, BF, False), (row, BF, False), ((FRAMES, ROWS, COLS, 256), BF, False),
            ((4, 128), F32, False), ((OWN,), F32, False), ((OWN,), F32, False), ((64, 256), BF, False),
            ((64, 256), BF, False), ((CELLS, 256), BF, False), ((216, 512), BF, False), ((2, 256, 216), BF, False),
            ((256, 128), F32, False),
        ],
        [vm((OWN,), F32), vm((8, 128), F32), vm((128, 128), BF), dma((14,))],
    )
    one, two = swap(one, two, "rows")
    mine = exchange(send)
    above, below, one, two = call(
        columns_kernel,
        near(inner, two, one),
        [(rim, F32, False), (rim, F32, False), (rim, BF, False), (rim, BF, False)],
        [vm(rim, F32), vm(rim, F32)],
        flops=10**10,
    )
    own, wide, utp, u, ring = call(
        prepare_kernel,
        near(above, inner.reshape(CELLS, 256), ut, m_one, m_two),
        [
            ((CELLS, 256), F32, False), ((256, 256), BF, False), ((64, 256), BF, False), ((256, 64), BF, False),
            ((2, 4, 128), F32, False),
        ],
        [vm((8, 128), F32)],
        flops=10**10,
    )
    mine, _ = lax.optimization_barrier((mine, above))
    other = in_chip(mine)
    table, weights = call(
        table_kernel,
        near(mine, other, take, kind),
        [((TABLE, 128), BF, False), ((9, 256, 64), BF, False)],
        [vm((TABLE, 128), F32)],
        flops=10000000000,
    )
    one, two = swap(one, two, "cols")
    send, grads, pixels, outp = call(
        forward_kernel,
        near(own, wide, above, below, two, one, weights, cot, ot, give, kind),
        [((512, 128), BF, False), ((TABLE, 128), F32, False), ((96, 128), F32, False), ((CELLS, 256), F32, False)],
        [
            vm((CELLS, 128), F32), vm((512, 128), F32), vm((3, 240, 256), BF), vm((FRAMES, 8, 8, 256), F32),
            vm((2, SIDE, 256), F32), vm((2, SIDE, 256), F32),
        ],
        flops=10**7,
    )
    got = in_chip(send)
    (keep,) = call(keep_kernel, near(grads, pixels, give, kind), [((512, 128), F32, False)], [], flops=10**9)
    (send,) = call(add_kernel, near(keep, got), [((512, 128), BF, False)], [])
    got = exchange(send)
    send, latest = call(
        adam_kernel,
        near(got, core_ring, ring),
        [((512, 128), BF, False), ((3, 4, 128), F32, False)],
        [vm((592, 128), F32)],
    )
    mine = exchange(send)
    (back,) = call(turn_kernel, near(table), [((9, 192, 64), BF, False)], [])
    core_next, one_next, two_next = call(flat_kernel, near(latest), [((OWN,), F32, False)] * 3, [])
    mine, back, core_next, one_next, two_next = lax.optimization_barrier((mine, back, core_next, one_next, two_next))
    other = in_chip(mine)
    (frames_grad,) = call(
        backward_kernel,
        near(mine, outp, back, utp),
        [((CELLS, 256), BF, False)],
        [vm((512, 128), F32), vm((96, 256), F32), vm((FRAMES, 8, 8, 256), F32), vm((3, 240, 256), BF)],
        flops=10**9,
    )
    other, frames_grad = lax.optimization_barrier((other, frames_grad))
    (kernel_next,) = call(
        build_kernel,
        near(mine, other, u, ot, take, kind),
        [((27, 256, 256), BF, True)],
        [vm((TABLE, 128), F32), vm((27, 64, 256), BF), vm((27, 256, 256), BF), dma((9,))],
    )
    frames_grad = frames_grad.reshape(FRAMES, ROWS, COLS, 256)
    return frames_grad, core_next, one_next, two_next, kernel_next


def solution(mesh):
    in_specs = (
        P(None, "rows", "cols", None),
        P(None, "rows", "cols", None),
        P(AXES),
        P(AXES),
        P(AXES),
        P(),
        P(),
    )
    out_specs = (
        P(None, "rows", "cols", None),
        P(AXES),
        P(AXES),
        P(AXES),
        P(),
    )
    return jax.shard_map(body, mesh=mesh, in_specs=in_specs, out_specs=out_specs, check_vma=False)
```

```python
import jax
import jax.numpy as jnp
import numpy as np
from jax import lax
from jax.experimental import pallas as pl
from jax.experimental.pallas import tpu as pltpu
from jax.sharding import PartitionSpec as P

beta_one = 0.9
beta_two = 0.999
learn_rate = 0.06
epsilon = 1e-08
fix_one = 1.0 - 0.9**10
fix_two = 1.0 - 0.999**10

BF = jnp.bfloat16
F32 = jnp.float32
AXES = ("rows", "cols")

OWN = 432
FRAMES, ROWS, COLS = 3, 6, 8
CELLS = FRAMES * ROWS * COLS
SIDE = FRAMES * 8
TABLE = 864


RELAYS = ((7, 0, 0), (4, 0, 0), (3, 3, 64), (0, 3, 64), (2, 0, 16), (5, 0, 32))
SLOTS = (
    (0, 24, -1, 0), (24, 24, 1, 0), (48, 18, 0, -1), (66, 18, 0, 1),
    (84, 3, -1, -1), (87, 3, -1, 1), (90, 3, 1, -1), (93, 3, 1, 1),
)


def ring_tables():
    take = np.zeros((216, 512), np.float32)
    give = np.zeros((2, 256, 216), np.float32)
    kind = np.zeros((256, 128), np.float32)
    for r in range(8):
        for c in range(8):
            first = 27 * r + 27 * c // 8
            col = 128 * (r % 2) + 32 * (r // 2) + 4 * c
            for j in range(4):
                take[first + j, col + j] = 1
                give[r % 2, col % 128 + j, first + j] = 1
            wrapped = 48 * c % 128 + OWN - 512
            if wrapped > 0:
                take[first + 4, 256 + col] = 1
                give[r % 2, 128 + col % 128, first + 4] = 1
                kind[col, :wrapped] = 1
        for c, j, at in RELAYS:
            kind[128 * (r % 2) + 32 * (r // 2) + 4 * c + j, at : at + 64] = 2
    return take, give, kind


def dot(a, b):
    return jnp.dot(a, b, preferred_element_type=F32)


def dot_nt(a, b):
    return lax.dot_general(a, b, (((1,), (1,)), ((), ())), preferred_element_type=F32)


def dot_tn(a, b):
    return lax.dot_general(a, b, (((0,), (0,)), ((), ())), preferred_element_type=F32)


def lane(shape):
    return lax.broadcasted_iota(jnp.int32, shape, 1)


def sublane(shape):
    return lax.broadcasted_iota(jnp.int32, shape, 0)


def ring_shift():
    return lax.rem(lax.axis_index("cols") * 48, 128)


def to_ring(v, shift):
    turned = pltpu.roll(v, shift, axis=1)
    above = jnp.concatenate([turned[3:4], turned[0:3]], axis=0)
    return jnp.where(lane(v.shape) >= shift, turned, above)


def from_ring(v, shift):
    turned = pltpu.roll(v, lax.rem(128 - shift, 128), axis=1)
    below = jnp.concatenate([turned[1:4], turned[0:1]], axis=0)
    return jnp.where(lane(v.shape) < 128 - shift, turned, below)


def in_ring(shift):
    place = sublane((4, 128)) * 128 + lane((4, 128)) - shift
    place = jnp.where(place < 0, place + 512, place)
    return place < OWN


def load_flat(ref, scratch):
    scratch[...] = jnp.zeros_like(scratch)
    for k in range(3):
        scratch[k, :] = ref[pl.ds(128 * k, 128)]
    scratch[3, 0 : OWN - 384] = ref[pl.ds(384, OWN - 384)]
    return scratch[0:4, :]


def store_flat(ref, v):
    for k in range(3):
        ref[pl.ds(128 * k, 128)] = v[k]
    ref[pl.ds(384, OWN - 384)] = v[3, 0 : OWN - 384]


def fetch(pairs, sems):
    copies = [pltpu.make_async_copy(src, dst, sems.at[k]) for k, (src, dst) in enumerate(pairs)]
    for copy in copies:
        copy.start()
    return copies


def even_first(axis, first, last):
    even = jnp.full(first.shape, lax.rem(lax.axis_index(axis), 2), jnp.int32) == 0
    return jnp.where(even, last, first), jnp.where(even, first, last)


def start_kernel(
    core_ref, x_ref, one_ref, two_ref, ut_ref, ot_ref, cot_ref, take_ref, give_ref, kind_ref,
    send_ref, near_ref, far_ref, inner_ref, ring_ref, one_out, two_out, ut_out, ot_out, cot_out, take_out, give_out, kind_out,
    own, flat, block, sems,
):
    copies = fetch(
        (
            (core_ref, own), (x_ref, inner_ref), (one_ref, one_out), (two_ref, two_out), (ut_ref, ut_out),
            (ot_ref, ot_out), (take_ref, take_out), (kind_ref, kind_out), (give_ref, give_out), (cot_ref, cot_out),
        ),
        sems,
    )
    copies[0].wait()
    v = to_ring(load_flat(own, flat), ring_shift())
    ring_ref[...] = v
    rows = jnp.concatenate([v, v, v, v], axis=0).astype(BF)
    for k in range(8):
        block[16 * k : 16 * k + 16, :] = rows
    sends = fetch([(block, send_ref.at[pl.ds(128 * k, 128)]) for k in range(4)], sems.at[pl.ds(10, 4)])
    copies[1].wait()
    for f in range(FRAMES):
        first, last = inner_ref[f, 0].astype(F32), inner_ref[f, ROWS - 1].astype(F32)
        one, two = even_first("rows", first, last)
        near_ref[f] = one.astype(BF)
        far_ref[f] = two.astype(BF)
    for copy in copies[2:] + sends:
        copy.wait()


def columns_kernel(inner_ref, two_ref, one_ref, above_ref, below_ref, left_ref, right_ref, low, high):
    for f in range(FRAMES):
        below, above = even_first("rows", two_ref[f].astype(F32), one_ref[f].astype(F32))
        above_ref[8 * f : 8 * f + 8, :] = above
        below_ref[8 * f : 8 * f + 8, :] = below
        for y in range(8):
            tile = above if y == 0 else below if y == 7 else inner_ref[f, y - 1].astype(F32)
            low[8 * f + y : 8 * f + y + 1, :] = tile[0:1, :]
            high[8 * f + y : 8 * f + y + 1, :] = tile[7:8, :]
    one, two = even_first("cols", low[...], high[...])
    left_ref[...] = one.astype(BF)
    right_ref[...] = two.astype(BF)


def shifted(tile, left, right, bounds, period):
    at = lane(tile.shape) % period
    row = sublane(tile.shape)
    back = jnp.where(row == 0, left, pltpu.roll(tile, 1, axis=0))
    ahead = jnp.where(row == 7, right, pltpu.roll(tile, 7, axis=0))
    return jnp.where(at < bounds[0], back, jnp.where(at < bounds[1], tile, ahead))


def prepare_kernel(_, x_ref, ut_ref, one_ref, two_ref, own_ref, wide_ref, utp_ref, u_ref, ring_ref, flat):
    row = sublane((256, 64))
    at = row % 128
    pick = (lane((256, 64)) == (at % 32) * 2 + row // 128) & (at < 96)
    half_row = sublane((64, 64))
    half_pick = lane((64, 64)) == (half_row % 32) * 2 + half_row // 32
    wide = dot(pick.astype(BF), ut_ref[...]).astype(BF)
    wide_ref[...] = wide
    utp = dot(half_pick.astype(BF), ut_ref[...])
    utp_ref[...] = utp.astype(BF)
    u_ref[...] = utp.T.astype(BF)
    own_ref[...] = dot_nt(x_ref[...], wide).astype(BF).astype(F32)
    shift = ring_shift()
    ring_ref[0] = to_ring(load_flat(one_ref, flat), shift)
    ring_ref[1] = to_ring(load_flat(two_ref, flat), shift)


def stack_rows(tiles, out_ref):
    for b in range(3):
        out_ref[b, 0:48, :] = jnp.zeros((48, 256), BF)
        out_ref[b, 192:240, :] = jnp.zeros((48, 256), BF)
        for f in range(FRAMES):
            rows = tiles[f, b : b + ROWS].reshape(48, 256)
            out_ref[b, 48 * f + 48 : 48 * f + 96, :] = rows.astype(BF)


def stack_inputs(own_ref, wide_ref, above_ref, below_ref, two_ref, one_ref, q_ref, tiles, edge, rims):
    wide = wide_ref[...]

    def project(v):
        return dot_nt(v.astype(BF), wide).astype(BF).astype(F32)

    rims[0] = project(above_ref[...])
    rims[1] = project(below_ref[...])
    right, left = even_first("cols", project(two_ref[...]), project(one_ref[...]))
    edge[0] = left
    edge[1] = right
    for f in range(FRAMES):
        for y in range(8):
            k = 8 * f + y
            if y in (0, 7):
                tile = rims[y // 7, 8 * f : 8 * f + 8, :]
            else:
                at = 48 * f + 8 * (y - 1)
                tile = own_ref[at : at + 8, :]
            left = jnp.broadcast_to(edge[0, k : k + 1, :], (8, 256))
            right = jnp.broadcast_to(edge[1, k : k + 1, :], (8, 256))
            tiles[f, y] = shifted(tile, left, right, (32, 64), 128)
    stack_rows(tiles, q_ref)


def core_index(shape):
    return jnp.full(shape, lax.rem(lax.axis_index("rows"), 2), jnp.int32)


def gather_table(mine_ref, other_ref, take_ref, kind_ref, table_ref):
    kind = kind_ref[...]
    take = take_ref[...]
    first = core_index((128, 128)) == 0
    for g in range(4):
        mine, other = mine_ref[128 * g : 128 * g + 128, :], other_ref[128 * g : 128 * g + 128, :]
        block = jnp.concatenate([jnp.where(first, mine, other), jnp.where(first, other, mine)], axis=0)
        none = jnp.zeros_like(block)
        both = jnp.concatenate(
            [jnp.where(kind == 0, block, none), jnp.where(kind == 1, block, none)], axis=0
        )
        table_ref[216 * g : 216 * g + 216, :] = dot(take, both)


def inside(lanes, at):
    return (lanes >= at) & (lanes < at + 64)


def gradient_blocks(half, grads, pixels, give_ref, kind_ref, blocks):
    wrapped = kind_ref[0:128, :] == 1
    for g in range(4):
        source = grads[216 * g : 216 * g + 216, :].astype(BF)
        part = dot(give_ref[half], source)
        blocks[128 * g : 128 * g + 128, :] = jnp.where(wrapped, part[128:256], part[0:128])
    lanes = lane((16, 128))
    row = lax.axis_index("rows")
    for a, (c, j, at) in enumerate(RELAYS):
        slot = sublane((16, 128)) + 16 * a
        across = ((slot < 48) | (slot >= 84)).astype(jnp.int32)
        goes = lax.rem(jnp.full((16, 128), row + half, jnp.int32) + across, 2) == 0
        pixel = jnp.where(goes, pixels[16 * a : 16 * a + 16, :], 0.0)
        if at % 64:
            pixel = pltpu.roll(pixel, at, axis=1)
        spot = pl.ds(4 * c + j, 16, stride=32)
        blocks[spot, :] = jnp.where(inside(lanes, at), pixel, blocks[spot, :])


def table_kernel(mine_ref, other_ref, take_ref, kind_ref, table_out, weights_ref, table):
    gather_table(mine_ref, other_ref, take_ref, kind_ref, table)
    table_out[...] = table[...].astype(BF)
    none = jnp.zeros((32, 64), BF)
    for k in range(9):
        part = table[96 * k : 96 * k + 96, :]
        weights_ref[k, 0:96, :] = part[:, 0:64].astype(BF)
        weights_ref[k, 96:128, :] = none
        weights_ref[k, 128:224, :] = part[:, 64:128].astype(BF)
        weights_ref[k, 224:256, :] = none


def forward_kernel(
    own_ref, wide_ref, above_ref, below_ref, two_ref, one_ref, weights_ref, cot_ref, ot_ref, give_ref, kind_ref,
    send_ref, grads, pixels, outp_ref, border, blocks, q_ref, tiles, edge, rims,
):
    stack_inputs(own_ref, wide_ref, above_ref, below_ref, two_ref, one_ref, q_ref, tiles, edge, rims)
    total = jnp.zeros((CELLS, 64), F32)
    for a in range(3):
        for b in range(3):
            total = total + dot(q_ref[b, 48 * a : 48 * a + CELLS, :], weights_ref[3 * a + b])
    mid = total.astype(BF)
    pre = dot(mid, ot_ref[...])
    sig = jax.nn.sigmoid(pre)
    slope = (cot_ref[...].astype(F32) * sig * (1.0 + pre * (1.0 - sig))).astype(BF)
    ot = ot_ref[...]
    out_t = dot_nt(ot, slope).astype(BF)
    wide = jnp.concatenate([ot, ot, ot, ot], axis=0)
    outp = dot_nt(slope, wide).astype(BF).astype(F32)
    outp_ref[...] = outp
    border[...] = outp[:, 0:128]
    for f in range(FRAMES):
        pixels[8 * f : 8 * f + 8, :] = border[48 * f : 48 * f + 8, :]
        pixels[24 + 8 * f : 32 + 8 * f, :] = border[48 * f + 40 : 48 * f + 48, :]
    pixels[48:66, :] = border[pl.ds(0, 18, stride=8), :]
    pixels[66:84, :] = border[pl.ds(7, 18, stride=8), :]
    for k, cell in enumerate((0, 7, 40, 47)):
        pixels[84 + 3 * k : 87 + 3 * k, :] = border[pl.ds(cell, 3, stride=48), :]
    for a in range(3):
        for b in range(3):
            k = 3 * a + b
            part = dot(out_t, q_ref[b, 48 * a : 48 * a + CELLS, :])
            stack = jnp.concatenate([part[:, 0:128], part[:, 128:256]], axis=0)
            grads[96 * k : 96 * k + 96, :] = stack.T[0:96, :]
    gradient_blocks(1 - lax.rem(lax.axis_index("rows"), 2), grads, pixels, give_ref, kind_ref, blocks)
    send_ref[...] = blocks[...].astype(BF)


def keep_kernel(grads, pixels, give_ref, kind_ref, keep_ref):
    gradient_blocks(lax.rem(lax.axis_index("rows"), 2), grads, pixels, give_ref, kind_ref, keep_ref)


def add_kernel(keep_ref, got_ref, send_ref):
    send_ref[...] = (keep_ref[...] + got_ref[...].astype(F32)).astype(BF)


def adam_kernel(got_ref, core_ref, ring_ref, send_ref, next_ref, passed):
    total = jnp.zeros((8, 128), F32)
    passed[0:40, :] = jnp.zeros((40, 128), F32)
    passed[552:592, :] = jnp.zeros((40, 128), F32)
    for g in range(4):
        part = got_ref[128 * g : 128 * g + 128, :].astype(F32)
        passed[128 * g + 40 : 128 * g + 168, :] = part
        total = total + part.reshape(16, 8, 128).sum(axis=0)
    grad = (total[0:4] + total[4:8]) * (1.0 / 192.0)
    core, one, two = core_ref[...], ring_ref[0], ring_ref[1]
    one = beta_one * one + (1.0 - beta_one) * grad
    two = beta_two * two + (1.0 - beta_two) * grad * grad
    core = core - learn_rate * (one / fix_one) / (jnp.sqrt(two / fix_two) + epsilon)
    next_ref[0] = core
    next_ref[1] = one
    next_ref[2] = two
    own = jnp.where(in_ring(ring_shift()), core, 0.0)
    own = jnp.concatenate([own, own], axis=0)
    row, col = lax.axis_index("rows"), lax.axis_index("cols")
    slot, parity, mask = lax.div(row, 2), lax.rem(row, 2), jnp.zeros((8, 128), jnp.bool_)
    for a, (c, j, at) in enumerate(RELAYS):
        slot = slot + jnp.where(col == c, 16 * a, 0)
        spot = (sublane((8, 128)) % 4 == j) & inside(lane((8, 128)), at)
        mask = mask | (spot & (jnp.full((8, 128), col, jnp.int32) == c))
    up, right = 0, 0
    for first, count, rows, cols in SLOTS:
        here = (slot >= first) & (slot < first + count)
        up = up + jnp.where(here, rows, 0)
        right = right + jnp.where(here, cols, 0)
    source = lax.rem(parity - up + 2, 2)
    chips = lax.div(source + up - parity + 2, 2) - 1
    start = 40 - 4 * (8 * chips + right)
    for k in range(32):
        upper = passed[pl.ds(start + 16 * k, 8), :]
        lower = passed[pl.ds(start + 16 * k + 8, 8), :]
        block = jnp.concatenate([jnp.where(mask, upper, own), jnp.where(mask, lower, own)], axis=0)
        send_ref[16 * k : 16 * k + 16, :] = block.astype(BF)


def flat_kernel(next_ref, core_ref, one_ref, two_ref):
    shift = ring_shift()
    for k, ref in enumerate((core_ref, one_ref, two_ref)):
        store_flat(ref, from_ring(next_ref[k], shift))


def turn_kernel(table_ref, back_ref):
    for k in range(9):
        for c in range(3):
            t = 3 * k + c
            part = table_ref[32 * t : 32 * t + 32, :].astype(F32).T
            cube = jnp.concatenate([part[0:64], part[64:128]], axis=1)
            back_ref[k, 64 * (2 - c) : 64 * (2 - c) + 64, :] = cube.astype(BF)


def backward_kernel(mine_ref, outp_ref, back_ref, utp_ref, grad_ref, got, pixels, tiles, qs):
    row, col = lax.axis_index("rows"), lax.axis_index("cols")
    got[...] = mine_ref[...].astype(F32)
    for a, (c, j, at) in enumerate(RELAYS):
        pixel = got[pl.ds(4 * c + j, 16, stride=32), :]
        pixels[16 * a : 16 * a + 16, 0:128] = pltpu.roll(pixel, 128 - at, axis=1) if at else pixel
    spread = (sublane((64, 256)) == lane((64, 256)) % 64).astype(BF)
    pixels[...] = dot(pixels[:, 0:64].astype(BF), spread)
    zero = jnp.zeros((8, 256), F32)

    def kept(flag, v):
        return jnp.where(jnp.full((8, 256), flag.astype(jnp.int32), jnp.int32) > 0, v, zero)

    def spot(k):
        return jnp.broadcast_to(pixels[k : k + 1, :], (8, 256))

    for f in range(FRAMES):
        for y in range(8):
            if y == 0:
                tile, left, right = pixels[24 + 8 * f : 32 + 8 * f, :], spot(93 + f), spot(90 + f)
            elif y == 7:
                tile, left, right = pixels[8 * f : 8 * f + 8, :], spot(87 + f), spot(84 + f)
            else:
                at = 48 * f + 8 * (y - 1)
                tile = outp_ref[at : at + 8, :]
                left, right = spot(66 + 6 * f + y - 1), spot(48 + 6 * f + y - 1)
            tile = shifted(tile, kept(col > 0, left), kept(col < 7, right), (64, 128), 256)
            if y == 0:
                tile = kept(row > 0, tile)
            elif y == 7:
                tile = kept(row < 31, tile)
            tiles[f, y] = tile
    stack_rows(tiles, qs)
    total = jnp.zeros((CELLS, 64), F32)
    for a in range(3):
        for b in range(3):
            rows = qs[2 - b, 48 * (2 - a) : 48 * (2 - a) + CELLS, :]
            total = total + dot(rows[:, 0:192], back_ref[3 * a + b])
    grad_ref[...] = dot(total.astype(BF), utp_ref[...]).astype(BF)

def build_kernel(mine_ref, other_ref, u_ref, ot_ref, take_ref, kind_ref, out_ref, table, half, result, sems):
    gather_table(mine_ref, other_ref, take_ref, kind_ref, table)
    cube = table[...].astype(BF)
    even = dot(cube[:, 0:64], ot_ref[...]).astype(BF)
    odd = dot(cube[:, 64:128], ot_ref[...]).astype(BF)
    for t in range(27):
        half[t, 0:32, :] = even[32 * t : 32 * t + 32]
        half[t, 32:64, :] = odd[32 * t : 32 * t + 32]
    u = u_ref[...]

    def store(a):
        part = pl.ds(3 * a, 3)
        return pltpu.make_async_copy(result.at[part], out_ref.at[part], sems.at[a])

    for a in range(9):
        for t in range(3 * a, 3 * a + 3):
            result[t] = dot(u, half[t]).astype(BF)
        store(a).start()
    for a in range(9):
        store(a).wait()


def call(kernel, args, outs, scratch, flops=10**7):
    def spec(far):
        return pl.BlockSpec(memory_space=pltpu.HBM if far else pltpu.VMEM)

    return pl.pallas_call(
        kernel,
        out_shape=[jax.ShapeDtypeStruct(shape, dtype) for shape, dtype, _ in outs],
        in_specs=[spec(far) for _, far in args],
        out_specs=[spec(far) for _, _, far in outs],
        scratch_shapes=scratch,
        compiler_params=pltpu.CompilerParams(vmem_limit_bytes=32 << 20),
        cost_estimate=pl.CostEstimate(flops=flops, bytes_accessed=10**5, transcendentals=0),
    )(*[pltpu.with_memory_space_constraint(arg, pltpu.HBM) if far else arg for arg, far in args])


def near(*args):
    return [(arg, False) for arg in args]


def far(*args):
    return [(arg, True) for arg in args]


def swap(one, two, axis):
    count = lax.axis_size(axis)
    pairs = [[(i, i + 1) for i in range(k, count - 1, 2)] for k in range(2)]
    two, one = (
        lax.ppermute(x, axis, forward + [(b, a) for a, b in forward]) for x, forward in ((two, pairs[1]), (one, pairs[0]))
    )
    return one, two


def device(k, chip, col):
    return 8 * (2 * chip + k) + col


ORDER = [[device(k, chip, col) for chip in range(16) for col in range(8)] for k in range(2)]


def exchange(x):
    return lax.all_to_all(x, AXES, 0, 0, tiled=True, axis_index_groups=ORDER[::-1])


def in_chip(x):
    return lax.ppermute(x, "rows", [(r, r ^ 1) for r in range(32)])


def body(frames_in, cotangent, core, moment_one, moment_two, u_in, u_out):
    take, give, kind = ring_tables()
    take, give, kind = jnp.asarray(take, BF), jnp.asarray(give, BF), jnp.asarray(kind, F32)
    vm, dma = pltpu.VMEM, pltpu.SemaphoreType.DMA
    rim = (FRAMES * 8, 256)
    row = (FRAMES, 8, 256)

    send, one, two, inner, core_ring, m_one, m_two, ut, ot, cot, take, give, kind = call(
        start_kernel,
        far(
            core, frames_in, moment_one, moment_two, u_in.T, u_out.T, cotangent.reshape(CELLS, 256), take, give, kind,
        ),
        [
            ((512, 128), BF, True), (row, BF, False), (row, BF, False), ((FRAMES, ROWS, COLS, 256), BF, False),
            ((4, 128), F32, False), ((OWN,), F32, False), ((OWN,), F32, False), ((64, 256), BF, False),
            ((64, 256), BF, False), ((CELLS, 256), BF, False), ((216, 512), BF, False), ((2, 256, 216), BF, False),
            ((256, 128), F32, False),
        ],
        [vm((OWN,), F32), vm((8, 128), F32), vm((128, 128), BF), dma((14,))],
    )
    one, two = swap(one, two, "rows")
    mine = exchange(send)
    above, below, one, two = call(
        columns_kernel,
        near(inner, two, one),
        [(rim, F32, False), (rim, F32, False), (rim, BF, False), (rim, BF, False)],
        [vm(rim, F32), vm(rim, F32)],
        flops=10**10,
    )
    own, wide, utp, u, ring = call(
        prepare_kernel,
        near(above, inner.reshape(CELLS, 256), ut, m_one, m_two),
        [
            ((CELLS, 256), F32, False), ((256, 256), BF, False), ((64, 256), BF, False), ((256, 64), BF, False),
            ((2, 4, 128), F32, False),
        ],
        [vm((8, 128), F32)],
        flops=10**10,
    )
    mine, _ = lax.optimization_barrier((mine, above))
    other = in_chip(mine)
    table, weights = call(
        table_kernel,
        near(mine, other, take, kind),
        [((TABLE, 128), BF, False), ((9, 256, 64), BF, False)],
        [vm((TABLE, 128), F32)],
        flops=10000000000,
    )
    one, two = swap(one, two, "cols")
    send, grads, pixels, outp = call(
        forward_kernel,
        near(own, wide, above, below, two, one, weights, cot, ot, give, kind),
        [((512, 128), BF, False), ((TABLE, 128), F32, False), ((96, 128), F32, False), ((CELLS, 256), F32, False)],
        [
            vm((CELLS, 128), F32), vm((512, 128), F32), vm((3, 240, 256), BF), vm((FRAMES, 8, 8, 256), F32),
            vm((2, SIDE, 256), F32), vm((2, SIDE, 256), F32),
        ],
        flops=10**7,
    )
    got = in_chip(send)
    (keep,) = call(keep_kernel, near(grads, pixels, give, kind), [((512, 128), F32, False)], [], flops=10**9)
    (send,) = call(add_kernel, near(keep, got), [((512, 128), BF, False)], [])
    got = exchange(send)
    send, latest = call(
        adam_kernel,
        near(got, core_ring, ring),
        [((512, 128), BF, False), ((3, 4, 128), F32, False)],
        [vm((592, 128), F32)],
    )
    mine = exchange(send)
    (back,) = call(turn_kernel, near(table), [((9, 192, 64), BF, False)], [])
    core_next, one_next, two_next = call(flat_kernel, near(latest), [((OWN,), F32, False)] * 3, [])
    mine, back, core_next, one_next, two_next = lax.optimization_barrier((mine, back, core_next, one_next, two_next))
    other = in_chip(mine)
    (frames_grad,) = call(
        backward_kernel,
        near(mine, outp, back, utp),
        [((CELLS, 256), BF, False)],
        [vm((512, 128), F32), vm((96, 256), F32), vm((FRAMES, 8, 8, 256), F32), vm((3, 240, 256), BF)],
        flops=10**9,
    )
    other, frames_grad = lax.optimization_barrier((other, frames_grad))
    (kernel_next,) = call(
        build_kernel,
        near(mine, other, u, ot, take, kind),
        [((27, 256, 256), BF, True)],
        [vm((TABLE, 128), F32), vm((27, 64, 256), BF), vm((27, 256, 256), BF), dma((9,))],
    )
    frames_grad = frames_grad.reshape(FRAMES, ROWS, COLS, 256)
    return frames_grad, core_next, one_next, two_next, kernel_next


def solution(mesh):
    in_specs = (
        P(None, "rows", "cols", None),
        P(None, "rows", "cols", None),
        P(AXES),
        P(AXES),
        P(AXES),
        P(),
        P(),
    )
    out_specs = (
        P(None, "rows", "cols", None),
        P(AXES),
        P(AXES),
        P(AXES),
        P(),
    )
    return jax.shard_map(body, mesh=mesh, in_specs=in_specs, out_specs=out_specs, check_vma=False)
```
